32 devices in a mesh: dp: 8 (over z, y), seq: 2 (over x), shard: 2 (over core).
Axes of the slice: x: 2, y: 2, z: 4, core: 2. Of those that a mesh axis runs over, the one named last changes fastest.
Arguments:
- inputs: float32 [16, 256, 512], P(('dp', 'shard'), 'seq'), may hold values from -5 to 5
- cotangent: float32 [16, 256, 512], P(('dp', 'shard'), 'seq'), may hold values from -6 to 6
- w_up: float32 [512, 4096], P(('dp', 'seq', 'shard')), may hold values from -0.25 to 0.25
- w_down: float32 [512, 4096], P(('dp', 'seq', 'shard')), may hold values from -0.25 to 0.25
- w_qkv: float32 [512, 1536], P(('dp', 'seq', 'shard')), may hold values from -0.25 to 0.25
- w_out: float32 [512, 512], P(('dp', 'seq', 'shard')), may hold values from -1.5 to 1.5
- w_glu: float32 [512, 1024], P(('dp', 'seq', 'shard')), may hold values from -0.25 to 0.25
- w_point: float32 [512, 512], P(('dp', 'seq', 'shard')), may hold values from -0.375 to 0.375
- vectors: float32 [512, 7], P(('dp', 'seq', 'shard')), may hold values from -2.5 to 2.5, as said below
- depth_kernel: float32 [512, 31], P(('dp', 'seq', 'shard')), may hold values from -1 to 1
- rel_bias: float32 [128, 8], P(('dp', 'seq', 'shard')), may hold values from -2.5 to 2.5
- bucket_table: int32 [511], replicated, may hold values from 0 to 127
- m_up: float32 [512, 4096], P(('dp', 'seq', 'shard')), may hold values from -128 to 128
- m_down: float32 [512, 4096], P(('dp', 'seq', 'shard')), may hold values from -128 to 128
- m_qkv: float32 [512, 1536], P(('dp', 'seq', 'shard')), may hold values from -128 to 128
- m_out: float32 [512, 512], P(('dp', 'seq', 'shard')), may hold values from -2000 to 2000
- m_glu: float32 [512, 1024], P(('dp', 'seq', 'shard')), may hold values from -128 to 128
- m_point: float32 [512, 512], P(('dp', 'seq', 'shard')), may hold values from -2000 to 2000
- m_vectors: float32 [512, 7], P(('dp', 'seq', 'shard')), may hold values from -400 to 400
- m_depth: float32 [512, 31], P(('dp', 'seq', 'shard')), may hold values from -400 to 400
- m_rel: float32 [128, 8], P(('dp', 'seq', 'shard')), may hold values from -400 to 400
Outputs:
- outputs: float32 [16, 256, 512], P(('dp', 'shard'), 'seq')
- input_grad: float32 [16, 256, 512], P(('dp', 'shard'), 'seq')
- grad_up: float32 [512, 4096], P(('dp', 'seq', 'shard'))
- grad_down: float32 [512, 4096], P(('dp', 'seq', 'shard'))
- grad_qkv: float32 [512, 1536], P(('dp', 'seq', 'shard'))
- grad_out: float32 [512, 512], P(('dp', 'seq', 'shard'))
- grad_glu: float32 [512, 1024], P(('dp', 'seq', 'shard'))
- grad_point: float32 [512, 512], P(('dp', 'seq', 'shard'))
- grad_vectors: float32 [512, 7], P(('dp', 'seq', 'shard'))
- grad_depth: float32 [512, 31], P(('dp', 'seq', 'shard'))
- grad_rel: float32 [128, 8], P(('dp', 'seq', 'shard'))
- new_up: float32 [512, 4096], P(('dp', 'seq', 'shard'))
- new_down: float32 [512, 4096], P(('dp', 'seq', 'shard'))
- new_qkv: float32 [512, 1536], P(('dp', 'seq', 'shard'))
- new_out: float32 [512, 512], P(('dp', 'seq', 'shard'))
- new_glu: float32 [512, 1024], P(('dp', 'seq', 'shard'))
- new_point: float32 [512, 512], P(('dp', 'seq', 'shard'))
- new_vectors: float32 [512, 7], P(('dp', 'seq', 'shard'))
- new_depth: float32 [512, 31], P(('dp', 'seq', 'shard'))
- new_rel: float32 [128, 8], P(('dp', 'seq', 'shard'))
- next_m_up: float32 [512, 4096], P(('dp', 'seq', 'shard'))
- next_m_down: float32 [512, 4096], P(('dp', 'seq', 'shard'))
- next_m_qkv: float32 [512, 1536], P(('dp', 'seq', 'shard'))
- next_m_out: float32 [512, 512], P(('dp', 'seq', 'shard'))
- next_m_glu: float32 [512, 1024], P(('dp', 'seq', 'shard'))
- next_m_point: float32 [512, 512], P(('dp', 'seq', 'shard'))
- next_m_vectors: float32 [512, 7], P(('dp', 'seq', 'shard'))
- next_m_depth: float32 [512, 31], P(('dp', 'seq', 'shard'))
- next_m_rel: float32 [128, 8], P(('dp', 'seq', 'shard'))
The draws below stay inside these ranges and needn't reach their ends.
Inputs may be any that keep to these rules, and one draw needn't show every extreme that they name: `bucket_table`: entry r is the bucket of the relative offset r - 255. `vectors`: LayerNorm and BatchNorm gains near one in columns 0 to 5, the BatchNorm bias in column 6.
All inputs are finite; a program needn't handle non-finite values.
Results may differ from the reference program's by a relative error of at most 0.019.
Values may be sent and summed in bfloat16 or wider, within the bound.
A program may use at most 192 MiB of HBM per device.

```python
import jax
import jax.numpy as jnp
from jax import lax

D = 512
FF = 2048
H = 8
DH = 64
K = 31
NB = 128
SEQ_LEN = 256
BATCH = 16
TOKENS = 4096


def draw_inputs(key, part):
    noise_key, level_key = jax.random.split(jax.random.fold_in(key, 37))
    order = jnp.arange(BATCH, dtype=jnp.float32)[:, None, None]
    rise = 0.4 + 0.8 * order / (BATCH - 1)
    noise = jax.random.normal(noise_key, (BATCH, SEQ_LEN, D), jnp.float32)
    levels = jnp.clip(jax.random.normal(level_key, (BATCH, 1, D), jnp.float32), -1.5, 1.5)
    return jnp.clip(noise + rise * levels, -5.0, 5.0)


def draw_vectors(key, part):
    first_key, second_key = jax.random.split(jax.random.fold_in(key, 11))
    gain_values = 1.0 + 0.15 * jax.random.uniform(first_key, (D, 7), jnp.float32, -1.0, 1.0)
    shifts = jnp.clip(0.5 * jax.random.normal(second_key, (D, 7), jnp.float32), -2.5, 2.5)
    column = jnp.arange(7)[None, :]
    return jnp.where(column == 6, shifts, gain_values)


def draw_rel_bias(key, part):
    first_key = jax.random.fold_in(key, 23)
    return jnp.clip(jax.random.normal(first_key, (NB, H), jnp.float32), -2.5, 2.5)


def square_moment(key, size):
    row = jnp.arange(size)[:, None]
    col = jnp.arange(size)[None, :]
    noise = jnp.clip(jax.random.normal(key, (size, size), jnp.float32), -6.0, 6.0)
    diagonal = jnp.where(row == col, 60.0 * jnp.sqrt(jnp.float32(size)), 0.0)
    return jnp.clip(20.0 * noise + diagonal, -2000.0, 2000.0)


def draw_m_out(key, part):
    return square_moment(jax.random.fold_in(key, 41), D)


def draw_m_point(key, part):
    return square_moment(jax.random.fold_in(key, 43), D)


def rising_moment(key, rows, cols):
    place = jnp.arange(rows, dtype=jnp.float32)[:, None] / (rows - 1)
    noise = jnp.clip(jax.random.normal(key, (rows, cols), jnp.float32), -6.0, 6.0)
    scale = 20.0 * jnp.power(6.0, 2.0 * place - 1.0)
    return jnp.clip(noise * scale, -400.0, 400.0)


def draw_m_vectors(key, part):
    return rising_moment(jax.random.fold_in(key, 61), D, 7)


def draw_m_depth(key, part):
    return rising_moment(jax.random.fold_in(key, 67), D, K)


def draw_m_rel(key, part):
    return rising_moment(jax.random.fold_in(key, 71), NB, H)


def touch_ends(drawn, key, smallest, top_value):
    longest = drawn.shape.index(max(drawn.shape))
    spots = []
    for shift in (0, 1):
        where = [jax.random.randint(jax.random.fold_in(key, axis), (), 0, length) for axis, length in enumerate(drawn.shape)]
        where[longest] = (where[longest] + shift) % drawn.shape[longest]
        spots.append(tuple(where))
    return drawn.at[spots[0]].set(smallest).at[spots[1]].set(top_value)


def block_scale(stream_key, shape, pieces, least, high):
    level = 1.0
    for dim, shards_of in pieces:
        draws = jax.random.uniform(jax.random.fold_in(jax.random.fold_in(stream_key, 6), dim), (shards_of,), jnp.float32, least / len(pieces), high / len(pieces))
        level = level * jnp.repeat(jnp.exp(draws), shape[dim] // shards_of).reshape((-1,) + (1,) * (len(shape) - 1 - dim))
    return level


def bell_draw(rng, extent, deviation, limit, shards=(), kind=jnp.bfloat16):
    factor_of = block_scale(rng, extent, shards, -0.22, 0.18) if shards else 1.0
    drawn = jax.random.normal(rng, extent, jnp.float32) * deviation * factor_of
    return jnp.minimum(jnp.maximum(drawn, -limit), limit).astype(kind)


def setup_inputs(seed: int = 0) -> dict:
    arg_keys = jax.random.split(jax.random.key(seed), 22)
    inputs = draw_inputs(jax.random.fold_in(arg_keys[21], 71), 0)
    cotangent = bell_draw(arg_keys[1], (BATCH, SEQ_LEN, D), 1.0, 6.0, ((0, 16), (1, 2)), jnp.float32)
    w_up = bell_draw(arg_keys[2], (D, 2 * FF), D ** -0.5, 0.25, ((0, 32),), jnp.float32)
    w_down = bell_draw(arg_keys[3], (D, 2 * FF), (FF // 4) ** -0.5, 0.25, ((0, 32),), jnp.float32)
    w_qkv = bell_draw(arg_keys[4], (D, 3 * D), D ** -0.5, 0.25, ((0, 32),), jnp.float32)
    w_out = bell_draw(arg_keys[5], (D, D), (max(1, D * 8 // SEQ_LEN)) ** -0.5, 1.5, ((0, 32),), jnp.float32)
    w_glu = bell_draw(arg_keys[6], (D, 2 * D), D ** -0.5, 0.25, ((0, 32),), jnp.float32)
    w_point = bell_draw(arg_keys[7], (D, D), (D // 2) ** -0.5, 0.375, ((0, 32),), jnp.float32)
    vectors = draw_vectors(jax.random.fold_in(arg_keys[21], 71), 0)
    depth_kernel = bell_draw(arg_keys[9], (D, K), K ** -0.5, 1.0, ((0, 32),), jnp.float32)
    rel_bias = draw_rel_bias(jax.random.fold_in(arg_keys[21], 71), 0)
    bucket_table = touch_ends(jax.random.randint(arg_keys[11], (2 * SEQ_LEN - 1,), 0, NB), jax.random.fold_in(arg_keys[11], 1), 0, NB - 1).astype(jnp.int32)
    m_up = bell_draw(arg_keys[12], (D, 2 * FF), 20.0, 128.0, ((0, 32),), jnp.float32)
    m_down = bell_draw(arg_keys[13], (D, 2 * FF), 20.0, 128.0, ((0, 32),), jnp.float32)
    m_qkv = bell_draw(arg_keys[14], (D, 3 * D), 20.0, 128.0, ((0, 32),), jnp.float32)
    m_out = draw_m_out(jax.random.fold_in(arg_keys[21], 71), 0)
    m_glu = bell_draw(arg_keys[16], (D, 2 * D), 20.0, 128.0, ((0, 32),), jnp.float32)
    m_point = draw_m_point(jax.random.fold_in(arg_keys[21], 71), 0)
    m_vectors = draw_m_vectors(jax.random.fold_in(arg_keys[21], 71), 0)
    m_depth = draw_m_depth(jax.random.fold_in(arg_keys[21], 71), 0)
    m_rel = draw_m_rel(jax.random.fold_in(arg_keys[21], 71), 0)
    return {"inputs": inputs, "cotangent": cotangent, "w_up": w_up, "w_down": w_down, "w_qkv": w_qkv, "w_out": w_out, "w_glu": w_glu, "w_point": w_point, "vectors": vectors, "depth_kernel": depth_kernel, "rel_bias": rel_bias, "bucket_table": bucket_table, "m_up": m_up, "m_down": m_down, "m_qkv": m_qkv, "m_out": m_out, "m_glu": m_glu, "m_point": m_point, "m_vectors": m_vectors, "m_depth": m_depth, "m_rel": m_rel}


EPS_NORM = 1e-05
EPS_BATCH = 1e-05
EPS_SCALE = 1e-06
MOMENTUM = 0.9
RATE_MATRIX = 1.0
RATE_VECTOR = 0.25
COEF_A = 3.4445
COEF_B = -4.775
COEF_C = 2.0315
HIGHEST = lax.Precision.HIGHEST

def lowered(values):
    return lax.optimization_barrier(values.astype(jnp.bfloat16))

def widened(values):
    return values.astype(jnp.float32)

def matmul(left, right):
    return jnp.dot(left, right, preferred_element_type=jnp.float32)

def layer_norm(field, gain):
    centre = lax.optimization_barrier(jnp.mean(field, axis=-1, keepdims=True))
    shifted = field - centre
    inverse = lax.rsqrt(lax.optimization_barrier(jnp.mean(shifted * shifted, axis=-1, keepdims=True)) + EPS_NORM)
    normed = shifted * inverse
    return (normed * gain, normed, inverse)

def norm_back(grad_out, normed, inverse, gain):
    scaled = grad_out * gain
    grad_in = inverse * (scaled - lax.optimization_barrier(jnp.mean(scaled, axis=-1, keepdims=True)) - normed * lax.optimization_barrier(jnp.mean(scaled * normed, axis=-1, keepdims=True)))
    return (grad_in, lax.optimization_barrier(jnp.sum(grad_out * normed, axis=0)))

def silu_slope(values):
    sigma = jax.nn.sigmoid(values)
    return sigma * (1.0 + values * (1.0 - sigma))

def ffn_forward(field, gain, w_in, w_back):
    normed_out, normed, inverse = layer_norm(field, gain)
    lifted = lowered(normed_out)
    hidden_pre = matmul(lifted, w_in)
    hidden_act = lowered(jax.nn.silu(hidden_pre))
    return (field + 0.5 * matmul(hidden_act, w_back.T), (lifted, hidden_pre, hidden_act, normed, inverse))

def ffn_backward(grad, saved, gain, w_in, w_back):
    lifted, hidden_pre, hidden_act, normed, inverse = saved
    grad_branch = lowered(0.5 * grad)
    grad_back = matmul(grad_branch.T, hidden_act)
    grad_act = matmul(grad_branch, w_back)
    grad_pre = lowered(grad_act * silu_slope(hidden_pre))
    grad_in = matmul(lifted.T, grad_pre)
    grad_field, grad_gain = norm_back(matmul(grad_pre, w_in.T), normed, inverse, gain)
    return (grad + grad_field, grad_in, grad_back, grad_gain)

def depthwise(wide, kernel, count):
    total = wide[0:count] * kernel[:, 0]
    for tap_idx in range(1, K):
        total = total + wide[tap_idx:tap_idx + count] * kernel[:, tap_idx]
    return total

def attention_forward(field, gain, qkv_w, out_w, bias):
    normed_out, normed, inverse = layer_norm(field, gain)
    lifted = lowered(normed_out)
    projected = lowered(matmul(lifted, qkv_w))
    length = projected.shape[0]
    query = widened(projected[:, :D]).reshape(length, H, DH)
    keys = widened(projected[:, D:2 * D]).reshape(length, H, DH)
    values = widened(projected[:, 2 * D:]).reshape(length, H, DH)
    scores = jnp.einsum('ihd,jhd->hij', query, keys) * DH ** (-0.5) + bias
    row_max = lax.optimization_barrier(jnp.max(scores, axis=2, keepdims=True))
    shifted_exp = jnp.exp(scores - row_max)
    row_total = lax.optimization_barrier(jnp.sum(shifted_exp, axis=2, keepdims=True))
    prob_low = lowered(shifted_exp / row_total)
    attended = jnp.einsum('hij,jhd->ihd', widened(prob_low), values).reshape(length, D)
    log_total = row_max + jnp.log(row_total)
    attended_low = lowered(attended)
    saved = (lifted, normed, inverse, query, keys, values, log_total, attended, attended_low)
    return (field + matmul(attended_low, out_w), saved)

def attention_backward(grad, saved, gain, qkv_w, out_w, bias, index):
    lifted, normed, inverse, query, keys, values, log_total, attended, attended_low = saved
    length = grad.shape[0]
    grad_low = lowered(grad)
    grad_out = matmul(attended_low.T, grad_low)
    grad_attended = widened(lowered(matmul(grad_low, out_w.T)))
    delta = lax.optimization_barrier(jnp.sum((grad_attended * attended).reshape(length, H, DH), axis=2))
    scores = jnp.einsum('ihd,jhd->hij', query, keys) * DH ** (-0.5) + bias
    prob = jnp.exp(scores - log_total)
    prob_low = widened(lowered(prob))
    grad_heads = grad_attended.reshape(length, H, DH)
    grad_values = jnp.einsum('hij,ihd->jhd', prob_low, grad_heads)
    grad_prob = jnp.einsum('ihd,jhd->hij', grad_heads, values)
    grad_scores = prob * (grad_prob - delta.T[:, :, None])
    score_low = widened(lowered(grad_scores))
    grad_query = jnp.einsum('hij,jhd->ihd', score_low, keys) * DH ** (-0.5)
    grad_keys = jnp.einsum('hij,ihd->jhd', score_low, query) * DH ** (-0.5)
    grad_offsets = jax.ops.segment_sum(grad_scores.reshape(H, -1).T, index.reshape(-1), num_segments=2 * length - 1)
    grad_proj = lowered(jnp.concatenate([grad_query.reshape(length, D), grad_keys.reshape(length, D), grad_values.reshape(length, D)], axis=1))
    grad_qkv = matmul(lifted.T, grad_proj)
    grad_field, grad_gain = norm_back(matmul(grad_proj, qkv_w.T), normed, inverse, gain)
    return (grad + grad_field, grad_qkv, grad_out, grad_offsets, grad_gain)

def conv_forward(field, gain, glu_w, kernel):
    normed_out, normed, inverse = layer_norm(field, gain)
    lifted = lowered(normed_out)
    gates = matmul(lifted, glu_w)
    first_half = gates[:, :D]
    sig_gate = jax.nn.sigmoid(gates[:, D:])
    glu = first_half * sig_gate
    wide = jnp.pad(glu, ((K // 2, K // 2), (0, 0)))
    return (depthwise(wide, kernel, field.shape[0]), (lifted, normed, inverse, first_half, sig_gate, wide))

def conv_tail(grad_conv, grad_wide, saved, gain, glu_w, kernel):
    lifted, normed, inverse, first_half, sig_gate, wide = saved
    count = grad_conv.shape[0]
    grad_glu = grad_wide[K - 1:K - 1 + count] * kernel[:, 0]
    for tap_idx in range(1, K):
        grad_glu = grad_glu + grad_wide[K - 1 - tap_idx:K - 1 - tap_idx + count] * kernel[:, tap_idx]
    grad_kernel = jnp.stack([lax.optimization_barrier(jnp.sum(grad_conv * wide[tap_idx:tap_idx + count], axis=0)) for tap_idx in range(K)], axis=1)
    grad_gates = lowered(jnp.concatenate([grad_glu * sig_gate, grad_glu * first_half * sig_gate * (1.0 - sig_gate)], axis=1))
    grad_glu_w = matmul(lifted.T, grad_gates)
    grad_field, grad_gain = norm_back(matmul(grad_gates, glu_w.T), normed, inverse, gain)
    return (grad_field, grad_glu_w, grad_kernel, grad_gain)

def orthogonalize(matrix):
    iterate = matrix / (jnp.sqrt(jnp.sum(matrix * matrix)) + 1e-07)
    for iter_step in range(5):
        gram = jnp.dot(iterate, iterate.T, precision=HIGHEST)
        mixed = COEF_B * gram + COEF_C * jnp.dot(gram, gram, precision=HIGHEST)
        iterate = COEF_A * iterate + jnp.dot(mixed, iterate, precision=HIGHEST)
    return iterate

def vector_step(weight, moment, grad):
    updated = MOMENTUM * moment + grad
    scale = lax.rsqrt(lax.optimization_barrier(jnp.mean(updated * updated, axis=0)) + EPS_SCALE)
    return (weight - RATE_VECTOR * updated * scale, updated)

def reference(inputs, cotangent, w_up, w_down, w_qkv, w_out, w_glu, w_point, vectors, depth_kernel, rel_bias, bucket_table, m_up, m_down, m_qkv, m_out, m_glu, m_point, m_vectors, m_depth, m_rel):
    up_low = lowered(w_up)
    down_low = lowered(w_down)
    qkv_low = lowered(w_qkv)
    out_low = lowered(w_out)
    glu_low = lowered(w_glu)
    point_low = lowered(w_point)
    gains = widened(lowered(vectors))
    kernel = widened(lowered(depth_kernel))
    rel_values = widened(lowered(rel_bias))
    offsets = rel_values[bucket_table].T
    position = jnp.arange(SEQ_LEN, dtype=jnp.int32)
    index = (position[None, :] - position[:, None] + SEQ_LEN - 1).astype(jnp.int32)
    bias = offsets[:, index]
    up_first, up_second = (up_low[:, :FF], up_low[:, FF:])
    down_first, down_second = (down_low[:, :FF], down_low[:, FF:])

    def front(sequence):
        section_one, ffn_saved = ffn_forward(sequence, gains[:, 0], up_first, down_first)
        section_two, attn_saved = attention_forward(section_one, gains[:, 1], qkv_low, out_low, bias)
        conv, conv_saved = conv_forward(section_two, gains[:, 2], glu_low, kernel)
        return (ffn_saved, section_two, attn_saved, conv, conv_saved)

    def first_pass(total, sequence):
        conv = front(sequence)[3]
        return (total + lax.optimization_barrier(jnp.sum(conv, axis=0)), conv)
    conv_sum, conv_all = lax.scan(first_pass, jnp.zeros((D,), jnp.float32), inputs)
    mean = conv_sum / TOKENS
    variance = lax.optimization_barrier(jnp.sum(jnp.square(conv_all - mean), axis=(0, 1))) / TOKENS
    inv_std = lax.rsqrt(variance + EPS_BATCH)

    def second_pass(carry, items):
        sequence, grad_y = items
        ffn_saved, section_two, attn_saved, conv, conv_saved = front(sequence)
        normed_bn = (conv - mean) * inv_std
        batch_out = normed_bn * gains[:, 5] + gains[:, 6]
        swish_low = lowered(jax.nn.silu(batch_out))
        section_three = section_two + matmul(swish_low, point_low)
        section_four, tail_saved = ffn_forward(section_three, gains[:, 3], up_second, down_second)
        outputs, normed_five, inverse_five = layer_norm(section_four, gains[:, 4])
        grad_four, gain_four = norm_back(grad_y, normed_five, inverse_five, gains[:, 4])
        grad_three, grad_up_two, grad_down_two, gain_three = ffn_backward(grad_four, tail_saved, gains[:, 3], up_second, down_second)
        grad_three_low = lowered(grad_three)
        grad_point = matmul(swish_low.T, grad_three_low)
        grad_batch = matmul(grad_three_low, point_low.T) * silu_slope(batch_out)
        grad_normed = grad_batch * gains[:, 5]
        updates = (grad_up_two, grad_down_two, gain_three, gain_four, grad_point, lax.optimization_barrier(jnp.sum(grad_batch * normed_bn, axis=0)), lax.optimization_barrier(jnp.sum(grad_batch, axis=0)), lax.optimization_barrier(jnp.sum(grad_normed, axis=0)), lax.optimization_barrier(jnp.sum(grad_normed * normed_bn, axis=0)))
        return (jax.tree.map(jnp.add, carry, updates), (outputs, grad_normed, grad_three))
    zero_d = jnp.zeros((D,), jnp.float32)
    start_two = (jnp.zeros((D, FF), jnp.float32), jnp.zeros((D, FF), jnp.float32), zero_d, zero_d, jnp.zeros((D, D), jnp.float32), zero_d, zero_d, zero_d, zero_d)
    carry_two, (outputs_all, grad_normed_all, grad_three_all) = lax.scan(second_pass, start_two, (inputs, cotangent))
    grad_up_two, grad_down_two, gain_three, gain_four, grad_point, bn_gain_grad, bn_bias_grad, sum_normed, sum_cross = carry_two

    def third_pass(carry, items):
        sequence, grad_normed, grad_three = items
        ffn_saved, section_two, attn_saved, conv, conv_saved = front(sequence)
        normed_bn = (conv - mean) * inv_std
        grad_conv = inv_std * (grad_normed - sum_normed / TOKENS - normed_bn * sum_cross / TOKENS)
        grad_wide = jnp.pad(grad_conv, ((K // 2, K // 2), (0, 0)))
        grad_two_part, grad_glu, grad_kernel, gain_two = conv_tail(grad_conv, grad_wide, conv_saved, gains[:, 2], glu_low, kernel)
        grad_two = grad_three + grad_two_part
        grad_one, grad_qkv, grad_out, grad_offsets, gain_one = attention_backward(grad_two, attn_saved, gains[:, 1], qkv_low, out_low, bias, index)
        grad_input, grad_up_one, grad_down_one, gain_zero = ffn_backward(grad_one, ffn_saved, gains[:, 0], up_first, down_first)
        updates = (grad_up_one, grad_down_one, gain_zero, gain_one, gain_two, grad_qkv, grad_out, grad_glu, grad_kernel, grad_offsets)
        return (jax.tree.map(jnp.add, carry, updates), grad_input)
    start_three = (jnp.zeros((D, FF), jnp.float32), jnp.zeros((D, FF), jnp.float32), zero_d, zero_d, zero_d, jnp.zeros((D, 3 * D), jnp.float32), jnp.zeros((D, D), jnp.float32), jnp.zeros((D, 2 * D), jnp.float32), jnp.zeros((D, K), jnp.float32), jnp.zeros((2 * SEQ_LEN - 1, H), jnp.float32))
    carry_three, input_grad = lax.scan(third_pass, start_three, (inputs, grad_normed_all, grad_three_all))
    grad_up_one, grad_down_one, gain_zero, gain_one, gain_two, grad_qkv, grad_out, grad_glu, grad_depth, grad_offsets = carry_three
    grad_up = jnp.concatenate([grad_up_one, grad_up_two], axis=1)
    grad_down = jnp.concatenate([grad_down_one, grad_down_two], axis=1)
    grad_vectors = jnp.stack([gain_zero, gain_one, gain_two, gain_three, gain_four, bn_gain_grad, bn_bias_grad], axis=1)
    grad_rel = jax.ops.segment_sum(grad_offsets, bucket_table, num_segments=NB)
    next_m_up = MOMENTUM * m_up + grad_up
    next_m_down = MOMENTUM * m_down + grad_down
    next_m_qkv = MOMENTUM * m_qkv + grad_qkv
    next_m_out = MOMENTUM * m_out + grad_out
    next_m_glu = MOMENTUM * m_glu + grad_glu
    next_m_point = MOMENTUM * m_point + grad_point
    new_up = w_up - RATE_MATRIX * jnp.concatenate([orthogonalize(next_m_up[:, :FF]), orthogonalize(next_m_up[:, FF:])], axis=1)
    new_down = w_down - RATE_MATRIX * jnp.concatenate([orthogonalize(next_m_down[:, :FF]), orthogonalize(next_m_down[:, FF:])], axis=1)
    new_qkv = w_qkv - RATE_MATRIX * orthogonalize(next_m_qkv)
    new_out = w_out - RATE_MATRIX * orthogonalize(next_m_out)
    new_glu = w_glu - RATE_MATRIX * orthogonalize(next_m_glu)
    new_point = w_point - RATE_MATRIX * orthogonalize(next_m_point)
    new_vectors, next_m_vectors = vector_step(vectors, m_vectors, grad_vectors)
    new_depth, next_m_depth = vector_step(depth_kernel, m_depth, grad_depth)
    new_rel, next_m_rel = vector_step(rel_bias, m_rel, grad_rel)
    return (outputs_all, input_grad, grad_up, grad_down, grad_qkv, grad_out, grad_glu, grad_point, grad_vectors, grad_depth, grad_rel, new_up, new_down, new_qkv, new_out, new_glu, new_point, new_vectors, new_depth, new_rel, next_m_up, next_m_down, next_m_qkv, next_m_out, next_m_glu, next_m_point, next_m_vectors, next_m_depth, next_m_rel)
```

```python
import functools

import jax
import jax.numpy as jnp
from jax import lax
from jax.experimental import pallas as pl
from jax.experimental.pallas import tpu as pltpu
from jax.sharding import PartitionSpec as P

D = 512
FF = 2048
H = 8
DH = 64
K = 31
NB = 128


EPS_NORM = 1e-05
EPS_BATCH = 1e-05
EPS_SCALE = 1e-06
MOMENTUM = 0.9
RATE_MATRIX = 1.0
RATE_VECTOR = 0.25
COEF_A = 3.4445
COEF_B = -4.775
COEF_C = 2.0315
HIGHEST = lax.Precision.HIGHEST


AXES = ("dp", "seq", "shard")
MESH = pl.DeviceIdType.MESH
WIDTHS = (FF, FF, FF, FF, 3 * D, D, 2 * D, D)
STARTS = tuple(sum(WIDTHS[:i]) for i in range(9))
BLOCK = 512


class Cube:
    def __init__(self, dp_size):
        self.dp_size = dp_size
        self.levels = dp_size.bit_length() - 1
        self.digits = self.levels + 2
        self.total = dp_size * 4
        high = list(range(self.levels - 1))
        low, seq, core = self.levels - 1, self.levels, self.levels + 1
        self.gather_orders = (high + [low, seq, core], high + [seq, low, core])
        self.scatter_orders = tuple(order[::-1] for order in self.gather_orders)

    def mine(self):
        d = lax.axis_index("dp")
        bits = [lax.rem(d // (1 << (self.levels - 1 - k)), 2) for k in range(self.levels)]
        return bits + [lax.axis_index("seq"), lax.axis_index("shard")]

    def partner(self, k):
        d, s, c = lax.axis_index("dp"), lax.axis_index("seq"), lax.axis_index("shard")
        if k == self.levels:
            return (d, 1 - s, c)
        if k == self.levels + 1:
            return (d, s, 1 - c)
        step = 1 << (self.levels - 1 - k)
        bit = lax.rem(d // step, 2)
        return (d + (1 - 2 * bit) * step, s, c)

    def index(self):
        return (lax.axis_index("dp") * 2 + lax.axis_index("seq")) * 2 + lax.axis_index("shard")

    def coords(self, index):
        return (index // 4, lax.rem(index // 2, 2), lax.rem(index, 2))

    def greet_partners(self):
        barrier = pltpu.get_barrier_semaphore()
        for k in range(self.digits):
            pl.semaphore_signal(barrier, inc=1, device_id=self.partner(k), device_id_type=MESH)
        pl.semaphore_wait(barrier, self.digits)

    def greet_all(self):
        barrier = pltpu.get_barrier_semaphore()
        me = self.index()

        @pl.loop(1, self.total)
        def _(i):
            peer = self.coords(lax.rem(me + i, self.total))
            pl.semaphore_signal(barrier, inc=1, device_id=peer, device_id_type=MESH)

        pl.semaphore_wait(barrier, self.total - 1)


def halves(width):
    cut = (width // 128 + 1) // 2 * 128
    return ((0, cut), (cut, width - cut))


def remote(src, dst, send_sem, recv_sem, peer):
    return pltpu.make_async_remote_copy(
        src_ref=src,
        dst_ref=dst,
        send_sem=send_sem,
        recv_sem=recv_sem,
        device_id=peer,
        device_id_type=MESH,
    )


def gather_kernel(cube, groups, *refs):
    shards, outs = refs[:groups], refs[groups : 2 * groups]
    own_sem, send_sem, recv_sem = refs[2 * groups :]
    cube.greet_partners()
    mine = cube.mine()
    locals_ = []
    for g in range(groups):
        copy = pltpu.make_async_copy(shards[g], outs[g].at[tuple(mine)], own_sem.at[g])
        copy.start()
        locals_.append(copy)

    def make(g, half, stage):
        order = cube.gather_orders[half]
        columns = pl.ds(*halves(shards[g].shape[-1])[half])
        done = order[:stage]
        index = tuple(slice(None) if k in done else mine[k] for k in range(cube.digits))
        place = outs[g].at[index + (slice(None), columns)]
        source = shards[g].at[:, columns] if stage == 0 else place
        return remote(
            source,
            place,
            send_sem.at[g, half, stage],
            recv_sem.at[g, half, stage],
            cube.partner(order[stage]),
        )

    copies = {}
    for g in range(groups):
        for half in range(2):
            copies[g, half, 0] = make(g, half, 0)
            copies[g, half, 0].start()
    for tick in range(cube.digits + 2 * (groups - 1)):
        for g in range(groups):
            stage = tick - 2 * g
            if not 0 <= stage < cube.digits:
                continue
            for half in range(2):
                copies[g, half, stage].wait_recv()
                if stage == 0 and half == 0:
                    locals_[g].wait()
                if stage + 1 < cube.digits:
                    copies[g, half, stage + 1] = make(g, half, stage + 1)
                    copies[g, half, stage + 1].start()
    for copy in copies.values():
        copy.wait_send()


def gather_groups(cube, shards, collective_id):
    groups = len(shards)
    lead = (2,) * cube.digits
    return pl.pallas_call(
        functools.partial(gather_kernel, cube, groups),
        out_shape=[jax.ShapeDtypeStruct(lead + s.shape, s.dtype) for s in shards],
        in_specs=[pl.BlockSpec(memory_space=pl.ANY)] * groups,
        out_specs=[pl.BlockSpec(memory_space=pl.ANY)] * groups,
        scratch_shapes=[
            pltpu.SemaphoreType.DMA((groups,)),
            pltpu.SemaphoreType.DMA((groups, 2, cube.digits)),
            pltpu.SemaphoreType.DMA((groups, 2, cube.digits)),
        ],
        compiler_params=pltpu.CompilerParams(
            collective_id=collective_id, has_side_effects=True
        ),
        name="gather_weights",
    )(*shards)


def scatter_kernel(cube, groups, *refs):
    parts, outs = refs[:groups], refs[groups : 2 * groups]
    rest = refs[2 * groups :]
    sums = rest[:groups]
    landed = rest[groups : groups + groups * 2 * cube.digits]
    own_sem, send_sem, recv_sem = rest[groups + groups * 2 * cube.digits :]
    cube.greet_partners()
    mine = cube.mine()
    last = cube.digits - 1

    def slot(g, half, stage):
        return landed[(g * 2 + half) * cube.digits + stage]

    def place(g, half, stage, bit_of):
        order = cube.scatter_orders[half]
        columns = pl.ds(*halves(outs[g].shape[-1])[half])
        index = []
        for k in range(cube.digits - 1):
            at = order.index(k)
            if at > stage:
                index.append(slice(None))
            else:
                index.append(bit_of(k) if at == stage else mine[k])
        return tuple(index) + (slice(None), columns)

    def make(g, half, stage):
        order = cube.scatter_orders[half]
        if stage == 0:
            index = (slice(None),) * last + (1 - mine[last],)
            columns = pl.ds(*halves(outs[g].shape[-1])[half])
            source = parts[g].at[index + (slice(None), columns)]
        else:
            source = sums[g].at[place(g, half, stage, lambda k: 1 - mine[k])]
        return remote(
            source,
            slot(g, half, stage),
            send_sem.at[g, half, stage],
            recv_sem.at[g, half, stage],
            cube.partner(order[stage]),
        )

    copies = {}
    locals_ = []
    for g in range(groups):
        copy = pltpu.make_async_copy(
            parts[g].at[(slice(None),) * last + (mine[last],)], sums[g], own_sem.at[g]
        )
        copy.start()
        locals_.append(copy)
        for half in range(2):
            copies[g, half, 0] = make(g, half, 0)
            copies[g, half, 0].start()

    def add(g, half, stage):
        order = cube.scatter_orders[half]
        columns = pl.ds(*halves(outs[g].shape[-1])[half])
        free = [k for k in range(last) if order.index(k) > stage]
        count = 1 << len(free)
        target, extra = sums[g], slot(g, half, stage)

        def one(i):
            digit = {k: lax.rem(i // (1 << (len(free) - 1 - n)), 2) for n, k in enumerate(free)}
            full = tuple(digit.get(k, mine[k]) for k in range(last)) + (slice(None), columns)
            short = tuple(digit[k] for k in free)
            total = target[full].astype(jnp.float32) + extra[short + (slice(None), slice(None))].astype(jnp.float32)
            if stage == last:
                outs[g][:, columns] = total
            else:
                target[full] = total.astype(target.dtype)

        if count == 1:
            one(0)
        else:
            pl.loop(0, count)(one)

    for stage in range(cube.digits):
        for g in range(groups):
            if stage == 0:
                locals_[g].wait()
            for half in range(2):
                copies[g, half, stage].wait_recv()
                add(g, half, stage)
                if stage < last:
                    copies[g, half, stage + 1] = make(g, half, stage + 1)
                    copies[g, half, stage + 1].start()
    for copy in copies.values():
        copy.wait_send()


def scatter_groups(cube, parts, collective_id):
    groups = len(parts)
    scratch = [pltpu.VMEM((2,) * (cube.digits - 1) + p.shape[-2:], p.dtype) for p in parts]
    for p in parts:
        for half in range(2):
            for stage in range(cube.digits):
                lead = (2,) * (cube.digits - 1 - stage)
                scratch.append(pltpu.VMEM(lead + (p.shape[-2], halves(p.shape[-1])[half][1]), p.dtype))
    scratch += [
        pltpu.SemaphoreType.DMA((groups,)),
        pltpu.SemaphoreType.DMA((groups, 2, cube.digits)),
        pltpu.SemaphoreType.DMA((groups, 2, cube.digits)),
    ]
    return pl.pallas_call(
        functools.partial(scatter_kernel, cube, groups),
        out_shape=[jax.ShapeDtypeStruct(p.shape[-2:], jnp.float32) for p in parts],
        in_specs=[pl.BlockSpec(memory_space=pl.ANY)] * groups,
        out_specs=[pl.BlockSpec(memory_space=pltpu.VMEM)] * groups,
        scratch_shapes=scratch,
        compiler_params=pltpu.CompilerParams(
            collective_id=collective_id, has_side_effects=True, vmem_limit_bytes=48 << 20
        ),
        name="scatter_grads",
    )(*parts)


def collect_kernel(cube, x_ref, o_ref, send_sem, recv_sem):
    me = cube.index()
    cube.greet_all()

    def make(i):
        to = lax.rem(me + i, cube.total)
        return remote(x_ref, o_ref.at[i], send_sem.at[i], recv_sem.at[i], cube.coords(to))

    @pl.loop(1, cube.total)
    def _(i):
        make(i).start()

    o_ref[0] = x_ref[...]

    @pl.loop(1, cube.total)
    def _(i):
        make(i).wait()


def collect(cube, x, collective_id):
    return pl.pallas_call(
        functools.partial(collect_kernel, cube),
        out_shape=jax.ShapeDtypeStruct((cube.total,) + x.shape, x.dtype),
        in_specs=[pl.BlockSpec(memory_space=pltpu.VMEM)],
        out_specs=pl.BlockSpec(memory_space=pltpu.VMEM),
        scratch_shapes=[
            pltpu.SemaphoreType.DMA((cube.total,)),
            pltpu.SemaphoreType.DMA((cube.total,)),
        ],
        compiler_params=pltpu.CompilerParams(
            collective_id=collective_id, has_side_effects=True
        ),
        name="collect_stats",
    )(x)


def by_matrix(j, action):
    for width in sorted(set(WIDTHS)):
        members = [i for i in range(8) if WIDTHS[i] == width]
        hit = functools.reduce(jnp.logical_or, [j == i for i in members])
        pl.when(hit)(functools.partial(action, width // 4))


def quarter_start(t):
    j, q = t // 4, lax.rem(t, 4)
    start = 0
    for i in range(8):
        start = start + jnp.where(j == i, STARTS[i] + q * (WIDTHS[i] // 4), 0)
    return pl.multiple_of(start, 128)


def owner_coords(cube, t):
    return ((t // 4) * (cube.dp_size // 8), lax.rem(t // 2, 2), lax.rem(t, 2))


def spread_kernel(cube, x_ref, o_ref, own_sem, send_sem, recv_sem):
    me = cube.index()
    repeat = cube.dp_size // 8
    d, s, c = lax.axis_index("dp"), lax.axis_index("seq"), lax.axis_index("shard")
    owner = lax.rem(d, repeat) == 0
    mine = ((d // repeat) * 2 + s) * 2 + c
    cube.greet_all()

    def send(i, wait):
        t = lax.rem(mine + i, 32)
        peer = owner_coords(cube, t)
        other = jnp.logical_or(jnp.logical_not(owner), i > 0)

        def go(width):
            src = x_ref.at[:, pl.ds(quarter_start(t), width)]
            dst = o_ref.at[me, :, pl.ds(0, width)]
            copy = remote(src, dst, send_sem.at[i], recv_sem.at[me], peer)
            if wait:
                copy.wait_send()
            else:
                copy.start()

        pl.when(other)(lambda: by_matrix(t // 4, go))

    pl.loop(0, 32)(functools.partial(send, wait=False))

    def keep(width):
        copy = pltpu.make_async_copy(
            x_ref.at[:, pl.ds(quarter_start(mine), width)],
            o_ref.at[me, :, pl.ds(0, width)],
            own_sem,
        )
        copy.start()
        copy.wait()

    def receive(width):
        @pl.loop(1, cube.total)
        def _(i):
            source = lax.rem(me + i, cube.total)
            place = o_ref.at[source, :, pl.ds(0, width)]
            remote(
                place, place, send_sem.at[0], recv_sem.at[source], cube.coords(source)
            ).wait_recv()

    @pl.when(owner)
    def _():
        by_matrix(mine // 4, keep)
        by_matrix(mine // 4, receive)

    pl.loop(0, 32)(functools.partial(send, wait=True))


def spread(cube, x, collective_id):
    return pl.pallas_call(
        functools.partial(spread_kernel, cube),
        out_shape=jax.ShapeDtypeStruct((cube.total, x.shape[0], BLOCK), x.dtype),
        in_specs=[pl.BlockSpec(memory_space=pl.ANY)],
        out_specs=pl.BlockSpec(memory_space=pl.ANY),
        scratch_shapes=[
            pltpu.SemaphoreType.DMA,
            pltpu.SemaphoreType.DMA((32,)),
            pltpu.SemaphoreType.DMA((cube.total,)),
        ],
        compiler_params=pltpu.CompilerParams(
            collective_id=collective_id, has_side_effects=True
        ),
        name="spread_momentum",
    )(x)


def restore_kernel(cube, x_ref, o_ref, own_sem, send_sem, recv_sem):
    me = cube.index()
    repeat = cube.dp_size // 8
    d, s, c = lax.axis_index("dp"), lax.axis_index("seq"), lax.axis_index("shard")
    owner = lax.rem(d, repeat) == 0
    mine = ((d // repeat) * 2 + s) * 2 + c
    cube.greet_all()

    def send_all(wait, width):
        @pl.loop(1, cube.total)
        def _(i):
            to = lax.rem(me + i, cube.total)
            src = x_ref.at[to, :, pl.ds(0, width)]
            dst = o_ref.at[:, pl.ds(quarter_start(mine), width)]
            copy = remote(src, dst, send_sem.at[i], recv_sem.at[mine], cube.coords(to))
            if wait:
                copy.wait_send()
            else:
                copy.start()

    def keep(width):
        copy = pltpu.make_async_copy(
            x_ref.at[me, :, pl.ds(0, width)],
            o_ref.at[:, pl.ds(quarter_start(mine), width)],
            own_sem,
        )
        copy.start()
        copy.wait()

    @pl.when(owner)
    def _():
        by_matrix(mine // 4, functools.partial(send_all, False))
        by_matrix(mine // 4, keep)

    def receive(i):
        t = lax.rem(mine + i, 32)
        other = jnp.logical_or(jnp.logical_not(owner), i > 0)

        def go(width):
            place = o_ref.at[:, pl.ds(quarter_start(t), width)]
            remote(
                place, place, send_sem.at[0], recv_sem.at[t], owner_coords(cube, t)
            ).wait_recv()

        pl.when(other)(lambda: by_matrix(t // 4, go))

    pl.loop(0, 32)(receive)

    @pl.when(owner)
    def _():
        by_matrix(mine // 4, functools.partial(send_all, True))


def restore(cube, x, collective_id):
    return pl.pallas_call(
        functools.partial(restore_kernel, cube),
        out_shape=jax.ShapeDtypeStruct((x.shape[1], STARTS[8]), x.dtype),
        in_specs=[pl.BlockSpec(memory_space=pl.ANY)],
        out_specs=pl.BlockSpec(memory_space=pl.ANY),
        scratch_shapes=[
            pltpu.SemaphoreType.DMA,
            pltpu.SemaphoreType.DMA((cube.total,)),
            pltpu.SemaphoreType.DMA((32,)),
        ],
        compiler_params=pltpu.CompilerParams(
            collective_id=collective_id, has_side_effects=True
        ),
        name="restore_rows",
    )(x)


def split(value):
    high = value.astype(jnp.bfloat16)
    low = (value - high.astype(jnp.float32)).astype(jnp.bfloat16)
    return high, low


def product(left, right):
    (lh, ll), (rh, rl) = left, right
    dot = functools.partial(jnp.dot, preferred_element_type=jnp.float32)
    return dot(lh, rh) + (dot(lh, rl) + dot(ll, rh))


def orthogonalize_kernel(cube, x_ref, o_ref, gram_ref, work, landed, send_sem, recv_sem):
    barrier = pltpu.get_barrier_semaphore()
    peers = (cube.partner(cube.levels + 1), cube.partner(cube.levels))
    for peer in peers:
        pl.semaphore_signal(barrier, inc=1, device_id=peer, device_id_type=MESH)
    pl.semaphore_wait(barrier, 2)
    repeat = cube.dp_size // 8
    j = lax.axis_index("dp") // repeat
    width = 0
    for i in range(8):
        width = width + jnp.where(j == i, WIDTHS[i] // 4, 0)
    column = lax.broadcasted_iota(jnp.int32, (D, BLOCK), 1)
    block = jnp.where(column < width, x_ref[...].astype(jnp.float32), 0.0)
    bh, bl = split(block)
    dot_t = lambda a, b: lax.dot_general(
        a, b, (((1,), (1,)), ((), ())), preferred_element_type=jnp.float32
    )
    gram_ref[0] = dot_t(bh, bh) + (dot_t(bh, bl) + dot_t(bl, bh))
    for step in range(2):
        copy = remote(
            gram_ref.at[step], landed.at[step], send_sem.at[step], recv_sem.at[step], peers[step]
        )
        copy.start()
        copy.wait()
        gram_ref[step + 1] = gram_ref[step] + landed[step]
    gram = gram_ref[2]
    row = lax.broadcasted_iota(jnp.int32, (D, D), 0)
    col = lax.broadcasted_iota(jnp.int32, (D, D), 1)
    eye = row == col
    square = jnp.sum(jnp.sum(jnp.where(eye, gram, 0.0), axis=1, keepdims=True), axis=0, keepdims=True)
    scale = 1.0 / (jnp.sqrt(square) + 1e-07)
    gram = gram * (scale * scale)
    block = block * scale
    for step in range(5):
        parts = split(gram)
        mixed = COEF_B * gram + COEF_C * product(parts, parts)
        mixed = jnp.where(eye, mixed + COEF_A, mixed)
        mixed_parts = split(mixed)
        block = product(mixed_parts, split(block))
        if step < 4:
            gram = product(mixed_parts, split(product(mixed_parts, parts)))
    o_ref[...] = block.astype(o_ref.dtype)


def orthogonalize_blocks(cube, x, out_dtype, collective_id):
    return pl.pallas_call(
        functools.partial(orthogonalize_kernel, cube),
        out_shape=jax.ShapeDtypeStruct((D, BLOCK), out_dtype),
        in_specs=[pl.BlockSpec(memory_space=pltpu.VMEM)],
        out_specs=pl.BlockSpec(memory_space=pltpu.VMEM),
        scratch_shapes=[
            pltpu.VMEM((3, D, D), jnp.float32),
            pltpu.VMEM((8, 128), jnp.float32),
            pltpu.VMEM((2, D, D), jnp.float32),
            pltpu.SemaphoreType.DMA((2,)),
            pltpu.SemaphoreType.DMA((2,)),
        ],
        compiler_params=pltpu.CompilerParams(
            collective_id=collective_id, has_side_effects=True, vmem_limit_bytes=48 << 20
        ),
        name="orthogonalize",
    )(x)

def with_halo(value, sides, width):
    for axis, dim in sides:
        devices, length = (lax.axis_size(axis), value.shape[dim])
        up = [(i, (i + 1) % devices) for i in range(devices - 1)]
        down = [(j, i) for i, j in up]
        last = lax.slice_in_dim(value, length - width, length, axis=dim)
        first = lax.slice_in_dim(value, 0, width, axis=dim)
        before = lax.ppermute(last, axis, up)
        after = lax.ppermute(first, axis, down)
        value = jnp.concatenate([before, value, after], axis=dim)
    return value


def matmul(left, right):
    return jnp.dot(left, right, preferred_element_type=jnp.float32)


def matmul_right_t(left, right):
    return lax.dot_general(
        left, right, (((1,), (1,)), ((), ())), preferred_element_type=jnp.float32
    )


def matmul_left_t(left, right):
    return lax.dot_general(
        left, right, (((0,), (0,)), ((), ())), preferred_element_type=jnp.float32
    )


def layer_norm(field, gain):
    centre = jnp.mean(field, axis=-1, keepdims=True)
    shifted = field - centre
    inverse = lax.rsqrt(jnp.mean(shifted * shifted, axis=-1, keepdims=True) + EPS_NORM)
    normed = shifted * inverse
    return (normed * gain, normed, inverse)


def norm_back(grad_out, normed, inverse, gain):
    scaled = grad_out * gain
    grad_in = inverse * (
        scaled
        - jnp.mean(scaled, axis=-1, keepdims=True)
        - normed * jnp.mean(scaled * normed, axis=-1, keepdims=True)
    )
    return (grad_in, jnp.sum(grad_out * normed, axis=0))


def silu_slope(values):
    sigma = jax.nn.sigmoid(values)
    return sigma * (1.0 + values * (1.0 - sigma))


def ffn_forward(field, gain, w_in, w_back):
    normed_out, normed, inverse = layer_norm(field, gain)
    lifted = normed_out.astype(jnp.bfloat16)
    hidden_pre = matmul(lifted, w_in)
    hidden_act = jax.nn.silu(hidden_pre).astype(jnp.bfloat16)
    return (
        field + 0.5 * matmul_right_t(hidden_act, w_back),
        (lifted, hidden_pre, hidden_act, normed, inverse),
    )


def ffn_backward(grad, saved, gain, w_in, w_back):
    lifted, hidden_pre, hidden_act, normed, inverse = saved
    grad_branch = (0.5 * grad).astype(jnp.bfloat16)
    grad_back = matmul_left_t(grad_branch, hidden_act)
    grad_act = matmul(grad_branch, w_back)
    grad_pre = (grad_act * silu_slope(hidden_pre)).astype(jnp.bfloat16)
    grad_in = matmul_left_t(lifted, grad_pre)
    grad_field, grad_gain = norm_back(matmul_right_t(grad_pre, w_in), normed, inverse, gain)
    return (grad + grad_field, grad_in, grad_back, grad_gain)


def depthwise(wide, kernel, count):
    total = wide[0:count] * kernel[:, 0]
    for tap_idx in range(1, K):
        total = total + wide[tap_idx : tap_idx + count] * kernel[:, tap_idx]
    return total


def spread_rows(window, count, keys_len):
    padded = jnp.concatenate([window, jnp.zeros((1,), window.dtype)])
    tiled = jnp.broadcast_to(padded[None, :], (count, keys_len + count)).reshape(-1)
    shaped = tiled[: count * (keys_len + count - 1)].reshape(count, keys_len + count - 1)
    return shaped[:, count - 1 : count - 1 + keys_len]


def collect_rows(grid, count, keys_len):
    placed = jnp.concatenate([jnp.zeros((count, count - 1), grid.dtype), grid], axis=1).reshape(-1)
    placed = jnp.concatenate([placed, jnp.zeros((count,), grid.dtype)])
    return jnp.sum(placed.reshape(count, keys_len + count), axis=0)[: keys_len + count - 1]


def attention_scores(query, keys, offsets, first_row, row_start, block, head_idx):
    length = keys.shape[0]
    columns = slice(head_idx * DH, (head_idx + 1) * DH)
    anchor = length - block - first_row - row_start
    window = lax.dynamic_slice_in_dim(offsets[head_idx], anchor, length + block - 1)
    product = matmul_right_t(query[row_start : row_start + block, columns], keys[:, columns])
    return product * DH ** (-0.5) + spread_rows(window, block, length)


def attention_forward(query, keys, values, offsets, first_row):
    total_rows = query.shape[0]
    block = min(512, total_rows)
    head_outs = []
    head_lse = []
    for head_idx in range(H):
        scores = attention_scores(query, keys, offsets, first_row, 0, block, head_idx)
        row_max = jnp.max(scores, axis=1, keepdims=True)
        shifted_exp = jnp.exp(scores - row_max)
        row_total = jnp.sum(shifted_exp, axis=1, keepdims=True)
        prob_low = (shifted_exp / row_total).astype(jnp.bfloat16)
        head_outs.append(matmul(prob_low, values[:, head_idx * DH : (head_idx + 1) * DH]))
        head_lse.append((row_max + jnp.log(row_total))[:, 0])
    out_blocks = jnp.concatenate(head_outs, axis=1)
    lse_blocks = jnp.stack(head_lse, axis=0)
    return (out_blocks, lse_blocks)


def attention_backward(query, keys, values, offsets, first_row, log_total, grad_attended, delta):
    total_rows = query.shape[0]
    length = keys.shape[0]
    block = min(512, total_rows)
    scale = DH ** (-0.5)
    key_parts = [jnp.zeros((length, DH), jnp.float32) for head_idx in range(H)]
    value_parts = [jnp.zeros((length, DH), jnp.float32) for head_idx in range(H)]
    offset_rows = [jnp.zeros((2 * length - 1,), jnp.float32) for head_idx in range(H)]
    head_grads = []
    for head_idx in range(H):
        columns = slice(head_idx * DH, (head_idx + 1) * DH)
        scores = attention_scores(query, keys, offsets, first_row, 0, block, head_idx)
        prob = jnp.exp(scores - log_total[head_idx, 0:block][:, None])
        prob_low = prob.astype(jnp.bfloat16)
        grad_piece = grad_attended[0:block, columns]
        value_parts[head_idx] = matmul_left_t(prob_low, grad_piece)
        grad_prob = matmul_right_t(grad_piece, values[:, columns])
        grad_score = prob * (grad_prob - delta[0:block, head_idx][:, None])
        score_low = grad_score.astype(jnp.bfloat16)
        head_grads.append(matmul(score_low, keys[:, columns]) * scale)
        key_parts[head_idx] = matmul_left_t(score_low, query[0:block, columns]) * scale
        anchor = length - block - first_row - 0
        offset_rows[head_idx] = lax.dynamic_update_slice_in_dim(
            offset_rows[head_idx], collect_rows(grad_score, block, length), anchor, 0
        )
    query_blocks = jnp.concatenate(head_grads, axis=1)
    return (
        query_blocks,
        jnp.concatenate(key_parts, axis=1),
        jnp.concatenate(value_parts, axis=1),
        jnp.stack(offset_rows, axis=0),
    )


def local(
    cube,
    inputs,
    cotangent,
    w_up,
    w_down,
    w_qkv,
    w_out,
    w_glu,
    w_point,
    vectors,
    depth_kernel,
    rel_bias,
    bucket_table,
    m_up,
    m_down,
    m_qkv,
    m_out,
    m_glu,
    m_point,
    m_vectors,
    m_depth,
    m_rel,
):
    bf16 = jnp.bfloat16
    rows = w_up.shape[0]
    small = jnp.concatenate([vectors, depth_kernel, rel_bias.reshape(rows, -1)], axis=1)
    small_count = small.shape[1]
    small = jnp.pad(small, ((0, 0), (0, 128 - small_count)))
    shard_groups = (
        jnp.concatenate([w_up[:, :FF], w_down[:, :FF], small], axis=1).astype(bf16),
        jnp.concatenate([w_qkv, w_out, w_glu, w_point], axis=1).astype(bf16),
        jnp.concatenate([w_up[:, FF:], w_down[:, FF:]], axis=1).astype(bf16),
    )
    first, middle, second = [
        full.reshape(D, -1) for full in gather_groups(cube, shard_groups, 0)
    ]
    up_first, down_first, small_low = first[:, :FF], first[:, FF : 2 * FF], first[:, 2 * FF :]
    qkv_w, out_w = middle[:, : 3 * D], middle[:, 3 * D : 4 * D]
    glu_w, point_w = middle[:, 4 * D : 6 * D], middle[:, 6 * D :]
    up_second, down_second = second[:, :FF], second[:, FF:]
    gains = small_low[:, :7].astype(jnp.float32)
    kernel = small_low[:, 7 : 7 + K].astype(jnp.float32)
    rel_low = small_low[:, 7 + K : small_count].reshape(NB, H)
    bucket_hit = (bucket_table[:, None] == jnp.arange(NB, dtype=jnp.int32)[None, :]).astype(
        jnp.float32
    )
    offsets = jnp.dot(bucket_hit, rel_low.astype(jnp.float32), precision=HIGHEST).T
    seq_rows = inputs[0]
    row_count = seq_rows.shape[0]
    first_row = lax.axis_index("seq") * row_count
    token_total = row_count * lax.axis_size(("dp", "seq", "shard"))
    section_one, ffn_saved = ffn_forward(seq_rows, gains[:, 0], up_first, down_first)
    normed_out2, normed2, inverse2 = layer_norm(section_one, gains[:, 1])
    lifted2 = normed_out2.astype(bf16)
    projected = matmul(lifted2, qkv_w).astype(bf16)
    query = projected[:, :D]
    pair = [(0, 1), (1, 0)]
    other = lax.ppermute(projected[:, D:], "seq", pair)
    early = lax.axis_index("seq") == 0
    both = jnp.concatenate(
        [
            jnp.where(early, projected[:, D:], other),
            jnp.where(early, other, projected[:, D:]),
        ],
        axis=0,
    )
    keys, values = both[:, :D], both[:, D:]
    attended, log_total = attention_forward(query, keys, values, offsets, first_row)
    attended_low = attended.astype(bf16)
    section_two = section_one + matmul(attended_low, out_w)
    normed_out3, normed3, inverse3 = layer_norm(section_two, gains[:, 2])
    lifted3 = normed_out3.astype(bf16)
    gates = matmul(lifted3, glu_w)
    first_half = gates[:, :D]
    sig_gate = jax.nn.sigmoid(gates[:, D:])
    glu = first_half * sig_gate
    glu_wide = with_halo(glu, (("seq", 0),), K // 2)
    conv = depthwise(glu_wide, kernel, row_count)
    part_sum = jnp.sum(conv, axis=0)
    part_mean = part_sum / row_count
    part_square = jnp.sum(jnp.square(conv - part_mean), axis=0)
    stats = collect(cube, jnp.concatenate([part_sum, part_square]).reshape(8, 128), 1)
    stats = stats.reshape(cube.total, 2, D)
    mean = jnp.sum(stats[:, 0], axis=0) / token_total
    spread_of_means = jnp.square(stats[:, 0] / row_count - mean) * row_count
    variance = jnp.sum(stats[:, 1] + spread_of_means, axis=0) / token_total
    centred = conv - mean
    inv_std = lax.rsqrt(variance + EPS_BATCH)
    normed_bn = centred * inv_std
    batch_out = normed_bn * gains[:, 5] + gains[:, 6]
    swish_low = jax.nn.silu(batch_out).astype(bf16)
    section_three = section_two + matmul(swish_low, point_w)
    section_four, tail_saved = ffn_forward(
        section_three, gains[:, 3], up_second, down_second
    )
    outputs, normed5, inverse5 = layer_norm(section_four, gains[:, 4])
    grad_four, gain_four = norm_back(cotangent[0], normed5, inverse5, gains[:, 4])
    grad_three, grad_up_two, grad_down_two, gain_three = ffn_backward(
        grad_four, tail_saved, gains[:, 3], up_second, down_second
    )
    grad_three_low = grad_three.astype(bf16)
    grad_point = matmul_left_t(swish_low, grad_three_low)
    grad_batch = matmul_right_t(grad_three_low, point_w) * silu_slope(batch_out)
    grad_normed = grad_batch * gains[:, 5]
    sums = jnp.concatenate(
        [jnp.sum(grad_normed, axis=0), jnp.sum(grad_normed * normed_bn, axis=0)]
    )
    sums = jnp.sum(collect(cube, sums.reshape(8, 128), 2), axis=0).reshape(2, D)
    sum_normed, sum_cross = sums[0], sums[1]
    grad_conv = inv_std * (
        grad_normed - sum_normed / token_total - normed_bn * sum_cross / token_total
    )
    grad_wide = with_halo(grad_conv, (("seq", 0),), K // 2)
    grad_glu = grad_wide[K - 1 : K - 1 + row_count] * kernel[:, 0]
    for tap_idx in range(1, K):
        grad_glu = (
            grad_glu
            + grad_wide[K - 1 - tap_idx : K - 1 - tap_idx + row_count] * kernel[:, tap_idx]
        )
    grad_kernel = jnp.stack(
        [
            jnp.sum(grad_conv * glu_wide[tap_idx : tap_idx + row_count], axis=0)
            for tap_idx in range(K)
        ],
        axis=1,
    )
    grad_gates = jnp.concatenate(
        [grad_glu * sig_gate, grad_glu * first_half * sig_gate * (1.0 - sig_gate)], axis=1
    ).astype(bf16)
    grad_glu_w = matmul_left_t(lifted3, grad_gates)
    grad_two_part, gain_two = norm_back(
        matmul_right_t(grad_gates, glu_w), normed3, inverse3, gains[:, 2]
    )
    grad_two = grad_three + grad_two_part
    grad_two_low = grad_two.astype(bf16)
    grad_out_w = matmul_left_t(attended_low, grad_two_low)
    grad_attended = matmul_right_t(grad_two_low, out_w).astype(bf16)
    delta = jnp.sum(
        (grad_attended.astype(jnp.float32) * attended).reshape(row_count, H, DH), axis=2
    )
    query_grad, key_grad, value_grad, offset_grad = attention_backward(
        query, keys, values, offsets, first_row, log_total, grad_attended, delta
    )
    keys_grad = jnp.concatenate([key_grad, value_grad], axis=1)
    theirs = lax.dynamic_slice_in_dim(keys_grad, row_count - first_row, row_count, 0)
    own = lax.dynamic_slice_in_dim(keys_grad, first_row, row_count, 0)
    own = own + lax.ppermute(theirs, "seq", pair)
    key_own, value_own = own[:, :D], own[:, D:]
    grad_proj = jnp.concatenate([query_grad, key_own, value_own], axis=1).astype(bf16)
    grad_qkv_w = matmul_left_t(lifted2, grad_proj)
    grad_one_part, gain_one = norm_back(
        matmul_right_t(grad_proj, qkv_w), normed2, inverse2, gains[:, 1]
    )
    grad_one = grad_two + grad_one_part
    input_grad, grad_up_one, grad_down_one, gain_zero = ffn_backward(
        grad_one, ffn_saved, gains[:, 0], up_first, down_first
    )
    grad_vec_local = jnp.stack(
        [
            gain_zero,
            gain_one,
            gain_two,
            gain_three,
            gain_four,
            jnp.sum(grad_batch * normed_bn, axis=0),
            jnp.sum(grad_batch, axis=0),
        ],
        axis=1,
    )
    grad_rel_local = jnp.dot(bucket_hit.T, offset_grad.T, precision=HIGHEST)
    small_grads = jnp.concatenate(
        [grad_vec_local, grad_kernel, grad_rel_local.reshape(D, -1)], axis=1
    )
    small_grads = jnp.pad(small_grads, ((0, 0), (0, 128 - small_count)))
    lead = (2,) * cube.digits
    grad_groups = [
        jnp.concatenate(group, axis=1).astype(bf16).reshape(lead + (rows, -1))
        for group in (
            (grad_up_two, grad_down_two),
            (grad_qkv_w, grad_out_w, grad_glu_w, grad_point),
            (grad_up_one, grad_down_one, small_grads),
        )
    ]
    share_second, share_middle, share_first = scatter_groups(cube, grad_groups, 3)
    grad_up = jnp.concatenate([share_first[:, :FF], share_second[:, :FF]], axis=1)
    grad_down = jnp.concatenate([share_first[:, FF : 2 * FF], share_second[:, FF:]], axis=1)
    grad_qkv, grad_out = share_middle[:, : 3 * D], share_middle[:, 3 * D : 4 * D]
    grad_glu, grad_pnt = share_middle[:, 4 * D : 6 * D], share_middle[:, 6 * D :]
    grad_vectors = share_first[:, 2 * FF : 2 * FF + 7]
    grad_depth = share_first[:, 2 * FF + 7 : 2 * FF + 7 + K]
    grad_rel = share_first[:, 2 * FF + 7 + K : 2 * FF + small_count].reshape(-1, H)
    next_m_up = MOMENTUM * m_up + grad_up
    next_m_down = MOMENTUM * m_down + grad_down
    next_m_qkv = MOMENTUM * m_qkv + grad_qkv
    next_m_out = MOMENTUM * m_out + grad_out
    next_m_glu = MOMENTUM * m_glu + grad_glu
    next_m_point = MOMENTUM * m_point + grad_pnt
    stacked = jnp.concatenate(
        [next_m_up, next_m_down, next_m_qkv, next_m_out, next_m_glu, next_m_point], axis=1
    )
    owned = spread(cube, stacked, 4).reshape(D, BLOCK)
    ortho = orthogonalize_blocks(cube, owned, bf16, 5)
    mine = restore(cube, ortho.reshape(cube.total, rows, BLOCK), 6).astype(jnp.float32)
    new_up = w_up - RATE_MATRIX * mine[:, : 2 * FF]
    new_down = w_down - RATE_MATRIX * mine[:, 2 * FF : 4 * FF]
    new_qkv = w_qkv - RATE_MATRIX * mine[:, STARTS[4] : STARTS[5]]
    new_out = w_out - RATE_MATRIX * mine[:, STARTS[5] : STARTS[6]]
    new_glu = w_glu - RATE_MATRIX * mine[:, STARTS[6] : STARTS[7]]
    new_point = w_point - RATE_MATRIX * mine[:, STARTS[7] :]
    next_m_vectors = MOMENTUM * m_vectors + grad_vectors
    next_m_depth = MOMENTUM * m_depth + grad_depth
    next_m_rel = MOMENTUM * m_rel + grad_rel
    squares = jnp.concatenate(
        [
            jnp.sum(next_m_vectors * next_m_vectors, axis=0),
            jnp.sum(next_m_depth * next_m_depth, axis=0),
            jnp.sum(next_m_rel * next_m_rel, axis=0),
        ]
    )
    squares = jnp.pad(squares, (0, 128 - squares.shape[0])).reshape(1, 128)
    squares = jnp.sum(collect(cube, jnp.pad(squares, ((0, 7), (0, 0))), 7), axis=0)[0]
    square_vec, square_depth = squares[:7], squares[7 : 7 + K]
    square_rel = squares[7 + K : 7 + K + H]
    new_vectors = vectors - RATE_VECTOR * next_m_vectors * lax.rsqrt(square_vec / D + EPS_SCALE)
    new_depth = depth_kernel - RATE_VECTOR * next_m_depth * lax.rsqrt(square_depth / D + EPS_SCALE)
    new_rel = rel_bias - RATE_VECTOR * next_m_rel * lax.rsqrt(square_rel / NB + EPS_SCALE)
    return (
        outputs[None],
        input_grad[None],
        grad_up,
        grad_down,
        grad_qkv,
        grad_out,
        grad_glu,
        grad_pnt,
        grad_vectors,
        grad_depth,
        grad_rel,
        new_up,
        new_down,
        new_qkv,
        new_out,
        new_glu,
        new_point,
        new_vectors,
        new_depth,
        new_rel,
        next_m_up,
        next_m_down,
        next_m_qkv,
        next_m_out,
        next_m_glu,
        next_m_point,
        next_m_vectors,
        next_m_depth,
        next_m_rel,
    )


def solution(mesh):
    placed = (
        P(("dp", "shard"), "seq", None),
        P(("dp", "shard"), "seq", None),
        P(("dp", "seq", "shard"), None),
        P(("dp", "seq", "shard"), None),
        P(("dp", "seq", "shard"), None),
        P(("dp", "seq", "shard"), None),
        P(("dp", "seq", "shard"), None),
        P(("dp", "seq", "shard"), None),
        P(("dp", "seq", "shard"), None),
        P(("dp", "seq", "shard"), None),
        P(("dp", "seq", "shard"), None),
        P(),
        P(("dp", "seq", "shard"), None),
        P(("dp", "seq", "shard"), None),
        P(("dp", "seq", "shard"), None),
        P(("dp", "seq", "shard"), None),
        P(("dp", "seq", "shard"), None),
        P(("dp", "seq", "shard"), None),
        P(("dp", "seq", "shard"), None),
        P(("dp", "seq", "shard"), None),
        P(("dp", "seq", "shard"), None),
    )
    return jax.shard_map(
        functools.partial(local, Cube(mesh.shape["dp"])),
        mesh=mesh,
        in_specs=placed,
        out_specs=(
            P(("dp", "shard"), "seq", None),
            P(("dp", "shard"), "seq", None),
            P(("dp", "seq", "shard"), None),
            P(("dp", "seq", "shard"), None),
            P(("dp", "seq", "shard"), None),
            P(("dp", "seq", "shard"), None),
            P(("dp", "seq", "shard"), None),
            P(("dp", "seq", "shard"), None),
            P(("dp", "seq", "shard"), None),
            P(("dp", "seq", "shard"), None),
            P(("dp", "seq", "shard"), None),
            P(("dp", "seq", "shard"), None),
            P(("dp", "seq", "shard"), None),
            P(("dp", "seq", "shard"), None),
            P(("dp", "seq", "shard"), None),
            P(("dp", "seq", "shard"), None),
            P(("dp", "seq", "shard"), None),
            P(("dp", "seq", "shard"), None),
            P(("dp", "seq", "shard"), None),
            P(("dp", "seq", "shard"), None),
            P(("dp", "seq", "shard"), None),
            P(("dp", "seq", "shard"), None),
            P(("dp", "seq", "shard"), None),
            P(("dp", "seq", "shard"), None),
            P(("dp", "seq", "shard"), None),
            P(("dp", "seq", "shard"), None),
            P(("dp", "seq", "shard"), None),
            P(("dp", "seq", "shard"), None),
            P(("dp", "seq", "shard"), None),
        ),
        check_vma=False,
    )
```

```python
import functools
import types

import jax
import jax.numpy as jnp
from jax import lax
from jax.experimental import pallas as pl
from jax.experimental.pallas import tpu as pltpu
from jax.sharding import PartitionSpec as P

D = 512
FF = 2048
H = 8
DH = 64
K = 31
NB = 128


EPS_NORM = 1e-05
EPS_BATCH = 1e-05
EPS_SCALE = 1e-06
MOMENTUM = 0.9
RATE_MATRIX = 1.0
RATE_VECTOR = 0.25
COEF_A = 3.4445
COEF_B = -4.775
COEF_C = 2.0315
HIGHEST = lax.Precision.HIGHEST


AXES = ("dp", "seq", "shard")
MESH = pl.DeviceIdType.MESH
WIDTHS = (FF, FF, FF, FF, 3 * D, D, 2 * D, D)
STARTS = tuple(sum(WIDTHS[:i]) for i in range(9))
BLOCK = 512


class Cube:
    def __init__(self, dp_size):
        self.dp_size = dp_size
        self.levels = dp_size.bit_length() - 1
        self.digits = self.levels + 2
        self.total = dp_size * 4
        high = list(range(self.levels - 1))
        low, seq, core = self.levels - 1, self.levels, self.levels + 1
        self.gather_orders = (high + [low, seq, core], high + [seq, low, core])
        self.scatter_orders = tuple(order[::-1] for order in self.gather_orders)

    def mine(self):
        d = lax.axis_index("dp")
        bits = [lax.rem(d // (1 << (self.levels - 1 - k)), 2) for k in range(self.levels)]
        return bits + [lax.axis_index("seq"), lax.axis_index("shard")]

    def partner(self, k):
        d, s, c = lax.axis_index("dp"), lax.axis_index("seq"), lax.axis_index("shard")
        if k == self.levels:
            return (d, 1 - s, c)
        if k == self.levels + 1:
            return (d, s, 1 - c)
        step = 1 << (self.levels - 1 - k)
        bit = lax.rem(d // step, 2)
        return (d + (1 - 2 * bit) * step, s, c)

    def index(self):
        return (lax.axis_index("dp") * 2 + lax.axis_index("seq")) * 2 + lax.axis_index("shard")

    def coords(self, index):
        return (index // 4, lax.rem(index // 2, 2), lax.rem(index, 2))

    def greet_partners(self):
        barrier = pltpu.get_barrier_semaphore()
        for k in range(self.digits):
            pl.semaphore_signal(barrier, inc=1, device_id=self.partner(k), device_id_type=MESH)
        pl.semaphore_wait(barrier, self.digits)

    def greet_all(self):
        barrier = pltpu.get_barrier_semaphore()
        me = self.index()

        @pl.loop(1, self.total)
        def _(i):
            peer = self.coords(lax.rem(me + i, self.total))
            pl.semaphore_signal(barrier, inc=1, device_id=peer, device_id_type=MESH)

        pl.semaphore_wait(barrier, self.total - 1)


def halves(width):
    cut = (width // 128 + 1) // 2 * 128
    return ((0, cut), (cut, width - cut))


def remote(src, dst, send_sem, recv_sem, peer):
    return pltpu.make_async_remote_copy(
        src_ref=src,
        dst_ref=dst,
        send_sem=send_sem,
        recv_sem=recv_sem,
        device_id=peer,
        device_id_type=MESH,
    )


def gather_kernel(cube, groups, *refs):
    shards, outs = refs[:groups], refs[groups : 2 * groups]
    own_sem, send_sem, recv_sem = refs[2 * groups :]
    cube.greet_partners()
    mine = cube.mine()
    locals_ = []
    for g in range(groups):
        copy = pltpu.make_async_copy(shards[g], outs[g].at[tuple(mine)], own_sem.at[g])
        copy.start()
        locals_.append(copy)

    def make(g, half, stage):
        order = cube.gather_orders[half]
        columns = pl.ds(*halves(shards[g].shape[-1])[half])
        done = order[:stage]
        index = tuple(slice(None) if k in done else mine[k] for k in range(cube.digits))
        place = outs[g].at[index + (slice(None), columns)]
        source = shards[g].at[:, columns] if stage == 0 else place
        return remote(
            source,
            place,
            send_sem.at[g, half, stage],
            recv_sem.at[g, half, stage],
            cube.partner(order[stage]),
        )

    copies = {}
    for g in range(groups):
        for half in range(2):
            copies[g, half, 0] = make(g, half, 0)
            copies[g, half, 0].start()
    for tick in range(cube.digits + 2 * (groups - 1)):
        for g in range(groups):
            stage = tick - 2 * g
            if not 0 <= stage < cube.digits:
                continue
            for half in range(2):
                copies[g, half, stage].wait_recv()
                if stage == 0 and half == 0:
                    locals_[g].wait()
                if stage + 1 < cube.digits:
                    copies[g, half, stage + 1] = make(g, half, stage + 1)
                    copies[g, half, stage + 1].start()
    for copy in copies.values():
        copy.wait_send()


def gather_groups(cube, shards, collective_id):
    groups = len(shards)
    lead = (2,) * cube.digits
    return pl.pallas_call(
        functools.partial(gather_kernel, cube, groups),
        out_shape=[jax.ShapeDtypeStruct(lead + s.shape, s.dtype) for s in shards],
        in_specs=[pl.BlockSpec(memory_space=pl.ANY)] * groups,
        out_specs=[pl.BlockSpec(memory_space=pl.ANY)] * groups,
        scratch_shapes=[
            pltpu.SemaphoreType.DMA((groups,)),
            pltpu.SemaphoreType.DMA((groups, 2, cube.digits)),
            pltpu.SemaphoreType.DMA((groups, 2, cube.digits)),
        ],
        compiler_params=pltpu.CompilerParams(
            collective_id=collective_id, has_side_effects=True
        ),
        name="gather_weights",
    )(*shards)


def scatter_kernel(cube, groups, *refs):
    parts, outs = refs[:groups], refs[groups : 2 * groups]
    rest = refs[2 * groups :]
    sums = rest[:groups]
    landed = rest[groups : groups + groups * 2 * cube.digits]
    own_sem, send_sem, recv_sem = rest[groups + groups * 2 * cube.digits :]
    cube.greet_partners()
    mine = cube.mine()
    last = cube.digits - 1

    def slot(g, half, stage):
        return landed[(g * 2 + half) * cube.digits + stage]

    def place(g, half, stage, bit_of):
        order = cube.scatter_orders[half]
        columns = pl.ds(*halves(outs[g].shape[-1])[half])
        index = []
        for k in range(cube.digits - 1):
            at = order.index(k)
            if at > stage:
                index.append(slice(None))
            else:
                index.append(bit_of(k) if at == stage else mine[k])
        return tuple(index) + (slice(None), columns)

    def make(g, half, stage):
        order = cube.scatter_orders[half]
        if stage == 0:
            index = (slice(None),) * last + (1 - mine[last],)
            columns = pl.ds(*halves(outs[g].shape[-1])[half])
            source = parts[g].at[index + (slice(None), columns)]
        else:
            source = sums[g].at[place(g, half, stage, lambda k: 1 - mine[k])]
        return remote(
            source,
            slot(g, half, stage),
            send_sem.at[g, half, stage],
            recv_sem.at[g, half, stage],
            cube.partner(order[stage]),
        )

    copies = {}
    locals_ = []
    for g in range(groups):
        copy = pltpu.make_async_copy(
            parts[g].at[(slice(None),) * last + (mine[last],)], sums[g], own_sem.at[g]
        )
        copy.start()
        locals_.append(copy)
        for half in range(2):
            copies[g, half, 0] = make(g, half, 0)
            copies[g, half, 0].start()

    def add(g, half, stage):
        order = cube.scatter_orders[half]
        columns = pl.ds(*halves(outs[g].shape[-1])[half])
        free = [k for k in range(last) if order.index(k) > stage]
        count = 1 << len(free)
        target, extra = sums[g], slot(g, half, stage)

        def one(i):
            digit = {k: lax.rem(i // (1 << (len(free) - 1 - n)), 2) for n, k in enumerate(free)}
            full = tuple(digit.get(k, mine[k]) for k in range(last)) + (slice(None), columns)
            short = tuple(digit[k] for k in free)
            total = target[full].astype(jnp.float32) + extra[short + (slice(None), slice(None))].astype(jnp.float32)
            if stage == last:
                outs[g][:, columns] = total
            else:
                target[full] = total.astype(target.dtype)

        if count == 1:
            one(0)
        else:
            pl.loop(0, count)(one)

    for stage in range(cube.digits):
        for g in range(groups):
            if stage == 0:
                locals_[g].wait()
            for half in range(2):
                copies[g, half, stage].wait_recv()
                add(g, half, stage)
                if stage < last:
                    copies[g, half, stage + 1] = make(g, half, stage + 1)
                    copies[g, half, stage + 1].start()
    for copy in copies.values():
        copy.wait_send()


def scatter_groups(cube, parts, collective_id):
    groups = len(parts)
    scratch = [pltpu.VMEM((2,) * (cube.digits - 1) + p.shape[-2:], p.dtype) for p in parts]
    for p in parts:
        for half in range(2):
            for stage in range(cube.digits):
                lead = (2,) * (cube.digits - 1 - stage)
                scratch.append(pltpu.VMEM(lead + (p.shape[-2], halves(p.shape[-1])[half][1]), p.dtype))
    scratch += [
        pltpu.SemaphoreType.DMA((groups,)),
        pltpu.SemaphoreType.DMA((groups, 2, cube.digits)),
        pltpu.SemaphoreType.DMA((groups, 2, cube.digits)),
    ]
    return pl.pallas_call(
        functools.partial(scatter_kernel, cube, groups),
        out_shape=[jax.ShapeDtypeStruct(p.shape[-2:], jnp.float32) for p in parts],
        in_specs=[pl.BlockSpec(memory_space=pl.ANY)] * groups,
        out_specs=[pl.BlockSpec(memory_space=pltpu.VMEM)] * groups,
        scratch_shapes=scratch,
        compiler_params=pltpu.CompilerParams(
            collective_id=collective_id, has_side_effects=True, vmem_limit_bytes=48 << 20
        ),
        name="scatter_grads",
    )(*parts)


def collect_kernel(cube, x_ref, o_ref, send_sem, recv_sem):
    me = cube.index()
    cube.greet_all()

    def make(i):
        to = lax.rem(me + i, cube.total)
        return remote(x_ref, o_ref.at[i], send_sem.at[i], recv_sem.at[i], cube.coords(to))

    @pl.loop(1, cube.total)
    def _(i):
        make(i).start()

    o_ref[0] = x_ref[...]

    @pl.loop(1, cube.total)
    def _(i):
        make(i).wait()


def collect(cube, x, collective_id):
    return pl.pallas_call(
        functools.partial(collect_kernel, cube),
        out_shape=jax.ShapeDtypeStruct((cube.total,) + x.shape, x.dtype),
        in_specs=[pl.BlockSpec(memory_space=pltpu.VMEM)],
        out_specs=pl.BlockSpec(memory_space=pltpu.VMEM),
        scratch_shapes=[
            pltpu.SemaphoreType.DMA((cube.total,)),
            pltpu.SemaphoreType.DMA((cube.total,)),
        ],
        compiler_params=pltpu.CompilerParams(
            collective_id=collective_id, has_side_effects=True
        ),
        name="collect_stats",
    )(x)


def by_matrix(j, action):
    for width in sorted(set(WIDTHS)):
        members = [i for i in range(8) if WIDTHS[i] == width]
        hit = functools.reduce(jnp.logical_or, [j == i for i in members])
        pl.when(hit)(functools.partial(action, width // 4))


def quarter_start(t):
    j, q = t // 4, lax.rem(t, 4)
    start = 0
    for i in range(8):
        start = start + jnp.where(j == i, STARTS[i] + q * (WIDTHS[i] // 4), 0)
    return pl.multiple_of(start, 128)


def owner_coords(cube, t):
    return ((t // 4) * (cube.dp_size // 8), lax.rem(t // 2, 2), lax.rem(t, 2))


def spread_kernel(cube, x_ref, o_ref, own_sem, send_sem, recv_sem):
    me = cube.index()
    repeat = cube.dp_size // 8
    d, s, c = lax.axis_index("dp"), lax.axis_index("seq"), lax.axis_index("shard")
    owner = lax.rem(d, repeat) == 0
    mine = ((d // repeat) * 2 + s) * 2 + c
    cube.greet_all()

    def send(i, wait):
        t = lax.rem(mine + i, 32)
        peer = owner_coords(cube, t)
        other = jnp.logical_or(jnp.logical_not(owner), i > 0)

        def go(width):
            src = x_ref.at[:, pl.ds(quarter_start(t), width)]
            dst = o_ref.at[me, :, pl.ds(0, width)]
            copy = remote(src, dst, send_sem.at[i], recv_sem.at[me], peer)
            if wait:
                copy.wait_send()
            else:
                copy.start()

        pl.when(other)(lambda: by_matrix(t // 4, go))

    pl.loop(0, 32)(functools.partial(send, wait=False))

    def keep(width):
        copy = pltpu.make_async_copy(
            x_ref.at[:, pl.ds(quarter_start(mine), width)],
            o_ref.at[me, :, pl.ds(0, width)],
            own_sem,
        )
        copy.start()
        copy.wait()

    def receive(width):
        @pl.loop(1, cube.total)
        def _(i):
            source = lax.rem(me + i, cube.total)
            place = o_ref.at[source, :, pl.ds(0, width)]
            remote(
                place, place, send_sem.at[0], recv_sem.at[source], cube.coords(source)
            ).wait_recv()

    @pl.when(owner)
    def _():
        by_matrix(mine // 4, keep)
        by_matrix(mine // 4, receive)

    pl.loop(0, 32)(functools.partial(send, wait=True))


def spread(cube, x, collective_id):
    return pl.pallas_call(
        functools.partial(spread_kernel, cube),
        out_shape=jax.ShapeDtypeStruct((cube.total, x.shape[0], BLOCK), x.dtype),
        in_specs=[pl.BlockSpec(memory_space=pl.ANY)],
        out_specs=pl.BlockSpec(memory_space=pl.ANY),
        scratch_shapes=[
            pltpu.SemaphoreType.DMA,
            pltpu.SemaphoreType.DMA((32,)),
            pltpu.SemaphoreType.DMA((cube.total,)),
        ],
        compiler_params=pltpu.CompilerParams(
            collective_id=collective_id, has_side_effects=True
        ),
        name="spread_momentum",
    )(x)


def restore_kernel(cube, x_ref, o_ref, own_sem, send_sem, recv_sem):
    me = cube.index()
    repeat = cube.dp_size // 8
    d, s, c = lax.axis_index("dp"), lax.axis_index("seq"), lax.axis_index("shard")
    owner = lax.rem(d, repeat) == 0
    mine = ((d // repeat) * 2 + s) * 2 + c
    cube.greet_all()

    def send_all(wait, width):
        @pl.loop(1, cube.total)
        def _(i):
            to = lax.rem(me + i, cube.total)
            src = x_ref.at[to, :, pl.ds(0, width)]
            dst = o_ref.at[:, pl.ds(quarter_start(mine), width)]
            copy = remote(src, dst, send_sem.at[i], recv_sem.at[mine], cube.coords(to))
            if wait:
                copy.wait_send()
            else:
                copy.start()

    def keep(width):
        copy = pltpu.make_async_copy(
            x_ref.at[me, :, pl.ds(0, width)],
            o_ref.at[:, pl.ds(quarter_start(mine), width)],
            own_sem,
        )
        copy.start()
        copy.wait()

    @pl.when(owner)
    def _():
        by_matrix(mine // 4, functools.partial(send_all, False))
        by_matrix(mine // 4, keep)

    def receive(i):
        t = lax.rem(mine + i, 32)
        other = jnp.logical_or(jnp.logical_not(owner), i > 0)

        def go(width):
            place = o_ref.at[:, pl.ds(quarter_start(t), width)]
            remote(
                place, place, send_sem.at[0], recv_sem.at[t], owner_coords(cube, t)
            ).wait_recv()

        pl.when(other)(lambda: by_matrix(t // 4, go))

    pl.loop(0, 32)(receive)

    @pl.when(owner)
    def _():
        by_matrix(mine // 4, functools.partial(send_all, True))


def restore(cube, x, collective_id):
    return pl.pallas_call(
        functools.partial(restore_kernel, cube),
        out_shape=jax.ShapeDtypeStruct((x.shape[1], STARTS[8]), x.dtype),
        in_specs=[pl.BlockSpec(memory_space=pl.ANY)],
        out_specs=pl.BlockSpec(memory_space=pl.ANY),
        scratch_shapes=[
            pltpu.SemaphoreType.DMA,
            pltpu.SemaphoreType.DMA((cube.total,)),
            pltpu.SemaphoreType.DMA((32,)),
        ],
        compiler_params=pltpu.CompilerParams(
            collective_id=collective_id, has_side_effects=True
        ),
        name="restore_rows",
    )(x)


def split(value):
    high = value.astype(jnp.bfloat16)
    low = (value - high.astype(jnp.float32)).astype(jnp.bfloat16)
    return high, low


def product(left, right):
    (lh, ll), (rh, rl) = left, right
    dot = functools.partial(jnp.dot, preferred_element_type=jnp.float32)
    return dot(lh, rh) + (dot(lh, rl) + dot(ll, rh))


def orthogonalize_kernel(cube, x_ref, o_ref, gram_ref, work, landed, send_sem, recv_sem):
    barrier = pltpu.get_barrier_semaphore()
    peers = (cube.partner(cube.levels + 1), cube.partner(cube.levels))
    for peer in peers:
        pl.semaphore_signal(barrier, inc=1, device_id=peer, device_id_type=MESH)
    pl.semaphore_wait(barrier, 2)
    repeat = cube.dp_size // 8
    j = lax.axis_index("dp") // repeat
    width = 0
    for i in range(8):
        width = width + jnp.where(j == i, WIDTHS[i] // 4, 0)
    column = lax.broadcasted_iota(jnp.int32, (D, BLOCK), 1)
    block = jnp.where(column < width, x_ref[...].astype(jnp.float32), 0.0)
    bh, bl = split(block)
    dot_t = lambda a, b: lax.dot_general(
        a, b, (((1,), (1,)), ((), ())), preferred_element_type=jnp.float32
    )
    gram_ref[0] = dot_t(bh, bh) + (dot_t(bh, bl) + dot_t(bl, bh))
    for step in range(2):
        copy = remote(
            gram_ref.at[step], landed.at[step], send_sem.at[step], recv_sem.at[step], peers[step]
        )
        copy.start()
        copy.wait()
        gram_ref[step + 1] = gram_ref[step] + landed[step]
    gram = gram_ref[2]
    row = lax.broadcasted_iota(jnp.int32, (D, D), 0)
    col = lax.broadcasted_iota(jnp.int32, (D, D), 1)
    eye = row == col
    square = jnp.sum(jnp.sum(jnp.where(eye, gram, 0.0), axis=1, keepdims=True), axis=0, keepdims=True)
    scale = 1.0 / (jnp.sqrt(square) + 1e-07)
    gram = gram * (scale * scale)
    block = block * scale
    for step in range(5):
        parts = split(gram)
        mixed = COEF_B * gram + COEF_C * product(parts, parts)
        mixed = jnp.where(eye, mixed + COEF_A, mixed)
        mixed_parts = split(mixed)
        block = product(mixed_parts, split(block))
        if step < 4:
            gram = product(mixed_parts, split(product(mixed_parts, parts)))
    o_ref[...] = block.astype(o_ref.dtype)


def orthogonalize_blocks(cube, x, out_dtype, collective_id):
    return pl.pallas_call(
        functools.partial(orthogonalize_kernel, cube),
        out_shape=jax.ShapeDtypeStruct((D, BLOCK), out_dtype),
        in_specs=[pl.BlockSpec(memory_space=pltpu.VMEM)],
        out_specs=pl.BlockSpec(memory_space=pltpu.VMEM),
        scratch_shapes=[
            pltpu.VMEM((3, D, D), jnp.float32),
            pltpu.VMEM((8, 128), jnp.float32),
            pltpu.VMEM((2, D, D), jnp.float32),
            pltpu.SemaphoreType.DMA((2,)),
            pltpu.SemaphoreType.DMA((2,)),
        ],
        compiler_params=pltpu.CompilerParams(
            collective_id=collective_id, has_side_effects=True, vmem_limit_bytes=48 << 20
        ),
        name="orthogonalize",
    )(x)

def with_halo(value, sides, width):
    for axis, dim in sides:
        devices, length = (lax.axis_size(axis), value.shape[dim])
        up = [(i, (i + 1) % devices) for i in range(devices - 1)]
        down = [(j, i) for i, j in up]
        last = lax.slice_in_dim(value, length - width, length, axis=dim)
        first = lax.slice_in_dim(value, 0, width, axis=dim)
        before = lax.ppermute(last, axis, up)
        after = lax.ppermute(first, axis, down)
        value = jnp.concatenate([before, value, after], axis=dim)
    return value


def matmul(left, right):
    return jnp.dot(left, right, preferred_element_type=jnp.float32)


def matmul_right_t(left, right):
    return lax.dot_general(
        left, right, (((1,), (1,)), ((), ())), preferred_element_type=jnp.float32
    )


def matmul_left_t(left, right):
    return lax.dot_general(
        left, right, (((0,), (0,)), ((), ())), preferred_element_type=jnp.float32
    )


def layer_norm(field, gain):
    centre = jnp.mean(field, axis=-1, keepdims=True)
    shifted = field - centre
    inverse = lax.rsqrt(jnp.mean(shifted * shifted, axis=-1, keepdims=True) + EPS_NORM)
    normed = shifted * inverse
    return (normed * gain, normed, inverse)


def norm_back(grad_out, normed, inverse, gain):
    scaled = grad_out * gain
    grad_in = inverse * (
        scaled
        - jnp.mean(scaled, axis=-1, keepdims=True)
        - normed * jnp.mean(scaled * normed, axis=-1, keepdims=True)
    )
    return (grad_in, jnp.sum(grad_out * normed, axis=0))


def silu_slope(values):
    sigma = jax.nn.sigmoid(values)
    return sigma * (1.0 + values * (1.0 - sigma))


def ffn_forward(field, gain, w_in, w_back):
    normed_out, normed, inverse = layer_norm(field, gain)
    lifted = normed_out.astype(jnp.bfloat16)
    hidden_pre = matmul(lifted, w_in)
    hidden_act = jax.nn.silu(hidden_pre).astype(jnp.bfloat16)
    return (
        field + 0.5 * matmul_right_t(hidden_act, w_back),
        (lifted, hidden_pre, hidden_act, normed, inverse),
    )


def ffn_backward(grad, saved, gain, w_in, w_back):
    lifted, hidden_pre, hidden_act, normed, inverse = saved
    grad_branch = (0.5 * grad).astype(jnp.bfloat16)
    grad_back = matmul_left_t(grad_branch, hidden_act)
    grad_act = matmul(grad_branch, w_back)
    grad_pre = (grad_act * silu_slope(hidden_pre)).astype(jnp.bfloat16)
    grad_in = matmul_left_t(lifted, grad_pre)
    grad_field, grad_gain = norm_back(matmul_right_t(grad_pre, w_in), normed, inverse, gain)
    return (grad + grad_field, grad_in, grad_back, grad_gain)


def depthwise(wide, kernel, count):
    total = wide[0:count] * kernel[:, 0]
    for tap_idx in range(1, K):
        total = total + wide[tap_idx : tap_idx + count] * kernel[:, tap_idx]
    return total


def spread_rows(window, count, keys_len):
    padded = jnp.concatenate([window, jnp.zeros((1,), window.dtype)])
    tiled = jnp.broadcast_to(padded[None, :], (count, keys_len + count)).reshape(-1)
    shaped = tiled[: count * (keys_len + count - 1)].reshape(count, keys_len + count - 1)
    return shaped[:, count - 1 : count - 1 + keys_len]


def collect_rows(grid, count, keys_len):
    placed = jnp.concatenate([jnp.zeros((count, count - 1), grid.dtype), grid], axis=1).reshape(-1)
    placed = jnp.concatenate([placed, jnp.zeros((count,), grid.dtype)])
    return jnp.sum(placed.reshape(count, keys_len + count), axis=0)[: keys_len + count - 1]


def attention_scores(query, keys, offsets, first_row, row_start, block, head_idx):
    length = keys.shape[0]
    columns = slice(head_idx * DH, (head_idx + 1) * DH)
    anchor = length - block - first_row - row_start
    window = lax.dynamic_slice_in_dim(offsets[head_idx], anchor, length + block - 1)
    product = matmul_right_t(query[row_start : row_start + block, columns], keys[:, columns])
    return product * DH ** (-0.5) + spread_rows(window, block, length)


def attention_forward(query, keys, values, offsets, first_row):
    total_rows = query.shape[0]
    block = min(512, total_rows)
    head_outs = []
    head_lse = []
    for head_idx in range(H):
        scores = attention_scores(query, keys, offsets, first_row, 0, block, head_idx)
        row_max = jnp.max(scores, axis=1, keepdims=True)
        shifted_exp = jnp.exp(scores - row_max)
        row_total = jnp.sum(shifted_exp, axis=1, keepdims=True)
        prob_low = (shifted_exp / row_total).astype(jnp.bfloat16)
        head_outs.append(matmul(prob_low, values[:, head_idx * DH : (head_idx + 1) * DH]))
        head_lse.append((row_max + jnp.log(row_total))[:, 0])
    out_blocks = jnp.concatenate(head_outs, axis=1)
    lse_blocks = jnp.stack(head_lse, axis=0)
    return (out_blocks, lse_blocks)


def attention_backward(query, keys, values, offsets, first_row, log_total, grad_attended, delta):
    total_rows = query.shape[0]
    length = keys.shape[0]
    block = min(512, total_rows)
    scale = DH ** (-0.5)
    key_parts = [jnp.zeros((length, DH), jnp.float32) for head_idx in range(H)]
    value_parts = [jnp.zeros((length, DH), jnp.float32) for head_idx in range(H)]
    offset_rows = [jnp.zeros((2 * length - 1,), jnp.float32) for head_idx in range(H)]
    head_grads = []
    for head_idx in range(H):
        columns = slice(head_idx * DH, (head_idx + 1) * DH)
        scores = attention_scores(query, keys, offsets, first_row, 0, block, head_idx)
        prob = jnp.exp(scores - log_total[head_idx, 0:block][:, None])
        prob_low = prob.astype(jnp.bfloat16)
        grad_piece = grad_attended[0:block, columns]
        value_parts[head_idx] = matmul_left_t(prob_low, grad_piece)
        grad_prob = matmul_right_t(grad_piece, values[:, columns])
        grad_score = prob * (grad_prob - delta[0:block, head_idx][:, None])
        score_low = grad_score.astype(jnp.bfloat16)
        head_grads.append(matmul(score_low, keys[:, columns]) * scale)
        key_parts[head_idx] = matmul_left_t(score_low, query[0:block, columns]) * scale
        anchor = length - block - first_row - 0
        offset_rows[head_idx] = lax.dynamic_update_slice_in_dim(
            offset_rows[head_idx], collect_rows(grad_score, block, length), anchor, 0
        )
    query_blocks = jnp.concatenate(head_grads, axis=1)
    return (
        query_blocks,
        jnp.concatenate(key_parts, axis=1),
        jnp.concatenate(value_parts, axis=1),
        jnp.stack(offset_rows, axis=0),
    )


def mean_last(value):
    return jnp.mean(value, axis=-1, keepdims=True)


def normalize(field):
    shifted = field - mean_last(field)
    inverse = lax.rsqrt(mean_last(shifted * shifted) + EPS_NORM)
    return shifted * inverse, inverse


def norm_grad(grad_out, normed, inverse, gain):
    scaled = grad_out * gain
    grad_in = inverse * (scaled - mean_last(scaled) - normed * mean_last(scaled * normed))
    return grad_in, jnp.sum(grad_out * normed, axis=0, keepdims=True)


def row_to_tile(ref, base, row):
    for k in range(4):
        ref[base + k : base + k + 1, :] = row[:, 128 * k : 128 * (k + 1)]


def tile_to_row(tile):
    return jnp.concatenate([tile[k : k + 1, :] for k in range(4)], axis=1)


def skew(row, count):
    sub = lax.broadcasted_iota(jnp.int32, (8, 512), 0)
    block = jnp.broadcast_to(row, (8, 512))
    for bit in (1, 2, 4):
        block = jnp.where((sub // bit) % 2 == 1, pltpu.roll(block, bit, 1), block)
    size = 8
    while size < count:
        block = jnp.concatenate([block, pltpu.roll(block, size, 1)], axis=0)
        size *= 2
    return block


def unskew_sum(grid):
    size = grid.shape[0] // 2
    while size >= 8:
        grid = grid[:size] + pltpu.roll(grid[size:], 512 - size, 1)
        size //= 2
    sub = lax.broadcasted_iota(jnp.int32, (8, 512), 0)
    for bit in (1, 2, 4):
        grid = jnp.where((sub // bit) % 2 == 1, pltpu.roll(grid, 512 - bit, 1), grid)
    return jnp.sum(grid, axis=0, keepdims=True)


class Gather:
    def __init__(self, cube, mine, bands, send_sem, recv_sem):
        self.cube, self.mine, self.bands = cube, mine, bands
        self.send_sem, self.recv_sem = send_sem, recv_sem
        self.copies = {}

    def start(self, g, stage):
        for half in range(2):
            order = self.cube.gather_orders[half]
            columns = pl.ds(*halves(self.bands[g].shape[-1])[half])
            done = order[:stage]
            index = tuple(
                slice(None) if k in done else self.mine[k] for k in range(self.cube.digits)
            )
            place = self.bands[g].at[index + (slice(None), columns)]
            copy = remote(
                place,
                place,
                self.send_sem.at[g, half, stage],
                self.recv_sem.at[g, half, stage],
                self.cube.partner(order[stage]),
            )
            copy.start()
            self.copies[g, half, stage] = copy

    def arrive(self, g, stage):
        for half in range(2):
            self.copies[g, half, stage].wait_recv()

    def advance(self, g, stage):
        self.arrive(g, stage)
        self.start(g, stage + 1)

    def finish(self):
        for copy in self.copies.values():
            copy.wait_send()


class Scatter:
    def __init__(self, cube, mine, bands, landed, outs, send_sem, recv_sem):
        self.cube, self.mine, self.bands, self.landed, self.outs = cube, mine, bands, landed, outs
        self.send_sem, self.recv_sem = send_sem, recv_sem
        self.copies = {}

    def columns(self, g, half):
        return pl.ds(*halves(self.bands[g].shape[-1])[half])

    def start(self, g, stage):
        for half in range(2):
            order = self.cube.scatter_orders[half]
            index = []
            for k in range(self.cube.digits):
                at = order.index(k)
                if at > stage:
                    index.append(slice(None))
                else:
                    index.append(1 - self.mine[k] if at == stage else self.mine[k])
            source = self.bands[g].at[tuple(index) + (slice(None), self.columns(g, half))]
            copy = remote(
                source,
                self.landed[g, half, stage],
                self.send_sem.at[g, half, stage],
                self.recv_sem.at[g, half, stage],
                self.cube.partner(order[stage]),
            )
            copy.start()
            self.copies[g, half, stage] = copy

    def add(self, g, half, stage):
        order = self.cube.scatter_orders[half]
        columns = self.columns(g, half)
        free = [k for k in range(self.cube.digits) if order.index(k) > stage]
        target, extra = self.bands[g], self.landed[g, half, stage]
        everything = (slice(None), columns)

        def one(i):
            digit = {
                k: lax.rem(i // (1 << (len(free) - 1 - n)), 2) for n, k in enumerate(free)
            }
            full = tuple(digit.get(k, self.mine[k]) for k in range(self.cube.digits)) + everything
            short = tuple(digit[k] for k in free) + (slice(None), slice(None))
            total = target[full].astype(jnp.float32) + extra[short].astype(jnp.float32)
            if free:
                target[full] = total.astype(target.dtype)
            else:
                self.outs[g][:, columns] = total

        if free:
            pl.loop(0, 1 << len(free))(one)
        else:
            one(0)

    def advance(self, g, stage):
        for half in range(2):
            self.copies[g, half, stage].wait_recv()
            self.add(g, half, stage)
        if stage + 1 < self.cube.digits:
            self.start(g, stage + 1)

    def finish(self):
        for copy in self.copies.values():
            copy.wait_send()


class Collect:
    def __init__(self, cube, tile, slots, send_sem, recv_sem):
        self.cube, self.tile, self.slots = cube, tile, slots
        self.send_sem, self.recv_sem = send_sem, recv_sem

    def make(self, i):
        to = self.cube.coords(lax.rem(self.cube.index() + i, self.cube.total))
        return remote(
            self.tile, self.slots.at[i], self.send_sem.at[i], self.recv_sem.at[i], to
        )

    def start(self):
        pl.loop(1, self.cube.total)(lambda i: self.make(i).start())
        self.slots[0] = self.tile[...]

    def arrive(self):
        pl.loop(1, self.cube.total)(lambda i: self.make(i).wait())

    def total(self):
        result = self.slots[0]
        for i in range(1, self.cube.total):
            result = result + self.slots[i]
        return result


SMALL_REL, SMALL_VEC, SMALL_DEPTH = 0, H, H + 7
SMALL_END = H + 7 + K
EDGE = 16


def step_kernel(cube, rel_rows, r):
    bf16, f32 = jnp.bfloat16, jnp.float32
    x_ref, cot_ref, bucket_ref = r.inputs, r.cotangent, r.bucket
    tokens = x_ref.shape[0]
    token_total = tokens * cube.total
    rows = r.small.shape[0]
    mine = cube.mine()
    seq = lax.axis_index("seq")
    early = seq == 0
    first_row = pl.multiple_of(seq * tokens, tokens)
    other_row = pl.multiple_of((1 - seq) * tokens, tokens)
    across = cube.partner(cube.levels)
    lengths = [ref.shape[-1] for ref in (r.first, r.middle, r.second)]
    first, middle, second, d_first, d_middle, d_second = (
        ref.reshape(D, ref.shape[-1])
        for ref in (r.first, r.middle, r.second, r.d_first, r.d_middle, r.d_second)
    )
    a, xh = r.a, r.xh

    barrier = pltpu.get_barrier_semaphore()
    me = cube.index()

    @pl.loop(1, cube.total)
    def _(i):
        peer = cube.coords(lax.rem(me + i, cube.total))
        pl.semaphore_signal(barrier, inc=1, device_id=peer, device_id_type=MESH)

    own = tuple(mine)
    r.first[own + (slice(None), slice(0, FF))] = r.w_up[:, :FF].astype(bf16)
    r.first[own + (slice(None), slice(FF, 2 * FF))] = r.w_down[:, :FF].astype(bf16)
    r.first[own + (slice(None), slice(2 * FF, lengths[0]))] = r.small[...].astype(bf16)
    r.middle[own + (slice(None), slice(0, 3 * D))] = r.w_qkv[...].astype(bf16)
    r.middle[own + (slice(None), slice(3 * D, 4 * D))] = r.w_out[...].astype(bf16)
    r.middle[own + (slice(None), slice(4 * D, 6 * D))] = r.w_glu[...].astype(bf16)
    r.middle[own + (slice(None), slice(6 * D, 7 * D))] = r.w_point[...].astype(bf16)
    r.second[own + (slice(None), slice(0, FF))] = r.w_up[:, FF:].astype(bf16)
    r.second[own + (slice(None), slice(FF, 2 * FF))] = r.w_down[:, FF:].astype(bf16)
    pl.semaphore_wait(barrier, cube.total - 1)

    gather = Gather(
        cube, mine, (r.first, r.middle, r.second), r.g_send, r.g_recv
    )
    landed = {
        (g, half, stage): r.land[(g * 2 + half) * cube.digits + stage]
        for g in range(3)
        for half in range(2)
        for stage in range(cube.digits)
    }
    scatter = Scatter(
        cube,
        mine,
        (r.d_second, r.d_middle, r.d_first),
        landed,
        (r.share_second, r.share_middle, r.share_first),
        r.s_send,
        r.s_recv,
    )

    gather.start(0, 0)
    xh0, inv0 = normalize(x_ref[...])
    xh[0] = xh0
    rho = lax.broadcasted_iota(jnp.int32, (D, 2 * 256), 0)
    bucket_of = jnp.where(rho % rows < rel_rows, (rho // rows) * rel_rows + rho % rows, -2)
    r.hit[...] = (bucket_ref[...] == bucket_of).astype(f32).astype(bf16)
    gather.advance(0, 0)
    gather.start(1, 0)
    gather.advance(0, 1)
    gather.advance(1, 0)
    gather.start(2, 0)
    gather.advance(0, 2)
    gather.advance(1, 1)
    gather.advance(2, 0)
    gather.advance(0, 3)
    gather.advance(1, 2)
    gather.advance(2, 1)
    gather.arrive(0, 4)

    small = r.small_t
    small[...] = jnp.transpose(first[:, 2 * FF : 2 * FF + 128].astype(f32))
    gains = [small[SMALL_VEC + i : SMALL_VEC + i + 1, :] for i in range(7)]
    taps = [small[SMALL_DEPTH + k : SMALL_DEPTH + k + 1, :] for k in range(K)]
    CH = 512

    def ffn_forward_fused(index, field, normed, weights, u_ref, s_ref):
        low = (normed * gains[(0, 1, 2, 3)[index]]).astype(bf16)
        a[index] = low
        for c in range(0, FF, CH):
            u = matmul(low, weights[:, c : c + CH])
            u_ref[:, c : c + CH] = u
            s_ref[:, c : c + CH] = (u * jax.nn.sigmoid(u)).astype(bf16)
        return field + 0.5 * matmul_right_t(s_ref[...], weights[:, FF : 2 * FF])

    section1 = ffn_forward_fused(0, x_ref[...], xh[0], first, r.u1, r.s1)
    r.sec1[...] = section1
    xh1, inv1 = normalize(section1)
    xh[1] = xh1
    a[1] = (xh1 * gains[1]).astype(bf16)
    gather.advance(1, 3)
    offsets = matmul(small[0:8, :].astype(bf16), r.hit[...])
    offsets = jnp.where(
        early, pltpu.roll(offsets, 257, 1), pltpu.roll(offsets, (tokens + 257) % 512, 1)
    )
    for h in range(H):
        r.bias[h] = skew(offsets[h : h + 1, :], tokens)[:, : 2 * tokens]
    gather.arrive(1, 4)

    q_ref, kv = r.q, r.kv
    kv[pl.ds(first_row, tokens), :] = matmul(a[1], middle[:, D : 3 * D]).astype(bf16)
    kv_copy = remote(
        kv.at[pl.ds(first_row, tokens)],
        kv.at[pl.ds(first_row, tokens)],
        r.kv_send,
        r.kv_recv,
        across,
    )
    kv_copy.start()
    gather.advance(2, 2)
    q_ref[...] = matmul(a[1], middle[:, :D]).astype(bf16)
    kv_copy.wait_recv()
    lane = lax.broadcasted_iota(jnp.int32, (1, 128), 1)
    lane_masks = [(lane // DH == e).astype(f32) for e in range(2)]
    low_masks = [m.astype(bf16) for m in lane_masks]
    scale = DH ** (-0.5)
    for p in range(H // 2):
        columns = slice(128 * p, 128 * (p + 1))
        k_pair, v_pair = kv[:, columns], kv[:, D + 128 * p : D + 128 * (p + 1)]
        merged = None
        for e in range(2):
            q_head = q_ref[:, columns] * low_masks[e]
            scores = matmul_right_t(q_head, k_pair) * scale + r.bias[2 * p + e]
            shifted = jnp.exp(scores - jnp.max(scores, axis=1, keepdims=True))
            prob = shifted / jnp.sum(shifted, axis=1, keepdims=True)
            r.prob[2 * p + e] = prob
            out = matmul(prob.astype(bf16), v_pair) * lane_masks[e]
            merged = out if merged is None else merged + out
        r.att[:, columns] = merged
    att_low = r.att[...].astype(bf16)
    r.att_low[...] = att_low
    gather.advance(2, 3)
    section2 = r.sec1[...] + matmul(att_low, middle[:, 3 * D : 4 * D])
    r.sec2[...] = section2
    xh2, inv2 = normalize(section2)
    xh[2] = xh2
    a[2] = (xh2 * gains[2]).astype(bf16)
    gate_first = matmul(a[2], middle[:, 4 * D : 5 * D])
    sig = jax.nn.sigmoid(matmul(a[2], middle[:, 5 * D : 6 * D]))
    r.gate[...] = gate_first
    r.sig[...] = sig
    wide = r.wide
    wide[EDGE : EDGE + tokens, :] = gate_first * sig
    edge_row = pl.multiple_of(EDGE + (1 - seq) * (tokens - EDGE), EDGE)
    halo_copy = remote(
        wide.at[pl.ds(edge_row, EDGE)], r.halo, r.halo_send, r.halo_recv, across
    )
    halo_copy.start()
    zero_edge = jnp.zeros((EDGE, D), f32)
    halo_copy.wait()
    wide[0:EDGE, :] = jnp.where(early, zero_edge, r.halo[...])
    wide[EDGE + tokens :, :] = jnp.where(early, r.halo[...], zero_edge)
    conv_ref = r.conv
    for b in range(D // 128):
        cols = slice(128 * b, 128 * (b + 1))
        total = jnp.zeros((tokens, 128), f32)
        for k in range(K):
            total = total + wide[k + 1 : k + 1 + tokens, cols] * taps[k][:, cols]
        conv_ref[:, cols] = total
    conv = conv_ref[...]
    part_sum = jnp.sum(conv, axis=0, keepdims=True)
    part_off = conv - part_sum * (1.0 / tokens)
    part_square = jnp.sum(part_off * part_off, axis=0, keepdims=True)
    row_to_tile(r.tile1, 0, part_sum)
    row_to_tile(r.tile1, 4, part_square)
    stats = Collect(cube, r.tile1, r.slots1, r.c1_send, r.c1_recv)
    stats.start()
    gather.arrive(2, 4)
    stats.arrive()
    sums = stats.total()
    mean4 = sums[0:4] * (1.0 / token_total)
    spread4 = jnp.zeros((4, 128), f32)
    for i in range(cube.total):
        off = r.slots1[i][0:4] * (1.0 / tokens) - mean4
        spread4 = spread4 + off * off
    var4 = (sums[4:8] + spread4 * tokens) * (1.0 / token_total)
    mean = tile_to_row(mean4)
    inv_std = tile_to_row(lax.rsqrt(var4 + EPS_BATCH))

    xb = (conv_ref[...] - mean) * inv_std
    r.xb[...] = xb
    bn = xb * gains[5] + gains[6]
    r.bn[...] = bn
    sw = (bn * jax.nn.sigmoid(bn)).astype(bf16)
    r.sw[...] = sw
    section3 = r.sec2[...] + matmul(sw, middle[:, 6 * D : 7 * D])
    xh3, inv3 = normalize(section3)
    xh[3] = xh3
    section4 = ffn_forward_fused(3, section3, xh3, second, r.u2, r.s2)
    xh4, inv4 = normalize(section4)
    r.outputs[...] = xh4 * gains[4]

    sg = r.small_grad
    sg[...] = jnp.zeros_like(sg)
    cot = cot_ref[...]
    d4, sg[SMALL_VEC + 4 : SMALL_VEC + 5, :] = norm_grad(cot, xh4, inv4, gains[4])

    def slope(value):
        sigma = jax.nn.sigmoid(value)
        return sigma * (1.0 + value * (1.0 - sigma))

    def ffn_backward_fused(grad, weights, u_ref, du_ref):
        low = (0.5 * grad).astype(bf16)
        for c in range(0, FF, CH):
            act = matmul(low, weights[:, FF + c : FF + c + CH])
            du_ref[:, c : c + CH] = (act * slope(u_ref[:, c : c + CH])).astype(bf16)
        return low, matmul_right_t(du_ref[...], weights[:, :FF])

    def weight_grad(left, right_ref, target, start, width):
        for c in range(0, width, CH):
            target[:, start + c : start + c + CH] = matmul_left_t(
                left, right_ref[:, c : c + CH]
            ).astype(bf16)

    e2, back = ffn_backward_fused(d4, second, r.u2, r.du)
    r.e_low[...] = e2
    part, sg[SMALL_VEC + 3 : SMALL_VEC + 4, :] = norm_grad(back, xh[3], inv3, gains[3])
    d3 = d4 + part
    r.d[...] = d3
    e3 = d3.astype(bf16)
    r.e3[...] = e3
    dbn = matmul_right_t(e3, middle[:, 6 * D : 7 * D]) * slope(r.bn[...])
    xb = r.xb[...]
    sg[SMALL_VEC + 5 : SMALL_VEC + 6, :] = jnp.sum(dbn * xb, axis=0, keepdims=True)
    sg[SMALL_VEC + 6 : SMALL_VEC + 7, :] = jnp.sum(dbn, axis=0, keepdims=True)
    dxb = dbn * gains[5]
    r.dxb[...] = dxb
    row_to_tile(r.tile2, 0, jnp.sum(dxb, axis=0, keepdims=True))
    row_to_tile(r.tile2, 4, jnp.sum(dxb * xb, axis=0, keepdims=True))
    sums2 = Collect(cube, r.tile2, r.slots2, r.c2_send, r.c2_recv)
    sums2.start()
    token_edge = pl.multiple_of((1 - seq) * (tokens - EDGE), EDGE)
    edges = r.edges
    edges[0:EDGE, :] = r.dxb[pl.ds(token_edge, EDGE), :]
    edges[EDGE:, :] = r.xb[pl.ds(token_edge, EDGE), :]
    edge_copy = remote(edges, r.edges_in, r.edge_send, r.edge_recv, across)
    edge_copy.start()

    weight_grad(r.e_low[...], r.s2, d_second, FF, FF)
    weight_grad(a[3], r.du, d_second, 0, FF)
    scatter.start(0, 0)
    weight_grad(r.sw[...], r.e3, d_middle, 6 * D, D)
    edge_copy.wait()
    sums2.arrive()
    total2 = sums2.total()
    mean1 = tile_to_row(total2[0:4] * (1.0 / token_total))
    mean2 = tile_to_row(total2[4:8] * (1.0 / token_total))
    dwide = r.dwide
    dwide[EDGE : EDGE + tokens, :] = inv_std * (r.dxb[...] - mean1 - r.xb[...] * mean2)
    edge = inv_std * (r.edges_in[0:EDGE, :] - mean1 - r.edges_in[EDGE:, :] * mean2)
    dwide[0:EDGE, :] = jnp.where(early, zero_edge, edge)
    dwide[EDGE + tokens :, :] = jnp.where(early, edge, zero_edge)
    dglu_ref = r.conv
    for b in range(D // 128):
        cols = slice(128 * b, 128 * (b + 1))
        total = jnp.zeros((tokens, 128), f32)
        for k in range(K):
            total = total + dwide[31 - k : 31 - k + tokens, cols] * taps[k][:, cols]
        dglu_ref[:, cols] = total
    dglu, sig = dglu_ref[...], r.sig[...]
    r.dgates[:, :D] = (dglu * sig).astype(bf16)
    r.dgates[:, D:] = (dglu * r.gate[...] * sig * (1.0 - sig)).astype(bf16)
    scatter.advance(0, 0)
    back = matmul_right_t(r.dgates[...], middle[:, 4 * D : 6 * D])
    part, sg[SMALL_VEC + 2 : SMALL_VEC + 3, :] = norm_grad(back, xh[2], inv2, gains[2])
    d2 = r.d[...] + part
    r.d[...] = d2
    e1 = d2.astype(bf16)
    r.e_low[...] = e1
    dob = matmul_right_t(e1, middle[:, 3 * D : 4 * D]).astype(bf16)
    r.dob[...] = dob

    off_rows = []
    give, keep, got = r.give, r.keep, r.got
    kv_grads = []
    for p in range(H // 2):
        columns = slice(128 * p, 128 * (p + 1))
        k_pair, v_pair = kv[:, columns], kv[:, D + 128 * p : D + 128 * (p + 1)]
        att_pair = r.att[:, columns]
        dq = dk = dv = None
        for e in range(2):
            h = 2 * p + e
            dob_head = r.dob[:, columns] * low_masks[e]
            q_head = q_ref[:, columns] * low_masks[e]
            delta = jnp.sum(dob_head.astype(f32) * att_pair, axis=1, keepdims=True)
            prob = r.prob[h]
            ds = prob * (matmul_right_t(dob_head, v_pair) - delta)
            ds_low = ds.astype(bf16)
            dv_head = matmul_left_t(prob.astype(bf16), dob_head)
            dk_head = matmul_left_t(ds_low, q_head) * scale
            dq_head = matmul(ds_low, k_pair) * (lane_masks[e] * scale)
            dv = dv_head if dv is None else dv + dv_head
            dk = dk_head if dk is None else dk + dk_head
            dq = dq_head if dq is None else dq + dq_head
            padded = jnp.concatenate([ds, jnp.zeros((tokens, 512 - 2 * tokens), f32)], axis=1)
            off_rows.append(unskew_sum(padded))
        r.dqkv[:, columns] = dq.astype(bf16)
        for n, value in enumerate((dk, dv)):
            r.dkv[n] = value
            give[p, n] = r.dkv[n, pl.ds(other_row, tokens), :].astype(bf16)
            keep[p, n] = r.dkv[n, pl.ds(first_row, tokens), :]
        copy = remote(
            give.at[p], got.at[p], r.dkv_send.at[p], r.dkv_recv.at[p], across
        )
        copy.start()
        kv_grads.append(copy)
        if p == 1:
            scatter.advance(0, 1)
    off = jnp.concatenate(off_rows, axis=0)
    off = jnp.where(early, pltpu.roll(off, 255, 1), pltpu.roll(off, 255 - tokens, 1))
    off_high, off_low = split(off)
    sg[0:8, :] = matmul_right_t(off_high, r.hit[...]) + matmul_right_t(off_low, r.hit[...])
    weight_grad(r.att_low[...], r.e_low, d_middle, 3 * D, D)
    weight_grad(a[2], r.dgates, d_middle, 4 * D, 2 * D)
    for p in range(H // 2):
        kv_grads[p].wait()
        for n in range(2):
            at = D * (n + 1) + 128 * p
            r.dqkv[:, at : at + 128] = (keep[p, n] + got[p, n].astype(f32)).astype(bf16)
    scatter.advance(0, 2)
    weight_grad(a[1], r.dqkv, d_middle, 0, 3 * D)
    scatter.start(1, 0)
    back = matmul_right_t(r.dqkv[...], middle[:, : 3 * D])
    part, sg[SMALL_VEC + 1 : SMALL_VEC + 2, :] = norm_grad(back, xh[1], inv1, gains[1])
    d1 = r.d[...] + part
    scatter.advance(0, 3)
    e0, back = ffn_backward_fused(d1, first, r.u1, r.du)
    scatter.advance(1, 0)
    part, sg[SMALL_VEC : SMALL_VEC + 1, :] = norm_grad(back, xh[0], inv0, gains[0])
    r.input_grad[...] = d1 + part
    for b in range(D // 128):
        cols = slice(128 * b, 128 * (b + 1))
        dconv = dwide[EDGE : EDGE + tokens, cols]
        for k in range(K):
            sg[SMALL_DEPTH + k : SMALL_DEPTH + k + 1, cols] = jnp.sum(
                dconv * wide[k + 1 : k + 1 + tokens, cols], axis=0, keepdims=True
            )
    d_first[:, 2 * FF : 2 * FF + 128] = jnp.transpose(sg[...]).astype(bf16)
    weight_grad(e0, r.s1, d_first, FF, FF)
    weight_grad(a[0], r.du, d_first, 0, FF)
    scatter.start(2, 0)
    scatter.advance(0, 4)
    scatter.advance(1, 1)
    scatter.advance(2, 0)
    scatter.advance(1, 2)
    scatter.advance(2, 1)
    scatter.advance(1, 3)
    scatter.advance(2, 2)
    scatter.advance(1, 4)
    scatter.advance(2, 3)
    scatter.advance(2, 4)
    gather.finish()
    scatter.finish()
    kv_copy.wait_send()


def fused_step(cube, inputs, cotangent, weights, small, bucket, rel_rows, collective_id):
    bf16, f32 = jnp.bfloat16, jnp.float32
    tokens, rows = inputs.shape[0], small.shape[0]
    widths = (2 * FF + 128, 7 * D, 2 * FF)
    lead = (2,) * cube.digits
    named = dict(
        inputs=inputs,
        cotangent=cotangent,
        w_up=weights[0],
        w_down=weights[1],
        w_qkv=weights[2],
        w_out=weights[3],
        w_glu=weights[4],
        w_point=weights[5],
        small=small,
        bucket=bucket,
    )
    outs = dict(
        outputs=(tokens, D),
        input_grad=(tokens, D),
        share_first=(rows, widths[0]),
        share_middle=(rows, widths[1]),
        share_second=(rows, widths[2]),
    )
    field = pltpu.VMEM((tokens, D), f32)
    low = pltpu.VMEM((tokens, D), bf16)
    wide_low = pltpu.VMEM((tokens, FF), bf16)
    wide_field = pltpu.VMEM((tokens + 2 * EDGE, D), f32)
    grid = pltpu.VMEM((H, tokens, 2 * tokens), f32)
    pairs = pltpu.VMEM((H // 2, 2, tokens, 128), bf16)
    tile = pltpu.VMEM((8, 128), f32)
    slots = pltpu.VMEM((cube.total, 8, 128), f32)
    stages = pltpu.SemaphoreType.DMA((3, 2, cube.digits))
    everyone = pltpu.SemaphoreType.DMA((cube.total,))
    single = pltpu.SemaphoreType.DMA
    bands = [pltpu.VMEM(lead + (rows, w), bf16) for w in widths]
    land = []
    for w in (widths[2], widths[1], widths[0]):
        for half in range(2):
            for stage in range(cube.digits):
                shape = (2,) * (cube.digits - 1 - stage) + (rows, halves(w)[half][1])
                land.append(pltpu.VMEM(shape, bf16))
    scratch = dict(
        first=bands[0],
        middle=bands[1],
        second=bands[2],
        d_first=bands[0],
        d_middle=bands[1],
        d_second=bands[2],
        land=tuple(land),
        sec1=field,
        sec2=field,
        att=field,
        gate=field,
        sig=field,
        conv=field,
        xb=field,
        bn=field,
        dxb=field,
        d=field,
        q=low,
        att_low=low,
        sw=low,
        e_low=low,
        e3=low,
        dob=low,
        a=pltpu.VMEM((4, tokens, D), bf16),
        xh=pltpu.VMEM((4, tokens, D), f32),
        u1=pltpu.VMEM((tokens, FF), f32),
        u2=pltpu.VMEM((tokens, FF), f32),
        s1=wide_low,
        s2=wide_low,
        du=wide_low,
        kv=pltpu.VMEM((2 * tokens, 2 * D), bf16),
        bias=grid,
        prob=grid,
        wide=wide_field,
        dwide=wide_field,
        halo=pltpu.VMEM((EDGE, D), f32),
        edges=pltpu.VMEM((2 * EDGE, D), f32),
        edges_in=pltpu.VMEM((2 * EDGE, D), f32),
        dgates=pltpu.VMEM((tokens, 2 * D), bf16),
        dqkv=pltpu.VMEM((tokens, 3 * D), bf16),
        dkv=pltpu.VMEM((2, 2 * tokens, 128), f32),
        give=pairs,
        got=pairs,
        keep=pltpu.VMEM((H // 2, 2, tokens, 128), f32),
        hit=pltpu.VMEM((D, 512), bf16),
        small_t=pltpu.VMEM((128, D), f32),
        small_grad=pltpu.VMEM((128, D), f32),
        tile1=tile,
        tile2=tile,
        slots1=slots,
        slots2=slots,
        g_send=stages,
        g_recv=stages,
        s_send=stages,
        s_recv=stages,
        c1_send=everyone,
        c1_recv=everyone,
        c2_send=everyone,
        c2_recv=everyone,
        kv_send=single,
        kv_recv=single,
        halo_send=single,
        halo_recv=single,
        edge_send=single,
        edge_recv=single,
        dkv_send=pltpu.SemaphoreType.DMA((H // 2,)),
        dkv_recv=pltpu.SemaphoreType.DMA((H // 2,)),
    )

    def body(*refs):
        count = len(named) + len(outs)
        r = dict(zip(list(named) + list(outs), refs[:count])) | dict(zip(scratch, refs[count:]))
        step_kernel(cube, rel_rows, types.SimpleNamespace(**r))

    return pl.pallas_call(
        body,
        out_shape=[jax.ShapeDtypeStruct(shape, f32) for shape in outs.values()],
        in_specs=[pl.BlockSpec(memory_space=pltpu.VMEM)] * len(named),
        out_specs=[pl.BlockSpec(memory_space=pltpu.VMEM)] * len(outs),
        scratch_shapes=list(scratch.values()),
        compiler_params=pltpu.CompilerParams(
            collective_id=collective_id, has_side_effects=True, vmem_limit_bytes=60 << 20
        ),
        name="block_step",
    )(*named.values())


def unfused_step(
    cube,
    inputs,
    cotangent,
    w_up,
    w_down,
    w_qkv,
    w_out,
    w_glu,
    w_point,
    small,
    bucket_table,
):
    bf16 = jnp.bfloat16
    rows = w_up.shape[0]
    rel_rows = NB // cube.total
    shard_groups = (
        jnp.concatenate([w_up[:, :FF], w_down[:, :FF], small], axis=1).astype(bf16),
        jnp.concatenate([w_qkv, w_out, w_glu, w_point], axis=1).astype(bf16),
        jnp.concatenate([w_up[:, FF:], w_down[:, FF:]], axis=1).astype(bf16),
    )
    first, middle, second = [
        full.reshape(D, -1) for full in gather_groups(cube, shard_groups, 0)
    ]
    up_first, down_first, small_low = first[:, :FF], first[:, FF : 2 * FF], first[:, 2 * FF :]
    qkv_w, out_w = middle[:, : 3 * D], middle[:, 3 * D : 4 * D]
    glu_w, point_w = middle[:, 4 * D : 6 * D], middle[:, 6 * D :]
    up_second, down_second = second[:, :FF], second[:, FF:]
    gains = small_low[:, SMALL_VEC : SMALL_VEC + 7].astype(jnp.float32)
    kernel = small_low[:, SMALL_DEPTH : SMALL_DEPTH + K].astype(jnp.float32)
    rel_low = small_low[:, :H].reshape(cube.total, rows, H)[:, :rel_rows].reshape(NB, H)
    bucket_hit = (bucket_table[:, None] == jnp.arange(NB, dtype=jnp.int32)[None, :]).astype(
        jnp.float32
    )
    offsets = jnp.dot(bucket_hit, rel_low.astype(jnp.float32), precision=HIGHEST).T
    seq_rows = inputs[0]
    row_count = seq_rows.shape[0]
    first_row = lax.axis_index("seq") * row_count
    token_total = row_count * lax.axis_size(("dp", "seq", "shard"))
    section_one, ffn_saved = ffn_forward(seq_rows, gains[:, 0], up_first, down_first)
    normed_out2, normed2, inverse2 = layer_norm(section_one, gains[:, 1])
    lifted2 = normed_out2.astype(bf16)
    projected = matmul(lifted2, qkv_w).astype(bf16)
    query = projected[:, :D]
    pair = [(0, 1), (1, 0)]
    other = lax.ppermute(projected[:, D:], "seq", pair)
    early = lax.axis_index("seq") == 0
    both = jnp.concatenate(
        [
            jnp.where(early, projected[:, D:], other),
            jnp.where(early, other, projected[:, D:]),
        ],
        axis=0,
    )
    keys, values = both[:, :D], both[:, D:]
    attended, log_total = attention_forward(query, keys, values, offsets, first_row)
    attended_low = attended.astype(bf16)
    section_two = section_one + matmul(attended_low, out_w)
    normed_out3, normed3, inverse3 = layer_norm(section_two, gains[:, 2])
    lifted3 = normed_out3.astype(bf16)
    gates = matmul(lifted3, glu_w)
    first_half = gates[:, :D]
    sig_gate = jax.nn.sigmoid(gates[:, D:])
    glu = first_half * sig_gate
    glu_wide = with_halo(glu, (("seq", 0),), K // 2)
    conv = depthwise(glu_wide, kernel, row_count)
    part_sum = jnp.sum(conv, axis=0)
    part_mean = part_sum / row_count
    part_square = jnp.sum(jnp.square(conv - part_mean), axis=0)
    stats = collect(cube, jnp.concatenate([part_sum, part_square]).reshape(8, 128), 1)
    stats = stats.reshape(cube.total, 2, D)
    mean = jnp.sum(stats[:, 0], axis=0) / token_total
    spread_of_means = jnp.square(stats[:, 0] / row_count - mean) * row_count
    variance = jnp.sum(stats[:, 1] + spread_of_means, axis=0) / token_total
    centred = conv - mean
    inv_std = lax.rsqrt(variance + EPS_BATCH)
    normed_bn = centred * inv_std
    batch_out = normed_bn * gains[:, 5] + gains[:, 6]
    swish_low = jax.nn.silu(batch_out).astype(bf16)
    section_three = section_two + matmul(swish_low, point_w)
    section_four, tail_saved = ffn_forward(
        section_three, gains[:, 3], up_second, down_second
    )
    outputs, normed5, inverse5 = layer_norm(section_four, gains[:, 4])
    grad_four, gain_four = norm_back(cotangent[0], normed5, inverse5, gains[:, 4])
    grad_three, grad_up_two, grad_down_two, gain_three = ffn_backward(
        grad_four, tail_saved, gains[:, 3], up_second, down_second
    )
    grad_three_low = grad_three.astype(bf16)
    grad_point = matmul_left_t(swish_low, grad_three_low)
    grad_batch = matmul_right_t(grad_three_low, point_w) * silu_slope(batch_out)
    grad_normed = grad_batch * gains[:, 5]
    sums = jnp.concatenate(
        [jnp.sum(grad_normed, axis=0), jnp.sum(grad_normed * normed_bn, axis=0)]
    )
    sums = jnp.sum(collect(cube, sums.reshape(8, 128), 2), axis=0).reshape(2, D)
    sum_normed, sum_cross = sums[0], sums[1]
    grad_conv = inv_std * (
        grad_normed - sum_normed / token_total - normed_bn * sum_cross / token_total
    )
    grad_wide = with_halo(grad_conv, (("seq", 0),), K // 2)
    grad_glu = grad_wide[K - 1 : K - 1 + row_count] * kernel[:, 0]
    for tap_idx in range(1, K):
        grad_glu = (
            grad_glu
            + grad_wide[K - 1 - tap_idx : K - 1 - tap_idx + row_count] * kernel[:, tap_idx]
        )
    grad_kernel = jnp.stack(
        [
            jnp.sum(grad_conv * glu_wide[tap_idx : tap_idx + row_count], axis=0)
            for tap_idx in range(K)
        ],
        axis=1,
    )
    grad_gates = jnp.concatenate(
        [grad_glu * sig_gate, grad_glu * first_half * sig_gate * (1.0 - sig_gate)], axis=1
    ).astype(bf16)
    grad_glu_w = matmul_left_t(lifted3, grad_gates)
    grad_two_part, gain_two = norm_back(
        matmul_right_t(grad_gates, glu_w), normed3, inverse3, gains[:, 2]
    )
    grad_two = grad_three + grad_two_part
    grad_two_low = grad_two.astype(bf16)
    grad_out_w = matmul_left_t(attended_low, grad_two_low)
    grad_attended = matmul_right_t(grad_two_low, out_w).astype(bf16)
    delta = jnp.sum(
        (grad_attended.astype(jnp.float32) * attended).reshape(row_count, H, DH), axis=2
    )
    query_grad, key_grad, value_grad, offset_grad = attention_backward(
        query, keys, values, offsets, first_row, log_total, grad_attended, delta
    )
    keys_grad = jnp.concatenate([key_grad, value_grad], axis=1)
    theirs = lax.dynamic_slice_in_dim(keys_grad, row_count - first_row, row_count, 0)
    own = lax.dynamic_slice_in_dim(keys_grad, first_row, row_count, 0)
    own = own + lax.ppermute(theirs, "seq", pair)
    key_own, value_own = own[:, :D], own[:, D:]
    grad_proj = jnp.concatenate([query_grad, key_own, value_own], axis=1).astype(bf16)
    grad_qkv_w = matmul_left_t(lifted2, grad_proj)
    grad_one_part, gain_one = norm_back(
        matmul_right_t(grad_proj, qkv_w), normed2, inverse2, gains[:, 1]
    )
    grad_one = grad_two + grad_one_part
    input_grad, grad_up_one, grad_down_one, gain_zero = ffn_backward(
        grad_one, ffn_saved, gains[:, 0], up_first, down_first
    )
    grad_vec_local = jnp.stack(
        [
            gain_zero,
            gain_one,
            gain_two,
            gain_three,
            gain_four,
            jnp.sum(grad_batch * normed_bn, axis=0),
            jnp.sum(grad_batch, axis=0),
        ],
        axis=1,
    )
    grad_rel_local = jnp.dot(bucket_hit.T, offset_grad.T, precision=HIGHEST)
    rel_padded = jnp.pad(
        grad_rel_local.reshape(cube.total, rel_rows, H), ((0, 0), (0, rows - rel_rows), (0, 0))
    )
    small_grads = jnp.concatenate(
        [rel_padded.reshape(D, H), grad_vec_local, grad_kernel], axis=1
    )
    small_grads = jnp.pad(small_grads, ((0, 0), (0, 128 - SMALL_END)))
    lead = (2,) * cube.digits
    grad_groups = [
        jnp.concatenate(group, axis=1).astype(bf16).reshape(lead + (rows, -1))
        for group in (
            (grad_up_two, grad_down_two),
            (grad_qkv_w, grad_out_w, grad_glu_w, grad_point),
            (grad_up_one, grad_down_one, small_grads),
        )
    ]
    share_second, share_middle, share_first = scatter_groups(cube, grad_groups, 3)
    return outputs, input_grad, share_first, share_middle, share_second


def local(
    cube,
    inputs,
    cotangent,
    w_up,
    w_down,
    w_qkv,
    w_out,
    w_glu,
    w_point,
    vectors,
    depth_kernel,
    rel_bias,
    bucket_table,
    m_up,
    m_down,
    m_qkv,
    m_out,
    m_glu,
    m_point,
    m_vectors,
    m_depth,
    m_rel,
):
    bf16 = jnp.bfloat16
    rows, rel_rows = w_up.shape[0], rel_bias.shape[0]
    small = jnp.concatenate(
        [jnp.pad(rel_bias, ((0, rows - rel_rows), (0, 0))), vectors, depth_kernel], axis=1
    )
    small = jnp.pad(small, ((0, 0), (0, 128 - SMALL_END)))
    weights = (w_up, w_down, w_qkv, w_out, w_glu, w_point)
    if rows % 16 == 0:
        bucket = jnp.pad(bucket_table, (0, 1), constant_values=-1)[None]
        outputs, input_grad, share_first, share_middle, share_second = fused_step(
            cube, inputs[0], cotangent[0], weights, small, bucket, rel_rows, 0
        )
    else:
        outputs, input_grad, share_first, share_middle, share_second = unfused_step(
            cube, inputs, cotangent, *weights, small, bucket_table
        )
    grad_up = jnp.concatenate([share_first[:, :FF], share_second[:, :FF]], axis=1)
    grad_down = jnp.concatenate([share_first[:, FF : 2 * FF], share_second[:, FF:]], axis=1)
    grad_qkv, grad_out = share_middle[:, : 3 * D], share_middle[:, 3 * D : 4 * D]
    grad_glu, grad_pnt = share_middle[:, 4 * D : 6 * D], share_middle[:, 6 * D :]
    share_small = share_first[:, 2 * FF :]
    grad_vectors = share_small[:, SMALL_VEC : SMALL_VEC + 7]
    grad_depth = share_small[:, SMALL_DEPTH : SMALL_DEPTH + K]
    grad_rel = share_small[: rel_bias.shape[0], :H]
    next_m_up = MOMENTUM * m_up + grad_up
    next_m_down = MOMENTUM * m_down + grad_down
    next_m_qkv = MOMENTUM * m_qkv + grad_qkv
    next_m_out = MOMENTUM * m_out + grad_out
    next_m_glu = MOMENTUM * m_glu + grad_glu
    next_m_point = MOMENTUM * m_point + grad_pnt
    stacked = jnp.concatenate(
        [next_m_up, next_m_down, next_m_qkv, next_m_out, next_m_glu, next_m_point], axis=1
    )
    owned = spread(cube, stacked, 4).reshape(D, BLOCK)
    ortho = orthogonalize_blocks(cube, owned, bf16, 5)
    mine = restore(cube, ortho.reshape(cube.total, rows, BLOCK), 6).astype(jnp.float32)
    new_up = w_up - RATE_MATRIX * mine[:, : 2 * FF]
    new_down = w_down - RATE_MATRIX * mine[:, 2 * FF : 4 * FF]
    new_qkv = w_qkv - RATE_MATRIX * mine[:, STARTS[4] : STARTS[5]]
    new_out = w_out - RATE_MATRIX * mine[:, STARTS[5] : STARTS[6]]
    new_glu = w_glu - RATE_MATRIX * mine[:, STARTS[6] : STARTS[7]]
    new_point = w_point - RATE_MATRIX * mine[:, STARTS[7] :]
    next_m_vectors = MOMENTUM * m_vectors + grad_vectors
    next_m_depth = MOMENTUM * m_depth + grad_depth
    next_m_rel = MOMENTUM * m_rel + grad_rel
    squares = jnp.concatenate(
        [
            jnp.sum(next_m_vectors * next_m_vectors, axis=0),
            jnp.sum(next_m_depth * next_m_depth, axis=0),
            jnp.sum(next_m_rel * next_m_rel, axis=0),
        ]
    )
    squares = jnp.pad(squares, (0, 128 - squares.shape[0])).reshape(1, 128)
    squares = jnp.sum(collect(cube, jnp.pad(squares, ((0, 7), (0, 0))), 7), axis=0)[0]
    square_vec, square_depth = squares[:7], squares[7 : 7 + K]
    square_rel = squares[7 + K : 7 + K + H]
    new_vectors = vectors - RATE_VECTOR * next_m_vectors * lax.rsqrt(square_vec / D + EPS_SCALE)
    new_depth = depth_kernel - RATE_VECTOR * next_m_depth * lax.rsqrt(square_depth / D + EPS_SCALE)
    new_rel = rel_bias - RATE_VECTOR * next_m_rel * lax.rsqrt(square_rel / NB + EPS_SCALE)
    return (
        outputs[None],
        input_grad[None],
        grad_up,
        grad_down,
        grad_qkv,
        grad_out,
        grad_glu,
        grad_pnt,
        grad_vectors,
        grad_depth,
        grad_rel,
        new_up,
        new_down,
        new_qkv,
        new_out,
        new_glu,
        new_point,
        new_vectors,
        new_depth,
        new_rel,
        next_m_up,
        next_m_down,
        next_m_qkv,
        next_m_out,
        next_m_glu,
        next_m_point,
        next_m_vectors,
        next_m_depth,
        next_m_rel,
    )


def solution(mesh):
    placed = (
        P(("dp", "shard"), "seq", None),
        P(("dp", "shard"), "seq", None),
        P(("dp", "seq", "shard"), None),
        P(("dp", "seq", "shard"), None),
        P(("dp", "seq", "shard"), None),
        P(("dp", "seq", "shard"), None),
        P(("dp", "seq", "shard"), None),
        P(("dp", "seq", "shard"), None),
        P(("dp", "seq", "shard"), None),
        P(("dp", "seq", "shard"), None),
        P(("dp", "seq", "shard"), None),
        P(),
        P(("dp", "seq", "shard"), None),
        P(("dp", "seq", "shard"), None),
        P(("dp", "seq", "shard"), None),
        P(("dp", "seq", "shard"), None),
        P(("dp", "seq", "shard"), None),
        P(("dp", "seq", "shard"), None),
        P(("dp", "seq", "shard"), None),
        P(("dp", "seq", "shard"), None),
        P(("dp", "seq", "shard"), None),
    )
    return jax.shard_map(
        functools.partial(local, Cube(mesh.shape["dp"])),
        mesh=mesh,
        in_specs=placed,
        out_specs=(
            P(("dp", "shard"), "seq", None),
            P(("dp", "shard"), "seq", None),
            P(("dp", "seq", "shard"), None),
            P(("dp", "seq", "shard"), None),
            P(("dp", "seq", "shard"), None),
            P(("dp", "seq", "shard"), None),
            P(("dp", "seq", "shard"), None),
            P(("dp", "seq", "shard"), None),
            P(("dp", "seq", "shard"), None),
            P(("dp", "seq", "shard"), None),
            P(("dp", "seq", "shard"), None),
            P(("dp", "seq", "shard"), None),
            P(("dp", "seq", "shard"), None),
            P(("dp", "seq", "shard"), None),
            P(("dp", "seq", "shard"), None),
            P(("dp", "seq", "shard"), None),
            P(("dp", "seq", "shard"), None),
            P(("dp", "seq", "shard"), None),
            P(("dp", "seq", "shard"), None),
            P(("dp", "seq", "shard"), None),
            P(("dp", "seq", "shard"), None),
            P(("dp", "seq", "shard"), None),
            P(("dp", "seq", "shard"), None),
            P(("dp", "seq", "shard"), None),
            P(("dp", "seq", "shard"), None),
            P(("dp", "seq", "shard"), None),
            P(("dp", "seq", "shard"), None),
            P(("dp", "seq", "shard"), None),
            P(("dp", "seq", "shard"), None),
        ),
        check_vma=False,
    )
```

```python
import functools
import types

import jax
import jax.numpy as jnp
from jax import lax
from jax.experimental import pallas as pl
from jax.experimental.pallas import tpu as pltpu
from jax.sharding import PartitionSpec as P

D = 512
FF = 2048
H = 8
DH = 64
K = 31
NB = 128


EPS_NORM = 1e-05
EPS_BATCH = 1e-05
EPS_SCALE = 1e-06
MOMENTUM = 0.9
RATE_MATRIX = 1.0
RATE_VECTOR = 0.25
COEF_A = 3.4445
COEF_B = -4.775
COEF_C = 2.0315
HIGHEST = lax.Precision.HIGHEST


AXES = ("dp", "seq", "shard")
MESH = pl.DeviceIdType.MESH
WIDTHS = (FF, FF, FF, FF, 3 * D, D, 2 * D, D)
STARTS = tuple(sum(WIDTHS[:i]) for i in range(9))
BLOCK = 512


class Cube:
    def __init__(self, dp_size):
        self.dp_size = dp_size
        self.levels = dp_size.bit_length() - 1
        self.digits = self.levels + 2
        self.total = dp_size * 4
        high = list(range(self.levels - 1))
        low, seq, core = self.levels - 1, self.levels, self.levels + 1
        self.gather_orders = (high + [low, seq, core], high + [seq, low, core])
        self.scatter_orders = tuple(order[::-1] for order in self.gather_orders)

    def mine(self):
        d = lax.axis_index("dp")
        bits = [lax.rem(d // (1 << (self.levels - 1 - k)), 2) for k in range(self.levels)]
        return bits + [lax.axis_index("seq"), lax.axis_index("shard")]

    def partner(self, k):
        d, s, c = lax.axis_index("dp"), lax.axis_index("seq"), lax.axis_index("shard")
        if k == self.levels:
            return (d, 1 - s, c)
        if k == self.levels + 1:
            return (d, s, 1 - c)
        step = 1 << (self.levels - 1 - k)
        bit = lax.rem(d // step, 2)
        return (d + (1 - 2 * bit) * step, s, c)

    def index(self):
        return (lax.axis_index("dp") * 2 + lax.axis_index("seq")) * 2 + lax.axis_index("shard")

    def coords(self, index):
        return (index // 4, lax.rem(index // 2, 2), lax.rem(index, 2))

    def greet_partners(self):
        barrier = pltpu.get_barrier_semaphore()
        for k in range(self.digits):
            pl.semaphore_signal(barrier, inc=1, device_id=self.partner(k), device_id_type=MESH)
        pl.semaphore_wait(barrier, self.digits)

    def greet_all(self):
        barrier = pltpu.get_barrier_semaphore()
        me = self.index()

        @pl.loop(1, self.total)
        def _(i):
            peer = self.coords(lax.rem(me + i, self.total))
            pl.semaphore_signal(barrier, inc=1, device_id=peer, device_id_type=MESH)

        pl.semaphore_wait(barrier, self.total - 1)


def halves(width):
    cut = (width // 128 + 1) // 2 * 128
    return ((0, cut), (cut, width - cut))


def remote(src, dst, send_sem, recv_sem, peer):
    return pltpu.make_async_remote_copy(
        src_ref=src,
        dst_ref=dst,
        send_sem=send_sem,
        recv_sem=recv_sem,
        device_id=peer,
        device_id_type=MESH,
    )


def gather_kernel(cube, groups, *refs):
    shards, outs = refs[:groups], refs[groups : 2 * groups]
    own_sem, send_sem, recv_sem = refs[2 * groups :]
    cube.greet_partners()
    mine = cube.mine()
    locals_ = []
    for g in range(groups):
        copy = pltpu.make_async_copy(shards[g], outs[g].at[tuple(mine)], own_sem.at[g])
        copy.start()
        locals_.append(copy)

    def make(g, half, stage):
        order = cube.gather_orders[half]
        columns = pl.ds(*halves(shards[g].shape[-1])[half])
        done = order[:stage]
        index = tuple(slice(None) if k in done else mine[k] for k in range(cube.digits))
        place = outs[g].at[index + (slice(None), columns)]
        source = shards[g].at[:, columns] if stage == 0 else place
        return remote(
            source,
            place,
            send_sem.at[g, half, stage],
            recv_sem.at[g, half, stage],
            cube.partner(order[stage]),
        )

    copies = {}
    for g in range(groups):
        for half in range(2):
            copies[g, half, 0] = make(g, half, 0)
            copies[g, half, 0].start()
    for tick in range(cube.digits + 2 * (groups - 1)):
        for g in range(groups):
            stage = tick - 2 * g
            if not 0 <= stage < cube.digits:
                continue
            for half in range(2):
                copies[g, half, stage].wait_recv()
                if stage == 0 and half == 0:
                    locals_[g].wait()
                if stage + 1 < cube.digits:
                    copies[g, half, stage + 1] = make(g, half, stage + 1)
                    copies[g, half, stage + 1].start()
    for copy in copies.values():
        copy.wait_send()


def gather_groups(cube, shards, collective_id):
    groups = len(shards)
    lead = (2,) * cube.digits
    return pl.pallas_call(
        functools.partial(gather_kernel, cube, groups),
        out_shape=[jax.ShapeDtypeStruct(lead + s.shape, s.dtype) for s in shards],
        in_specs=[pl.BlockSpec(memory_space=pl.ANY)] * groups,
        out_specs=[pl.BlockSpec(memory_space=pl.ANY)] * groups,
        scratch_shapes=[
            pltpu.SemaphoreType.DMA((groups,)),
            pltpu.SemaphoreType.DMA((groups, 2, cube.digits)),
            pltpu.SemaphoreType.DMA((groups, 2, cube.digits)),
        ],
        compiler_params=pltpu.CompilerParams(
            collective_id=collective_id, has_side_effects=True
        ),
        name="gather_weights",
    )(*shards)


def scatter_kernel(cube, groups, *refs):
    parts, outs = refs[:groups], refs[groups : 2 * groups]
    rest = refs[2 * groups :]
    sums = rest[:groups]
    landed = rest[groups : groups + groups * 2 * cube.digits]
    own_sem, send_sem, recv_sem = rest[groups + groups * 2 * cube.digits :]
    cube.greet_partners()
    mine = cube.mine()
    last = cube.digits - 1

    def slot(g, half, stage):
        return landed[(g * 2 + half) * cube.digits + stage]

    def place(g, half, stage, bit_of):
        order = cube.scatter_orders[half]
        columns = pl.ds(*halves(outs[g].shape[-1])[half])
        index = []
        for k in range(cube.digits - 1):
            at = order.index(k)
            if at > stage:
                index.append(slice(None))
            else:
                index.append(bit_of(k) if at == stage else mine[k])
        return tuple(index) + (slice(None), columns)

    def make(g, half, stage):
        order = cube.scatter_orders[half]
        if stage == 0:
            index = (slice(None),) * last + (1 - mine[last],)
            columns = pl.ds(*halves(outs[g].shape[-1])[half])
            source = parts[g].at[index + (slice(None), columns)]
        else:
            source = sums[g].at[place(g, half, stage, lambda k: 1 - mine[k])]
        return remote(
            source,
            slot(g, half, stage),
            send_sem.at[g, half, stage],
            recv_sem.at[g, half, stage],
            cube.partner(order[stage]),
        )

    copies = {}
    locals_ = []
    for g in range(groups):
        copy = pltpu.make_async_copy(
            parts[g].at[(slice(None),) * last + (mine[last],)], sums[g], own_sem.at[g]
        )
        copy.start()
        locals_.append(copy)
        for half in range(2):
            copies[g, half, 0] = make(g, half, 0)
            copies[g, half, 0].start()

    def add(g, half, stage):
        order = cube.scatter_orders[half]
        columns = pl.ds(*halves(outs[g].shape[-1])[half])
        free = [k for k in range(last) if order.index(k) > stage]
        count = 1 << len(free)
        target, extra = sums[g], slot(g, half, stage)

        def one(i):
            digit = {k: lax.rem(i // (1 << (len(free) - 1 - n)), 2) for n, k in enumerate(free)}
            full = tuple(digit.get(k, mine[k]) for k in range(last)) + (slice(None), columns)
            short = tuple(digit[k] for k in free)
            total = target[full].astype(jnp.float32) + extra[short + (slice(None), slice(None))].astype(jnp.float32)
            if stage == last:
                outs[g][:, columns] = total
            else:
                target[full] = total.astype(target.dtype)

        if count == 1:
            one(0)
        else:
            pl.loop(0, count)(one)

    for stage in range(cube.digits):
        for g in range(groups):
            if stage == 0:
                locals_[g].wait()
            for half in range(2):
                copies[g, half, stage].wait_recv()
                add(g, half, stage)
                if stage < last:
                    copies[g, half, stage + 1] = make(g, half, stage + 1)
                    copies[g, half, stage + 1].start()
    for copy in copies.values():
        copy.wait_send()


def scatter_groups(cube, parts, collective_id):
    groups = len(parts)
    scratch = [pltpu.VMEM((2,) * (cube.digits - 1) + p.shape[-2:], p.dtype) for p in parts]
    for p in parts:
        for half in range(2):
            for stage in range(cube.digits):
                lead = (2,) * (cube.digits - 1 - stage)
                scratch.append(pltpu.VMEM(lead + (p.shape[-2], halves(p.shape[-1])[half][1]), p.dtype))
    scratch += [
        pltpu.SemaphoreType.DMA((groups,)),
        pltpu.SemaphoreType.DMA((groups, 2, cube.digits)),
        pltpu.SemaphoreType.DMA((groups, 2, cube.digits)),
    ]
    return pl.pallas_call(
        functools.partial(scatter_kernel, cube, groups),
        out_shape=[jax.ShapeDtypeStruct(p.shape[-2:], jnp.float32) for p in parts],
        in_specs=[pl.BlockSpec(memory_space=pl.ANY)] * groups,
        out_specs=[pl.BlockSpec(memory_space=pltpu.VMEM)] * groups,
        scratch_shapes=scratch,
        compiler_params=pltpu.CompilerParams(
            collective_id=collective_id, has_side_effects=True, vmem_limit_bytes=48 << 20
        ),
        name="scatter_grads",
    )(*parts)


def collect_kernel(cube, x_ref, o_ref, send_sem, recv_sem):
    me = cube.index()
    cube.greet_all()

    def make(i):
        to = lax.rem(me + i, cube.total)
        return remote(x_ref, o_ref.at[i], send_sem.at[i], recv_sem.at[i], cube.coords(to))

    @pl.loop(1, cube.total)
    def _(i):
        make(i).start()

    o_ref[0] = x_ref[...]

    @pl.loop(1, cube.total)
    def _(i):
        make(i).wait()


def collect(cube, x, collective_id):
    return pl.pallas_call(
        functools.partial(collect_kernel, cube),
        out_shape=jax.ShapeDtypeStruct((cube.total,) + x.shape, x.dtype),
        in_specs=[pl.BlockSpec(memory_space=pltpu.VMEM)],
        out_specs=pl.BlockSpec(memory_space=pltpu.VMEM),
        scratch_shapes=[
            pltpu.SemaphoreType.DMA((cube.total,)),
            pltpu.SemaphoreType.DMA((cube.total,)),
        ],
        compiler_params=pltpu.CompilerParams(
            collective_id=collective_id, has_side_effects=True
        ),
        name="collect_stats",
    )(x)


def by_matrix(j, action):
    for width in sorted(set(WIDTHS)):
        members = [i for i in range(8) if WIDTHS[i] == width]
        hit = functools.reduce(jnp.logical_or, [j == i for i in members])
        pl.when(hit)(functools.partial(action, width // 4))


def quarter_start(t):
    j, q = t // 4, lax.rem(t, 4)
    start = 0
    for i in range(8):
        start = start + jnp.where(j == i, STARTS[i] + q * (WIDTHS[i] // 4), 0)
    return pl.multiple_of(start, 128)


def owner_coords(cube, t):
    return ((t // 4) * (cube.dp_size // 8), lax.rem(t // 2, 2), lax.rem(t, 2))


def spread_kernel(cube, x_ref, o_ref, own_sem, send_sem, recv_sem):
    me = cube.index()
    repeat = cube.dp_size // 8
    d, s, c = lax.axis_index("dp"), lax.axis_index("seq"), lax.axis_index("shard")
    owner = lax.rem(d, repeat) == 0
    mine = ((d // repeat) * 2 + s) * 2 + c
    cube.greet_all()

    def send(i, wait):
        t = lax.rem(mine + i, 32)
        peer = owner_coords(cube, t)
        other = jnp.logical_or(jnp.logical_not(owner), i > 0)

        def go(width):
            src = x_ref.at[:, pl.ds(quarter_start(t), width)]
            dst = o_ref.at[me, :, pl.ds(0, width)]
            copy = remote(src, dst, send_sem.at[i], recv_sem.at[me], peer)
            if wait:
                copy.wait_send()
            else:
                copy.start()

        pl.when(other)(lambda: by_matrix(t // 4, go))

    pl.loop(0, 32)(functools.partial(send, wait=False))

    def keep(width):
        copy = pltpu.make_async_copy(
            x_ref.at[:, pl.ds(quarter_start(mine), width)],
            o_ref.at[me, :, pl.ds(0, width)],
            own_sem,
        )
        copy.start()
        copy.wait()

    def receive(width):
        @pl.loop(1, cube.total)
        def _(i):
            source = lax.rem(me + i, cube.total)
            place = o_ref.at[source, :, pl.ds(0, width)]
            remote(
                place, place, send_sem.at[0], recv_sem.at[source], cube.coords(source)
            ).wait_recv()

    @pl.when(owner)
    def _():
        by_matrix(mine // 4, keep)
        by_matrix(mine // 4, receive)

    pl.loop(0, 32)(functools.partial(send, wait=True))


def spread(cube, x, collective_id):
    return pl.pallas_call(
        functools.partial(spread_kernel, cube),
        out_shape=jax.ShapeDtypeStruct((cube.total, x.shape[0], BLOCK), x.dtype),
        in_specs=[pl.BlockSpec(memory_space=pl.ANY)],
        out_specs=pl.BlockSpec(memory_space=pl.ANY),
        scratch_shapes=[
            pltpu.SemaphoreType.DMA,
            pltpu.SemaphoreType.DMA((32,)),
            pltpu.SemaphoreType.DMA((cube.total,)),
        ],
        compiler_params=pltpu.CompilerParams(
            collective_id=collective_id, has_side_effects=True
        ),
        name="spread_momentum",
    )(x)


def restore_kernel(cube, x_ref, o_ref, own_sem, send_sem, recv_sem):
    me = cube.index()
    repeat = cube.dp_size // 8
    d, s, c = lax.axis_index("dp"), lax.axis_index("seq"), lax.axis_index("shard")
    owner = lax.rem(d, repeat) == 0
    mine = ((d // repeat) * 2 + s) * 2 + c
    cube.greet_all()

    def send_all(wait, width):
        @pl.loop(1, cube.total)
        def _(i):
            to = lax.rem(me + i, cube.total)
            src = x_ref.at[to, :, pl.ds(0, width)]
            dst = o_ref.at[:, pl.ds(quarter_start(mine), width)]
            copy = remote(src, dst, send_sem.at[i], recv_sem.at[mine], cube.coords(to))
            if wait:
                copy.wait_send()
            else:
                copy.start()

    def keep(width):
        copy = pltpu.make_async_copy(
            x_ref.at[me, :, pl.ds(0, width)],
            o_ref.at[:, pl.ds(quarter_start(mine), width)],
            own_sem,
        )
        copy.start()
        copy.wait()

    @pl.when(owner)
    def _():
        by_matrix(mine // 4, functools.partial(send_all, False))
        by_matrix(mine // 4, keep)

    def receive(i):
        t = lax.rem(mine + i, 32)
        other = jnp.logical_or(jnp.logical_not(owner), i > 0)

        def go(width):
            place = o_ref.at[:, pl.ds(quarter_start(t), width)]
            remote(
                place, place, send_sem.at[0], recv_sem.at[t], owner_coords(cube, t)
            ).wait_recv()

        pl.when(other)(lambda: by_matrix(t // 4, go))

    pl.loop(0, 32)(receive)

    @pl.when(owner)
    def _():
        by_matrix(mine // 4, functools.partial(send_all, True))


def restore(cube, x, collective_id):
    return pl.pallas_call(
        functools.partial(restore_kernel, cube),
        out_shape=jax.ShapeDtypeStruct((x.shape[1], STARTS[8]), x.dtype),
        in_specs=[pl.BlockSpec(memory_space=pl.ANY)],
        out_specs=pl.BlockSpec(memory_space=pl.ANY),
        scratch_shapes=[
            pltpu.SemaphoreType.DMA,
            pltpu.SemaphoreType.DMA((cube.total,)),
            pltpu.SemaphoreType.DMA((32,)),
        ],
        compiler_params=pltpu.CompilerParams(
            collective_id=collective_id, has_side_effects=True
        ),
        name="restore_rows",
    )(x)


def split(value):
    high = value.astype(jnp.bfloat16)
    low = (value - high.astype(jnp.float32)).astype(jnp.bfloat16)
    return high, low


def product(left, right):
    (lh, ll), (rh, rl) = left, right
    dot = functools.partial(jnp.dot, preferred_element_type=jnp.float32)
    return dot(lh, rh) + (dot(lh, rl) + dot(ll, rh))


def orthogonalize_kernel(cube, x_ref, o_ref, gram_ref, work, landed, send_sem, recv_sem):
    barrier = pltpu.get_barrier_semaphore()
    peers = (cube.partner(cube.levels + 1), cube.partner(cube.levels))
    for peer in peers:
        pl.semaphore_signal(barrier, inc=1, device_id=peer, device_id_type=MESH)
    pl.semaphore_wait(barrier, 2)
    repeat = cube.dp_size // 8
    j = lax.axis_index("dp") // repeat
    width = 0
    for i in range(8):
        width = width + jnp.where(j == i, WIDTHS[i] // 4, 0)
    column = lax.broadcasted_iota(jnp.int32, (D, BLOCK), 1)
    block = jnp.where(column < width, x_ref[...].astype(jnp.float32), 0.0)
    bh, bl = split(block)
    dot_t = lambda a, b: lax.dot_general(
        a, b, (((1,), (1,)), ((), ())), preferred_element_type=jnp.float32
    )
    gram_ref[0] = dot_t(bh, bh) + (dot_t(bh, bl) + dot_t(bl, bh))
    for step in range(2):
        copy = remote(
            gram_ref.at[step], landed.at[step], send_sem.at[step], recv_sem.at[step], peers[step]
        )
        copy.start()
        copy.wait()
        gram_ref[step + 1] = gram_ref[step] + landed[step]
    gram = gram_ref[2]
    row = lax.broadcasted_iota(jnp.int32, (D, D), 0)
    col = lax.broadcasted_iota(jnp.int32, (D, D), 1)
    eye = row == col
    square = jnp.sum(jnp.sum(jnp.where(eye, gram, 0.0), axis=1, keepdims=True), axis=0, keepdims=True)
    scale = 1.0 / (jnp.sqrt(square) + 1e-07)
    gram = gram * (scale * scale)
    block = block * scale
    for step in range(5):
        parts = split(gram)
        mixed = COEF_B * gram + COEF_C * product(parts, parts)
        mixed = jnp.where(eye, mixed + COEF_A, mixed)
        mixed_parts = split(mixed)
        block = product(mixed_parts, split(block))
        if step < 4:
            gram = product(mixed_parts, split(product(mixed_parts, parts)))
    o_ref[...] = block.astype(o_ref.dtype)


def orthogonalize_blocks(cube, x, out_dtype, collective_id):
    return pl.pallas_call(
        functools.partial(orthogonalize_kernel, cube),
        out_shape=jax.ShapeDtypeStruct((D, BLOCK), out_dtype),
        in_specs=[pl.BlockSpec(memory_space=pltpu.VMEM)],
        out_specs=pl.BlockSpec(memory_space=pltpu.VMEM),
        scratch_shapes=[
            pltpu.VMEM((3, D, D), jnp.float32),
            pltpu.VMEM((8, 128), jnp.float32),
            pltpu.VMEM((2, D, D), jnp.float32),
            pltpu.SemaphoreType.DMA((2,)),
            pltpu.SemaphoreType.DMA((2,)),
        ],
        compiler_params=pltpu.CompilerParams(
            collective_id=collective_id, has_side_effects=True, vmem_limit_bytes=48 << 20
        ),
        name="orthogonalize",
    )(x)

def with_halo(value, sides, width):
    for axis, dim in sides:
        devices, length = (lax.axis_size(axis), value.shape[dim])
        up = [(i, (i + 1) % devices) for i in range(devices - 1)]
        down = [(j, i) for i, j in up]
        last = lax.slice_in_dim(value, length - width, length, axis=dim)
        first = lax.slice_in_dim(value, 0, width, axis=dim)
        before = lax.ppermute(last, axis, up)
        after = lax.ppermute(first, axis, down)
        value = jnp.concatenate([before, value, after], axis=dim)
    return value


def matmul(left, right):
    return jnp.dot(left, right, preferred_element_type=jnp.float32)


def matmul_right_t(left, right):
    return lax.dot_general(
        left, right, (((1,), (1,)), ((), ())), preferred_element_type=jnp.float32
    )


def matmul_left_t(left, right):
    return lax.dot_general(
        left, right, (((0,), (0,)), ((), ())), preferred_element_type=jnp.float32
    )


def layer_norm(field, gain):
    centre = jnp.mean(field, axis=-1, keepdims=True)
    shifted = field - centre
    inverse = lax.rsqrt(jnp.mean(shifted * shifted, axis=-1, keepdims=True) + EPS_NORM)
    normed = shifted * inverse
    return (normed * gain, normed, inverse)


def norm_back(grad_out, normed, inverse, gain):
    scaled = grad_out * gain
    grad_in = inverse * (
        scaled
        - jnp.mean(scaled, axis=-1, keepdims=True)
        - normed * jnp.mean(scaled * normed, axis=-1, keepdims=True)
    )
    return (grad_in, jnp.sum(grad_out * normed, axis=0))


def silu_slope(values):
    sigma = jax.nn.sigmoid(values)
    return sigma * (1.0 + values * (1.0 - sigma))


def ffn_forward(field, gain, w_in, w_back):
    normed_out, normed, inverse = layer_norm(field, gain)
    lifted = normed_out.astype(jnp.bfloat16)
    hidden_pre = matmul(lifted, w_in)
    hidden_act = jax.nn.silu(hidden_pre).astype(jnp.bfloat16)
    return (
        field + 0.5 * matmul_right_t(hidden_act, w_back),
        (lifted, hidden_pre, hidden_act, normed, inverse),
    )


def ffn_backward(grad, saved, gain, w_in, w_back):
    lifted, hidden_pre, hidden_act, normed, inverse = saved
    grad_branch = (0.5 * grad).astype(jnp.bfloat16)
    grad_back = matmul_left_t(grad_branch, hidden_act)
    grad_act = matmul(grad_branch, w_back)
    grad_pre = (grad_act * silu_slope(hidden_pre)).astype(jnp.bfloat16)
    grad_in = matmul_left_t(lifted, grad_pre)
    grad_field, grad_gain = norm_back(matmul_right_t(grad_pre, w_in), normed, inverse, gain)
    return (grad + grad_field, grad_in, grad_back, grad_gain)


def depthwise(wide, kernel, count):
    total = wide[0:count] * kernel[:, 0]
    for tap_idx in range(1, K):
        total = total + wide[tap_idx : tap_idx + count] * kernel[:, tap_idx]
    return total


def spread_rows(window, count, keys_len):
    padded = jnp.concatenate([window, jnp.zeros((1,), window.dtype)])
    tiled = jnp.broadcast_to(padded[None, :], (count, keys_len + count)).reshape(-1)
    shaped = tiled[: count * (keys_len + count - 1)].reshape(count, keys_len + count - 1)
    return shaped[:, count - 1 : count - 1 + keys_len]


def collect_rows(grid, count, keys_len):
    placed = jnp.concatenate([jnp.zeros((count, count - 1), grid.dtype), grid], axis=1).reshape(-1)
    placed = jnp.concatenate([placed, jnp.zeros((count,), grid.dtype)])
    return jnp.sum(placed.reshape(count, keys_len + count), axis=0)[: keys_len + count - 1]


def attention_scores(query, keys, offsets, first_row, row_start, block, head_idx):
    length = keys.shape[0]
    columns = slice(head_idx * DH, (head_idx + 1) * DH)
    anchor = length - block - first_row - row_start
    window = lax.dynamic_slice_in_dim(offsets[head_idx], anchor, length + block - 1)
    product = matmul_right_t(query[row_start : row_start + block, columns], keys[:, columns])
    return product * DH ** (-0.5) + spread_rows(window, block, length)


def attention_forward(query, keys, values, offsets, first_row):
    total_rows = query.shape[0]
    block = min(512, total_rows)
    head_outs = []
    head_lse = []
    for head_idx in range(H):
        scores = attention_scores(query, keys, offsets, first_row, 0, block, head_idx)
        row_max = jnp.max(scores, axis=1, keepdims=True)
        shifted_exp = jnp.exp(scores - row_max)
        row_total = jnp.sum(shifted_exp, axis=1, keepdims=True)
        prob_low = (shifted_exp / row_total).astype(jnp.bfloat16)
        head_outs.append(matmul(prob_low, values[:, head_idx * DH : (head_idx + 1) * DH]))
        head_lse.append((row_max + jnp.log(row_total))[:, 0])
    out_blocks = jnp.concatenate(head_outs, axis=1)
    lse_blocks = jnp.stack(head_lse, axis=0)
    return (out_blocks, lse_blocks)


def attention_backward(query, keys, values, offsets, first_row, log_total, grad_attended, delta):
    total_rows = query.shape[0]
    length = keys.shape[0]
    block = min(512, total_rows)
    scale = DH ** (-0.5)
    key_parts = [jnp.zeros((length, DH), jnp.float32) for head_idx in range(H)]
    value_parts = [jnp.zeros((length, DH), jnp.float32) for head_idx in range(H)]
    offset_rows = [jnp.zeros((2 * length - 1,), jnp.float32) for head_idx in range(H)]
    head_grads = []
    for head_idx in range(H):
        columns = slice(head_idx * DH, (head_idx + 1) * DH)
        scores = attention_scores(query, keys, offsets, first_row, 0, block, head_idx)
        prob = jnp.exp(scores - log_total[head_idx, 0:block][:, None])
        prob_low = prob.astype(jnp.bfloat16)
        grad_piece = grad_attended[0:block, columns]
        value_parts[head_idx] = matmul_left_t(prob_low, grad_piece)
        grad_prob = matmul_right_t(grad_piece, values[:, columns])
        grad_score = prob * (grad_prob - delta[0:block, head_idx][:, None])
        score_low = grad_score.astype(jnp.bfloat16)
        head_grads.append(matmul(score_low, keys[:, columns]) * scale)
        key_parts[head_idx] = matmul_left_t(score_low, query[0:block, columns]) * scale
        anchor = length - block - first_row - 0
        offset_rows[head_idx] = lax.dynamic_update_slice_in_dim(
            offset_rows[head_idx], collect_rows(grad_score, block, length), anchor, 0
        )
    query_blocks = jnp.concatenate(head_grads, axis=1)
    return (
        query_blocks,
        jnp.concatenate(key_parts, axis=1),
        jnp.concatenate(value_parts, axis=1),
        jnp.stack(offset_rows, axis=0),
    )


def mean_last(value):
    return jnp.mean(value, axis=-1, keepdims=True)


def normalize(field):
    shifted = field - mean_last(field)
    inverse = lax.rsqrt(mean_last(shifted * shifted) + EPS_NORM)
    return shifted * inverse, inverse


def norm_grad(grad_out, normed, inverse, gain):
    scaled = grad_out * gain
    grad_in = inverse * (scaled - mean_last(scaled) - normed * mean_last(scaled * normed))
    return grad_in, jnp.sum(grad_out * normed, axis=0, keepdims=True)


def row_to_tile(ref, base, row):
    for k in range(4):
        ref[base + k : base + k + 1, :] = row[:, 128 * k : 128 * (k + 1)]


def tile_to_row(tile):
    return jnp.concatenate([tile[k : k + 1, :] for k in range(4)], axis=1)


def skew(row, count):
    sub = lax.broadcasted_iota(jnp.int32, (8, 512), 0)
    block = jnp.broadcast_to(row, (8, 512))
    for bit in (1, 2, 4):
        block = jnp.where((sub // bit) % 2 == 1, pltpu.roll(block, bit, 1), block)
    size = 8
    while size < count:
        block = jnp.concatenate([block, pltpu.roll(block, size, 1)], axis=0)
        size *= 2
    return block


def unskew_sum(grid):
    size = grid.shape[0] // 2
    while size >= 8:
        grid = grid[:size] + pltpu.roll(grid[size:], 512 - size, 1)
        size //= 2
    sub = lax.broadcasted_iota(jnp.int32, (8, 512), 0)
    for bit in (1, 2, 4):
        grid = jnp.where((sub // bit) % 2 == 1, pltpu.roll(grid, 512 - bit, 1), grid)
    return jnp.sum(grid, axis=0, keepdims=True)


def chunk_pairs(width, pairs):
    left, start, ranges = width // 128, 0, []
    for n in range(2 * pairs, 0, -1):
        count = -(-left // n)
        ranges.append((start, 128 * count))
        start, left = start + 128 * count, left - count
    return [ranges[2 * n : 2 * n + 2] for n in range(pairs)]


class Gather:
    def __init__(self, cube, mine, bands, send_sem, recv_sem):
        self.cube, self.mine = cube, mine
        self.chunks = [(band, pair) for band in bands for pair in chunk_pairs(band.shape[-1], PAIRS)]
        self.send_sem, self.recv_sem = send_sem, recv_sem
        self.copies = {}
        arrivals = [(GATHER_STEP * n + GATHER_AT[s], n, s) for n in range(len(self.chunks)) for s in range(5)]
        self.events = [(n, s) for _, n, s in sorted(arrivals)]

    def start(self, n, stage):
        band, pair = self.chunks[n]
        for half in range(2):
            order = self.cube.gather_orders[half]
            done = order[:stage]
            index = tuple(
                slice(None) if k in done else self.mine[k] for k in range(self.cube.digits)
            )
            place = band.at[index + (slice(None), pl.ds(*pair[half]))]
            copy = remote(
                place,
                place,
                self.send_sem.at[n, half, stage],
                self.recv_sem.at[n, half, stage],
                self.cube.partner(order[stage]),
            )
            copy.start()
            self.copies[n, half, stage] = copy

    def advance(self, n, stage):
        for half in range(2):
            self.copies[n, half, stage].wait_recv()
        if stage + 1 < self.cube.digits:
            self.start(n, stage + 1)
        if stage == 0 and n + 1 < len(self.chunks):
            self.start(n + 1, 0)

    def run_to(self, n, stage):
        while (n, stage) in self.events:
            self.advance(*self.events.pop(0))

    def finish(self):
        for copy in self.copies.values():
            copy.wait_send()


class Scatter:
    def __init__(self, cube, mine, bands, landed, outs, send_sem, recv_sem):
        self.cube, self.mine, self.landed = cube, mine, landed
        self.chunks = [
            (band, out, pair)
            for band, out in zip(bands, outs)
            for pair in chunk_pairs(band.shape[-1], PAIRS)
        ]
        self.send_sem, self.recv_sem = send_sem, recv_sem
        self.copies = {}

    def start(self, n, stage):
        band, _, pair = self.chunks[n]
        for half in range(2):
            order = self.cube.scatter_orders[half]
            index = []
            for k in range(self.cube.digits):
                at = order.index(k)
                if at > stage:
                    index.append(slice(None))
                else:
                    index.append(1 - self.mine[k] if at == stage else self.mine[k])
            copy = remote(
                band.at[tuple(index) + (slice(None), pl.ds(*pair[half]))],
                self.landed[(n * 2 + half) * self.cube.digits + stage],
                self.send_sem.at[n, half, stage],
                self.recv_sem.at[n, half, stage],
                self.cube.partner(order[stage]),
            )
            copy.start()
            self.copies[n, half, stage] = copy

    def add(self, n, half, stage):
        order = self.cube.scatter_orders[half]
        band, out, pair = self.chunks[n]
        columns = pl.ds(*pair[half])
        free = [k for k in range(self.cube.digits) if order.index(k) > stage]
        extra = self.landed[(n * 2 + half) * self.cube.digits + stage]
        everything = (slice(None), columns)

        def one(i):
            digit = {
                k: lax.rem(i // (1 << (len(free) - 1 - m)), 2) for m, k in enumerate(free)
            }
            full = tuple(digit.get(k, self.mine[k]) for k in range(self.cube.digits)) + everything
            short = tuple(digit[k] for k in free) + (slice(None), slice(None))
            total = band[full].astype(jnp.float32) + extra[short].astype(jnp.float32)
            if free:
                band[full] = total.astype(band.dtype)
            else:
                out[:, columns] = total

        if free:
            pl.loop(0, 1 << len(free))(one)
        else:
            one(0)

    def advance(self, n, stage):
        for half in range(2):
            self.copies[n, half, stage].wait_recv()
            self.add(n, half, stage)
        if stage + 1 < self.cube.digits:
            self.start(n, stage + 1)

    def finish(self):
        for copy in self.copies.values():
            copy.wait_send()


class Collect:
    def __init__(self, cube, tile, slots, send_sem, recv_sem):
        self.cube, self.tile, self.slots = cube, tile, slots
        self.send_sem, self.recv_sem = send_sem, recv_sem

    def make(self, i):
        to = self.cube.coords(lax.rem(self.cube.index() + i, self.cube.total))
        return remote(
            self.tile, self.slots.at[i], self.send_sem.at[i], self.recv_sem.at[i], to
        )

    def start(self):
        pl.loop(1, self.cube.total)(lambda i: self.make(i).start())
        self.slots[0] = self.tile[...]

    def arrive(self):
        pl.loop(1, self.cube.total)(lambda i: self.make(i).wait())

    def total(self):
        result = self.slots[0]
        for i in range(1, self.cube.total):
            result = result + self.slots[i]
        return result


class Momenta:
    def __init__(self, cube, r):
        self.cube, self.r = cube, r
        self.me = cube.index()
        self.repeat = cube.dp_size // 8
        d = lax.axis_index("dp")
        self.is_owner = lax.rem(d, self.repeat) == 0
        self.matrix = d // self.repeat
        self.quarter = lax.axis_index("seq") * 2 + lax.axis_index("shard")
        self.owned_index = self.matrix * 4 + self.quarter

    def holds(self, t):
        return jnp.logical_and(self.is_owner, self.owned_index == t)

    def rows(self, j):
        r = self.r
        if j < 4:
            old, share = ((r.m_up, r.m_down)[j // 2], (r.share_first, r.share_second)[j % 2])
            return old[:, FF * (j % 2) : FF * (j % 2 + 1)], share[:, FF * (j // 2) : FF * (j // 2 + 1)]
        start = STARTS[j] - STARTS[4]
        old = (r.m_qkv, r.m_out, r.m_glu, r.m_point)[j - 4]
        return old[...], r.share_middle[:, start : start + WIDTHS[j]]

    def copy(self, t):
        width = WIDTHS[t // 4] // 4
        r = self.r
        return remote(
            r.leaving.at[t, :, pl.ds(0, width)],
            r.owned.at[self.me, :, pl.ds(0, width)],
            r.m_send.at[t],
            r.m_recv.at[self.me],
            owner_coords(self.cube, t),
        )

    def send(self, j):
        old, share = self.rows(j)
        value = (MOMENTUM * old + share).astype(jnp.bfloat16)
        width = WIDTHS[j] // 4
        for q in range(4):
            t = 4 * j + q
            part = value[:, width * q : width * (q + 1)]
            self.r.leaving[t, :, 0:width] = part
            pl.when(jnp.logical_not(self.holds(t)))(lambda t=t: self.copy(t).start())

            @pl.when(self.holds(t))
            def _(part=part, width=width):
                self.r.owned[self.me, :, 0:width] = part

    def receive(self):
        r, cube = self.r, self.cube

        def go(width):
            @pl.loop(1, cube.total)
            def _(i):
                source = lax.rem(self.me + i, cube.total)
                place = r.owned.at[source, :, pl.ds(0, width)]
                remote(
                    place, place, r.m_send.at[0], r.m_recv.at[source], cube.coords(source)
                ).wait_recv()

        pl.when(self.is_owner)(lambda: by_matrix(self.matrix, go))

    def back(self, i, width):
        r, cube = self.r, self.cube
        to = lax.rem(self.me + i, cube.total)
        return remote(
            r.solved.at[to, :, pl.ds(0, width)],
            r.returned.at[self.owned_index, :, pl.ds(0, width)],
            r.b_send.at[i],
            r.b_recv.at[self.owned_index],
            cube.coords(to),
        )

    def send_back(self):
        r = self.r

        def go(width):
            pl.loop(1, self.cube.total)(lambda i: self.back(i, width).start())
            r.returned[self.owned_index, :, 0:width] = r.solved[self.me, :, 0:width]

        pl.when(self.is_owner)(lambda: by_matrix(self.matrix, go))

    def receive_back(self):
        r = self.r
        for t in range(32):
            place = r.returned.at[t, :, pl.ds(0, WIDTHS[t // 4] // 4)]
            copy = remote(
                place, place, r.b_send.at[0], r.b_recv.at[t], owner_coords(self.cube, t)
            )
            pl.when(jnp.logical_not(self.holds(t)))(copy.wait_recv)

    def finish(self):
        for t in range(32):
            pl.when(jnp.logical_not(self.holds(t)))(lambda t=t: self.copy(t).wait_send())

        def go(width):
            pl.loop(1, self.cube.total)(lambda i: self.back(i, width).wait_send())

        pl.when(self.is_owner)(lambda: by_matrix(self.matrix, go))


GRAM_SHARES = (
    ((0, 0), (0, 1), (0, 2), (0, 3), (3, 3)),
    ((1, 1), (1, 2), (1, 3), (2, 2), (2, 3)),
)


def orthogonalize(cube, r):
    f32 = jnp.float32
    core, seq = lax.axis_index("shard"), lax.axis_index("seq")
    block = r.owned.reshape(D, BLOCK)
    lines = [slice(128 * i, 128 * (i + 1)) for i in range(4)]
    for share in range(2):
        for n, (i, j) in enumerate(GRAM_SHARES[share]):
            r.packed[share, n] = matmul_right_t(block[lines[i], :], block[lines[j], :])
    peers = (cube.partner(cube.levels + 1), cube.partner(cube.levels))
    first = remote(
        r.packed.at[1 - core], r.packed_in.at[0], r.n_send.at[0], r.n_recv.at[0], peers[0]
    )
    first.start()
    first.wait()
    r.summed[...] = r.packed[core] + r.packed_in[0]
    second = remote(r.summed, r.packed_in.at[1], r.n_send.at[1], r.n_recv.at[1], peers[1])
    second.start()
    second.wait()
    r.whole[core] = r.summed[...] + r.packed_in[1]
    third = remote(
        r.whole.at[core], r.whole.at[core], r.n_send.at[2], r.n_recv.at[2], peers[0]
    )
    third.start()
    third.wait()
    for share in range(2):
        for n, (i, j) in enumerate(GRAM_SHARES[share]):
            value = r.whole[share, n]
            r.gram[lines[i], lines[j]] = value
            if i != j:
                r.gram[lines[j], lines[i]] = jnp.transpose(value)
    row = lax.broadcasted_iota(jnp.int32, (D, D), 0)
    col = lax.broadcasted_iota(jnp.int32, (D, D), 1)
    eye = row == col
    gram = r.gram[...]
    square = jnp.sum(
        jnp.sum(jnp.where(eye, gram, 0.0), axis=1, keepdims=True), axis=0, keepdims=True
    )
    scale = 1.0 / (jnp.sqrt(square) + 1e-07)
    gram = gram * (scale * scale)
    value = None
    for step in range(5):
        parts = split(gram)
        mixed = COEF_B * gram + COEF_C * product(parts, parts)
        mixed = jnp.where(eye, mixed + COEF_A, mixed)
        high, low = split(mixed)
        if step == 0:
            start_high, start_low = split(mixed * scale)
            value = matmul(start_high, block[...]) + matmul(start_low, block[...])
        elif step < 4:
            value = product((high, low), split(value))
        else:
            value = matmul(high, value.astype(jnp.bfloat16))
        if step < 4:
            gram = product((high, low), split(product((high, low), parts)))
    r.solved.reshape(D, BLOCK)[...] = value.astype(jnp.bfloat16)


SMALL_REL, SMALL_VEC, SMALL_DEPTH = 0, H, H + 7
SMALL_END = H + 7 + K
EDGE = 16
PAIRS = 2
GATHER_STEP = 8.0
GATHER_AT = (4.0, 8.0, 13.0, 21.0, 24.0)
SECOND, MIDDLE, FIRST = 0, PAIRS, 2 * PAIRS


def step_kernel(cube, rel_rows, r):
    bf16, f32 = jnp.bfloat16, jnp.float32
    x_ref, cot_ref, bucket_ref = r.inputs, r.cotangent, r.bucket
    tokens = x_ref.shape[0]
    token_total = tokens * cube.total
    rows = r.small.shape[0]
    mine = cube.mine()
    seq = lax.axis_index("seq")
    early = seq == 0
    first_row = pl.multiple_of(seq * tokens, tokens)
    other_row = pl.multiple_of((1 - seq) * tokens, tokens)
    across = cube.partner(cube.levels)
    lengths = [ref.shape[-1] for ref in (r.first, r.middle, r.second)]
    first, middle, second, d_first, d_middle, d_second = (
        ref.reshape(D, ref.shape[-1])
        for ref in (r.first, r.middle, r.second, r.d_first, r.d_middle, r.d_second)
    )
    a, xh = r.a, r.xh

    barrier = pltpu.get_barrier_semaphore()
    me = cube.index()
    momenta = Momenta(cube, r)

    @pl.loop(0, cube.total)
    def _(i):
        r.owned[i] = jnp.zeros(r.owned.shape[1:], bf16)

    @pl.loop(1, cube.total)
    def _(i):
        peer = cube.coords(lax.rem(me + i, cube.total))
        pl.semaphore_signal(barrier, inc=1, device_id=peer, device_id_type=MESH)

    own = tuple(mine)
    r.first[own + (slice(None), slice(0, FF))] = r.w_up[:, :FF].astype(bf16)
    r.first[own + (slice(None), slice(FF, 2 * FF))] = r.w_down[:, :FF].astype(bf16)
    r.first[own + (slice(None), slice(2 * FF, lengths[0]))] = r.small[...].astype(bf16)
    r.middle[own + (slice(None), slice(0, 3 * D))] = r.w_qkv[...].astype(bf16)
    r.middle[own + (slice(None), slice(3 * D, 4 * D))] = r.w_out[...].astype(bf16)
    r.middle[own + (slice(None), slice(4 * D, 6 * D))] = r.w_glu[...].astype(bf16)
    r.middle[own + (slice(None), slice(6 * D, 7 * D))] = r.w_point[...].astype(bf16)
    r.second[own + (slice(None), slice(0, FF))] = r.w_up[:, FF:].astype(bf16)
    r.second[own + (slice(None), slice(FF, 2 * FF))] = r.w_down[:, FF:].astype(bf16)
    pl.semaphore_wait(barrier, cube.total - 1)

    gather = Gather(
        cube, mine, (r.first, r.middle, r.second), r.g_send, r.g_recv
    )
    scatter = Scatter(
        cube,
        mine,
        (r.d_second, r.d_middle, r.d_first),
        r.land,
        (r.share_second, r.share_middle, r.share_first),
        r.s_send,
        r.s_recv,
    )

    gather.start(0, 0)
    xh0, inv0 = normalize(x_ref[...])
    xh[0] = xh0
    rho = lax.broadcasted_iota(jnp.int32, (D, 2 * 256), 0)
    bucket_of = jnp.where(rho % rows < rel_rows, (rho // rows) * rel_rows + rho % rows, -2)
    r.hit[...] = (bucket_ref[...] == bucket_of).astype(f32).astype(bf16)
    gather.run_to(PAIRS - 1, 4)

    small = r.small_t
    small[...] = jnp.transpose(first[:, 2 * FF : 2 * FF + 128].astype(f32))
    gains = [small[SMALL_VEC + i : SMALL_VEC + i + 1, :] for i in range(7)]
    taps = [small[SMALL_DEPTH + k : SMALL_DEPTH + k + 1, :] for k in range(K)]
    CH = 512

    def ffn_forward_fused(index, field, normed, weights, u_ref, s_ref):
        low = (normed * gains[(0, 1, 2, 3)[index]]).astype(bf16)
        a[index] = low
        for c in range(0, FF, CH):
            u = matmul(low, weights[:, c : c + CH])
            u_ref[:, c : c + CH] = u
            s_ref[:, c : c + CH] = (u * jax.nn.sigmoid(u)).astype(bf16)
        return field + 0.5 * matmul_right_t(s_ref[...], weights[:, FF : 2 * FF])

    section1 = ffn_forward_fused(0, x_ref[...], xh[0], first, r.u1, r.s1)
    r.sec1[...] = section1
    xh1, inv1 = normalize(section1)
    xh[1] = xh1
    a[1] = (xh1 * gains[1]).astype(bf16)
    offsets = matmul(small[0:8, :].astype(bf16), r.hit[...])
    offsets = jnp.where(
        early, pltpu.roll(offsets, 257, 1), pltpu.roll(offsets, (tokens + 257) % 512, 1)
    )
    for h in range(H):
        r.bias[h] = skew(offsets[h : h + 1, :], tokens)[:, : 2 * tokens]
    gather.run_to(2 * PAIRS - 1, 4)

    q_ref, kv = r.q, r.kv
    kv[pl.ds(first_row, tokens), :] = matmul(a[1], middle[:, D : 3 * D]).astype(bf16)
    kv_copy = remote(
        kv.at[pl.ds(first_row, tokens)],
        kv.at[pl.ds(first_row, tokens)],
        r.kv_send,
        r.kv_recv,
        across,
    )
    kv_copy.start()
    q_ref[...] = matmul(a[1], middle[:, :D]).astype(bf16)
    kv_copy.wait_recv()
    lane = lax.broadcasted_iota(jnp.int32, (1, 128), 1)
    lane_masks = [(lane // DH == e).astype(f32) for e in range(2)]
    low_masks = [m.astype(bf16) for m in lane_masks]
    scale = DH ** (-0.5)
    for p in range(H // 2):
        columns = slice(128 * p, 128 * (p + 1))
        k_pair, v_pair = kv[:, columns], kv[:, D + 128 * p : D + 128 * (p + 1)]
        merged = None
        for e in range(2):
            q_head = q_ref[:, columns] * low_masks[e]
            scores = matmul_right_t(q_head, k_pair) * scale + r.bias[2 * p + e]
            shifted = jnp.exp(scores - jnp.max(scores, axis=1, keepdims=True))
            prob = shifted / jnp.sum(shifted, axis=1, keepdims=True)
            r.prob[2 * p + e] = prob
            out = matmul(prob.astype(bf16), v_pair) * lane_masks[e]
            merged = out if merged is None else merged + out
        r.att[:, columns] = merged
    att_low = r.att[...].astype(bf16)
    r.att_low[...] = att_low
    gather.run_to(3 * PAIRS - 1, 2)
    section2 = r.sec1[...] + matmul(att_low, middle[:, 3 * D : 4 * D])
    r.sec2[...] = section2
    xh2, inv2 = normalize(section2)
    xh[2] = xh2
    a[2] = (xh2 * gains[2]).astype(bf16)
    gate_first = matmul(a[2], middle[:, 4 * D : 5 * D])
    sig = jax.nn.sigmoid(matmul(a[2], middle[:, 5 * D : 6 * D]))
    r.gate[...] = gate_first
    r.sig[...] = sig
    wide = r.wide
    wide[EDGE : EDGE + tokens, :] = gate_first * sig
    edge_row = pl.multiple_of(EDGE + (1 - seq) * (tokens - EDGE), EDGE)
    halo_copy = remote(
        wide.at[pl.ds(edge_row, EDGE)], r.halo, r.halo_send, r.halo_recv, across
    )
    halo_copy.start()
    zero_edge = jnp.zeros((EDGE, D), f32)
    halo_copy.wait()
    wide[0:EDGE, :] = jnp.where(early, zero_edge, r.halo[...])
    wide[EDGE + tokens :, :] = jnp.where(early, r.halo[...], zero_edge)
    conv_ref = r.conv
    for b in range(D // 128):
        cols = slice(128 * b, 128 * (b + 1))
        total = jnp.zeros((tokens, 128), f32)
        for k in range(K):
            total = total + wide[k + 1 : k + 1 + tokens, cols] * taps[k][:, cols]
        conv_ref[:, cols] = total
    conv = conv_ref[...]
    part_sum = jnp.sum(conv, axis=0, keepdims=True)
    part_off = conv - part_sum * (1.0 / tokens)
    part_square = jnp.sum(part_off * part_off, axis=0, keepdims=True)
    row_to_tile(r.tile1, 0, part_sum)
    row_to_tile(r.tile1, 4, part_square)
    stats = Collect(cube, r.tile1, r.slots1, r.c1_send, r.c1_recv)
    stats.start()
    gather.run_to(3 * PAIRS - 1, 4)
    stats.arrive()
    sums = stats.total()
    mean4 = sums[0:4] * (1.0 / token_total)
    spread4 = jnp.zeros((4, 128), f32)
    for i in range(cube.total):
        off = r.slots1[i][0:4] * (1.0 / tokens) - mean4
        spread4 = spread4 + off * off
    var4 = (sums[4:8] + spread4 * tokens) * (1.0 / token_total)
    mean = tile_to_row(mean4)
    inv_std = tile_to_row(lax.rsqrt(var4 + EPS_BATCH))

    xb = (conv_ref[...] - mean) * inv_std
    r.xb[...] = xb
    bn = xb * gains[5] + gains[6]
    r.bn[...] = bn
    sw = (bn * jax.nn.sigmoid(bn)).astype(bf16)
    r.sw[...] = sw
    section3 = r.sec2[...] + matmul(sw, middle[:, 6 * D : 7 * D])
    xh3, inv3 = normalize(section3)
    xh[3] = xh3
    section4 = ffn_forward_fused(3, section3, xh3, second, r.u2, r.s2)
    xh4, inv4 = normalize(section4)
    r.outputs[...] = xh4 * gains[4]

    sg = r.small_grad
    sg[...] = jnp.zeros_like(sg)
    cot = cot_ref[...]
    d4, sg[SMALL_VEC + 4 : SMALL_VEC + 5, :] = norm_grad(cot, xh4, inv4, gains[4])

    def slope(value):
        sigma = jax.nn.sigmoid(value)
        return sigma * (1.0 + value * (1.0 - sigma))

    def ffn_backward_fused(grad, weights, u_ref, du_ref):
        low = (0.5 * grad).astype(bf16)
        for c in range(0, FF, CH):
            act = matmul(low, weights[:, FF + c : FF + c + CH])
            du_ref[:, c : c + CH] = (act * slope(u_ref[:, c : c + CH])).astype(bf16)
        return low, matmul_right_t(du_ref[...], weights[:, :FF])

    def weight_grad(left, right_ref, target, start, width):
        for c in range(0, width, CH):
            target[:, start + c : start + c + CH] = matmul_left_t(
                left, right_ref[:, c : c + CH]
            ).astype(bf16)

    e2, back = ffn_backward_fused(d4, second, r.u2, r.du)
    r.e_low[...] = e2
    part, sg[SMALL_VEC + 3 : SMALL_VEC + 4, :] = norm_grad(back, xh[3], inv3, gains[3])
    d3 = d4 + part
    r.d[...] = d3
    e3 = d3.astype(bf16)
    r.e3[...] = e3
    dbn = matmul_right_t(e3, middle[:, 6 * D : 7 * D]) * slope(r.bn[...])
    xb = r.xb[...]
    sg[SMALL_VEC + 5 : SMALL_VEC + 6, :] = jnp.sum(dbn * xb, axis=0, keepdims=True)
    sg[SMALL_VEC + 6 : SMALL_VEC + 7, :] = jnp.sum(dbn, axis=0, keepdims=True)
    dxb = dbn * gains[5]
    r.dxb[...] = dxb
    row_to_tile(r.tile2, 0, jnp.sum(dxb, axis=0, keepdims=True))
    row_to_tile(r.tile2, 4, jnp.sum(dxb * xb, axis=0, keepdims=True))
    sums2 = Collect(cube, r.tile2, r.slots2, r.c2_send, r.c2_recv)
    sums2.start()
    token_edge = pl.multiple_of((1 - seq) * (tokens - EDGE), EDGE)
    edges = r.edges
    edges[0:EDGE, :] = r.dxb[pl.ds(token_edge, EDGE), :]
    edges[EDGE:, :] = r.xb[pl.ds(token_edge, EDGE), :]
    edge_copy = remote(edges, r.edges_in, r.edge_send, r.edge_recv, across)
    edge_copy.start()

    weight_grad(r.e_low[...], r.s2, d_second, FF, FF)
    weight_grad(a[3], r.du, d_second, 0, FF)
    for n in range(PAIRS):
        scatter.start(SECOND + n, 0)
    weight_grad(r.sw[...], r.e3, d_middle, 6 * D, D)
    edge_copy.wait()
    sums2.arrive()
    total2 = sums2.total()
    mean1 = tile_to_row(total2[0:4] * (1.0 / token_total))
    mean2 = tile_to_row(total2[4:8] * (1.0 / token_total))
    dwide = r.dwide
    dwide[EDGE : EDGE + tokens, :] = inv_std * (r.dxb[...] - mean1 - r.xb[...] * mean2)
    edge = inv_std * (r.edges_in[0:EDGE, :] - mean1 - r.edges_in[EDGE:, :] * mean2)
    dwide[0:EDGE, :] = jnp.where(early, zero_edge, edge)
    dwide[EDGE + tokens :, :] = jnp.where(early, edge, zero_edge)
    dglu_ref = r.conv
    for b in range(D // 128):
        cols = slice(128 * b, 128 * (b + 1))
        total = jnp.zeros((tokens, 128), f32)
        for k in range(K):
            total = total + dwide[31 - k : 31 - k + tokens, cols] * taps[k][:, cols]
        dglu_ref[:, cols] = total
    dglu, sig = dglu_ref[...], r.sig[...]
    r.dgates[:, :D] = (dglu * sig).astype(bf16)
    r.dgates[:, D:] = (dglu * r.gate[...] * sig * (1.0 - sig)).astype(bf16)
    for n in range(PAIRS):
        scatter.advance(SECOND + n, 0)
    back = matmul_right_t(r.dgates[...], middle[:, 4 * D : 6 * D])
    part, sg[SMALL_VEC + 2 : SMALL_VEC + 3, :] = norm_grad(back, xh[2], inv2, gains[2])
    d2 = r.d[...] + part
    r.d[...] = d2
    e1 = d2.astype(bf16)
    r.e_low[...] = e1
    dob = matmul_right_t(e1, middle[:, 3 * D : 4 * D]).astype(bf16)
    r.dob[...] = dob

    off_rows = []
    give, keep, got = r.give, r.keep, r.got
    kv_grads = []
    for p in range(H // 2):
        columns = slice(128 * p, 128 * (p + 1))
        k_pair, v_pair = kv[:, columns], kv[:, D + 128 * p : D + 128 * (p + 1)]
        att_pair = r.att[:, columns]
        dq = dk = dv = None
        for e in range(2):
            h = 2 * p + e
            dob_head = r.dob[:, columns] * low_masks[e]
            q_head = q_ref[:, columns] * low_masks[e]
            delta = jnp.sum(dob_head.astype(f32) * att_pair, axis=1, keepdims=True)
            prob = r.prob[h]
            ds = prob * (matmul_right_t(dob_head, v_pair) - delta)
            ds_low = ds.astype(bf16)
            dv_head = matmul_left_t(prob.astype(bf16), dob_head)
            dk_head = matmul_left_t(ds_low, q_head) * scale
            dq_head = matmul(ds_low, k_pair) * (lane_masks[e] * scale)
            dv = dv_head if dv is None else dv + dv_head
            dk = dk_head if dk is None else dk + dk_head
            dq = dq_head if dq is None else dq + dq_head
            padded = jnp.concatenate([ds, jnp.zeros((tokens, 512 - 2 * tokens), f32)], axis=1)
            off_rows.append(unskew_sum(padded))
        r.dqkv[:, columns] = dq.astype(bf16)
        for n, value in enumerate((dk, dv)):
            r.dkv[n] = value
            give[p, n] = r.dkv[n, pl.ds(other_row, tokens), :].astype(bf16)
            keep[p, n] = r.dkv[n, pl.ds(first_row, tokens), :]
        copy = remote(
            give.at[p], got.at[p], r.dkv_send.at[p], r.dkv_recv.at[p], across
        )
        copy.start()
        kv_grads.append(copy)
        if p == 1:
            scatter.advance(SECOND, 1)
    off = jnp.concatenate(off_rows, axis=0)
    off = jnp.where(early, pltpu.roll(off, 255, 1), pltpu.roll(off, 255 - tokens, 1))
    off_high, off_low = split(off)
    sg[0:8, :] = matmul_right_t(off_high, r.hit[...]) + matmul_right_t(off_low, r.hit[...])
    weight_grad(r.att_low[...], r.e_low, d_middle, 3 * D, D)
    weight_grad(a[2], r.dgates, d_middle, 4 * D, 2 * D)
    for p in range(H // 2):
        kv_grads[p].wait()
        for n in range(2):
            at = D * (n + 1) + 128 * p
            r.dqkv[:, at : at + 128] = (keep[p, n] + got[p, n].astype(f32)).astype(bf16)
    scatter.advance(SECOND + 1, 1)
    scatter.advance(SECOND, 2)
    weight_grad(a[1], r.dqkv, d_middle, 0, 3 * D)
    for n in range(PAIRS):
        scatter.start(MIDDLE + n, 0)
    back = matmul_right_t(r.dqkv[...], middle[:, : 3 * D])
    part, sg[SMALL_VEC + 1 : SMALL_VEC + 2, :] = norm_grad(back, xh[1], inv1, gains[1])
    d1 = r.d[...] + part
    scatter.advance(SECOND + 1, 2)
    scatter.advance(SECOND, 3)
    e0, back = ffn_backward_fused(d1, first, r.u1, r.du)
    for n in range(PAIRS):
        scatter.advance(MIDDLE + n, 0)
    part, sg[SMALL_VEC : SMALL_VEC + 1, :] = norm_grad(back, xh[0], inv0, gains[0])
    r.input_grad[...] = d1 + part
    for b in range(D // 128):
        cols = slice(128 * b, 128 * (b + 1))
        dconv = dwide[EDGE : EDGE + tokens, cols]
        for k in range(K):
            sg[SMALL_DEPTH + k : SMALL_DEPTH + k + 1, cols] = jnp.sum(
                dconv * wide[k + 1 : k + 1 + tokens, cols], axis=0, keepdims=True
            )
    d_first[:, 2 * FF : 2 * FF + 128] = jnp.transpose(sg[...]).astype(bf16)
    weight_grad(e0, r.s1, d_first, FF, FF)
    weight_grad(a[0], r.du, d_first, 0, FF)
    for n in range(PAIRS):
        scatter.start(FIRST + n, 0)
    scatter.advance(SECOND + 1, 3)
    scatter.advance(SECOND, 4)
    for n in range(PAIRS):
        scatter.advance(FIRST + n, 0)
    scatter.advance(MIDDLE, 1)
    scatter.advance(SECOND + 1, 4)
    for j in (1, 3):
        momenta.send(j)
    scatter.advance(MIDDLE + 1, 1)
    scatter.advance(MIDDLE, 2)
    scatter.advance(FIRST, 1)
    scatter.advance(MIDDLE + 1, 2)
    scatter.advance(MIDDLE, 3)
    scatter.advance(FIRST + 1, 1)
    scatter.advance(MIDDLE, 4)
    scatter.advance(MIDDLE + 1, 3)
    scatter.advance(FIRST, 2)
    scatter.advance(MIDDLE + 1, 4)
    for j in (4, 5, 6, 7):
        momenta.send(j)
    scatter.advance(FIRST + 1, 2)
    scatter.advance(FIRST, 3)
    scatter.advance(FIRST + 1, 3)
    scatter.advance(FIRST, 4)
    scatter.advance(FIRST + 1, 4)
    for j in (0, 2):
        momenta.send(j)
    next_small = MOMENTUM * r.m_small[...] + r.share_first[:, 2 * FF :]
    r.tile3[...] = jnp.zeros_like(r.tile3)
    r.tile3[0:1, :] = jnp.sum(next_small * next_small, axis=0, keepdims=True)
    squares = Collect(cube, r.tile3, r.slots3, r.c3_send, r.c3_recv)
    squares.start()
    momenta.receive()
    orthogonalize(cube, r)
    momenta.send_back()
    squares.arrive()
    r.squares[...] = squares.total()
    momenta.receive_back()
    momenta.finish()
    gather.finish()
    scatter.finish()
    kv_copy.wait_send()


def fused_step(cube, inputs, cotangent, weights, momenta, small, bucket, rel_rows, collective_id):
    bf16, f32 = jnp.bfloat16, jnp.float32
    tokens, rows = inputs.shape[0], small.shape[0]
    widths = (2 * FF + 128, 7 * D, 2 * FF)
    lead = (2,) * cube.digits
    named = dict(
        inputs=inputs,
        cotangent=cotangent,
        w_up=weights[0],
        w_down=weights[1],
        w_qkv=weights[2],
        w_out=weights[3],
        w_glu=weights[4],
        w_point=weights[5],
        m_up=momenta[0],
        m_down=momenta[1],
        m_qkv=momenta[2],
        m_out=momenta[3],
        m_glu=momenta[4],
        m_point=momenta[5],
        m_small=momenta[6],
        small=small,
        bucket=bucket,
    )
    outs = dict(
        outputs=jax.ShapeDtypeStruct((tokens, D), f32),
        input_grad=jax.ShapeDtypeStruct((tokens, D), f32),
        share_first=jax.ShapeDtypeStruct((rows, widths[0]), f32),
        share_middle=jax.ShapeDtypeStruct((rows, widths[1]), f32),
        share_second=jax.ShapeDtypeStruct((rows, widths[2]), f32),
        returned=jax.ShapeDtypeStruct((32, rows, BLOCK), bf16),
        squares=jax.ShapeDtypeStruct((8, 128), f32),
    )
    field = pltpu.VMEM((tokens, D), f32)
    low = pltpu.VMEM((tokens, D), bf16)
    wide_low = pltpu.VMEM((tokens, FF), bf16)
    wide_field = pltpu.VMEM((tokens + 2 * EDGE, D), f32)
    grid = pltpu.VMEM((H, tokens, 2 * tokens), f32)
    pairs = pltpu.VMEM((H // 2, 2, tokens, 128), bf16)
    tile = pltpu.VMEM((8, 128), f32)
    slots = pltpu.VMEM((cube.total, 8, 128), f32)
    stages = pltpu.SemaphoreType.DMA((3 * PAIRS, 2, cube.digits))
    everyone = pltpu.SemaphoreType.DMA((cube.total,))
    single = pltpu.SemaphoreType.DMA
    bands = [pltpu.VMEM(lead + (rows, w), bf16) for w in widths]
    land = []
    for w in (widths[2], widths[1], widths[0]):
        for pair in chunk_pairs(w, PAIRS):
            for _, part in pair:
                for stage in range(cube.digits):
                    shape = (2,) * (cube.digits - 1 - stage) + (rows, part)
                    land.append(pltpu.VMEM(shape, bf16))
    scratch = dict(
        first=bands[0],
        middle=bands[1],
        second=bands[2],
        d_first=bands[0],
        d_middle=bands[1],
        d_second=bands[2],
        land=tuple(land),
        sec1=field,
        sec2=field,
        att=field,
        gate=field,
        sig=field,
        conv=field,
        xb=field,
        bn=field,
        dxb=field,
        d=field,
        q=low,
        att_low=low,
        sw=low,
        e_low=low,
        e3=low,
        dob=low,
        a=pltpu.VMEM((4, tokens, D), bf16),
        xh=pltpu.VMEM((4, tokens, D), f32),
        u1=pltpu.VMEM((tokens, FF), f32),
        u2=pltpu.VMEM((tokens, FF), f32),
        s1=wide_low,
        s2=wide_low,
        du=wide_low,
        kv=pltpu.VMEM((2 * tokens, 2 * D), bf16),
        bias=grid,
        prob=grid,
        wide=wide_field,
        dwide=wide_field,
        halo=pltpu.VMEM((EDGE, D), f32),
        edges=pltpu.VMEM((2 * EDGE, D), f32),
        edges_in=pltpu.VMEM((2 * EDGE, D), f32),
        dgates=pltpu.VMEM((tokens, 2 * D), bf16),
        dqkv=pltpu.VMEM((tokens, 3 * D), bf16),
        dkv=pltpu.VMEM((2, 2 * tokens, 128), f32),
        give=pairs,
        got=pairs,
        keep=pltpu.VMEM((H // 2, 2, tokens, 128), f32),
        hit=pltpu.VMEM((D, 512), bf16),
        small_t=pltpu.VMEM((128, D), f32),
        small_grad=pltpu.VMEM((128, D), f32),
        tile1=tile,
        tile2=tile,
        slots1=slots,
        slots2=slots,
        tile3=tile,
        slots3=slots,
        leaving=pltpu.VMEM((32, rows, BLOCK), bf16),
        owned=pltpu.VMEM((cube.total, rows, BLOCK), bf16),
        solved=pltpu.VMEM((cube.total, rows, BLOCK), bf16),
        packed=pltpu.VMEM((2, 5, 128, 128), f32),
        packed_in=pltpu.VMEM((2, 5, 128, 128), f32),
        summed=pltpu.VMEM((5, 128, 128), f32),
        whole=pltpu.VMEM((2, 5, 128, 128), f32),
        gram=pltpu.VMEM((D, D), f32),
        m_send=pltpu.SemaphoreType.DMA((32,)),
        m_recv=everyone,
        b_send=everyone,
        b_recv=pltpu.SemaphoreType.DMA((32,)),
        n_send=pltpu.SemaphoreType.DMA((3,)),
        n_recv=pltpu.SemaphoreType.DMA((3,)),
        c3_send=everyone,
        c3_recv=everyone,
        g_send=stages,
        g_recv=stages,
        s_send=stages,
        s_recv=stages,
        c1_send=everyone,
        c1_recv=everyone,
        c2_send=everyone,
        c2_recv=everyone,
        kv_send=single,
        kv_recv=single,
        halo_send=single,
        halo_recv=single,
        edge_send=single,
        edge_recv=single,
        dkv_send=pltpu.SemaphoreType.DMA((H // 2,)),
        dkv_recv=pltpu.SemaphoreType.DMA((H // 2,)),
    )

    def body(*refs):
        count = len(named) + len(outs)
        r = dict(zip(list(named) + list(outs), refs[:count])) | dict(zip(scratch, refs[count:]))
        step_kernel(cube, rel_rows, types.SimpleNamespace(**r))

    return pl.pallas_call(
        body,
        out_shape=list(outs.values()),
        in_specs=[pl.BlockSpec(memory_space=pltpu.VMEM)] * len(named),
        out_specs=[pl.BlockSpec(memory_space=pltpu.VMEM)] * len(outs),
        scratch_shapes=list(scratch.values()),
        compiler_params=pltpu.CompilerParams(
            collective_id=collective_id, has_side_effects=True, vmem_limit_bytes=60 << 20
        ),
        name="block_step",
    )(*named.values())


def finish_kernel(rel_rows, r):
    f32 = jnp.float32
    for j in range(8):
        width = WIDTHS[j]
        if j < 4:
            columns = slice(FF * (j % 2), FF * (j % 2 + 1))
            share = (r.share_first, r.share_second)[j % 2]
            grad = share[:, FF * (j // 2) : FF * (j // 2 + 1)]
        else:
            columns = slice(0, width)
            start = STARTS[j] - STARTS[4]
            grad = r.share_middle[:, start : start + width]
        n = j // 2 if j < 4 else j - 2
        updated = MOMENTUM * r.moment[n][:, columns] + grad
        r.grad[n][:, columns] = grad
        r.next[n][:, columns] = updated
        solved = [
            r.returned[4 * j + q, :, 0 : width // 4].astype(f32) for q in range(4)
        ]
        r.new[n][:, columns] = r.weight[n][:, columns] - RATE_MATRIX * jnp.concatenate(
            solved, axis=1
        )
    grad = r.share_first[:, 2 * FF :]
    updated = MOMENTUM * r.m_small[...] + grad
    lane = lax.broadcasted_iota(jnp.int32, (1, 128), 1)
    count = jnp.where(lane < SMALL_VEC, float(NB), float(D))
    scale = lax.rsqrt(r.squares[0:1, :] / count + EPS_SCALE)
    new = r.small[...] - RATE_VECTOR * updated * scale
    for value, outs in ((grad, r.grad), (new, r.new), (updated, r.next)):
        outs[6][...] = value[:, SMALL_VEC : SMALL_VEC + 7]
        outs[7][...] = value[:, SMALL_DEPTH : SMALL_DEPTH + K]
        outs[8][...] = value[0:rel_rows, 0:H]


def finish_step(shares, returned, squares, weights, momenta, small, shapes, rel_rows):
    operands = (*shares, returned, squares, *weights, small, *momenta)

    def body(*refs):
        outs = refs[len(operands) :]
        finish_kernel(
            rel_rows,
            types.SimpleNamespace(
                share_first=refs[0],
                share_middle=refs[1],
                share_second=refs[2],
                returned=refs[3],
                squares=refs[4],
                weight=refs[5:11],
                small=refs[11],
                moment=refs[12:18],
                m_small=refs[18],
                grad=outs[:9],
                new=outs[9:18],
                next=outs[18:],
            ),
        )

    return pl.pallas_call(
        body,
        out_shape=[jax.ShapeDtypeStruct(s, jnp.float32) for s in shapes * 3],
        in_specs=[pl.BlockSpec(memory_space=pltpu.VMEM)] * len(operands),
        out_specs=[pl.BlockSpec(memory_space=pltpu.VMEM)] * 27,
        compiler_params=pltpu.CompilerParams(vmem_limit_bytes=32 << 20),
        name="finish_step",
    )(*operands)


def unfused_step(
    cube,
    inputs,
    cotangent,
    w_up,
    w_down,
    w_qkv,
    w_out,
    w_glu,
    w_point,
    small,
    bucket_table,
):
    bf16 = jnp.bfloat16
    rows = w_up.shape[0]
    rel_rows = NB // cube.total
    shard_groups = (
        jnp.concatenate([w_up[:, :FF], w_down[:, :FF], small], axis=1).astype(bf16),
        jnp.concatenate([w_qkv, w_out, w_glu, w_point], axis=1).astype(bf16),
        jnp.concatenate([w_up[:, FF:], w_down[:, FF:]], axis=1).astype(bf16),
    )
    first, middle, second = [
        full.reshape(D, -1) for full in gather_groups(cube, shard_groups, 0)
    ]
    up_first, down_first, small_low = first[:, :FF], first[:, FF : 2 * FF], first[:, 2 * FF :]
    qkv_w, out_w = middle[:, : 3 * D], middle[:, 3 * D : 4 * D]
    glu_w, point_w = middle[:, 4 * D : 6 * D], middle[:, 6 * D :]
    up_second, down_second = second[:, :FF], second[:, FF:]
    gains = small_low[:, SMALL_VEC : SMALL_VEC + 7].astype(jnp.float32)
    kernel = small_low[:, SMALL_DEPTH : SMALL_DEPTH + K].astype(jnp.float32)
    rel_low = small_low[:, :H].reshape(cube.total, rows, H)[:, :rel_rows].reshape(NB, H)
    bucket_hit = (bucket_table[:, None] == jnp.arange(NB, dtype=jnp.int32)[None, :]).astype(
        jnp.float32
    )
    offsets = jnp.dot(bucket_hit, rel_low.astype(jnp.float32), precision=HIGHEST).T
    seq_rows = inputs[0]
    row_count = seq_rows.shape[0]
    first_row = lax.axis_index("seq") * row_count
    token_total = row_count * lax.axis_size(("dp", "seq", "shard"))
    section_one, ffn_saved = ffn_forward(seq_rows, gains[:, 0], up_first, down_first)
    normed_out2, normed2, inverse2 = layer_norm(section_one, gains[:, 1])
    lifted2 = normed_out2.astype(bf16)
    projected = matmul(lifted2, qkv_w).astype(bf16)
    query = projected[:, :D]
    pair = [(0, 1), (1, 0)]
    other = lax.ppermute(projected[:, D:], "seq", pair)
    early = lax.axis_index("seq") == 0
    both = jnp.concatenate(
        [
            jnp.where(early, projected[:, D:], other),
            jnp.where(early, other, projected[:, D:]),
        ],
        axis=0,
    )
    keys, values = both[:, :D], both[:, D:]
    attended, log_total = attention_forward(query, keys, values, offsets, first_row)
    attended_low = attended.astype(bf16)
    section_two = section_one + matmul(attended_low, out_w)
    normed_out3, normed3, inverse3 = layer_norm(section_two, gains[:, 2])
    lifted3 = normed_out3.astype(bf16)
    gates = matmul(lifted3, glu_w)
    first_half = gates[:, :D]
    sig_gate = jax.nn.sigmoid(gates[:, D:])
    glu = first_half * sig_gate
    glu_wide = with_halo(glu, (("seq", 0),), K // 2)
    conv = depthwise(glu_wide, kernel, row_count)
    part_sum = jnp.sum(conv, axis=0)
    part_mean = part_sum / row_count
    part_square = jnp.sum(jnp.square(conv - part_mean), axis=0)
    stats = collect(cube, jnp.concatenate([part_sum, part_square]).reshape(8, 128), 1)
    stats = stats.reshape(cube.total, 2, D)
    mean = jnp.sum(stats[:, 0], axis=0) / token_total
    spread_of_means = jnp.square(stats[:, 0] / row_count - mean) * row_count
    variance = jnp.sum(stats[:, 1] + spread_of_means, axis=0) / token_total
    centred = conv - mean
    inv_std = lax.rsqrt(variance + EPS_BATCH)
    normed_bn = centred * inv_std
    batch_out = normed_bn * gains[:, 5] + gains[:, 6]
    swish_low = jax.nn.silu(batch_out).astype(bf16)
    section_three = section_two + matmul(swish_low, point_w)
    section_four, tail_saved = ffn_forward(
        section_three, gains[:, 3], up_second, down_second
    )
    outputs, normed5, inverse5 = layer_norm(section_four, gains[:, 4])
    grad_four, gain_four = norm_back(cotangent[0], normed5, inverse5, gains[:, 4])
    grad_three, grad_up_two, grad_down_two, gain_three = ffn_backward(
        grad_four, tail_saved, gains[:, 3], up_second, down_second
    )
    grad_three_low = grad_three.astype(bf16)
    grad_point = matmul_left_t(swish_low, grad_three_low)
    grad_batch = matmul_right_t(grad_three_low, point_w) * silu_slope(batch_out)
    grad_normed = grad_batch * gains[:, 5]
    sums = jnp.concatenate(
        [jnp.sum(grad_normed, axis=0), jnp.sum(grad_normed * normed_bn, axis=0)]
    )
    sums = jnp.sum(collect(cube, sums.reshape(8, 128), 2), axis=0).reshape(2, D)
    sum_normed, sum_cross = sums[0], sums[1]
    grad_conv = inv_std * (
        grad_normed - sum_normed / token_total - normed_bn * sum_cross / token_total
    )
    grad_wide = with_halo(grad_conv, (("seq", 0),), K // 2)
    grad_glu = grad_wide[K - 1 : K - 1 + row_count] * kernel[:, 0]
    for tap_idx in range(1, K):
        grad_glu = (
            grad_glu
            + grad_wide[K - 1 - tap_idx : K - 1 - tap_idx + row_count] * kernel[:, tap_idx]
        )
    grad_kernel = jnp.stack(
        [
            jnp.sum(grad_conv * glu_wide[tap_idx : tap_idx + row_count], axis=0)
            for tap_idx in range(K)
        ],
        axis=1,
    )
    grad_gates = jnp.concatenate(
        [grad_glu * sig_gate, grad_glu * first_half * sig_gate * (1.0 - sig_gate)], axis=1
    ).astype(bf16)
    grad_glu_w = matmul_left_t(lifted3, grad_gates)
    grad_two_part, gain_two = norm_back(
        matmul_right_t(grad_gates, glu_w), normed3, inverse3, gains[:, 2]
    )
    grad_two = grad_three + grad_two_part
    grad_two_low = grad_two.astype(bf16)
    grad_out_w = matmul_left_t(attended_low, grad_two_low)
    grad_attended = matmul_right_t(grad_two_low, out_w).astype(bf16)
    delta = jnp.sum(
        (grad_attended.astype(jnp.float32) * attended).reshape(row_count, H, DH), axis=2
    )
    query_grad, key_grad, value_grad, offset_grad = attention_backward(
        query, keys, values, offsets, first_row, log_total, grad_attended, delta
    )
    keys_grad = jnp.concatenate([key_grad, value_grad], axis=1)
    theirs = lax.dynamic_slice_in_dim(keys_grad, row_count - first_row, row_count, 0)
    own = lax.dynamic_slice_in_dim(keys_grad, first_row, row_count, 0)
    own = own + lax.ppermute(theirs, "seq", pair)
    key_own, value_own = own[:, :D], own[:, D:]
    grad_proj = jnp.concatenate([query_grad, key_own, value_own], axis=1).astype(bf16)
    grad_qkv_w = matmul_left_t(lifted2, grad_proj)
    grad_one_part, gain_one = norm_back(
        matmul_right_t(grad_proj, qkv_w), normed2, inverse2, gains[:, 1]
    )
    grad_one = grad_two + grad_one_part
    input_grad, grad_up_one, grad_down_one, gain_zero = ffn_backward(
        grad_one, ffn_saved, gains[:, 0], up_first, down_first
    )
    grad_vec_local = jnp.stack(
        [
            gain_zero,
            gain_one,
            gain_two,
            gain_three,
            gain_four,
            jnp.sum(grad_batch * normed_bn, axis=0),
            jnp.sum(grad_batch, axis=0),
        ],
        axis=1,
    )
    grad_rel_local = jnp.dot(bucket_hit.T, offset_grad.T, precision=HIGHEST)
    rel_padded = jnp.pad(
        grad_rel_local.reshape(cube.total, rel_rows, H), ((0, 0), (0, rows - rel_rows), (0, 0))
    )
    small_grads = jnp.concatenate(
        [rel_padded.reshape(D, H), grad_vec_local, grad_kernel], axis=1
    )
    small_grads = jnp.pad(small_grads, ((0, 0), (0, 128 - SMALL_END)))
    lead = (2,) * cube.digits
    grad_groups = [
        jnp.concatenate(group, axis=1).astype(bf16).reshape(lead + (rows, -1))
        for group in (
            (grad_up_two, grad_down_two),
            (grad_qkv_w, grad_out_w, grad_glu_w, grad_point),
            (grad_up_one, grad_down_one, small_grads),
        )
    ]
    share_second, share_middle, share_first = scatter_groups(cube, grad_groups, 3)
    return outputs, input_grad, share_first, share_middle, share_second


def local(
    cube,
    inputs,
    cotangent,
    w_up,
    w_down,
    w_qkv,
    w_out,
    w_glu,
    w_point,
    vectors,
    depth_kernel,
    rel_bias,
    bucket_table,
    m_up,
    m_down,
    m_qkv,
    m_out,
    m_glu,
    m_point,
    m_vectors,
    m_depth,
    m_rel,
):
    bf16 = jnp.bfloat16
    rows, rel_rows = w_up.shape[0], rel_bias.shape[0]
    pack = lambda rel, vec, depth: jnp.pad(
        jnp.concatenate([jnp.pad(rel, ((0, rows - rel_rows), (0, 0))), vec, depth], axis=1),
        ((0, 0), (0, 128 - SMALL_END)),
    )
    small = pack(rel_bias, vectors, depth_kernel)
    weights = (w_up, w_down, w_qkv, w_out, w_glu, w_point)
    if rows % 16 == 0 and cube.total % 32 == 0:
        bucket = jnp.pad(bucket_table, (0, 1), constant_values=-1)[None]
        momenta = (m_up, m_down, m_qkv, m_out, m_glu, m_point)
        momenta += (pack(m_rel, m_vectors, m_depth),)
        outputs, input_grad, *shares, returned, squares = fused_step(
            cube, inputs[0], cotangent[0], weights, momenta, small, bucket, rel_rows, 0
        )
        shapes = [v.shape for v in weights + (vectors, depth_kernel, rel_bias)]
        rest = finish_step(shares, returned, squares, weights, momenta, small, shapes, rel_rows)
        return (outputs[None], input_grad[None], *rest)
    outputs, input_grad, share_first, share_middle, share_second = unfused_step(
        cube, inputs, cotangent, *weights, small, bucket_table
    )
    grad_up = jnp.concatenate([share_first[:, :FF], share_second[:, :FF]], axis=1)
    grad_down = jnp.concatenate([share_first[:, FF : 2 * FF], share_second[:, FF:]], axis=1)
    grad_qkv, grad_out = share_middle[:, : 3 * D], share_middle[:, 3 * D : 4 * D]
    grad_glu, grad_pnt = share_middle[:, 4 * D : 6 * D], share_middle[:, 6 * D :]
    share_small = share_first[:, 2 * FF :]
    grad_vectors = share_small[:, SMALL_VEC : SMALL_VEC + 7]
    grad_depth = share_small[:, SMALL_DEPTH : SMALL_DEPTH + K]
    grad_rel = share_small[: rel_bias.shape[0], :H]
    next_m_up = MOMENTUM * m_up + grad_up
    next_m_down = MOMENTUM * m_down + grad_down
    next_m_qkv = MOMENTUM * m_qkv + grad_qkv
    next_m_out = MOMENTUM * m_out + grad_out
    next_m_glu = MOMENTUM * m_glu + grad_glu
    next_m_point = MOMENTUM * m_point + grad_pnt
    stacked = jnp.concatenate(
        [next_m_up, next_m_down, next_m_qkv, next_m_out, next_m_glu, next_m_point], axis=1
    )
    owned = spread(cube, stacked, 4).reshape(D, BLOCK)
    ortho = orthogonalize_blocks(cube, owned, bf16, 5)
    mine = restore(cube, ortho.reshape(cube.total, rows, BLOCK), 6).astype(jnp.float32)
    new_up = w_up - RATE_MATRIX * mine[:, : 2 * FF]
    new_down = w_down - RATE_MATRIX * mine[:, 2 * FF : 4 * FF]
    new_qkv = w_qkv - RATE_MATRIX * mine[:, STARTS[4] : STARTS[5]]
    new_out = w_out - RATE_MATRIX * mine[:, STARTS[5] : STARTS[6]]
    new_glu = w_glu - RATE_MATRIX * mine[:, STARTS[6] : STARTS[7]]
    new_point = w_point - RATE_MATRIX * mine[:, STARTS[7] :]
    next_m_vectors = MOMENTUM * m_vectors + grad_vectors
    next_m_depth = MOMENTUM * m_depth + grad_depth
    next_m_rel = MOMENTUM * m_rel + grad_rel
    squares = jnp.concatenate(
        [
            jnp.sum(next_m_vectors * next_m_vectors, axis=0),
            jnp.sum(next_m_depth * next_m_depth, axis=0),
            jnp.sum(next_m_rel * next_m_rel, axis=0),
        ]
    )
    squares = jnp.pad(squares, (0, 128 - squares.shape[0])).reshape(1, 128)
    squares = jnp.sum(collect(cube, jnp.pad(squares, ((0, 7), (0, 0))), 7), axis=0)[0]
    square_vec, square_depth = squares[:7], squares[7 : 7 + K]
    square_rel = squares[7 + K : 7 + K + H]
    new_vectors = vectors - RATE_VECTOR * next_m_vectors * lax.rsqrt(square_vec / D + EPS_SCALE)
    new_depth = depth_kernel - RATE_VECTOR * next_m_depth * lax.rsqrt(square_depth / D + EPS_SCALE)
    new_rel = rel_bias - RATE_VECTOR * next_m_rel * lax.rsqrt(square_rel / NB + EPS_SCALE)
    return (
        outputs[None],
        input_grad[None],
        grad_up,
        grad_down,
        grad_qkv,
        grad_out,
        grad_glu,
        grad_pnt,
        grad_vectors,
        grad_depth,
        grad_rel,
        new_up,
        new_down,
        new_qkv,
        new_out,
        new_glu,
        new_point,
        new_vectors,
        new_depth,
        new_rel,
        next_m_up,
        next_m_down,
        next_m_qkv,
        next_m_out,
        next_m_glu,
        next_m_point,
        next_m_vectors,
        next_m_depth,
        next_m_rel,
    )


def solution(mesh):
    placed = (
        P(("dp", "shard"), "seq", None),
        P(("dp", "shard"), "seq", None),
        P(("dp", "seq", "shard"), None),
        P(("dp", "seq", "shard"), None),
        P(("dp", "seq", "shard"), None),
        P(("dp", "seq", "shard"), None),
        P(("dp", "seq", "shard"), None),
        P(("dp", "seq", "shard"), None),
        P(("dp", "seq", "shard"), None),
        P(("dp", "seq", "shard"), None),
        P(("dp", "seq", "shard"), None),
        P(),
        P(("dp", "seq", "shard"), None),
        P(("dp", "seq", "shard"), None),
        P(("dp", "seq", "shard"), None),
        P(("dp", "seq", "shard"), None),
        P(("dp", "seq", "shard"), None),
        P(("dp", "seq", "shard"), None),
        P(("dp", "seq", "shard"), None),
        P(("dp", "seq", "shard"), None),
        P(("dp", "seq", "shard"), None),
    )
    return jax.shard_map(
        functools.partial(local, Cube(mesh.shape["dp"])),
        mesh=mesh,
        in_specs=placed,
        out_specs=(
            P(("dp", "shard"), "seq", None),
            P(("dp", "shard"), "seq", None),
            P(("dp", "seq", "shard"), None),
            P(("dp", "seq", "shard"), None),
            P(("dp", "seq", "shard"), None),
            P(("dp", "seq", "shard"), None),
            P(("dp", "seq", "shard"), None),
            P(("dp", "seq", "shard"), None),
            P(("dp", "seq", "shard"), None),
            P(("dp", "seq", "shard"), None),
            P(("dp", "seq", "shard"), None),
            P(("dp", "seq", "shard"), None),
            P(("dp", "seq", "shard"), None),
            P(("dp", "seq", "shard"), None),
            P(("dp", "seq", "shard"), None),
            P(("dp", "seq", "shard"), None),
            P(("dp", "seq", "shard"), None),
            P(("dp", "seq", "shard"), None),
            P(("dp", "seq", "shard"), None),
            P(("dp", "seq", "shard"), None),
            P(("dp", "seq", "shard"), None),
            P(("dp", "seq", "shard"), None),
            P(("dp", "seq", "shard"), None),
            P(("dp", "seq", "shard"), None),
            P(("dp", "seq", "shard"), None),
            P(("dp", "seq", "shard"), None),
            P(("dp", "seq", "shard"), None),
            P(("dp", "seq", "shard"), None),
            P(("dp", "seq", "shard"), None),
        ),
        check_vma=False,
    )
```

```python
import functools
import types

import jax
import jax.numpy as jnp
from jax import lax
from jax.experimental import pallas as pl
from jax.experimental.pallas import tpu as pltpu
from jax.sharding import PartitionSpec as P

D = 512
FF = 2048
H = 8
DH = 64
K = 31
NB = 128


EPS_NORM = 1e-05
EPS_BATCH = 1e-05
EPS_SCALE = 1e-06
MOMENTUM = 0.9
RATE_MATRIX = 1.0
RATE_VECTOR = 0.25
COEF_A = 3.4445
COEF_B = -4.775
COEF_C = 2.0315
HIGHEST = lax.Precision.HIGHEST


AXES = ("dp", "seq", "shard")
MESH = pl.DeviceIdType.MESH
WIDTHS = (FF, FF, FF, FF, 3 * D, D, 2 * D, D)
STARTS = tuple(sum(WIDTHS[:i]) for i in range(9))
BLOCK = 512


class Cube:
    def __init__(self, dp_size):
        self.dp_size = dp_size
        self.levels = dp_size.bit_length() - 1
        self.digits = self.levels + 2
        self.total = dp_size * 4
        high = list(range(self.levels - 1))
        low, seq, core = self.levels - 1, self.levels, self.levels + 1
        self.gather_orders = (high + [low, seq, core], high + [seq, low, core])
        self.gather_late_orders = ([seq, low] + high + [core], [low, seq] + high + [core])
        self.scatter_orders = tuple(order[::-1] for order in self.gather_orders)

    def mine(self):
        d = lax.axis_index("dp")
        bits = [lax.rem(d // (1 << (self.levels - 1 - k)), 2) for k in range(self.levels)]
        return bits + [lax.axis_index("seq"), lax.axis_index("shard")]

    def partner(self, k):
        d, s, c = lax.axis_index("dp"), lax.axis_index("seq"), lax.axis_index("shard")
        if k == self.levels:
            return (d, 1 - s, c)
        if k == self.levels + 1:
            return (d, s, 1 - c)
        step = 1 << (self.levels - 1 - k)
        bit = lax.rem(d // step, 2)
        return (d + (1 - 2 * bit) * step, s, c)

    def index(self):
        return (lax.axis_index("dp") * 2 + lax.axis_index("seq")) * 2 + lax.axis_index("shard")

    def coords(self, index):
        return (index // 4, lax.rem(index // 2, 2), lax.rem(index, 2))

    def greet_partners(self):
        barrier = pltpu.get_barrier_semaphore()
        for k in range(self.digits):
            pl.semaphore_signal(barrier, inc=1, device_id=self.partner(k), device_id_type=MESH)
        pl.semaphore_wait(barrier, self.digits)

    def greet_all(self):
        barrier = pltpu.get_barrier_semaphore()
        me = self.index()

        @pl.loop(1, self.total)
        def _(i):
            peer = self.coords(lax.rem(me + i, self.total))
            pl.semaphore_signal(barrier, inc=1, device_id=peer, device_id_type=MESH)

        pl.semaphore_wait(barrier, self.total - 1)


def halves(width):
    cut = (width // 128 + 1) // 2 * 128
    return ((0, cut), (cut, width - cut))


def remote(src, dst, send_sem, recv_sem, peer):
    return pltpu.make_async_remote_copy(
        src_ref=src,
        dst_ref=dst,
        send_sem=send_sem,
        recv_sem=recv_sem,
        device_id=peer,
        device_id_type=MESH,
    )


def gather_kernel(cube, groups, *refs):
    shards, outs = refs[:groups], refs[groups : 2 * groups]
    own_sem, send_sem, recv_sem = refs[2 * groups :]
    cube.greet_partners()
    mine = cube.mine()
    locals_ = []
    for g in range(groups):
        copy = pltpu.make_async_copy(shards[g], outs[g].at[tuple(mine)], own_sem.at[g])
        copy.start()
        locals_.append(copy)

    def make(g, half, stage):
        order = cube.gather_orders[half]
        columns = pl.ds(*halves(shards[g].shape[-1])[half])
        done = order[:stage]
        index = tuple(slice(None) if k in done else mine[k] for k in range(cube.digits))
        place = outs[g].at[index + (slice(None), columns)]
        source = shards[g].at[:, columns] if stage == 0 else place
        return remote(
            source,
            place,
            send_sem.at[g, half, stage],
            recv_sem.at[g, half, stage],
            cube.partner(order[stage]),
        )

    copies = {}
    for g in range(groups):
        for half in range(2):
            copies[g, half, 0] = make(g, half, 0)
            copies[g, half, 0].start()
    for tick in range(cube.digits + 2 * (groups - 1)):
        for g in range(groups):
            stage = tick - 2 * g
            if not 0 <= stage < cube.digits:
                continue
            for half in range(2):
                copies[g, half, stage].wait_recv()
                if stage == 0 and half == 0:
                    locals_[g].wait()
                if stage + 1 < cube.digits:
                    copies[g, half, stage + 1] = make(g, half, stage + 1)
                    copies[g, half, stage + 1].start()
    for copy in copies.values():
        copy.wait_send()


def gather_groups(cube, shards, collective_id):
    groups = len(shards)
    lead = (2,) * cube.digits
    return pl.pallas_call(
        functools.partial(gather_kernel, cube, groups),
        out_shape=[jax.ShapeDtypeStruct(lead + s.shape, s.dtype) for s in shards],
        in_specs=[pl.BlockSpec(memory_space=pl.ANY)] * groups,
        out_specs=[pl.BlockSpec(memory_space=pl.ANY)] * groups,
        scratch_shapes=[
            pltpu.SemaphoreType.DMA((groups,)),
            pltpu.SemaphoreType.DMA((groups, 2, cube.digits)),
            pltpu.SemaphoreType.DMA((groups, 2, cube.digits)),
        ],
        compiler_params=pltpu.CompilerParams(
            collective_id=collective_id, has_side_effects=True
        ),
        name="gather_weights",
    )(*shards)


def scatter_kernel(cube, groups, *refs):
    parts, outs = refs[:groups], refs[groups : 2 * groups]
    rest = refs[2 * groups :]
    sums = rest[:groups]
    landed = rest[groups : groups + groups * 2 * cube.digits]
    own_sem, send_sem, recv_sem = rest[groups + groups * 2 * cube.digits :]
    cube.greet_partners()
    mine = cube.mine()
    last = cube.digits - 1

    def slot(g, half, stage):
        return landed[(g * 2 + half) * cube.digits + stage]

    def place(g, half, stage, bit_of):
        order = cube.scatter_orders[half]
        columns = pl.ds(*halves(outs[g].shape[-1])[half])
        index = []
        for k in range(cube.digits - 1):
            at = order.index(k)
            if at > stage:
                index.append(slice(None))
            else:
                index.append(bit_of(k) if at == stage else mine[k])
        return tuple(index) + (slice(None), columns)

    def make(g, half, stage):
        order = cube.scatter_orders[half]
        if stage == 0:
            index = (slice(None),) * last + (1 - mine[last],)
            columns = pl.ds(*halves(outs[g].shape[-1])[half])
            source = parts[g].at[index + (slice(None), columns)]
        else:
            source = sums[g].at[place(g, half, stage, lambda k: 1 - mine[k])]
        return remote(
            source,
            slot(g, half, stage),
            send_sem.at[g, half, stage],
            recv_sem.at[g, half, stage],
            cube.partner(order[stage]),
        )

    copies = {}
    locals_ = []
    for g in range(groups):
        copy = pltpu.make_async_copy(
            parts[g].at[(slice(None),) * last + (mine[last],)], sums[g], own_sem.at[g]
        )
        copy.start()
        locals_.append(copy)
        for half in range(2):
            copies[g, half, 0] = make(g, half, 0)
            copies[g, half, 0].start()

    def add(g, half, stage):
        order = cube.scatter_orders[half]
        columns = pl.ds(*halves(outs[g].shape[-1])[half])
        free = [k for k in range(last) if order.index(k) > stage]
        count = 1 << len(free)
        target, extra = sums[g], slot(g, half, stage)

        def one(i):
            digit = {k: lax.rem(i // (1 << (len(free) - 1 - n)), 2) for n, k in enumerate(free)}
            full = tuple(digit.get(k, mine[k]) for k in range(last)) + (slice(None), columns)
            short = tuple(digit[k] for k in free)
            total = target[full].astype(jnp.float32) + extra[short + (slice(None), slice(None))].astype(jnp.float32)
            if stage == last:
                outs[g][:, columns] = total
            else:
                target[full] = total.astype(target.dtype)

        if count == 1:
            one(0)
        else:
            pl.loop(0, count)(one)

    for stage in range(cube.digits):
        for g in range(groups):
            if stage == 0:
                locals_[g].wait()
            for half in range(2):
                copies[g, half, stage].wait_recv()
                add(g, half, stage)
                if stage < last:
                    copies[g, half, stage + 1] = make(g, half, stage + 1)
                    copies[g, half, stage + 1].start()
    for copy in copies.values():
        copy.wait_send()


def scatter_groups(cube, parts, collective_id):
    groups = len(parts)
    scratch = [pltpu.VMEM((2,) * (cube.digits - 1) + p.shape[-2:], p.dtype) for p in parts]
    for p in parts:
        for half in range(2):
            for stage in range(cube.digits):
                lead = (2,) * (cube.digits - 1 - stage)
                scratch.append(pltpu.VMEM(lead + (p.shape[-2], halves(p.shape[-1])[half][1]), p.dtype))
    scratch += [
        pltpu.SemaphoreType.DMA((groups,)),
        pltpu.SemaphoreType.DMA((groups, 2, cube.digits)),
        pltpu.SemaphoreType.DMA((groups, 2, cube.digits)),
    ]
    return pl.pallas_call(
        functools.partial(scatter_kernel, cube, groups),
        out_shape=[jax.ShapeDtypeStruct(p.shape[-2:], jnp.float32) for p in parts],
        in_specs=[pl.BlockSpec(memory_space=pl.ANY)] * groups,
        out_specs=[pl.BlockSpec(memory_space=pltpu.VMEM)] * groups,
        scratch_shapes=scratch,
        compiler_params=pltpu.CompilerParams(
            collective_id=collective_id, has_side_effects=True, vmem_limit_bytes=48 << 20
        ),
        name="scatter_grads",
    )(*parts)


def collect_kernel(cube, x_ref, o_ref, send_sem, recv_sem):
    me = cube.index()
    cube.greet_all()

    def make(i):
        to = lax.rem(me + i, cube.total)
        return remote(x_ref, o_ref.at[i], send_sem.at[i], recv_sem.at[i], cube.coords(to))

    @pl.loop(1, cube.total)
    def _(i):
        make(i).start()

    o_ref[0] = x_ref[...]

    @pl.loop(1, cube.total)
    def _(i):
        make(i).wait()


def collect(cube, x, collective_id):
    return pl.pallas_call(
        functools.partial(collect_kernel, cube),
        out_shape=jax.ShapeDtypeStruct((cube.total,) + x.shape, x.dtype),
        in_specs=[pl.BlockSpec(memory_space=pltpu.VMEM)],
        out_specs=pl.BlockSpec(memory_space=pltpu.VMEM),
        scratch_shapes=[
            pltpu.SemaphoreType.DMA((cube.total,)),
            pltpu.SemaphoreType.DMA((cube.total,)),
        ],
        compiler_params=pltpu.CompilerParams(
            collective_id=collective_id, has_side_effects=True
        ),
        name="collect_stats",
    )(x)


def by_matrix(j, action):
    for width in sorted(set(WIDTHS)):
        members = [i for i in range(8) if WIDTHS[i] == width]
        hit = functools.reduce(jnp.logical_or, [j == i for i in members])
        pl.when(hit)(functools.partial(action, width // 4))


def quarter_start(t):
    j, q = t // 4, lax.rem(t, 4)
    start = 0
    for i in range(8):
        start = start + jnp.where(j == i, STARTS[i] + q * (WIDTHS[i] // 4), 0)
    return pl.multiple_of(start, 128)


def owner_coords(cube, t):
    return ((t // 4) * (cube.dp_size // 8), lax.rem(t // 2, 2), lax.rem(t, 2))


def spread_kernel(cube, x_ref, o_ref, own_sem, send_sem, recv_sem):
    me = cube.index()
    repeat = cube.dp_size // 8
    d, s, c = lax.axis_index("dp"), lax.axis_index("seq"), lax.axis_index("shard")
    owner = lax.rem(d, repeat) == 0
    mine = ((d // repeat) * 2 + s) * 2 + c
    cube.greet_all()

    def send(i, wait):
        t = lax.rem(mine + i, 32)
        peer = owner_coords(cube, t)
        other = jnp.logical_or(jnp.logical_not(owner), i > 0)

        def go(width):
            src = x_ref.at[:, pl.ds(quarter_start(t), width)]
            dst = o_ref.at[me, :, pl.ds(0, width)]
            copy = remote(src, dst, send_sem.at[i], recv_sem.at[me], peer)
            if wait:
                copy.wait_send()
            else:
                copy.start()

        pl.when(other)(lambda: by_matrix(t // 4, go))

    pl.loop(0, 32)(functools.partial(send, wait=False))

    def keep(width):
        copy = pltpu.make_async_copy(
            x_ref.at[:, pl.ds(quarter_start(mine), width)],
            o_ref.at[me, :, pl.ds(0, width)],
            own_sem,
        )
        copy.start()
        copy.wait()

    def receive(width):
        @pl.loop(1, cube.total)
        def _(i):
            source = lax.rem(me + i, cube.total)
            place = o_ref.at[source, :, pl.ds(0, width)]
            remote(
                place, place, send_sem.at[0], recv_sem.at[source], cube.coords(source)
            ).wait_recv()

    @pl.when(owner)
    def _():
        by_matrix(mine // 4, keep)
        by_matrix(mine // 4, receive)

    pl.loop(0, 32)(functools.partial(send, wait=True))


def spread(cube, x, collective_id):
    return pl.pallas_call(
        functools.partial(spread_kernel, cube),
        out_shape=jax.ShapeDtypeStruct((cube.total, x.shape[0], BLOCK), x.dtype),
        in_specs=[pl.BlockSpec(memory_space=pl.ANY)],
        out_specs=pl.BlockSpec(memory_space=pl.ANY),
        scratch_shapes=[
            pltpu.SemaphoreType.DMA,
            pltpu.SemaphoreType.DMA((32,)),
            pltpu.SemaphoreType.DMA((cube.total,)),
        ],
        compiler_params=pltpu.CompilerParams(
            collective_id=collective_id, has_side_effects=True
        ),
        name="spread_momentum",
    )(x)


def restore_kernel(cube, x_ref, o_ref, own_sem, send_sem, recv_sem):
    me = cube.index()
    repeat = cube.dp_size // 8
    d, s, c = lax.axis_index("dp"), lax.axis_index("seq"), lax.axis_index("shard")
    owner = lax.rem(d, repeat) == 0
    mine = ((d // repeat) * 2 + s) * 2 + c
    cube.greet_all()

    def send_all(wait, width):
        @pl.loop(1, cube.total)
        def _(i):
            to = lax.rem(me + i, cube.total)
            src = x_ref.at[to, :, pl.ds(0, width)]
            dst = o_ref.at[:, pl.ds(quarter_start(mine), width)]
            copy = remote(src, dst, send_sem.at[i], recv_sem.at[mine], cube.coords(to))
            if wait:
                copy.wait_send()
            else:
                copy.start()

    def keep(width):
        copy = pltpu.make_async_copy(
            x_ref.at[me, :, pl.ds(0, width)],
            o_ref.at[:, pl.ds(quarter_start(mine), width)],
            own_sem,
        )
        copy.start()
        copy.wait()

    @pl.when(owner)
    def _():
        by_matrix(mine // 4, functools.partial(send_all, False))
        by_matrix(mine // 4, keep)

    def receive(i):
        t = lax.rem(mine + i, 32)
        other = jnp.logical_or(jnp.logical_not(owner), i > 0)

        def go(width):
            place = o_ref.at[:, pl.ds(quarter_start(t), width)]
            remote(
                place, place, send_sem.at[0], recv_sem.at[t], owner_coords(cube, t)
            ).wait_recv()

        pl.when(other)(lambda: by_matrix(t // 4, go))

    pl.loop(0, 32)(receive)

    @pl.when(owner)
    def _():
        by_matrix(mine // 4, functools.partial(send_all, True))


def restore(cube, x, collective_id):
    return pl.pallas_call(
        functools.partial(restore_kernel, cube),
        out_shape=jax.ShapeDtypeStruct((x.shape[1], STARTS[8]), x.dtype),
        in_specs=[pl.BlockSpec(memory_space=pl.ANY)],
        out_specs=pl.BlockSpec(memory_space=pl.ANY),
        scratch_shapes=[
            pltpu.SemaphoreType.DMA,
            pltpu.SemaphoreType.DMA((cube.total,)),
            pltpu.SemaphoreType.DMA((32,)),
        ],
        compiler_params=pltpu.CompilerParams(
            collective_id=collective_id, has_side_effects=True
        ),
        name="restore_rows",
    )(x)


def split(value):
    high = value.astype(jnp.bfloat16)
    low = (value - high.astype(jnp.float32)).astype(jnp.bfloat16)
    return high, low


def product(left, right):
    (lh, ll), (rh, rl) = left, right
    dot = functools.partial(jnp.dot, preferred_element_type=jnp.float32)
    return dot(lh, rh) + (dot(lh, rl) + dot(ll, rh))


def orthogonalize_kernel(cube, x_ref, o_ref, gram_ref, work, landed, send_sem, recv_sem):
    barrier = pltpu.get_barrier_semaphore()
    peers = (cube.partner(cube.levels + 1), cube.partner(cube.levels))
    for peer in peers:
        pl.semaphore_signal(barrier, inc=1, device_id=peer, device_id_type=MESH)
    pl.semaphore_wait(barrier, 2)
    repeat = cube.dp_size // 8
    j = lax.axis_index("dp") // repeat
    width = 0
    for i in range(8):
        width = width + jnp.where(j == i, WIDTHS[i] // 4, 0)
    column = lax.broadcasted_iota(jnp.int32, (D, BLOCK), 1)
    block = jnp.where(column < width, x_ref[...].astype(jnp.float32), 0.0)
    bh, bl = split(block)
    dot_t = lambda a, b: lax.dot_general(
        a, b, (((1,), (1,)), ((), ())), preferred_element_type=jnp.float32
    )
    gram_ref[0] = dot_t(bh, bh) + (dot_t(bh, bl) + dot_t(bl, bh))
    for step in range(2):
        copy = remote(
            gram_ref.at[step], landed.at[step], send_sem.at[step], recv_sem.at[step], peers[step]
        )
        copy.start()
        copy.wait()
        gram_ref[step + 1] = gram_ref[step] + landed[step]
    gram = gram_ref[2]
    row = lax.broadcasted_iota(jnp.int32, (D, D), 0)
    col = lax.broadcasted_iota(jnp.int32, (D, D), 1)
    eye = row == col
    square = jnp.sum(jnp.sum(jnp.where(eye, gram, 0.0), axis=1, keepdims=True), axis=0, keepdims=True)
    scale = 1.0 / (jnp.sqrt(square) + 1e-07)
    gram = gram * (scale * scale)
    block = block * scale
    for step in range(5):
        parts = split(gram)
        mixed = COEF_B * gram + COEF_C * product(parts, parts)
        mixed = jnp.where(eye, mixed + COEF_A, mixed)
        mixed_parts = split(mixed)
        block = product(mixed_parts, split(block))
        if step < 4:
            gram = product(mixed_parts, split(product(mixed_parts, parts)))
    o_ref[...] = block.astype(o_ref.dtype)


def orthogonalize_blocks(cube, x, out_dtype, collective_id):
    return pl.pallas_call(
        functools.partial(orthogonalize_kernel, cube),
        out_shape=jax.ShapeDtypeStruct((D, BLOCK), out_dtype),
        in_specs=[pl.BlockSpec(memory_space=pltpu.VMEM)],
        out_specs=pl.BlockSpec(memory_space=pltpu.VMEM),
        scratch_shapes=[
            pltpu.VMEM((3, D, D), jnp.float32),
            pltpu.VMEM((8, 128), jnp.float32),
            pltpu.VMEM((2, D, D), jnp.float32),
            pltpu.SemaphoreType.DMA((2,)),
            pltpu.SemaphoreType.DMA((2,)),
        ],
        compiler_params=pltpu.CompilerParams(
            collective_id=collective_id, has_side_effects=True, vmem_limit_bytes=48 << 20
        ),
        name="orthogonalize",
    )(x)

def with_halo(value, sides, width):
    for axis, dim in sides:
        devices, length = (lax.axis_size(axis), value.shape[dim])
        up = [(i, (i + 1) % devices) for i in range(devices - 1)]
        down = [(j, i) for i, j in up]
        last = lax.slice_in_dim(value, length - width, length, axis=dim)
        first = lax.slice_in_dim(value, 0, width, axis=dim)
        before = lax.ppermute(last, axis, up)
        after = lax.ppermute(first, axis, down)
        value = jnp.concatenate([before, value, after], axis=dim)
    return value


def matmul(left, right):
    return jnp.dot(left, right, preferred_element_type=jnp.float32)


def matmul_right_t(left, right):
    return lax.dot_general(
        left, right, (((1,), (1,)), ((), ())), preferred_element_type=jnp.float32
    )


def matmul_left_t(left, right):
    return lax.dot_general(
        left, right, (((0,), (0,)), ((), ())), preferred_element_type=jnp.float32
    )


def layer_norm(field, gain):
    centre = jnp.mean(field, axis=-1, keepdims=True)
    shifted = field - centre
    inverse = lax.rsqrt(jnp.mean(shifted * shifted, axis=-1, keepdims=True) + EPS_NORM)
    normed = shifted * inverse
    return (normed * gain, normed, inverse)


def norm_back(grad_out, normed, inverse, gain):
    scaled = grad_out * gain
    grad_in = inverse * (
        scaled
        - jnp.mean(scaled, axis=-1, keepdims=True)
        - normed * jnp.mean(scaled * normed, axis=-1, keepdims=True)
    )
    return (grad_in, jnp.sum(grad_out * normed, axis=0))


def silu_slope(values):
    sigma = jax.nn.sigmoid(values)
    return sigma * (1.0 + values * (1.0 - sigma))


def ffn_forward(field, gain, w_in, w_back):
    normed_out, normed, inverse = layer_norm(field, gain)
    lifted = normed_out.astype(jnp.bfloat16)
    hidden_pre = matmul(lifted, w_in)
    hidden_act = jax.nn.silu(hidden_pre).astype(jnp.bfloat16)
    return (
        field + 0.5 * matmul_right_t(hidden_act, w_back),
        (lifted, hidden_pre, hidden_act, normed, inverse),
    )


def ffn_backward(grad, saved, gain, w_in, w_back):
    lifted, hidden_pre, hidden_act, normed, inverse = saved
    grad_branch = (0.5 * grad).astype(jnp.bfloat16)
    grad_back = matmul_left_t(grad_branch, hidden_act)
    grad_act = matmul(grad_branch, w_back)
    grad_pre = (grad_act * silu_slope(hidden_pre)).astype(jnp.bfloat16)
    grad_in = matmul_left_t(lifted, grad_pre)
    grad_field, grad_gain = norm_back(matmul_right_t(grad_pre, w_in), normed, inverse, gain)
    return (grad + grad_field, grad_in, grad_back, grad_gain)


def depthwise(wide, kernel, count):
    total = wide[0:count] * kernel[:, 0]
    for tap_idx in range(1, K):
        total = total + wide[tap_idx : tap_idx + count] * kernel[:, tap_idx]
    return total


def spread_rows(window, count, keys_len):
    padded = jnp.concatenate([window, jnp.zeros((1,), window.dtype)])
    tiled = jnp.broadcast_to(padded[None, :], (count, keys_len + count)).reshape(-1)
    shaped = tiled[: count * (keys_len + count - 1)].reshape(count, keys_len + count - 1)
    return shaped[:, count - 1 : count - 1 + keys_len]


def collect_rows(grid, count, keys_len):
    placed = jnp.concatenate([jnp.zeros((count, count - 1), grid.dtype), grid], axis=1).reshape(-1)
    placed = jnp.concatenate([placed, jnp.zeros((count,), grid.dtype)])
    return jnp.sum(placed.reshape(count, keys_len + count), axis=0)[: keys_len + count - 1]


def attention_scores(query, keys, offsets, first_row, row_start, block, head_idx):
    length = keys.shape[0]
    columns = slice(head_idx * DH, (head_idx + 1) * DH)
    anchor = length - block - first_row - row_start
    window = lax.dynamic_slice_in_dim(offsets[head_idx], anchor, length + block - 1)
    product = matmul_right_t(query[row_start : row_start + block, columns], keys[:, columns])
    return product * DH ** (-0.5) + spread_rows(window, block, length)


def attention_forward(query, keys, values, offsets, first_row):
    total_rows = query.shape[0]
    block = min(512, total_rows)
    head_outs = []
    head_lse = []
    for head_idx in range(H):
        scores = attention_scores(query, keys, offsets, first_row, 0, block, head_idx)
        row_max = jnp.max(scores, axis=1, keepdims=True)
        shifted_exp = jnp.exp(scores - row_max)
        row_total = jnp.sum(shifted_exp, axis=1, keepdims=True)
        prob_low = (shifted_exp / row_total).astype(jnp.bfloat16)
        head_outs.append(matmul(prob_low, values[:, head_idx * DH : (head_idx + 1) * DH]))
        head_lse.append((row_max + jnp.log(row_total))[:, 0])
    out_blocks = jnp.concatenate(head_outs, axis=1)
    lse_blocks = jnp.stack(head_lse, axis=0)
    return (out_blocks, lse_blocks)


def attention_backward(query, keys, values, offsets, first_row, log_total, grad_attended, delta):
    total_rows = query.shape[0]
    length = keys.shape[0]
    block = min(512, total_rows)
    scale = DH ** (-0.5)
    key_parts = [jnp.zeros((length, DH), jnp.float32) for head_idx in range(H)]
    value_parts = [jnp.zeros((length, DH), jnp.float32) for head_idx in range(H)]
    offset_rows = [jnp.zeros((2 * length - 1,), jnp.float32) for head_idx in range(H)]
    head_grads = []
    for head_idx in range(H):
        columns = slice(head_idx * DH, (head_idx + 1) * DH)
        scores = attention_scores(query, keys, offsets, first_row, 0, block, head_idx)
        prob = jnp.exp(scores - log_total[head_idx, 0:block][:, None])
        prob_low = prob.astype(jnp.bfloat16)
        grad_piece = grad_attended[0:block, columns]
        value_parts[head_idx] = matmul_left_t(prob_low, grad_piece)
        grad_prob = matmul_right_t(grad_piece, values[:, columns])
        grad_score = prob * (grad_prob - delta[0:block, head_idx][:, None])
        score_low = grad_score.astype(jnp.bfloat16)
        head_grads.append(matmul(score_low, keys[:, columns]) * scale)
        key_parts[head_idx] = matmul_left_t(score_low, query[0:block, columns]) * scale
        anchor = length - block - first_row - 0
        offset_rows[head_idx] = lax.dynamic_update_slice_in_dim(
            offset_rows[head_idx], collect_rows(grad_score, block, length), anchor, 0
        )
    query_blocks = jnp.concatenate(head_grads, axis=1)
    return (
        query_blocks,
        jnp.concatenate(key_parts, axis=1),
        jnp.concatenate(value_parts, axis=1),
        jnp.stack(offset_rows, axis=0),
    )


def mean_last(value):
    return jnp.mean(value, axis=-1, keepdims=True)


def normalize(field):
    shifted = field - mean_last(field)
    inverse = lax.rsqrt(mean_last(shifted * shifted) + EPS_NORM)
    return shifted * inverse, inverse


def norm_grad(grad_out, normed, inverse, gain):
    scaled = grad_out * gain
    grad_in = inverse * (scaled - mean_last(scaled) - normed * mean_last(scaled * normed))
    return grad_in, jnp.sum(grad_out * normed, axis=0, keepdims=True)


def row_to_tile(ref, base, row):
    for k in range(4):
        ref[base + k : base + k + 1, :] = row[:, 128 * k : 128 * (k + 1)]


def tile_to_row(tile):
    return jnp.concatenate([tile[k : k + 1, :] for k in range(4)], axis=1)


def skew(row, count):
    sub = lax.broadcasted_iota(jnp.int32, (8, 512), 0)
    block = jnp.broadcast_to(row, (8, 512))
    for bit in (1, 2, 4):
        block = jnp.where((sub // bit) % 2 == 1, pltpu.roll(block, bit, 1), block)
    size = 8
    while size < count:
        block = jnp.concatenate([block, pltpu.roll(block, size, 1)], axis=0)
        size *= 2
    return block


def unskew_sum(grid):
    size = grid.shape[0] // 2
    while size >= 8:
        grid = grid[:size] + pltpu.roll(grid[size:], 512 - size, 1)
        size //= 2
    sub = lax.broadcasted_iota(jnp.int32, (8, 512), 0)
    for bit in (1, 2, 4):
        grid = jnp.where((sub // bit) % 2 == 1, pltpu.roll(grid, 512 - bit, 1), grid)
    return jnp.sum(grid, axis=0, keepdims=True)


def tile_ranges(start, count, parts):
    ranges = []
    for n in range(parts, 0, -1):
        size = -(-count // n)
        ranges.append((128 * start, 128 * size))
        start, count = start + size, count - size
    return ranges


def gather_chunks(widths):
    chunks = []
    for g in range(2):
        ranges = tile_ranges(0, widths[g] // 128, 4)
        chunks += [(g, ranges[0:2], 0), (g, ranges[2:4], 0)]
    tiles = widths[2] // 128
    cut = tiles * 2 // 5
    chunks.append((2, tile_ranges(0, cut, 2), 0))
    ranges = tile_ranges(cut, tiles - cut, 6)
    return chunks + [(2, ranges[2 * n : 2 * n + 2], 1) for n in range(3)]


class Gather:
    def __init__(self, cube, mine, bands, send_sem, recv_sem):
        self.cube, self.mine, self.bands = cube, mine, bands
        self.chunks = gather_chunks([band.shape[-1] for band in bands])
        self.send_sem, self.recv_sem = send_sem, recv_sem
        self.copies = {}
        self.events = list(GATHER_EVENTS)
        self.last = cube.digits - 1

    def start(self, n, stage):
        g, pair, kind = self.chunks[n]
        for half in range(2):
            order = (self.cube.gather_orders, self.cube.gather_late_orders)[kind][half]
            done = order[:stage]
            index = tuple(
                slice(None) if k in done else self.mine[k] for k in range(self.cube.digits)
            )
            place = self.bands[g].at[index + (slice(None), pl.ds(*pair[half]))]
            copy = remote(
                place,
                place,
                self.send_sem.at[n, half, stage],
                self.recv_sem.at[n, half, stage],
                self.cube.partner(order[stage]),
            )
            copy.start()
            self.copies[n, half, stage] = copy

    def begin(self):
        self.start(0, 0)
        self.start(5, 0)

    def advance(self, n, stage):
        for half in range(2):
            self.copies[n, half, stage].wait_recv()
        if stage < self.last and (n, stage + 1) not in GATHER_HELD:
            self.start(n, stage + 1)
        for other in GATHER_AFTER.get((n, stage), ()):
            self.start(*other)

    def run_to(self, n, stage):
        while (n, stage) in self.events:
            self.advance(*self.events.pop(0))

    def finish(self):
        for copy in self.copies.values():
            copy.wait_send()


class Scatter:
    def __init__(self, cube, mine, bands, landed, outs, send_sem, recv_sem):
        self.cube, self.mine, self.landed = cube, mine, landed
        self.chunks = [(bands[g], outs[g], pair) for g, pair in SCATTER_CHUNKS]
        self.send_sem, self.recv_sem = send_sem, recv_sem
        self.copies = {}

    def start(self, n, stage):
        band, _, pair = self.chunks[n]
        for half in range(2):
            order = self.cube.scatter_orders[half]
            index = []
            for k in range(self.cube.digits):
                at = order.index(k)
                if at > stage:
                    index.append(slice(None))
                else:
                    index.append(1 - self.mine[k] if at == stage else self.mine[k])
            copy = remote(
                band.at[tuple(index) + (slice(None), pl.ds(*pair[half]))],
                self.landed[(n * 2 + half) * self.cube.digits + stage],
                self.send_sem.at[n, half, stage],
                self.recv_sem.at[n, half, stage],
                self.cube.partner(order[stage]),
            )
            copy.start()
            self.copies[n, half, stage] = copy

    def add(self, n, half, stage):
        order = self.cube.scatter_orders[half]
        band, out, pair = self.chunks[n]
        columns = pl.ds(*pair[half])
        free = [k for k in range(self.cube.digits) if order.index(k) > stage]
        extra = self.landed[(n * 2 + half) * self.cube.digits + stage]
        everything = (slice(None), columns)

        def one(i):
            digit = {
                k: lax.rem(i // (1 << (len(free) - 1 - m)), 2) for m, k in enumerate(free)
            }
            full = tuple(digit.get(k, self.mine[k]) for k in range(self.cube.digits)) + everything
            short = tuple(digit[k] for k in free) + (slice(None), slice(None))
            total = band[full].astype(jnp.float32) + extra[short].astype(jnp.float32)
            if free:
                band[full] = total.astype(band.dtype)
            else:
                out[:, columns] = total

        if free:
            pl.loop(0, 1 << len(free))(one)
        else:
            one(0)

    def advance(self, n, stage):
        for half in range(2):
            self.copies[n, half, stage].wait_recv()
            self.add(n, half, stage)
        if stage + 1 < self.cube.digits:
            self.start(n, stage + 1)

    def finish(self):
        for copy in self.copies.values():
            copy.wait_send()


class Collect:
    def __init__(self, cube, tile, slots, send_sem, recv_sem):
        self.cube, self.tile, self.slots = cube, tile, slots
        self.send_sem, self.recv_sem = send_sem, recv_sem

    def make(self, i):
        to = self.cube.coords(lax.rem(self.cube.index() + i, self.cube.total))
        return remote(
            self.tile, self.slots.at[i], self.send_sem.at[i], self.recv_sem.at[i], to
        )

    def start(self):
        pl.loop(1, self.cube.total)(lambda i: self.make(i).start())
        self.slots[0] = self.tile[...]

    def arrive(self):
        pl.loop(1, self.cube.total)(lambda i: self.make(i).wait())

    def total(self):
        result = self.slots[0]
        for i in range(1, self.cube.total):
            result = result + self.slots[i]
        return result


def share_columns(j):
    place = j // 2 if j % 2 else 1 - j // 2
    return slice(FF * place, FF * (place + 1))


def matrix_of(d):
    return sum(jnp.where(d == OWNER_PLACES[i], i, 0) for i in range(8))


def pack_small(target, turn, rel, vec, depth):
    rows = target.shape[0]
    turn[...] = jnp.zeros_like(turn)
    turn[0:7, 0:rows] = vec[...]
    target[...] = jnp.zeros_like(target)
    target[0 : rel.shape[0], SMALL_REL : SMALL_REL + H] = rel[...]
    target[:, SMALL_VEC : SMALL_VEC + 7] = jnp.transpose(turn[...])[0:rows, 0:7]
    target[:, SMALL_DEPTH : SMALL_DEPTH + K] = depth[...]


OWNER_PLACES = (2, 3, 5, 4, 0, 1, 7, 6)


def owner_place(cube, t):
    return (OWNER_PLACES[t // 4] * (cube.dp_size // 8), t // 2 % 2, t % 2)


class Momenta:
    def __init__(self, cube, r):
        self.cube, self.r = cube, r
        self.me = cube.index()
        self.repeat = cube.dp_size // 8
        d = lax.axis_index("dp")
        self.is_owner = lax.rem(d, self.repeat) == 0
        self.matrix = matrix_of(d // self.repeat)
        self.quarter = lax.axis_index("seq") * 2 + lax.axis_index("shard")
        self.owned_index = self.matrix * 4 + self.quarter

    def holds(self, t):
        return jnp.logical_and(self.is_owner, self.owned_index == t)

    def rows(self, j):
        r = self.r
        if j < 4:
            old, share = ((r.m_up, r.m_down)[j // 2], (r.share_first, r.share_second)[j % 2])
            return old[:, FF * (j % 2) : FF * (j % 2 + 1)], share[:, share_columns(j)]
        start = STARTS[j] - STARTS[4]
        old = (r.m_qkv, r.m_out, r.m_glu, r.m_point)[j - 4]
        return old[...], r.share_middle[:, start : start + WIDTHS[j]]

    def copy(self, t):
        width = WIDTHS[t // 4] // 4
        r = self.r
        return remote(
            r.leaving.at[t, :, pl.ds(0, width)],
            r.owned.at[self.me, :, pl.ds(0, width)],
            r.m_send.at[t],
            r.m_recv.at[self.me],
            owner_place(self.cube, t),
        )

    def send(self, j):
        old, share = self.rows(j)
        value = (MOMENTUM * old + share).astype(jnp.bfloat16)
        width = WIDTHS[j] // 4
        for q in range(4):
            t = 4 * j + q
            part = value[:, width * q : width * (q + 1)]
            self.r.leaving[t, :, 0:width] = part
            pl.when(jnp.logical_not(self.holds(t)))(lambda t=t: self.copy(t).start())

            @pl.when(self.holds(t))
            def _(part=part, width=width):
                self.r.owned[self.me, :, 0:width] = part

    def receive(self):
        r, cube = self.r, self.cube

        def go(width):
            @pl.loop(1, cube.total)
            def _(i):
                source = lax.rem(self.me + i, cube.total)
                place = r.owned.at[source, :, pl.ds(0, width)]
                remote(
                    place, place, r.m_send.at[0], r.m_recv.at[source], cube.coords(source)
                ).wait_recv()

        pl.when(self.is_owner)(lambda: by_matrix(self.matrix, go))

    def back(self, i, width):
        r, cube = self.r, self.cube
        to = lax.rem(self.me + i, cube.total)
        return remote(
            r.solved.at[to, :, pl.ds(0, width)],
            r.returned.at[self.owned_index, :, pl.ds(0, width)],
            r.b_send.at[i],
            r.b_recv.at[self.owned_index],
            cube.coords(to),
        )

    def keep(self, width):
        r = self.r
        return pltpu.make_async_copy(
            r.solved.at[self.me, :, pl.ds(0, width)],
            r.returned.at[self.owned_index, :, pl.ds(0, width)],
            r.k_sem,
        )

    def send_back(self):
        r = self.r

        def go(width):
            pl.loop(1, self.cube.total)(lambda i: self.back(i, width).start())
            self.keep(width).start()

        pl.when(self.is_owner)(lambda: by_matrix(self.matrix, go))

    def receive_back(self):
        r = self.r
        for t in range(32):
            place = r.returned.at[t, :, pl.ds(0, WIDTHS[t // 4] // 4)]
            copy = remote(
                place, place, r.b_send.at[0], r.b_recv.at[t], owner_place(self.cube, t)
            )
            pl.when(jnp.logical_not(self.holds(t)))(copy.wait_recv)

    def finish(self):
        for t in range(32):
            pl.when(jnp.logical_not(self.holds(t)))(lambda t=t: self.copy(t).wait_send())

        def go(width):
            pl.loop(1, self.cube.total)(lambda i: self.back(i, width).wait_send())
            self.keep(width).wait()

        pl.when(self.is_owner)(lambda: by_matrix(self.matrix, go))


def symmetric_product(left, right):
    half = D // 2
    (lh, ll), (rh, rl) = left, right
    top = product((lh[:half], ll[:half]), right)
    corner = product((lh[half:], ll[half:]), (rh[:, half:], rl[:, half:]))
    low = jnp.concatenate([jnp.transpose(top[:, half:]), corner], axis=1)
    return jnp.concatenate([top, low], axis=0)


GRAM_SHARES = (
    ((0, 0), (0, 1), (0, 2), (0, 3), (3, 3)),
    ((1, 1), (1, 2), (1, 3), (2, 2), (2, 3)),
)


def orthogonalize(cube, r):
    f32 = jnp.float32
    core, seq = lax.axis_index("shard"), lax.axis_index("seq")
    block = r.owned.reshape(D, BLOCK)
    lines = [slice(128 * i, 128 * (i + 1)) for i in range(4)]
    for share in range(2):
        for n, (i, j) in enumerate(GRAM_SHARES[share]):
            r.packed[share, n] = matmul_right_t(block[lines[i], :], block[lines[j], :])
    peers = (cube.partner(cube.levels + 1), cube.partner(cube.levels))
    first = remote(
        r.packed.at[1 - core], r.packed_in.at[0], r.n_send.at[0], r.n_recv.at[0], peers[0]
    )
    first.start()
    first.wait()
    r.summed[...] = r.packed[core] + r.packed_in[0]
    second = remote(r.summed, r.packed_in.at[1], r.n_send.at[1], r.n_recv.at[1], peers[1])
    second.start()
    second.wait()
    r.whole[core] = r.summed[...] + r.packed_in[1]
    third = remote(
        r.whole.at[core], r.whole.at[core], r.n_send.at[2], r.n_recv.at[2], peers[0]
    )
    third.start()
    third.wait()
    for share in range(2):
        for n, (i, j) in enumerate(GRAM_SHARES[share]):
            value = r.whole[share, n]
            r.gram[lines[i], lines[j]] = value
            if i != j:
                r.gram[lines[j], lines[i]] = jnp.transpose(value)
    row = lax.broadcasted_iota(jnp.int32, (D, D), 0)
    col = lax.broadcasted_iota(jnp.int32, (D, D), 1)
    eye = row == col
    gram = r.gram[...]
    square = jnp.sum(
        jnp.sum(jnp.where(eye, gram, 0.0), axis=1, keepdims=True), axis=0, keepdims=True
    )
    scale = 1.0 / (jnp.sqrt(square) + 1e-07)
    gram = gram * (scale * scale)
    value = None
    for step in range(5):
        parts = split(gram)
        mixed = COEF_B * gram + COEF_C * symmetric_product(parts, parts)
        mixed = jnp.where(eye, mixed + COEF_A, mixed)
        high, low = split(mixed)
        if step == 0:
            start_high, start_low = split(mixed * scale)
            value = matmul(start_high, block[...]) + matmul(start_low, block[...])
        elif step < 4:
            value = product((high, low), split(value))
        else:
            value = matmul(high, value.astype(jnp.bfloat16))
        if step < 4:
            inner = symmetric_product((high, low), parts)
            gram = symmetric_product((high, low), split(inner))
    r.solved.reshape(D, BLOCK)[...] = value.astype(jnp.bfloat16)


SMALL_REL, SMALL_VEC, SMALL_DEPTH = 0, H, H + 7
SMALL_END = H + 7 + K
EDGE = 16
GATHER_EVENTS = (
    ((5, 0), (5, 1), (0, 0), (6, 0), (6, 1), (7, 0), (0, 1), (1, 0), (7, 1), (0, 2))
    + ((1, 1), (2, 0), (2, 1), (3, 0), (1, 2), (0, 3), (3, 1), (4, 0), (0, 4), (4, 1))
    + ((2, 2), (5, 2), (3, 2), (1, 3), (1, 4), (6, 2), (5, 3), (4, 2), (2, 3), (5, 4))
    + ((2, 4), (3, 3), (7, 2), (6, 3), (3, 4), (6, 4), (4, 3), (7, 3), (4, 4), (7, 4))
)
SCATTER_EVENTS = (
    ((0, 3), (4, 0), (2, 1), (5, 0), (0, 4), (1, 2), (1, 3), (3, 1), (1, 4), (4, 1), (2, 2))
    + ((2, 3), (5, 1), (2, 4), (3, 2), (4, 2), (3, 3), (5, 2), (4, 3), (3, 4), (5, 3))
    + ((4, 4), (5, 4))
)
SCATTER_STORES = ((), (4,), (), (3,), (), (2,))
EARLY_LOADS = tuple("w_up w_down w_qkv w_out".split()) + tuple("w_glu w_point rel vec".split())
EARLY_LOADS += tuple("depth m_rel m_vec m_depth".split())
SCATTER_MATRICES = ((3,), (1,), (), (4, 5, 6, 7), (2,), (0,))
GATHER_HELD = ((5, 2), (6, 2), (7, 2))
GATHER_AFTER = {
    (0, 0): [(1, 0)],
    (1, 0): [(2, 0)],
    (2, 0): [(3, 0)],
    (3, 0): [(4, 0)],
    (5, 0): [(6, 0)],
    (6, 0): [(7, 0)],
    (4, 1): [(5, 2)],
    (5, 2): [(6, 2)],
    (6, 2): [(7, 2)],
}
FIRST_READY, MIDDLE_READY, SECOND_READY = (1, 4), (3, 4), (7, 4)
SCATTER_CHUNKS = (
    (0, tile_ranges(16, 16, 2)),
    (0, tile_ranges(0, 16, 2)),
    (1, tile_ranges(12, 16, 2)),
    (1, tile_ranges(0, 12, 2)),
    (2, tile_ranges(0, 16, 2)),
    (2, tile_ranges(16, 17, 2)),
)


def step_kernel(cube, r):
    bf16, f32 = jnp.bfloat16, jnp.float32
    x_ref, cot_ref, bucket_ref = r.inputs, r.cotangent, r.bucket
    tokens = x_ref.shape[0]
    token_total = tokens * cube.total
    rows = r.w_up.shape[0]
    rel_rows = r.rel.shape[0]
    mine = cube.mine()
    seq = lax.axis_index("seq")
    early = seq == 0
    first_row = pl.multiple_of(seq * tokens, tokens)
    other_row = pl.multiple_of((1 - seq) * tokens, tokens)
    across = cube.partner(cube.levels)
    lengths = [ref.shape[-1] for ref in (r.first, r.middle, r.second)]
    first, middle, second, d_first, d_middle, d_second = (
        ref.reshape(D, ref.shape[-1])
        for ref in (r.first, r.middle, r.second, r.d_first, r.d_middle, r.d_second)
    )
    a, xh = r.a, r.xh

    barrier = pltpu.get_barrier_semaphore()
    me = cube.index()
    momenta = Momenta(cube, r)
    for load in r.loads.values():
        load.start()
    r.owned[...] = jnp.zeros_like(r.owned)

    @pl.loop(1, cube.total)
    def _(i):
        peer = cube.coords(lax.rem(me + i, cube.total))
        pl.semaphore_signal(barrier, inc=1, device_id=peer, device_id_type=MESH)

    for name in EARLY_LOADS:
        r.loads[name].wait()
    pack_small(r.small, r.turn, r.rel, r.vec, r.depth)
    pack_small(r.m_small, r.turn, r.m_rel, r.m_vec, r.m_depth)
    own = tuple(mine)
    r.first[own + (slice(None), slice(FF, 2 * FF))] = r.w_up[:, :FF].astype(bf16)
    r.first[own + (slice(None), slice(0, FF))] = r.w_down[:, :FF].astype(bf16)
    r.first[own + (slice(None), slice(2 * FF, lengths[0]))] = r.small[...].astype(bf16)
    r.middle[own + (slice(None), slice(0, 3 * D))] = r.w_qkv[...].astype(bf16)
    r.middle[own + (slice(None), slice(3 * D, 4 * D))] = r.w_out[...].astype(bf16)
    r.middle[own + (slice(None), slice(4 * D, 6 * D))] = r.w_glu[...].astype(bf16)
    r.middle[own + (slice(None), slice(6 * D, 7 * D))] = r.w_point[...].astype(bf16)
    r.second[own + (slice(None), slice(0, FF))] = r.w_up[:, FF:].astype(bf16)
    r.second[own + (slice(None), slice(FF, 2 * FF))] = r.w_down[:, FF:].astype(bf16)
    pl.semaphore_wait(barrier, cube.total - 1)

    gather = Gather(
        cube, mine, (r.first, r.middle, r.second), r.g_send, r.g_recv
    )
    scatter = Scatter(
        cube,
        mine,
        (r.d_second, r.d_middle, r.d_first),
        r.land,
        (r.share_second, r.share_middle, r.share_first),
        r.s_send,
        r.s_recv,
    )

    gather.begin()
    for name in [name for name in r.loads if name not in EARLY_LOADS]:
        r.loads[name].wait()
    xh0, inv0 = normalize(x_ref[...])
    xh[0] = xh0
    rho = lax.broadcasted_iota(jnp.int32, (D, bucket_ref.shape[1]), 0)
    bucket_of = jnp.where(rho % rows < rel_rows, (rho // rows) * rel_rows + rho % rows, -2)
    r.hit[...] = jnp.zeros_like(r.hit)
    offset_count = bucket_ref.shape[1]
    r.hit[:, 0:offset_count] = (bucket_ref[...] == bucket_of).astype(f32).astype(bf16)
    gather.run_to(*FIRST_READY)

    small = r.small_t
    small[...] = jnp.transpose(first[:, 2 * FF : 2 * FF + 128].astype(f32))
    gains = [small[SMALL_VEC + i : SMALL_VEC + i + 1, :] for i in range(7)]
    taps = [small[SMALL_DEPTH + k : SMALL_DEPTH + k + 1, :] for k in range(K)]
    CH = 512

    def ffn_forward_fused(index, field, normed, up, down, u_ref, s_ref):
        low = (normed * gains[(0, 1, 2, 3)[index]]).astype(bf16)
        a[index] = low
        for c in range(0, FF, CH):
            u = matmul(low, up[:, c : c + CH])
            u_ref[:, c : c + CH] = u
            s_ref[:, c : c + CH] = (u * jax.nn.sigmoid(u)).astype(bf16)
        return field + 0.5 * matmul_right_t(s_ref[...], down[...])

    down1, up1 = first.at[:, pl.ds(0, FF)], first.at[:, pl.ds(FF, FF)]
    up2, down2 = second.at[:, pl.ds(0, FF)], second.at[:, pl.ds(FF, FF)]
    section1 = ffn_forward_fused(0, x_ref[...], xh[0], up1, down1, r.u1, r.s1)
    r.sec1[...] = section1
    xh1, inv1 = normalize(section1)
    xh[1] = xh1
    a[1] = (xh1 * gains[1]).astype(bf16)
    offsets = matmul(small[0:8, :].astype(bf16), r.hit[...])
    offsets = jnp.where(
        early, pltpu.roll(offsets, 257, 1), pltpu.roll(offsets, (tokens + 257) % 512, 1)
    )
    for h in range(H):
        r.bias[h] = skew(offsets[h : h + 1, :], tokens)[:, : 2 * tokens]
    gather.run_to(*MIDDLE_READY)

    q_ref, kv = r.q, r.kv
    kv[pl.ds(first_row, tokens), :] = matmul(a[1], middle[:, D : 3 * D]).astype(bf16)
    kv_copy = remote(
        kv.at[pl.ds(first_row, tokens)],
        kv.at[pl.ds(first_row, tokens)],
        r.kv_send,
        r.kv_recv,
        across,
    )
    kv_copy.start()
    q_ref[...] = matmul(a[1], middle[:, :D]).astype(bf16)
    gather.run_to(4, 3)
    kv_copy.wait_recv()
    lane = lax.broadcasted_iota(jnp.int32, (1, 128), 1)
    lane_masks = [(lane // DH == e).astype(f32) for e in range(2)]
    low_masks = [m.astype(bf16) for m in lane_masks]
    scale = DH ** (-0.5)
    for p in range(H // 2):
        columns = slice(128 * p, 128 * (p + 1))
        k_pair, v_pair = kv[:, columns], kv[:, D + 128 * p : D + 128 * (p + 1)]
        merged = None
        for e in range(2):
            q_head = q_ref[:, columns] * low_masks[e]
            scores = matmul_right_t(q_head, k_pair) * scale + r.bias[2 * p + e]
            shifted = jnp.exp(scores - jnp.max(scores, axis=1, keepdims=True))
            prob = shifted / jnp.sum(shifted, axis=1, keepdims=True)
            r.prob[2 * p + e] = prob
            out = matmul(prob.astype(bf16), v_pair) * lane_masks[e]
            merged = out if merged is None else merged + out
        r.att[:, columns] = merged
    gather.run_to(*SECOND_READY)
    att_low = r.att[...].astype(bf16)
    r.att_low[...] = att_low
    section2 = r.sec1[...] + matmul(att_low, middle[:, 3 * D : 4 * D])
    r.sec2[...] = section2
    xh2, inv2 = normalize(section2)
    xh[2] = xh2
    a[2] = (xh2 * gains[2]).astype(bf16)
    gate_first = matmul(a[2], middle[:, 4 * D : 5 * D])
    sig = jax.nn.sigmoid(matmul(a[2], middle[:, 5 * D : 6 * D]))
    r.gate[...] = gate_first
    r.sig[...] = sig
    wide = r.wide
    wide[EDGE : EDGE + tokens, :] = gate_first * sig
    edge_row = pl.multiple_of(EDGE + (1 - seq) * (tokens - EDGE), EDGE)
    halo_copy = remote(
        wide.at[pl.ds(edge_row, EDGE)], r.halo, r.halo_send, r.halo_recv, across
    )
    halo_copy.start()
    zero_edge = jnp.zeros((EDGE, D), f32)
    halo_copy.wait()
    wide[0:EDGE, :] = jnp.where(early, zero_edge, r.halo[...])
    wide[EDGE + tokens :, :] = jnp.where(early, r.halo[...], zero_edge)
    conv_ref = r.conv
    for b in range(D // 128):
        cols = slice(128 * b, 128 * (b + 1))
        total = jnp.zeros((tokens, 128), f32)
        for k in range(K):
            total = total + wide[k + 1 : k + 1 + tokens, cols] * taps[k][:, cols]
        conv_ref[:, cols] = total
    conv = conv_ref[...]
    part_sum = jnp.sum(conv, axis=0, keepdims=True)
    part_off = conv - part_sum * (1.0 / tokens)
    part_square = jnp.sum(part_off * part_off, axis=0, keepdims=True)
    row_to_tile(r.tile1, 0, part_sum)
    row_to_tile(r.tile1, 4, part_square)
    stats = Collect(cube, r.tile1, r.slots1, r.c1_send, r.c1_recv)
    stats.start()
    stats.arrive()
    sums = stats.total()
    mean4 = sums[0:4] * (1.0 / token_total)
    spread4 = jnp.zeros((4, 128), f32)
    for i in range(cube.total):
        off = r.slots1[i][0:4] * (1.0 / tokens) - mean4
        spread4 = spread4 + off * off
    var4 = (sums[4:8] + spread4 * tokens) * (1.0 / token_total)
    mean = tile_to_row(mean4)
    inv_std = tile_to_row(lax.rsqrt(var4 + EPS_BATCH))

    xb = (conv_ref[...] - mean) * inv_std
    r.xb[...] = xb
    bn = xb * gains[5] + gains[6]
    r.bn[...] = bn
    sw = (bn * jax.nn.sigmoid(bn)).astype(bf16)
    r.sw[...] = sw
    section3 = r.sec2[...] + matmul(sw, middle[:, 6 * D : 7 * D])
    xh3, inv3 = normalize(section3)
    xh[3] = xh3
    section4 = ffn_forward_fused(3, section3, xh3, up2, down2, r.u2, r.s2)
    xh4, inv4 = normalize(section4)
    r.outputs[...] = xh4 * gains[4]
    r.stores[0].start()

    sg = r.small_grad
    sg[...] = jnp.zeros_like(sg)
    cot = cot_ref[...]
    d4, sg[SMALL_VEC + 4 : SMALL_VEC + 5, :] = norm_grad(cot, xh4, inv4, gains[4])

    def slope(value):
        sigma = jax.nn.sigmoid(value)
        return sigma * (1.0 + value * (1.0 - sigma))

    def slopes(low, down, u_ref, du_ref):
        for c in range(0, FF, CH):
            act = matmul(low, down[:, c : c + CH])
            du_ref[:, c : c + CH] = (act * slope(u_ref[:, c : c + CH])).astype(bf16)

    def weight_grad(left, right_ref, target, start, width):
        for c in range(0, width, CH):
            target[:, start + c : start + c + CH] = matmul_left_t(
                left, right_ref[:, c : c + CH]
            ).astype(bf16)

    r.e_low[...] = (0.5 * d4).astype(bf16)
    slopes(r.e_low[...], down2, r.u2, r.du)
    back = matmul_right_t(r.du[...], up2[...])
    part, sg[SMALL_VEC + 3 : SMALL_VEC + 4, :] = norm_grad(back, xh[3], inv3, gains[3])
    d3 = d4 + part
    r.d[...] = d3
    e3 = d3.astype(bf16)
    r.e3[...] = e3
    dbn = matmul_right_t(e3, middle[:, 6 * D : 7 * D]) * slope(r.bn[...])
    xb = r.xb[...]
    sg[SMALL_VEC + 5 : SMALL_VEC + 6, :] = jnp.sum(dbn * xb, axis=0, keepdims=True)
    sg[SMALL_VEC + 6 : SMALL_VEC + 7, :] = jnp.sum(dbn, axis=0, keepdims=True)
    dxb = dbn * gains[5]
    r.dxb[...] = dxb
    row_to_tile(r.tile2, 0, jnp.sum(dxb, axis=0, keepdims=True))
    row_to_tile(r.tile2, 4, jnp.sum(dxb * xb, axis=0, keepdims=True))
    sums2 = Collect(cube, r.tile2, r.slots2, r.c2_send, r.c2_recv)
    sums2.start()
    token_edge = pl.multiple_of((1 - seq) * (tokens - EDGE), EDGE)
    edges = r.edges
    edges[0:EDGE, :] = r.dxb[pl.ds(token_edge, EDGE), :]
    edges[EDGE:, :] = r.xb[pl.ds(token_edge, EDGE), :]
    edge_copy = remote(edges, r.edges_in, r.edge_send, r.edge_recv, across)
    edge_copy.start()

    weight_grad(r.e_low[...], r.s2, d_second, FF, FF)
    scatter.start(0, 0)
    weight_grad(a[3], r.du, d_second, 0, FF)
    scatter.start(1, 0)
    weight_grad(r.sw[...], r.e3, d_middle, 6 * D, D)
    edge_copy.wait()
    sums2.arrive()
    total2 = sums2.total()
    mean1 = tile_to_row(total2[0:4] * (1.0 / token_total))
    mean2 = tile_to_row(total2[4:8] * (1.0 / token_total))
    dwide = r.dwide
    dwide[EDGE : EDGE + tokens, :] = inv_std * (r.dxb[...] - mean1 - r.xb[...] * mean2)
    edge = inv_std * (r.edges_in[0:EDGE, :] - mean1 - r.edges_in[EDGE:, :] * mean2)
    dwide[0:EDGE, :] = jnp.where(early, zero_edge, edge)
    dwide[EDGE + tokens :, :] = jnp.where(early, edge, zero_edge)
    dglu_ref = r.conv
    for b in range(D // 128):
        cols = slice(128 * b, 128 * (b + 1))
        total = jnp.zeros((tokens, 128), f32)
        for k in range(K):
            total = total + dwide[31 - k : 31 - k + tokens, cols] * taps[k][:, cols]
        dglu_ref[:, cols] = total
    dglu, sig = dglu_ref[...], r.sig[...]
    r.dgates[:, :D] = (dglu * sig).astype(bf16)
    r.dgates[:, D:] = (dglu * r.gate[...] * sig * (1.0 - sig)).astype(bf16)
    scatter.advance(0, 0)
    back = matmul_right_t(r.dgates[...], middle[:, 4 * D : 6 * D])
    part, sg[SMALL_VEC + 2 : SMALL_VEC + 3, :] = norm_grad(back, xh[2], inv2, gains[2])
    d2 = r.d[...] + part
    r.d[...] = d2
    e1 = d2.astype(bf16)
    r.e_low[...] = e1
    dob = matmul_right_t(e1, middle[:, 3 * D : 4 * D]).astype(bf16)
    r.dob[...] = dob
    weight_grad(r.att_low[...], r.e_low, d_middle, 3 * D, D)
    weight_grad(a[2], r.dgates, d_middle, 4 * D, 2 * D)
    scatter.advance(1, 0)
    scatter.start(2, 0)

    off_rows = []
    give, keep, got = r.give, r.keep, r.got
    kv_grads = []
    for p in range(H // 2):
        columns = slice(128 * p, 128 * (p + 1))
        k_pair, v_pair = kv[:, columns], kv[:, D + 128 * p : D + 128 * (p + 1)]
        att_pair = r.att[:, columns]
        dq = dk = dv = None
        for e in range(2):
            h = 2 * p + e
            dob_head = r.dob[:, columns] * low_masks[e]
            q_head = q_ref[:, columns] * low_masks[e]
            delta = jnp.sum(dob_head.astype(f32) * att_pair, axis=1, keepdims=True)
            prob = r.prob[h]
            ds = prob * (matmul_right_t(dob_head, v_pair) - delta)
            ds_low = ds.astype(bf16)
            dv_head = matmul_left_t(prob.astype(bf16), dob_head)
            dk_head = matmul_left_t(ds_low, q_head) * scale
            dq_head = matmul(ds_low, k_pair) * (lane_masks[e] * scale)
            dv = dv_head if dv is None else dv + dv_head
            dk = dk_head if dk is None else dk + dk_head
            dq = dq_head if dq is None else dq + dq_head
            padded = jnp.concatenate([ds, jnp.zeros((tokens, 512 - 2 * tokens), f32)], axis=1)
            off_rows.append(unskew_sum(padded))
        r.dqkv[:, columns] = dq.astype(bf16)
        for n, value in enumerate((dk, dv)):
            r.dkv[n] = value
            give[p, n] = r.dkv[n, pl.ds(other_row, tokens), :].astype(bf16)
            keep[p, n] = r.dkv[n, pl.ds(first_row, tokens), :]
        copy = remote(
            give.at[p], got.at[p], r.dkv_send.at[p], r.dkv_recv.at[p], across
        )
        copy.start()
        kv_grads.append(copy)
        if p == 2:
            scatter.advance(0, 1)
    off = jnp.concatenate(off_rows, axis=0)
    off = jnp.where(early, pltpu.roll(off, 255, 1), pltpu.roll(off, 255 - tokens, 1))
    off_high, off_low = split(off)
    sg[0:8, :] = matmul_right_t(off_high, r.hit[...]) + matmul_right_t(off_low, r.hit[...])
    for b in range(D // 128):
        cols = slice(128 * b, 128 * (b + 1))
        dconv = dwide[EDGE : EDGE + tokens, cols]
        for k in range(K):
            sg[SMALL_DEPTH + k : SMALL_DEPTH + k + 1, cols] = jnp.sum(
                dconv * wide[k + 1 : k + 1 + tokens, cols], axis=0, keepdims=True
            )
    scatter.advance(2, 0)
    for p in range(H // 2):
        kv_grads[p].wait()
        for n in range(2):
            at = D * (n + 1) + 128 * p
            r.dqkv[:, at : at + 128] = (keep[p, n] + got[p, n].astype(f32)).astype(bf16)
    back = matmul_right_t(r.dqkv[...], middle[:, : 3 * D])
    part, sg[SMALL_VEC + 1 : SMALL_VEC + 2, :] = norm_grad(back, xh[1], inv1, gains[1])
    d1 = r.d[...] + part
    e0 = (0.5 * d1).astype(bf16)
    weight_grad(a[1], r.dqkv, d_middle, 0, 3 * D)
    scatter.start(3, 0)
    scatter.advance(1, 1)
    weight_grad(e0, r.s1, d_first, 0, FF)
    scatter.start(4, 0)
    scatter.advance(0, 2)
    slopes(e0, down1, r.u1, r.du)
    back = matmul_right_t(r.du[...], up1[...])
    part, sg[SMALL_VEC : SMALL_VEC + 1, :] = norm_grad(back, xh[0], inv0, gains[0])
    r.input_grad[...] = d1 + part
    r.stores[1].start()
    scatter.advance(3, 0)
    d_first[:, 2 * FF : 2 * FF + 128] = jnp.transpose(sg[...]).astype(bf16)
    weight_grad(a[0], r.du, d_first, FF, FF)
    scatter.start(5, 0)
    for n, stage in SCATTER_EVENTS:
        scatter.advance(n, stage)
        if stage == scatter.cube.digits - 1:
            for j in SCATTER_MATRICES[n]:
                momenta.send(j)
            for store in SCATTER_STORES[n]:
                r.stores[store].start()
    next_small = MOMENTUM * r.m_small[...] + r.share_first[:, 2 * FF :]
    r.tile3[...] = jnp.zeros_like(r.tile3)
    r.tile3[0:1, :] = jnp.sum(next_small * next_small, axis=0, keepdims=True)
    squares = Collect(cube, r.tile3, r.slots3, r.c3_send, r.c3_recv)
    squares.start()
    momenta.receive()
    orthogonalize(cube, r)
    momenta.send_back()
    squares.arrive()
    r.squares[...] = squares.total()
    r.stores[5].start()
    momenta.receive_back()
    momenta.finish()
    gather.finish()
    scatter.finish()
    for store in r.stores:
        store.wait()
    kv_copy.wait_send()


def fused_step(cube, inputs, cotangent, weights, momenta, bucket, collective_id):
    bf16, f32 = jnp.bfloat16, jnp.float32
    tokens, rows = inputs.shape[0], weights[0].shape[0]
    widths = (2 * FF + 128, 7 * D, 2 * FF)
    lead = (2,) * cube.digits
    named = dict(
        inputs=inputs,
        cotangent=cotangent,
        w_up=weights[0],
        w_down=weights[1],
        w_qkv=weights[2],
        w_out=weights[3],
        w_glu=weights[4],
        w_point=weights[5],
        vec=weights[6],
        depth=weights[7],
        rel=weights[8],
        m_up=momenta[0],
        m_down=momenta[1],
        m_qkv=momenta[2],
        m_out=momenta[3],
        m_glu=momenta[4],
        m_point=momenta[5],
        m_vec=momenta[6],
        m_depth=momenta[7],
        m_rel=momenta[8],
        bucket=bucket,
    )
    outs = dict(
        outputs=jax.ShapeDtypeStruct((tokens, D), f32),
        input_grad=jax.ShapeDtypeStruct((tokens, D), f32),
        share_first=jax.ShapeDtypeStruct((rows, widths[0]), f32),
        share_middle=jax.ShapeDtypeStruct((rows, widths[1]), f32),
        share_second=jax.ShapeDtypeStruct((rows, widths[2]), f32),
        returned=jax.ShapeDtypeStruct((32, rows, BLOCK), bf16),
        squares=jax.ShapeDtypeStruct((8, 128), f32),
    )
    field = pltpu.VMEM((tokens, D), f32)
    low = pltpu.VMEM((tokens, D), bf16)
    wide_low = pltpu.VMEM((tokens, FF), bf16)
    wide_field = pltpu.VMEM((tokens + 2 * EDGE, D), f32)
    grid = pltpu.VMEM((H, tokens, 2 * tokens), f32)
    pairs = pltpu.VMEM((H // 2, 2, tokens, 128), bf16)
    tile = pltpu.VMEM((8, 128), f32)
    slots = pltpu.VMEM((cube.total, 8, 128), f32)
    stages = pltpu.SemaphoreType.DMA((6, 2, cube.digits))
    gather_stages = pltpu.SemaphoreType.DMA((8, 2, cube.digits))
    everyone = pltpu.SemaphoreType.DMA((cube.total,))
    single = pltpu.SemaphoreType.DMA
    bands = [pltpu.VMEM(lead + (rows, w), bf16) for w in widths]
    land = []
    for _, pair in SCATTER_CHUNKS:
        for _, part in pair:
            for stage in range(cube.digits):
                shape = (2,) * (cube.digits - 1 - stage) + (rows, part)
                land.append(pltpu.VMEM(shape, bf16))
    scratch = dict(
        first=bands[0],
        middle=bands[1],
        second=bands[2],
        d_first=bands[0],
        d_middle=bands[1],
        d_second=bands[2],
        land=tuple(land),
        sec1=field,
        sec2=field,
        att=field,
        gate=field,
        sig=field,
        conv=field,
        xb=field,
        bn=field,
        dxb=field,
        d=field,
        q=low,
        att_low=low,
        sw=low,
        e_low=low,
        e3=low,
        dob=low,
        a=pltpu.VMEM((4, tokens, D), bf16),
        xh=pltpu.VMEM((4, tokens, D), f32),
        u1=pltpu.VMEM((tokens, FF), f32),
        u2=pltpu.VMEM((tokens, FF), f32),
        s1=wide_low,
        s2=wide_low,
        du=wide_low,
        kv=pltpu.VMEM((2 * tokens, 2 * D), bf16),
        bias=grid,
        prob=grid,
        wide=wide_field,
        dwide=wide_field,
        halo=pltpu.VMEM((EDGE, D), f32),
        edges=pltpu.VMEM((2 * EDGE, D), f32),
        edges_in=pltpu.VMEM((2 * EDGE, D), f32),
        dgates=pltpu.VMEM((tokens, 2 * D), bf16),
        dqkv=pltpu.VMEM((tokens, 3 * D), bf16),
        dkv=pltpu.VMEM((2, 2 * tokens, 128), f32),
        give=pairs,
        got=pairs,
        keep=pltpu.VMEM((H // 2, 2, tokens, 128), f32),
        small=pltpu.VMEM((rows, 128), f32),
        m_small=pltpu.VMEM((rows, 128), f32),
        turn=pltpu.VMEM((128, 128), f32),
        hit=pltpu.VMEM((D, 512), bf16),
        small_t=pltpu.VMEM((128, D), f32),
        small_grad=pltpu.VMEM((128, D), f32),
        tile1=tile,
        tile2=tile,
        slots1=slots,
        slots2=slots,
        tile3=tile,
        slots3=slots,
        leaving=pltpu.VMEM((32, rows, BLOCK), bf16),
        owned=pltpu.VMEM((cube.total, rows, BLOCK), bf16),
        solved=pltpu.VMEM((cube.total, rows, BLOCK), bf16),
        packed=pltpu.VMEM((2, 5, 128, 128), f32),
        packed_in=pltpu.VMEM((2, 5, 128, 128), f32),
        summed=pltpu.VMEM((5, 128, 128), f32),
        whole=pltpu.VMEM((2, 5, 128, 128), f32),
        gram=pltpu.VMEM((D, D), f32),
        m_send=pltpu.SemaphoreType.DMA((32,)),
        m_recv=everyone,
        b_send=everyone,
        b_recv=pltpu.SemaphoreType.DMA((32,)),
        n_send=pltpu.SemaphoreType.DMA((3,)),
        n_recv=pltpu.SemaphoreType.DMA((3,)),
        c3_send=everyone,
        c3_recv=everyone,
        g_send=gather_stages,
        g_recv=gather_stages,
        s_send=stages,
        s_recv=stages,
        c1_send=everyone,
        c1_recv=everyone,
        c2_send=everyone,
        c2_recv=everyone,
        kv_send=single,
        kv_recv=single,
        halo_send=single,
        halo_recv=single,
        edge_send=single,
        edge_recv=single,
        dkv_send=pltpu.SemaphoreType.DMA((H // 2,)),
        dkv_recv=pltpu.SemaphoreType.DMA((H // 2,)),
    )

    kept = [n for n in outs if n != "returned"]
    buffers = dict({n: pltpu.VMEM(v.shape, v.dtype) for n, v in named.items()})
    buffers |= {n: pltpu.VMEM(outs[n].shape, outs[n].dtype) for n in kept}
    scratch |= buffers
    scratch |= dict(
        load_sem=pltpu.SemaphoreType.DMA((len(named),)),
        store_sem=pltpu.SemaphoreType.DMA((len(kept),)),
        k_sem=single,
    )

    def body(*refs):
        count = len(named) + len(outs)
        far = dict(zip(list(named) + list(outs), refs[:count]))
        near = dict(zip(scratch, refs[count:]))
        near["returned"] = far["returned"]
        near["loads"] = {
            name: pltpu.make_async_copy(far[name], near[name], near["load_sem"].at[n])
            for n, name in enumerate(named)
        }
        near["stores"] = [
            pltpu.make_async_copy(near[name], far[name], near["store_sem"].at[n])
            for n, name in enumerate(kept)
        ]
        step_kernel(cube, types.SimpleNamespace(**near))

    return pl.pallas_call(
        body,
        out_shape=list(outs.values()),
        in_specs=[pl.BlockSpec(memory_space=pl.ANY)] * len(named),
        out_specs=[pl.BlockSpec(memory_space=pl.ANY)] * len(outs),
        scratch_shapes=list(scratch.values()),
        compiler_params=pltpu.CompilerParams(
            collective_id=collective_id, has_side_effects=True, vmem_limit_bytes=60 << 20
        ),
        name="block_step",
    )(*named.values())


def finish_kernel(r):
    f32 = jnp.float32
    for load in r.loads:
        load.start()
    for load in r.loads:
        load.wait()
    pack_small(r.small, r.turn, r.weight[8], r.weight[6], r.weight[7])
    pack_small(r.m_small, r.turn, r.moment[8], r.moment[6], r.moment[7])
    share_first, share_middle, share_second, returned, squares = r.results
    for j in range(8):
        width = WIDTHS[j]
        if j < 4:
            columns = slice(FF * (j % 2), FF * (j % 2 + 1))
            grad = (share_first, share_second)[j % 2][:, share_columns(j)]
        else:
            columns = slice(0, width)
            start = STARTS[j] - STARTS[4]
            grad = share_middle[:, start : start + width]
        n = j // 2 if j < 4 else j - 2
        updated = MOMENTUM * r.moment[n][:, columns] + grad
        r.grad[n][:, columns] = grad
        r.next[n][:, columns] = updated
        solved = [returned[4 * j + q, :, 0 : width // 4].astype(f32) for q in range(4)]
        r.new[n][:, columns] = r.weight[n][:, columns] - RATE_MATRIX * jnp.concatenate(
            solved, axis=1
        )
    grad = share_first[:, 2 * FF :]
    updated = MOMENTUM * r.m_small[...] + grad
    lane = lax.broadcasted_iota(jnp.int32, (1, 128), 1)
    count = jnp.where(lane < SMALL_VEC, float(NB), float(D))
    scale = lax.rsqrt(squares[0:1, :] / count + EPS_SCALE)
    new = r.small[...] - RATE_VECTOR * updated * scale
    rows, rel_rows = r.small.shape[0], r.weight[8].shape[0]
    for value, outs in ((grad, r.grad), (new, r.new), (updated, r.next)):
        r.turn[...] = jnp.zeros_like(r.turn)
        r.turn[0:rows, :] = value
        turned = jnp.transpose(r.turn[...])
        outs[6][...] = turned[SMALL_VEC : SMALL_VEC + 7, 0:rows]
        outs[7][...] = value[:, SMALL_DEPTH : SMALL_DEPTH + K]
        outs[8][...] = value[0:rel_rows, SMALL_REL : SMALL_REL + H]
    for store in r.stores:
        store.start()
    for store in r.stores:
        store.wait()


def finish_step(fields, shares, returned, squares, weights, momenta):
    sources = (*shares, returned, squares, *weights, *momenta)
    operands = sources + tuple(fields)
    rows, count = weights[0].shape[0], len(sources)
    shapes = [jax.ShapeDtypeStruct(v.shape, v.dtype) for v in weights] * 3
    shapes += [jax.ShapeDtypeStruct(v.shape, v.dtype) for v in fields]

    def body(*refs):
        ins, refs = refs[: len(operands)], refs[len(operands) :]
        outs, refs = refs[: len(shapes)], refs[len(shapes) :]
        near, refs = refs[: count + 2], refs[count + 2 :]
        made, refs = refs[:27], refs[27:]
        small, m_small, turn, sem = refs
        pairs = list(zip(ins, near)) + list(zip(made + near[-2:], outs))
        moves = [pltpu.make_async_copy(a, b, sem.at[n]) for n, (a, b) in enumerate(pairs)]
        finish_kernel(
            types.SimpleNamespace(
                loads=moves[: count + 2],
                stores=moves[count + 2 :],
                results=near[:5],
                weight=near[5:14],
                moment=near[14:23],
                grad=made[:9],
                new=made[9:18],
                next=made[18:27],
                small=small,
                m_small=m_small,
                turn=turn,
            ),
        )

    return pl.pallas_call(
        body,
        out_shape=shapes,
        in_specs=[pl.BlockSpec(memory_space=pl.ANY)] * len(operands),
        out_specs=[pl.BlockSpec(memory_space=pl.ANY)] * len(shapes),
        scratch_shapes=[pltpu.VMEM(v.shape, v.dtype) for v in list(operands) + shapes[:27]]
        + [
            pltpu.VMEM((rows, 128), jnp.float32),
            pltpu.VMEM((rows, 128), jnp.float32),
            pltpu.VMEM((128, 128), jnp.float32),
            pltpu.SemaphoreType.DMA((len(operands) + len(shapes),)),
        ],
        compiler_params=pltpu.CompilerParams(vmem_limit_bytes=60 << 20),
        name="finish_step",
    )(*operands)


def unfused_step(
    cube,
    inputs,
    cotangent,
    w_up,
    w_down,
    w_qkv,
    w_out,
    w_glu,
    w_point,
    small,
    bucket_table,
):
    bf16 = jnp.bfloat16
    rows = w_up.shape[0]
    rel_rows = NB // cube.total
    shard_groups = (
        jnp.concatenate([w_up[:, :FF], w_down[:, :FF], small], axis=1).astype(bf16),
        jnp.concatenate([w_qkv, w_out, w_glu, w_point], axis=1).astype(bf16),
        jnp.concatenate([w_up[:, FF:], w_down[:, FF:]], axis=1).astype(bf16),
    )
    first, middle, second = [
        full.reshape(D, -1) for full in gather_groups(cube, shard_groups, 0)
    ]
    up_first, down_first, small_low = first[:, :FF], first[:, FF : 2 * FF], first[:, 2 * FF :]
    qkv_w, out_w = middle[:, : 3 * D], middle[:, 3 * D : 4 * D]
    glu_w, point_w = middle[:, 4 * D : 6 * D], middle[:, 6 * D :]
    up_second, down_second = second[:, :FF], second[:, FF:]
    gains = small_low[:, SMALL_VEC : SMALL_VEC + 7].astype(jnp.float32)
    kernel = small_low[:, SMALL_DEPTH : SMALL_DEPTH + K].astype(jnp.float32)
    rel_low = small_low[:, :H].reshape(cube.total, rows, H)[:, :rel_rows].reshape(NB, H)
    bucket_hit = (bucket_table[:, None] == jnp.arange(NB, dtype=jnp.int32)[None, :]).astype(
        jnp.float32
    )
    offsets = jnp.dot(bucket_hit, rel_low.astype(jnp.float32), precision=HIGHEST).T
    seq_rows = inputs[0]
    row_count = seq_rows.shape[0]
    first_row = lax.axis_index("seq") * row_count
    token_total = row_count * lax.axis_size(("dp", "seq", "shard"))
    section_one, ffn_saved = ffn_forward(seq_rows, gains[:, 0], up_first, down_first)
    normed_out2, normed2, inverse2 = layer_norm(section_one, gains[:, 1])
    lifted2 = normed_out2.astype(bf16)
    projected = matmul(lifted2, qkv_w).astype(bf16)
    query = projected[:, :D]
    pair = [(0, 1), (1, 0)]
    other = lax.ppermute(projected[:, D:], "seq", pair)
    early = lax.axis_index("seq") == 0
    both = jnp.concatenate(
        [
            jnp.where(early, projected[:, D:], other),
            jnp.where(early, other, projected[:, D:]),
        ],
        axis=0,
    )
    keys, values = both[:, :D], both[:, D:]
    attended, log_total = attention_forward(query, keys, values, offsets, first_row)
    attended_low = attended.astype(bf16)
    section_two = section_one + matmul(attended_low, out_w)
    normed_out3, normed3, inverse3 = layer_norm(section_two, gains[:, 2])
    lifted3 = normed_out3.astype(bf16)
    gates = matmul(lifted3, glu_w)
    first_half = gates[:, :D]
    sig_gate = jax.nn.sigmoid(gates[:, D:])
    glu = first_half * sig_gate
    glu_wide = with_halo(glu, (("seq", 0),), K // 2)
    conv = depthwise(glu_wide, kernel, row_count)
    part_sum = jnp.sum(conv, axis=0)
    part_mean = part_sum / row_count
    part_square = jnp.sum(jnp.square(conv - part_mean), axis=0)
    stats = collect(cube, jnp.concatenate([part_sum, part_square]).reshape(8, 128), 1)
    stats = stats.reshape(cube.total, 2, D)
    mean = jnp.sum(stats[:, 0], axis=0) / token_total
    spread_of_means = jnp.square(stats[:, 0] / row_count - mean) * row_count
    variance = jnp.sum(stats[:, 1] + spread_of_means, axis=0) / token_total
    centred = conv - mean
    inv_std = lax.rsqrt(variance + EPS_BATCH)
    normed_bn = centred * inv_std
    batch_out = normed_bn * gains[:, 5] + gains[:, 6]
    swish_low = jax.nn.silu(batch_out).astype(bf16)
    section_three = section_two + matmul(swish_low, point_w)
    section_four, tail_saved = ffn_forward(
        section_three, gains[:, 3], up_second, down_second
    )
    outputs, normed5, inverse5 = layer_norm(section_four, gains[:, 4])
    grad_four, gain_four = norm_back(cotangent[0], normed5, inverse5, gains[:, 4])
    grad_three, grad_up_two, grad_down_two, gain_three = ffn_backward(
        grad_four, tail_saved, gains[:, 3], up_second, down_second
    )
    grad_three_low = grad_three.astype(bf16)
    grad_point = matmul_left_t(swish_low, grad_three_low)
    grad_batch = matmul_right_t(grad_three_low, point_w) * silu_slope(batch_out)
    grad_normed = grad_batch * gains[:, 5]
    sums = jnp.concatenate(
        [jnp.sum(grad_normed, axis=0), jnp.sum(grad_normed * normed_bn, axis=0)]
    )
    sums = jnp.sum(collect(cube, sums.reshape(8, 128), 2), axis=0).reshape(2, D)
    sum_normed, sum_cross = sums[0], sums[1]
    grad_conv = inv_std * (
        grad_normed - sum_normed / token_total - normed_bn * sum_cross / token_total
    )
    grad_wide = with_halo(grad_conv, (("seq", 0),), K // 2)
    grad_glu = grad_wide[K - 1 : K - 1 + row_count] * kernel[:, 0]
    for tap_idx in range(1, K):
        grad_glu = (
            grad_glu
            + grad_wide[K - 1 - tap_idx : K - 1 - tap_idx + row_count] * kernel[:, tap_idx]
        )
    grad_kernel = jnp.stack(
        [
            jnp.sum(grad_conv * glu_wide[tap_idx : tap_idx + row_count], axis=0)
            for tap_idx in range(K)
        ],
        axis=1,
    )
    grad_gates = jnp.concatenate(
        [grad_glu * sig_gate, grad_glu * first_half * sig_gate * (1.0 - sig_gate)], axis=1
    ).astype(bf16)
    grad_glu_w = matmul_left_t(lifted3, grad_gates)
    grad_two_part, gain_two = norm_back(
        matmul_right_t(grad_gates, glu_w), normed3, inverse3, gains[:, 2]
    )
    grad_two = grad_three + grad_two_part
    grad_two_low = grad_two.astype(bf16)
    grad_out_w = matmul_left_t(attended_low, grad_two_low)
    grad_attended = matmul_right_t(grad_two_low, out_w).astype(bf16)
    delta = jnp.sum(
        (grad_attended.astype(jnp.float32) * attended).reshape(row_count, H, DH), axis=2
    )
    query_grad, key_grad, value_grad, offset_grad = attention_backward(
        query, keys, values, offsets, first_row, log_total, grad_attended, delta
    )
    keys_grad = jnp.concatenate([key_grad, value_grad], axis=1)
    theirs = lax.dynamic_slice_in_dim(keys_grad, row_count - first_row, row_count, 0)
    own = lax.dynamic_slice_in_dim(keys_grad, first_row, row_count, 0)
    own = own + lax.ppermute(theirs, "seq", pair)
    key_own, value_own = own[:, :D], own[:, D:]
    grad_proj = jnp.concatenate([query_grad, key_own, value_own], axis=1).astype(bf16)
    grad_qkv_w = matmul_left_t(lifted2, grad_proj)
    grad_one_part, gain_one = norm_back(
        matmul_right_t(grad_proj, qkv_w), normed2, inverse2, gains[:, 1]
    )
    grad_one = grad_two + grad_one_part
    input_grad, grad_up_one, grad_down_one, gain_zero = ffn_backward(
        grad_one, ffn_saved, gains[:, 0], up_first, down_first
    )
    grad_vec_local = jnp.stack(
        [
            gain_zero,
            gain_one,
            gain_two,
            gain_three,
            gain_four,
            jnp.sum(grad_batch * normed_bn, axis=0),
            jnp.sum(grad_batch, axis=0),
        ],
        axis=1,
    )
    grad_rel_local = jnp.dot(bucket_hit.T, offset_grad.T, precision=HIGHEST)
    rel_padded = jnp.pad(
        grad_rel_local.reshape(cube.total, rel_rows, H), ((0, 0), (0, rows - rel_rows), (0, 0))
    )
    small_grads = jnp.concatenate(
        [rel_padded.reshape(D, H), grad_vec_local, grad_kernel], axis=1
    )
    small_grads = jnp.pad(small_grads, ((0, 0), (0, 128 - SMALL_END)))
    lead = (2,) * cube.digits
    grad_groups = [
        jnp.concatenate(group, axis=1).astype(bf16).reshape(lead + (rows, -1))
        for group in (
            (grad_up_two, grad_down_two),
            (grad_qkv_w, grad_out_w, grad_glu_w, grad_point),
            (grad_up_one, grad_down_one, small_grads),
        )
    ]
    share_second, share_middle, share_first = scatter_groups(cube, grad_groups, 3)
    return outputs, input_grad, share_first, share_middle, share_second


def local(
    cube,
    inputs,
    cotangent,
    w_up,
    w_down,
    w_qkv,
    w_out,
    w_glu,
    w_point,
    vectors,
    depth_kernel,
    rel_bias,
    bucket_table,
    m_up,
    m_down,
    m_qkv,
    m_out,
    m_glu,
    m_point,
    m_vectors,
    m_depth,
    m_rel,
):
    bf16 = jnp.bfloat16
    rows, rel_rows = w_up.shape[0], rel_bias.shape[0]
    pack = lambda rel, vec, depth: jnp.pad(
        jnp.concatenate([jnp.pad(rel, ((0, rows - rel_rows), (0, 0))), vec, depth], axis=1),
        ((0, 0), (0, 128 - SMALL_END)),
    )
    small = pack(rel_bias, vectors, depth_kernel)
    weights = (w_up, w_down, w_qkv, w_out, w_glu, w_point)
    if rows % 16 == 0 and cube.total == 32:
        bucket = bucket_table[None]
        weights += (vectors.T, depth_kernel, rel_bias)
        momenta = (m_up, m_down, m_qkv, m_out, m_glu, m_point, m_vectors.T, m_depth, m_rel)
        outputs, input_grad, *shares, returned, squares = fused_step(
            cube, inputs[0], cotangent[0], weights, momenta, bucket, 0
        )
        *rest, outputs, input_grad = finish_step(
            (outputs, input_grad), shares, returned, squares, weights, momenta
        )
        for n in (6, 15, 24):
            rest[n] = rest[n].T
        return (outputs[None], input_grad[None], *rest)
    outputs, input_grad, share_first, share_middle, share_second = unfused_step(
        cube, inputs, cotangent, *weights, small, bucket_table
    )
    grad_up = jnp.concatenate([share_first[:, :FF], share_second[:, :FF]], axis=1)
    grad_down = jnp.concatenate([share_first[:, FF : 2 * FF], share_second[:, FF:]], axis=1)
    grad_qkv, grad_out = share_middle[:, : 3 * D], share_middle[:, 3 * D : 4 * D]
    grad_glu, grad_pnt = share_middle[:, 4 * D : 6 * D], share_middle[:, 6 * D :]
    share_small = share_first[:, 2 * FF :]
    grad_vectors = share_small[:, SMALL_VEC : SMALL_VEC + 7]
    grad_depth = share_small[:, SMALL_DEPTH : SMALL_DEPTH + K]
    grad_rel = share_small[: rel_bias.shape[0], :H]
    next_m_up = MOMENTUM * m_up + grad_up
    next_m_down = MOMENTUM * m_down + grad_down
    next_m_qkv = MOMENTUM * m_qkv + grad_qkv
    next_m_out = MOMENTUM * m_out + grad_out
    next_m_glu = MOMENTUM * m_glu + grad_glu
    next_m_point = MOMENTUM * m_point + grad_pnt
    stacked = jnp.concatenate(
        [next_m_up, next_m_down, next_m_qkv, next_m_out, next_m_glu, next_m_point], axis=1
    )
    owned = spread(cube, stacked, 4).reshape(D, BLOCK)
    ortho = orthogonalize_blocks(cube, owned, bf16, 5)
    mine = restore(cube, ortho.reshape(cube.total, rows, BLOCK), 6).astype(jnp.float32)
    new_up = w_up - RATE_MATRIX * mine[:, : 2 * FF]
    new_down = w_down - RATE_MATRIX * mine[:, 2 * FF : 4 * FF]
    new_qkv = w_qkv - RATE_MATRIX * mine[:, STARTS[4] : STARTS[5]]
    new_out = w_out - RATE_MATRIX * mine[:, STARTS[5] : STARTS[6]]
    new_glu = w_glu - RATE_MATRIX * mine[:, STARTS[6] : STARTS[7]]
    new_point = w_point - RATE_MATRIX * mine[:, STARTS[7] :]
    next_m_vectors = MOMENTUM * m_vectors + grad_vectors
    next_m_depth = MOMENTUM * m_depth + grad_depth
    next_m_rel = MOMENTUM * m_rel + grad_rel
    squares = jnp.concatenate(
        [
            jnp.sum(next_m_vectors * next_m_vectors, axis=0),
            jnp.sum(next_m_depth * next_m_depth, axis=0),
            jnp.sum(next_m_rel * next_m_rel, axis=0),
        ]
    )
    squares = jnp.pad(squares, (0, 128 - squares.shape[0])).reshape(1, 128)
    squares = jnp.sum(collect(cube, jnp.pad(squares, ((0, 7), (0, 0))), 7), axis=0)[0]
    square_vec, square_depth = squares[:7], squares[7 : 7 + K]
    square_rel = squares[7 + K : 7 + K + H]
    new_vectors = vectors - RATE_VECTOR * next_m_vectors * lax.rsqrt(square_vec / D + EPS_SCALE)
    new_depth = depth_kernel - RATE_VECTOR * next_m_depth * lax.rsqrt(square_depth / D + EPS_SCALE)
    new_rel = rel_bias - RATE_VECTOR * next_m_rel * lax.rsqrt(square_rel / NB + EPS_SCALE)
    return (
        outputs[None],
        input_grad[None],
        grad_up,
        grad_down,
        grad_qkv,
        grad_out,
        grad_glu,
        grad_pnt,
        grad_vectors,
        grad_depth,
        grad_rel,
        new_up,
        new_down,
        new_qkv,
        new_out,
        new_glu,
        new_point,
        new_vectors,
        new_depth,
        new_rel,
        next_m_up,
        next_m_down,
        next_m_qkv,
        next_m_out,
        next_m_glu,
        next_m_point,
        next_m_vectors,
        next_m_depth,
        next_m_rel,
    )


def solution(mesh):
    placed = (
        P(("dp", "shard"), "seq", None),
        P(("dp", "shard"), "seq", None),
        P(("dp", "seq", "shard"), None),
        P(("dp", "seq", "shard"), None),
        P(("dp", "seq", "shard"), None),
        P(("dp", "seq", "shard"), None),
        P(("dp", "seq", "shard"), None),
        P(("dp", "seq", "shard"), None),
        P(("dp", "seq", "shard"), None),
        P(("dp", "seq", "shard"), None),
        P(("dp", "seq", "shard"), None),
        P(),
        P(("dp", "seq", "shard"), None),
        P(("dp", "seq", "shard"), None),
        P(("dp", "seq", "shard"), None),
        P(("dp", "seq", "shard"), None),
        P(("dp", "seq", "shard"), None),
        P(("dp", "seq", "shard"), None),
        P(("dp", "seq", "shard"), None),
        P(("dp", "seq", "shard"), None),
        P(("dp", "seq", "shard"), None),
    )
    return jax.shard_map(
        functools.partial(local, Cube(mesh.shape["dp"])),
        mesh=mesh,
        in_specs=placed,
        out_specs=(
            P(("dp", "shard"), "seq", None),
            P(("dp", "shard"), "seq", None),
            P(("dp", "seq", "shard"), None),
            P(("dp", "seq", "shard"), None),
            P(("dp", "seq", "shard"), None),
            P(("dp", "seq", "shard"), None),
            P(("dp", "seq", "shard"), None),
            P(("dp", "seq", "shard"), None),
            P(("dp", "seq", "shard"), None),
            P(("dp", "seq", "shard"), None),
            P(("dp", "seq", "shard"), None),
            P(("dp", "seq", "shard"), None),
            P(("dp", "seq", "shard"), None),
            P(("dp", "seq", "shard"), None),
            P(("dp", "seq", "shard"), None),
            P(("dp", "seq", "shard"), None),
            P(("dp", "seq", "shard"), None),
            P(("dp", "seq", "shard"), None),
            P(("dp", "seq", "shard"), None),
            P(("dp", "seq", "shard"), None),
            P(("dp", "seq", "shard"), None),
            P(("dp", "seq", "shard"), None),
            P(("dp", "seq", "shard"), None),
            P(("dp", "seq", "shard"), None),
            P(("dp", "seq", "shard"), None),
            P(("dp", "seq", "shard"), None),
            P(("dp", "seq", "shard"), None),
            P(("dp", "seq", "shard"), None),
            P(("dp", "seq", "shard"), None),
        ),
        check_vma=False,
    )
```

```python
import functools
import types

import jax
import jax.numpy as jnp
from jax import lax
from jax.experimental import pallas as pl
from jax.experimental.pallas import tpu as pltpu
from jax.sharding import PartitionSpec as P

D = 512
FF = 2048
H = 8
DH = 64
K = 31
NB = 128


EPS_NORM = 1e-05
EPS_BATCH = 1e-05
EPS_SCALE = 1e-06
MOMENTUM = 0.9
RATE_MATRIX = 1.0
RATE_VECTOR = 0.25
COEF_A = 3.4445
COEF_B = -4.775
COEF_C = 2.0315
HIGHEST = lax.Precision.HIGHEST


AXES = ("dp", "seq", "shard")
MESH = pl.DeviceIdType.MESH
WIDTHS = (FF, FF, FF, FF, 3 * D, D, 2 * D, D)
STARTS = tuple(sum(WIDTHS[:i]) for i in range(9))
BLOCK = 512


class Cube:
    def __init__(self, dp_size):
        self.dp_size = dp_size
        self.levels = dp_size.bit_length() - 1
        self.digits = self.levels + 2
        self.total = dp_size * 4
        high = list(range(self.levels - 1))
        low, seq, core = self.levels - 1, self.levels, self.levels + 1
        self.gather_orders = (high + [low, seq, core], high + [seq, low, core])
        self.gather_late_orders = ([seq, low] + high + [core], [low, seq] + high + [core])
        self.scatter_orders = tuple(order[::-1] for order in self.gather_orders)
        self.scatter_high_orders = tuple(order[::-1] for order in self.gather_late_orders)
        self.scatter_low_orders = ([core, low, seq] + high[::-1],) * 2

    def mine(self):
        d = lax.axis_index("dp")
        bits = [lax.rem(d // (1 << (self.levels - 1 - k)), 2) for k in range(self.levels)]
        return bits + [lax.axis_index("seq"), lax.axis_index("shard")]

    def partner(self, k):
        d, s, c = lax.axis_index("dp"), lax.axis_index("seq"), lax.axis_index("shard")
        if k == self.levels:
            return (d, 1 - s, c)
        if k == self.levels + 1:
            return (d, s, 1 - c)
        step = 1 << (self.levels - 1 - k)
        bit = lax.rem(d // step, 2)
        return (d + (1 - 2 * bit) * step, s, c)

    def index(self):
        return (lax.axis_index("dp") * 2 + lax.axis_index("seq")) * 2 + lax.axis_index("shard")

    def coords(self, index):
        return (index // 4, lax.rem(index // 2, 2), lax.rem(index, 2))

    def greet_partners(self):
        barrier = pltpu.get_barrier_semaphore()
        for k in range(self.digits):
            pl.semaphore_signal(barrier, inc=1, device_id=self.partner(k), device_id_type=MESH)
        pl.semaphore_wait(barrier, self.digits)

    def greet_all(self):
        barrier = pltpu.get_barrier_semaphore()
        me = self.index()

        @pl.loop(1, self.total)
        def _(i):
            peer = self.coords(lax.rem(me + i, self.total))
            pl.semaphore_signal(barrier, inc=1, device_id=peer, device_id_type=MESH)

        pl.semaphore_wait(barrier, self.total - 1)


def halves(width):
    cut = (width // 128 + 1) // 2 * 128
    return ((0, cut), (cut, width - cut))


def remote(src, dst, send_sem, recv_sem, peer):
    return pltpu.make_async_remote_copy(
        src_ref=src,
        dst_ref=dst,
        send_sem=send_sem,
        recv_sem=recv_sem,
        device_id=peer,
        device_id_type=MESH,
    )


def gather_kernel(cube, groups, *refs):
    shards, outs = refs[:groups], refs[groups : 2 * groups]
    own_sem, send_sem, recv_sem = refs[2 * groups :]
    cube.greet_partners()
    mine = cube.mine()
    locals_ = []
    for g in range(groups):
        copy = pltpu.make_async_copy(shards[g], outs[g].at[tuple(mine)], own_sem.at[g])
        copy.start()
        locals_.append(copy)

    def make(g, half, stage):
        order = cube.gather_orders[half]
        columns = pl.ds(*halves(shards[g].shape[-1])[half])
        done = order[:stage]
        index = tuple(slice(None) if k in done else mine[k] for k in range(cube.digits))
        place = outs[g].at[index + (slice(None), columns)]
        source = shards[g].at[:, columns] if stage == 0 else place
        return remote(
            source,
            place,
            send_sem.at[g, half, stage],
            recv_sem.at[g, half, stage],
            cube.partner(order[stage]),
        )

    copies = {}
    for g in range(groups):
        for half in range(2):
            copies[g, half, 0] = make(g, half, 0)
            copies[g, half, 0].start()
    for tick in range(cube.digits + 2 * (groups - 1)):
        for g in range(groups):
            stage = tick - 2 * g
            if not 0 <= stage < cube.digits:
                continue
            for half in range(2):
                copies[g, half, stage].wait_recv()
                if stage == 0 and half == 0:
                    locals_[g].wait()
                if stage + 1 < cube.digits:
                    copies[g, half, stage + 1] = make(g, half, stage + 1)
                    copies[g, half, stage + 1].start()
    for copy in copies.values():
        copy.wait_send()


def gather_groups(cube, shards, collective_id):
    groups = len(shards)
    lead = (2,) * cube.digits
    return pl.pallas_call(
        functools.partial(gather_kernel, cube, groups),
        out_shape=[jax.ShapeDtypeStruct(lead + s.shape, s.dtype) for s in shards],
        in_specs=[pl.BlockSpec(memory_space=pl.ANY)] * groups,
        out_specs=[pl.BlockSpec(memory_space=pl.ANY)] * groups,
        scratch_shapes=[
            pltpu.SemaphoreType.DMA((groups,)),
            pltpu.SemaphoreType.DMA((groups, 2, cube.digits)),
            pltpu.SemaphoreType.DMA((groups, 2, cube.digits)),
        ],
        compiler_params=pltpu.CompilerParams(
            collective_id=collective_id, has_side_effects=True
        ),
        name="gather_weights",
    )(*shards)


def scatter_kernel(cube, groups, *refs):
    parts, outs = refs[:groups], refs[groups : 2 * groups]
    rest = refs[2 * groups :]
    sums = rest[:groups]
    landed = rest[groups : groups + groups * 2 * cube.digits]
    own_sem, send_sem, recv_sem = rest[groups + groups * 2 * cube.digits :]
    cube.greet_partners()
    mine = cube.mine()
    last = cube.digits - 1

    def slot(g, half, stage):
        return landed[(g * 2 + half) * cube.digits + stage]

    def place(g, half, stage, bit_of):
        order = cube.scatter_orders[half]
        columns = pl.ds(*halves(outs[g].shape[-1])[half])
        index = []
        for k in range(cube.digits - 1):
            at = order.index(k)
            if at > stage:
                index.append(slice(None))
            else:
                index.append(bit_of(k) if at == stage else mine[k])
        return tuple(index) + (slice(None), columns)

    def make(g, half, stage):
        order = cube.scatter_orders[half]
        if stage == 0:
            index = (slice(None),) * last + (1 - mine[last],)
            columns = pl.ds(*halves(outs[g].shape[-1])[half])
            source = parts[g].at[index + (slice(None), columns)]
        else:
            source = sums[g].at[place(g, half, stage, lambda k: 1 - mine[k])]
        return remote(
            source,
            slot(g, half, stage),
            send_sem.at[g, half, stage],
            recv_sem.at[g, half, stage],
            cube.partner(order[stage]),
        )

    copies = {}
    locals_ = []
    for g in range(groups):
        copy = pltpu.make_async_copy(
            parts[g].at[(slice(None),) * last + (mine[last],)], sums[g], own_sem.at[g]
        )
        copy.start()
        locals_.append(copy)
        for half in range(2):
            copies[g, half, 0] = make(g, half, 0)
            copies[g, half, 0].start()

    def add(g, half, stage):
        order = cube.scatter_orders[half]
        columns = pl.ds(*halves(outs[g].shape[-1])[half])
        free = [k for k in range(last) if order.index(k) > stage]
        count = 1 << len(free)
        target, extra = sums[g], slot(g, half, stage)

        def one(i):
            digit = {k: lax.rem(i // (1 << (len(free) - 1 - n)), 2) for n, k in enumerate(free)}
            full = tuple(digit.get(k, mine[k]) for k in range(last)) + (slice(None), columns)
            short = tuple(digit[k] for k in free)
            total = target[full].astype(jnp.float32) + extra[short + (slice(None), slice(None))].astype(jnp.float32)
            if stage == last:
                outs[g][:, columns] = total
            else:
                target[full] = total.astype(target.dtype)

        if count == 1:
            one(0)
        else:
            pl.loop(0, count)(one)

    for stage in range(cube.digits):
        for g in range(groups):
            if stage == 0:
                locals_[g].wait()
            for half in range(2):
                copies[g, half, stage].wait_recv()
                add(g, half, stage)
                if stage < last:
                    copies[g, half, stage + 1] = make(g, half, stage + 1)
                    copies[g, half, stage + 1].start()
    for copy in copies.values():
        copy.wait_send()


def scatter_groups(cube, parts, collective_id):
    groups = len(parts)
    scratch = [pltpu.VMEM((2,) * (cube.digits - 1) + p.shape[-2:], p.dtype) for p in parts]
    for p in parts:
        for half in range(2):
            for stage in range(cube.digits):
                lead = (2,) * (cube.digits - 1 - stage)
                scratch.append(pltpu.VMEM(lead + (p.shape[-2], halves(p.shape[-1])[half][1]), p.dtype))
    scratch += [
        pltpu.SemaphoreType.DMA((groups,)),
        pltpu.SemaphoreType.DMA((groups, 2, cube.digits)),
        pltpu.SemaphoreType.DMA((groups, 2, cube.digits)),
    ]
    return pl.pallas_call(
        functools.partial(scatter_kernel, cube, groups),
        out_shape=[jax.ShapeDtypeStruct(p.shape[-2:], jnp.float32) for p in parts],
        in_specs=[pl.BlockSpec(memory_space=pl.ANY)] * groups,
        out_specs=[pl.BlockSpec(memory_space=pltpu.VMEM)] * groups,
        scratch_shapes=scratch,
        compiler_params=pltpu.CompilerParams(
            collective_id=collective_id, has_side_effects=True, vmem_limit_bytes=48 << 20
        ),
        name="scatter_grads",
    )(*parts)


def collect_kernel(cube, x_ref, o_ref, send_sem, recv_sem):
    me = cube.index()
    cube.greet_all()

    def make(i):
        to = lax.rem(me + i, cube.total)
        return remote(x_ref, o_ref.at[i], send_sem.at[i], recv_sem.at[i], cube.coords(to))

    @pl.loop(1, cube.total)
    def _(i):
        make(i).start()

    o_ref[0] = x_ref[...]

    @pl.loop(1, cube.total)
    def _(i):
        make(i).wait()


def collect(cube, x, collective_id):
    return pl.pallas_call(
        functools.partial(collect_kernel, cube),
        out_shape=jax.ShapeDtypeStruct((cube.total,) + x.shape, x.dtype),
        in_specs=[pl.BlockSpec(memory_space=pltpu.VMEM)],
        out_specs=pl.BlockSpec(memory_space=pltpu.VMEM),
        scratch_shapes=[
            pltpu.SemaphoreType.DMA((cube.total,)),
            pltpu.SemaphoreType.DMA((cube.total,)),
        ],
        compiler_params=pltpu.CompilerParams(
            collective_id=collective_id, has_side_effects=True
        ),
        name="collect_stats",
    )(x)


def by_matrix(j, action):
    for width in sorted(set(WIDTHS)):
        members = [i for i in range(8) if WIDTHS[i] == width]
        hit = functools.reduce(jnp.logical_or, [j == i for i in members])
        pl.when(hit)(functools.partial(action, width // 4))


def quarter_start(t):
    j, q = t // 4, lax.rem(t, 4)
    start = 0
    for i in range(8):
        start = start + jnp.where(j == i, STARTS[i] + q * (WIDTHS[i] // 4), 0)
    return pl.multiple_of(start, 128)


def owner_coords(cube, t):
    return ((t // 4) * (cube.dp_size // 8), lax.rem(t // 2, 2), lax.rem(t, 2))


def spread_kernel(cube, x_ref, o_ref, own_sem, send_sem, recv_sem):
    me = cube.index()
    repeat = cube.dp_size // 8
    d, s, c = lax.axis_index("dp"), lax.axis_index("seq"), lax.axis_index("shard")
    owner = lax.rem(d, repeat) == 0
    mine = ((d // repeat) * 2 + s) * 2 + c
    cube.greet_all()

    def send(i, wait):
        t = lax.rem(mine + i, 32)
        peer = owner_coords(cube, t)
        other = jnp.logical_or(jnp.logical_not(owner), i > 0)

        def go(width):
            src = x_ref.at[:, pl.ds(quarter_start(t), width)]
            dst = o_ref.at[me, :, pl.ds(0, width)]
            copy = remote(src, dst, send_sem.at[i], recv_sem.at[me], peer)
            if wait:
                copy.wait_send()
            else:
                copy.start()

        pl.when(other)(lambda: by_matrix(t // 4, go))

    pl.loop(0, 32)(functools.partial(send, wait=False))

    def keep(width):
        copy = pltpu.make_async_copy(
            x_ref.at[:, pl.ds(quarter_start(mine), width)],
            o_ref.at[me, :, pl.ds(0, width)],
            own_sem,
        )
        copy.start()
        copy.wait()

    def receive(width):
        @pl.loop(1, cube.total)
        def _(i):
            source = lax.rem(me + i, cube.total)
            place = o_ref.at[source, :, pl.ds(0, width)]
            remote(
                place, place, send_sem.at[0], recv_sem.at[source], cube.coords(source)
            ).wait_recv()

    @pl.when(owner)
    def _():
        by_matrix(mine // 4, keep)
        by_matrix(mine // 4, receive)

    pl.loop(0, 32)(functools.partial(send, wait=True))


def spread(cube, x, collective_id):
    return pl.pallas_call(
        functools.partial(spread_kernel, cube),
        out_shape=jax.ShapeDtypeStruct((cube.total, x.shape[0], BLOCK), x.dtype),
        in_specs=[pl.BlockSpec(memory_space=pl.ANY)],
        out_specs=pl.BlockSpec(memory_space=pl.ANY),
        scratch_shapes=[
            pltpu.SemaphoreType.DMA,
            pltpu.SemaphoreType.DMA((32,)),
            pltpu.SemaphoreType.DMA((cube.total,)),
        ],
        compiler_params=pltpu.CompilerParams(
            collective_id=collective_id, has_side_effects=True
        ),
        name="spread_momentum",
    )(x)


def restore_kernel(cube, x_ref, o_ref, own_sem, send_sem, recv_sem):
    me = cube.index()
    repeat = cube.dp_size // 8
    d, s, c = lax.axis_index("dp"), lax.axis_index("seq"), lax.axis_index("shard")
    owner = lax.rem(d, repeat) == 0
    mine = ((d // repeat) * 2 + s) * 2 + c
    cube.greet_all()

    def send_all(wait, width):
        @pl.loop(1, cube.total)
        def _(i):
            to = lax.rem(me + i, cube.total)
            src = x_ref.at[to, :, pl.ds(0, width)]
            dst = o_ref.at[:, pl.ds(quarter_start(mine), width)]
            copy = remote(src, dst, send_sem.at[i], recv_sem.at[mine], cube.coords(to))
            if wait:
                copy.wait_send()
            else:
                copy.start()

    def keep(width):
        copy = pltpu.make_async_copy(
            x_ref.at[me, :, pl.ds(0, width)],
            o_ref.at[:, pl.ds(quarter_start(mine), width)],
            own_sem,
        )
        copy.start()
        copy.wait()

    @pl.when(owner)
    def _():
        by_matrix(mine // 4, functools.partial(send_all, False))
        by_matrix(mine // 4, keep)

    def receive(i):
        t = lax.rem(mine + i, 32)
        other = jnp.logical_or(jnp.logical_not(owner), i > 0)

        def go(width):
            place = o_ref.at[:, pl.ds(quarter_start(t), width)]
            remote(
                place, place, send_sem.at[0], recv_sem.at[t], owner_coords(cube, t)
            ).wait_recv()

        pl.when(other)(lambda: by_matrix(t // 4, go))

    pl.loop(0, 32)(receive)

    @pl.when(owner)
    def _():
        by_matrix(mine // 4, functools.partial(send_all, True))


def restore(cube, x, collective_id):
    return pl.pallas_call(
        functools.partial(restore_kernel, cube),
        out_shape=jax.ShapeDtypeStruct((x.shape[1], STARTS[8]), x.dtype),
        in_specs=[pl.BlockSpec(memory_space=pl.ANY)],
        out_specs=pl.BlockSpec(memory_space=pl.ANY),
        scratch_shapes=[
            pltpu.SemaphoreType.DMA,
            pltpu.SemaphoreType.DMA((cube.total,)),
            pltpu.SemaphoreType.DMA((32,)),
        ],
        compiler_params=pltpu.CompilerParams(
            collective_id=collective_id, has_side_effects=True
        ),
        name="restore_rows",
    )(x)


def split(value):
    high = value.astype(jnp.bfloat16)
    low = (value - high.astype(jnp.float32)).astype(jnp.bfloat16)
    return high, low


def product(left, right):
    (lh, ll), (rh, rl) = left, right
    dot = functools.partial(jnp.dot, preferred_element_type=jnp.float32)
    return dot(lh, rh) + (dot(lh, rl) + dot(ll, rh))


def orthogonalize_kernel(cube, x_ref, o_ref, gram_ref, work, landed, send_sem, recv_sem):
    barrier = pltpu.get_barrier_semaphore()
    peers = (cube.partner(cube.levels + 1), cube.partner(cube.levels))
    for peer in peers:
        pl.semaphore_signal(barrier, inc=1, device_id=peer, device_id_type=MESH)
    pl.semaphore_wait(barrier, 2)
    repeat = cube.dp_size // 8
    j = lax.axis_index("dp") // repeat
    width = 0
    for i in range(8):
        width = width + jnp.where(j == i, WIDTHS[i] // 4, 0)
    column = lax.broadcasted_iota(jnp.int32, (D, BLOCK), 1)
    block = jnp.where(column < width, x_ref[...].astype(jnp.float32), 0.0)
    bh, bl = split(block)
    dot_t = lambda a, b: lax.dot_general(
        a, b, (((1,), (1,)), ((), ())), preferred_element_type=jnp.float32
    )
    gram_ref[0] = dot_t(bh, bh) + (dot_t(bh, bl) + dot_t(bl, bh))
    for step in range(2):
        copy = remote(
            gram_ref.at[step], landed.at[step], send_sem.at[step], recv_sem.at[step], peers[step]
        )
        copy.start()
        copy.wait()
        gram_ref[step + 1] = gram_ref[step] + landed[step]
    gram = gram_ref[2]
    row = lax.broadcasted_iota(jnp.int32, (D, D), 0)
    col = lax.broadcasted_iota(jnp.int32, (D, D), 1)
    eye = row == col
    square = jnp.sum(jnp.sum(jnp.where(eye, gram, 0.0), axis=1, keepdims=True), axis=0, keepdims=True)
    scale = 1.0 / (jnp.sqrt(square) + 1e-07)
    gram = gram * (scale * scale)
    block = block * scale
    for step in range(5):
        parts = split(gram)
        mixed = COEF_B * gram + COEF_C * product(parts, parts)
        mixed = jnp.where(eye, mixed + COEF_A, mixed)
        mixed_parts = split(mixed)
        block = product(mixed_parts, split(block))
        if step < 4:
            gram = product(mixed_parts, split(product(mixed_parts, parts)))
    o_ref[...] = block.astype(o_ref.dtype)


def orthogonalize_blocks(cube, x, out_dtype, collective_id):
    return pl.pallas_call(
        functools.partial(orthogonalize_kernel, cube),
        out_shape=jax.ShapeDtypeStruct((D, BLOCK), out_dtype),
        in_specs=[pl.BlockSpec(memory_space=pltpu.VMEM)],
        out_specs=pl.BlockSpec(memory_space=pltpu.VMEM),
        scratch_shapes=[
            pltpu.VMEM((3, D, D), jnp.float32),
            pltpu.VMEM((8, 128), jnp.float32),
            pltpu.VMEM((2, D, D), jnp.float32),
            pltpu.SemaphoreType.DMA((2,)),
            pltpu.SemaphoreType.DMA((2,)),
        ],
        compiler_params=pltpu.CompilerParams(
            collective_id=collective_id, has_side_effects=True, vmem_limit_bytes=48 << 20
        ),
        name="orthogonalize",
    )(x)

def with_halo(value, sides, width):
    for axis, dim in sides:
        devices, length = (lax.axis_size(axis), value.shape[dim])
        up = [(i, (i + 1) % devices) for i in range(devices - 1)]
        down = [(j, i) for i, j in up]
        last = lax.slice_in_dim(value, length - width, length, axis=dim)
        first = lax.slice_in_dim(value, 0, width, axis=dim)
        before = lax.ppermute(last, axis, up)
        after = lax.ppermute(first, axis, down)
        value = jnp.concatenate([before, value, after], axis=dim)
    return value


def matmul(left, right):
    return jnp.dot(left, right, preferred_element_type=jnp.float32)


def matmul_right_t(left, right):
    return lax.dot_general(
        left, right, (((1,), (1,)), ((), ())), preferred_element_type=jnp.float32
    )


def matmul_left_t(left, right):
    return lax.dot_general(
        left, right, (((0,), (0,)), ((), ())), preferred_element_type=jnp.float32
    )


def layer_norm(field, gain):
    centre = jnp.mean(field, axis=-1, keepdims=True)
    shifted = field - centre
    inverse = lax.rsqrt(jnp.mean(shifted * shifted, axis=-1, keepdims=True) + EPS_NORM)
    normed = shifted * inverse
    return (normed * gain, normed, inverse)


def norm_back(grad_out, normed, inverse, gain):
    scaled = grad_out * gain
    grad_in = inverse * (
        scaled
        - jnp.mean(scaled, axis=-1, keepdims=True)
        - normed * jnp.mean(scaled * normed, axis=-1, keepdims=True)
    )
    return (grad_in, jnp.sum(grad_out * normed, axis=0))


def silu_slope(values):
    sigma = jax.nn.sigmoid(values)
    return sigma * (1.0 + values * (1.0 - sigma))


def ffn_forward(field, gain, w_in, w_back):
    normed_out, normed, inverse = layer_norm(field, gain)
    lifted = normed_out.astype(jnp.bfloat16)
    hidden_pre = matmul(lifted, w_in)
    hidden_act = jax.nn.silu(hidden_pre).astype(jnp.bfloat16)
    return (
        field + 0.5 * matmul_right_t(hidden_act, w_back),
        (lifted, hidden_pre, hidden_act, normed, inverse),
    )


def ffn_backward(grad, saved, gain, w_in, w_back):
    lifted, hidden_pre, hidden_act, normed, inverse = saved
    grad_branch = (0.5 * grad).astype(jnp.bfloat16)
    grad_back = matmul_left_t(grad_branch, hidden_act)
    grad_act = matmul(grad_branch, w_back)
    grad_pre = (grad_act * silu_slope(hidden_pre)).astype(jnp.bfloat16)
    grad_in = matmul_left_t(lifted, grad_pre)
    grad_field, grad_gain = norm_back(matmul_right_t(grad_pre, w_in), normed, inverse, gain)
    return (grad + grad_field, grad_in, grad_back, grad_gain)


def depthwise(wide, kernel, count):
    total = wide[0:count] * kernel[:, 0]
    for tap_idx in range(1, K):
        total = total + wide[tap_idx : tap_idx + count] * kernel[:, tap_idx]
    return total


def spread_rows(window, count, keys_len):
    padded = jnp.concatenate([window, jnp.zeros((1,), window.dtype)])
    tiled = jnp.broadcast_to(padded[None, :], (count, keys_len + count)).reshape(-1)
    shaped = tiled[: count * (keys_len + count - 1)].reshape(count, keys_len + count - 1)
    return shaped[:, count - 1 : count - 1 + keys_len]


def collect_rows(grid, count, keys_len):
    placed = jnp.concatenate([jnp.zeros((count, count - 1), grid.dtype), grid], axis=1).reshape(-1)
    placed = jnp.concatenate([placed, jnp.zeros((count,), grid.dtype)])
    return jnp.sum(placed.reshape(count, keys_len + count), axis=0)[: keys_len + count - 1]


def attention_scores(query, keys, offsets, first_row, row_start, block, head_idx):
    length = keys.shape[0]
    columns = slice(head_idx * DH, (head_idx + 1) * DH)
    anchor = length - block - first_row - row_start
    window = lax.dynamic_slice_in_dim(offsets[head_idx], anchor, length + block - 1)
    product = matmul_right_t(query[row_start : row_start + block, columns], keys[:, columns])
    return product * DH ** (-0.5) + spread_rows(window, block, length)


def attention_forward(query, keys, values, offsets, first_row):
    total_rows = query.shape[0]
    block = min(512, total_rows)
    head_outs = []
    head_lse = []
    for head_idx in range(H):
        scores = attention_scores(query, keys, offsets, first_row, 0, block, head_idx)
        row_max = jnp.max(scores, axis=1, keepdims=True)
        shifted_exp = jnp.exp(scores - row_max)
        row_total = jnp.sum(shifted_exp, axis=1, keepdims=True)
        prob_low = (shifted_exp / row_total).astype(jnp.bfloat16)
        head_outs.append(matmul(prob_low, values[:, head_idx * DH : (head_idx + 1) * DH]))
        head_lse.append((row_max + jnp.log(row_total))[:, 0])
    out_blocks = jnp.concatenate(head_outs, axis=1)
    lse_blocks = jnp.stack(head_lse, axis=0)
    return (out_blocks, lse_blocks)


def attention_backward(query, keys, values, offsets, first_row, log_total, grad_attended, delta):
    total_rows = query.shape[0]
    length = keys.shape[0]
    block = min(512, total_rows)
    scale = DH ** (-0.5)
    key_parts = [jnp.zeros((length, DH), jnp.float32) for head_idx in range(H)]
    value_parts = [jnp.zeros((length, DH), jnp.float32) for head_idx in range(H)]
    offset_rows = [jnp.zeros((2 * length - 1,), jnp.float32) for head_idx in range(H)]
    head_grads = []
    for head_idx in range(H):
        columns = slice(head_idx * DH, (head_idx + 1) * DH)
        scores = attention_scores(query, keys, offsets, first_row, 0, block, head_idx)
        prob = jnp.exp(scores - log_total[head_idx, 0:block][:, None])
        prob_low = prob.astype(jnp.bfloat16)
        grad_piece = grad_attended[0:block, columns]
        value_parts[head_idx] = matmul_left_t(prob_low, grad_piece)
        grad_prob = matmul_right_t(grad_piece, values[:, columns])
        grad_score = prob * (grad_prob - delta[0:block, head_idx][:, None])
        score_low = grad_score.astype(jnp.bfloat16)
        head_grads.append(matmul(score_low, keys[:, columns]) * scale)
        key_parts[head_idx] = matmul_left_t(score_low, query[0:block, columns]) * scale
        anchor = length - block - first_row - 0
        offset_rows[head_idx] = lax.dynamic_update_slice_in_dim(
            offset_rows[head_idx], collect_rows(grad_score, block, length), anchor, 0
        )
    query_blocks = jnp.concatenate(head_grads, axis=1)
    return (
        query_blocks,
        jnp.concatenate(key_parts, axis=1),
        jnp.concatenate(value_parts, axis=1),
        jnp.stack(offset_rows, axis=0),
    )


def mean_last(value):
    return jnp.mean(value, axis=-1, keepdims=True)


def normalize(field):
    shifted = field - mean_last(field)
    inverse = lax.rsqrt(mean_last(shifted * shifted) + EPS_NORM)
    return shifted * inverse, inverse


def norm_grad(grad_out, normed, inverse, gain):
    scaled = grad_out * gain
    grad_in = inverse * (scaled - mean_last(scaled) - normed * mean_last(scaled * normed))
    return grad_in, jnp.sum(grad_out * normed, axis=0, keepdims=True)


def row_to_tile(ref, base, row):
    for k in range(4):
        ref[base + k : base + k + 1, :] = row[:, 128 * k : 128 * (k + 1)]


def tile_to_row(tile):
    return jnp.concatenate([tile[k : k + 1, :] for k in range(4)], axis=1)


def skew(row, count):
    sub = lax.broadcasted_iota(jnp.int32, (8, 512), 0)
    block = jnp.broadcast_to(row, (8, 512))
    for bit in (1, 2, 4):
        block = jnp.where((sub // bit) % 2 == 1, pltpu.roll(block, bit, 1), block)
    size = 8
    while size < count:
        block = jnp.concatenate([block, pltpu.roll(block, size, 1)], axis=0)
        size *= 2
    return block


def unskew_sum(grid):
    size = grid.shape[0] // 2
    while size >= 8:
        grid = grid[:size] + pltpu.roll(grid[size:], 512 - size, 1)
        size //= 2
    sub = lax.broadcasted_iota(jnp.int32, (8, 512), 0)
    for bit in (1, 2, 4):
        grid = jnp.where((sub // bit) % 2 == 1, pltpu.roll(grid, 512 - bit, 1), grid)
    return jnp.sum(grid, axis=0, keepdims=True)


def tile_ranges(start, count, parts):
    ranges = []
    for n in range(parts, 0, -1):
        size = -(-count // n)
        ranges.append((128 * start, 128 * size))
        start, count = start + size, count - size
    return ranges


def gather_chunks(widths):
    chunks = []
    for g in range(2):
        ranges = tile_ranges(0, widths[g] // 128, 4)
        chunks += [(g, ranges[0:2], 0), (g, ranges[2:4], 0)]
    tiles = widths[2] // 128
    cut = tiles * 2 // 5
    chunks.append((2, tile_ranges(0, cut, 2), 0))
    ranges = tile_ranges(cut, tiles - cut, 6)
    return chunks + [(2, ranges[2 * n : 2 * n + 2], 1) for n in range(3)]


class Gather:
    def __init__(self, cube, mine, bands, send_sem, recv_sem):
        self.cube, self.mine, self.bands = cube, mine, bands
        self.chunks = gather_chunks([band.shape[-1] for band in bands])
        self.send_sem, self.recv_sem = send_sem, recv_sem
        self.copies = {}
        self.events = list(GATHER_EVENTS)
        self.last = cube.digits - 1

    def start(self, n, stage):
        g, pair, kind = self.chunks[n]
        for half in range(2):
            order = (self.cube.gather_orders, self.cube.gather_late_orders)[kind][half]
            done = order[:stage]
            index = tuple(
                slice(None) if k in done else self.mine[k] for k in range(self.cube.digits)
            )
            place = self.bands[g].at[index + (slice(None), pl.ds(*pair[half]))]
            copy = remote(
                place,
                place,
                self.send_sem.at[n, half, stage],
                self.recv_sem.at[n, half, stage],
                self.cube.partner(order[stage]),
            )
            copy.start()
            self.copies[n, half, stage] = copy

    def begin(self):
        self.start(0, 0)
        self.start(5, 0)

    def advance(self, n, stage):
        for half in range(2):
            self.copies[n, half, stage].wait_recv()
        if stage < self.last and (n, stage + 1) not in GATHER_HELD:
            self.start(n, stage + 1)
        for other in GATHER_AFTER.get((n, stage), ()):
            self.start(*other)

    def run_to(self, n, stage):
        while (n, stage) in self.events:
            self.advance(*self.events.pop(0))

    def finish(self):
        for copy in self.copies.values():
            copy.wait_send()


class Scatter:
    def __init__(self, cube, mine, bands, landed, outs, send_sem, recv_sem):
        self.cube, self.mine, self.landed = cube, mine, landed
        kinds = (cube.scatter_orders, cube.scatter_high_orders, cube.scatter_low_orders)
        self.chunks = [(bands[g], outs[g], pair) for g, pair, _ in SCATTER_CHUNKS]
        self.orders = [kinds[kind] for _, _, kind in SCATTER_CHUNKS]
        self.send_sem, self.recv_sem = send_sem, recv_sem
        self.copies = {}

    def start(self, n, stage):
        band, _, pair = self.chunks[n]
        for half in range(2):
            order = self.orders[n][half]
            index = []
            for k in range(self.cube.digits):
                at = order.index(k)
                if at > stage:
                    index.append(slice(None))
                else:
                    index.append(1 - self.mine[k] if at == stage else self.mine[k])
            copy = remote(
                band.at[tuple(index) + (slice(None), pl.ds(*pair[half]))],
                self.landed[(n * 2 + half) * self.cube.digits + stage],
                self.send_sem.at[n, half, stage],
                self.recv_sem.at[n, half, stage],
                self.cube.partner(order[stage]),
            )
            copy.start()
            self.copies[n, half, stage] = copy

    def add(self, n, half, stage):
        order = self.orders[n][half]
        band, out, pair = self.chunks[n]
        columns = pl.ds(*pair[half])
        free = [k for k in range(self.cube.digits) if order.index(k) > stage]
        extra = self.landed[(n * 2 + half) * self.cube.digits + stage]
        everything = (slice(None), columns)

        def one(i):
            digit = {
                k: lax.rem(i // (1 << (len(free) - 1 - m)), 2) for m, k in enumerate(free)
            }
            full = tuple(digit.get(k, self.mine[k]) for k in range(self.cube.digits)) + everything
            short = tuple(digit[k] for k in free) + (slice(None), slice(None))
            if free:
                band[full] = band[full] + extra[short]
            else:
                out[:, columns] = band[full].astype(jnp.float32) + extra[short].astype(jnp.float32)

        if free:
            pl.loop(0, 1 << len(free))(one)
        else:
            one(0)

    def advance(self, n, stage):
        for half in range(2):
            self.copies[n, half, stage].wait_recv()
            self.add(n, half, stage)
        if stage + 1 < self.cube.digits:
            self.start(n, stage + 1)

    def finish(self):
        for copy in self.copies.values():
            copy.wait_send()


class Collect:
    def __init__(self, cube, tile, slots, send_sem, recv_sem):
        self.cube, self.tile, self.slots = cube, tile, slots
        self.send_sem, self.recv_sem = send_sem, recv_sem

    def make(self, i):
        to = self.cube.coords(lax.rem(self.cube.index() + i, self.cube.total))
        return remote(
            self.tile, self.slots.at[i], self.send_sem.at[i], self.recv_sem.at[i], to
        )

    def start(self):
        pl.loop(1, self.cube.total)(lambda i: self.make(i).start())
        self.slots[0] = self.tile[...]

    def arrive(self):
        pl.loop(1, self.cube.total)(lambda i: self.make(i).wait())

    def total(self):
        result = self.slots[0]
        for i in range(1, self.cube.total):
            result = result + self.slots[i]
        return result


def share_columns(j):
    place = j // 2 if j % 2 else 1 - j // 2
    return slice(FF * place, FF * (place + 1))


def matrix_of(d):
    return sum(jnp.where(d == OWNER_PLACES[i], i, 0) for i in range(8))


def pack_small(target, turn, rel, vec, depth):
    rows = target.shape[0]
    turn[...] = jnp.zeros_like(turn)
    turn[0:7, 0:rows] = vec[...]
    target[...] = jnp.zeros_like(target)
    target[0 : rel.shape[0], SMALL_REL : SMALL_REL + H] = rel[...]
    target[:, SMALL_VEC : SMALL_VEC + 7] = jnp.transpose(turn[...])[0:rows, 0:7]
    target[:, SMALL_DEPTH : SMALL_DEPTH + K] = depth[...]


OWNER_PLACES = (2, 3, 5, 4, 0, 1, 7, 6)


def owner_place(cube, t):
    return (OWNER_PLACES[t // 4] * (cube.dp_size // 8), t // 2 % 2, t % 2)


class Momenta:
    def __init__(self, cube, r):
        self.cube, self.r = cube, r
        self.me = cube.index()
        self.repeat = cube.dp_size // 8
        d = lax.axis_index("dp")
        self.is_owner = lax.rem(d, self.repeat) == 0
        self.matrix = matrix_of(d // self.repeat)
        self.quarter = lax.axis_index("seq") * 2 + lax.axis_index("shard")
        self.owned_index = self.matrix * 4 + self.quarter

    def holds(self, t):
        return jnp.logical_and(self.is_owner, self.owned_index == t)

    def rows(self, j):
        r = self.r
        if j < 4:
            old, share = ((r.m_up, r.m_down)[j // 2], (r.share_first, r.share_second)[j % 2])
            return old[:, FF * (j % 2) : FF * (j % 2 + 1)], share[:, share_columns(j)]
        start = STARTS[j] - STARTS[4]
        old = (r.m_qkv, r.m_out, r.m_glu, r.m_point)[j - 4]
        return old[...], r.share_middle[:, start : start + WIDTHS[j]]

    def copy(self, t):
        width = WIDTHS[t // 4] // 4
        r = self.r
        return remote(
            r.leaving.at[t, :, pl.ds(0, width)],
            r.owned.at[self.me, :, pl.ds(0, width)],
            r.m_send.at[t],
            r.m_recv.at[self.me],
            owner_place(self.cube, t),
        )

    def send(self, j):
        old, share = self.rows(j)
        value = (MOMENTUM * old + share).astype(jnp.bfloat16)
        width = WIDTHS[j] // 4
        for q in range(4):
            t = 4 * j + q
            part = value[:, width * q : width * (q + 1)]
            self.r.leaving[t, :, 0:width] = part
            pl.when(jnp.logical_not(self.holds(t)))(lambda t=t: self.copy(t).start())

            @pl.when(self.holds(t))
            def _(part=part, width=width):
                self.r.owned[self.me, :, 0:width] = part

    def receive(self):
        r, cube = self.r, self.cube

        def go(width):
            @pl.loop(1, cube.total)
            def _(i):
                source = lax.rem(self.me + i, cube.total)
                place = r.owned.at[source, :, pl.ds(0, width)]
                remote(
                    place, place, r.m_send.at[0], r.m_recv.at[source], cube.coords(source)
                ).wait_recv()

        pl.when(self.is_owner)(lambda: by_matrix(self.matrix, go))

    def back(self, i, width):
        r, cube = self.r, self.cube
        to = lax.rem(self.me + i, cube.total)
        return remote(
            r.solved.at[to, :, pl.ds(0, width)],
            r.returned.at[self.owned_index, :, pl.ds(0, width)],
            r.b_send.at[i],
            r.b_recv.at[self.owned_index],
            cube.coords(to),
        )

    def keep(self, width):
        r = self.r
        return pltpu.make_async_copy(
            r.solved.at[self.me, :, pl.ds(0, width)],
            r.returned.at[self.owned_index, :, pl.ds(0, width)],
            r.k_sem,
        )

    def send_back(self):
        r = self.r

        def go(width):
            pl.loop(1, self.cube.total)(lambda i: self.back(i, width).start())
            self.keep(width).start()

        pl.when(self.is_owner)(lambda: by_matrix(self.matrix, go))

    def receive_back(self):
        r = self.r
        for t in range(32):
            place = r.returned.at[t, :, pl.ds(0, WIDTHS[t // 4] // 4)]
            copy = remote(
                place, place, r.b_send.at[0], r.b_recv.at[t], owner_place(self.cube, t)
            )
            pl.when(jnp.logical_not(self.holds(t)))(copy.wait_recv)

    def finish(self):
        for t in range(32):
            pl.when(jnp.logical_not(self.holds(t)))(lambda t=t: self.copy(t).wait_send())

        def go(width):
            pl.loop(1, self.cube.total)(lambda i: self.back(i, width).wait_send())
            self.keep(width).wait()

        pl.when(self.is_owner)(lambda: by_matrix(self.matrix, go))


def symmetric_product(left, right):
    half = D // 2
    (lh, ll), (rh, rl) = left, right
    top = product((lh[:half], ll[:half]), right)
    corner = product((lh[half:], ll[half:]), (rh[:, half:], rl[:, half:]))
    low = jnp.concatenate([jnp.transpose(top[:, half:]), corner], axis=1)
    return jnp.concatenate([top, low], axis=0)


GRAM_SHARES = (
    ((0, 0), (0, 1), (0, 2), (0, 3), (3, 3)),
    ((1, 1), (1, 2), (1, 3), (2, 2), (2, 3)),
)


def orthogonalize(cube, r):
    f32 = jnp.float32
    core, seq = lax.axis_index("shard"), lax.axis_index("seq")
    block = r.owned.reshape(D, BLOCK)
    lines = [slice(128 * i, 128 * (i + 1)) for i in range(4)]
    peers = (cube.partner(cube.levels + 1), cube.partner(cube.levels))
    count = len(GRAM_SHARES[0])

    def piece(step, n):
        source, target, peer = (
            (r.packed.at[1 - core, n], r.packed_in.at[0, n], peers[0]),
            (r.summed.at[n], r.packed_in.at[1, n], peers[1]),
            (r.whole.at[core, n], r.whole.at[core, n], peers[0]),
        )[step]
        return remote(source, target, r.n_send.at[step, n], r.n_recv.at[step, n], peer)

    for n in range(count):
        for share in range(2):
            i, j = GRAM_SHARES[share][n]
            r.packed[share, n] = matmul_right_t(block[lines[i], :], block[lines[j], :])
        piece(0, n).start()
    for n in range(count):
        piece(0, n).wait()
        r.summed[n] = r.packed[core, n] + r.packed_in[0, n]
        piece(1, n).start()
    for n in range(count):
        piece(1, n).wait()
        r.whole[core, n] = r.summed[n] + r.packed_in[1, n]
        piece(2, n).start()
    for n in range(count):
        piece(2, n).wait()
    for share in range(2):
        for n, (i, j) in enumerate(GRAM_SHARES[share]):
            value = r.whole[share, n]
            r.gram[lines[i], lines[j]] = value
            if i != j:
                r.gram[lines[j], lines[i]] = jnp.transpose(value)
    row = lax.broadcasted_iota(jnp.int32, (D, D), 0)
    col = lax.broadcasted_iota(jnp.int32, (D, D), 1)
    eye = row == col
    gram = r.gram[...]
    square = jnp.sum(
        jnp.sum(jnp.where(eye, gram, 0.0), axis=1, keepdims=True), axis=0, keepdims=True
    )
    scale = 1.0 / (jnp.sqrt(square) + 1e-07)
    gram = gram * (scale * scale)
    value = None
    for step in range(5):
        parts = split(gram)
        mixed = COEF_B * gram + COEF_C * symmetric_product(parts, parts)
        mixed = jnp.where(eye, mixed + COEF_A, mixed)
        high, low = split(mixed)
        if step == 0:
            start_high, start_low = split(mixed * scale)
            value = matmul(start_high, block[...]) + matmul(start_low, block[...])
        elif step < 4:
            value = product((high, low), split(value))
        else:
            value = matmul(high, value.astype(jnp.bfloat16))
        if step < 4:
            inner = symmetric_product((high, low), parts)
            gram = symmetric_product((high, low), split(inner))
    r.solved.reshape(D, BLOCK)[...] = value.astype(jnp.bfloat16)


SMALL_REL, SMALL_VEC, SMALL_DEPTH = 0, H, H + 7
SMALL_END = H + 7 + K
EDGE = 16
GATHER_EVENTS = (
    ((5, 0), (5, 1), (0, 0), (6, 0), (6, 1), (7, 0), (0, 1), (1, 0), (7, 1), (0, 2))
    + ((1, 1), (2, 0), (2, 1), (3, 0), (1, 2), (0, 3), (3, 1), (4, 0), (0, 4), (4, 1))
    + ((2, 2), (5, 2), (3, 2), (1, 3), (1, 4), (6, 2), (5, 3), (4, 2), (2, 3), (5, 4))
    + ((2, 4), (3, 3), (7, 2), (6, 3), (3, 4), (6, 4), (4, 3), (7, 3), (4, 4), (7, 4))
)
SCATTER_EVENTS = (
    ((0, 1), (3, 0), (1, 1), (4, 0), (2, 1), (5, 0), (3, 1), (6, 1), (0, 2), (1, 2), (4, 1))
    + ((2, 2), (5, 1), (6, 2), (3, 2), (1, 3), (2, 3), (0, 3), (4, 2), (3, 3), (1, 4), (2, 4))
    + ((0, 4), (5, 2), (6, 3), (4, 3), (3, 4), (6, 4), (5, 3), (4, 4), (5, 4))
)
SCATTER_STORES = ((4,), (), (), (), (), (2,), (3,))
EARLY_LOADS = tuple("w_up w_down w_qkv w_out".split()) + tuple("w_glu w_point rel vec".split())
EARLY_LOADS += tuple("depth m_rel m_vec m_depth".split())
SCATTER_MATRICES = ((3,), (1,), (5,), (4,), (2,), (0,), (6, 7))
GATHER_HELD = ((5, 2), (6, 2), (7, 2))
GATHER_AFTER = {
    (0, 0): [(1, 0)],
    (1, 0): [(2, 0)],
    (2, 0): [(3, 0)],
    (3, 0): [(4, 0)],
    (5, 0): [(6, 0)],
    (6, 0): [(7, 0)],
    (4, 1): [(5, 2)],
    (5, 2): [(6, 2)],
    (6, 2): [(7, 2)],
}
FIRST_READY, MIDDLE_READY, SECOND_READY = (1, 4), (3, 4), (7, 4)
SCATTER_CHUNKS = (
    (0, tile_ranges(16, 16, 2), 1),
    (0, tile_ranges(0, 16, 2), 2),
    (1, tile_ranges(12, 4, 2), 0),
    (1, tile_ranges(0, 12, 2), 0),
    (2, tile_ranges(0, 16, 2), 0),
    (2, tile_ranges(16, 17, 2), 0),
    (1, tile_ranges(16, 12, 2), 1),
)


def step_kernel(cube, r):
    bf16, f32 = jnp.bfloat16, jnp.float32
    x_ref, cot_ref, bucket_ref = r.inputs, r.cotangent, r.bucket
    tokens = x_ref.shape[0]
    token_total = tokens * cube.total
    rows = r.w_up.shape[0]
    rel_rows = r.rel.shape[0]
    mine = cube.mine()
    seq = lax.axis_index("seq")
    early = seq == 0
    first_row = pl.multiple_of(seq * tokens, tokens)
    other_row = pl.multiple_of((1 - seq) * tokens, tokens)
    across = cube.partner(cube.levels)
    lengths = [ref.shape[-1] for ref in (r.first, r.middle, r.second)]
    first, middle, second, d_first, d_middle, d_second = (
        ref.reshape(D, ref.shape[-1])
        for ref in (r.first, r.middle, r.second, r.d_first, r.d_middle, r.d_second)
    )
    a, xh = r.a, r.xh

    barrier = pltpu.get_barrier_semaphore()
    me = cube.index()
    momenta = Momenta(cube, r)
    for load in r.loads.values():
        load.start()
    r.owned[...] = jnp.zeros_like(r.owned)

    @pl.loop(1, cube.total)
    def _(i):
        peer = cube.coords(lax.rem(me + i, cube.total))
        pl.semaphore_signal(barrier, inc=1, device_id=peer, device_id_type=MESH)

    for name in EARLY_LOADS:
        r.loads[name].wait()
    pack_small(r.small, r.turn, r.rel, r.vec, r.depth)
    pack_small(r.m_small, r.turn, r.m_rel, r.m_vec, r.m_depth)
    own = tuple(mine)
    r.first[own + (slice(None), slice(FF, 2 * FF))] = r.w_up[:, :FF].astype(bf16)
    r.first[own + (slice(None), slice(0, FF))] = r.w_down[:, :FF].astype(bf16)
    r.first[own + (slice(None), slice(2 * FF, lengths[0]))] = r.small[...].astype(bf16)
    r.middle[own + (slice(None), slice(0, 3 * D))] = r.w_qkv[...].astype(bf16)
    r.middle[own + (slice(None), slice(3 * D, 4 * D))] = r.w_out[...].astype(bf16)
    r.middle[own + (slice(None), slice(4 * D, 6 * D))] = r.w_glu[...].astype(bf16)
    r.middle[own + (slice(None), slice(6 * D, 7 * D))] = r.w_point[...].astype(bf16)
    r.second[own + (slice(None), slice(0, FF))] = r.w_up[:, FF:].astype(bf16)
    r.second[own + (slice(None), slice(FF, 2 * FF))] = r.w_down[:, FF:].astype(bf16)
    pl.semaphore_wait(barrier, cube.total - 1)

    gather = Gather(
        cube, mine, (r.first, r.middle, r.second), r.g_send, r.g_recv
    )
    scatter = Scatter(
        cube,
        mine,
        (r.d_second, r.d_middle, r.d_first),
        r.land,
        (r.share_second, r.share_middle, r.share_first),
        r.s_send,
        r.s_recv,
    )

    gather.begin()
    for name in [name for name in r.loads if name not in EARLY_LOADS]:
        r.loads[name].wait()
    xh0, inv0 = normalize(x_ref[...])
    xh[0] = xh0
    rho = lax.broadcasted_iota(jnp.int32, (D, bucket_ref.shape[1]), 0)
    bucket_of = jnp.where(rho % rows < rel_rows, (rho // rows) * rel_rows + rho % rows, -2)
    r.hit[...] = jnp.zeros_like(r.hit)
    offset_count = bucket_ref.shape[1]
    r.hit[:, 0:offset_count] = (bucket_ref[...] == bucket_of).astype(f32).astype(bf16)
    gather.run_to(*FIRST_READY)

    small = r.small_t
    small[...] = jnp.transpose(first[:, 2 * FF : 2 * FF + 128].astype(f32))
    gains = [small[SMALL_VEC + i : SMALL_VEC + i + 1, :] for i in range(7)]
    taps = [small[SMALL_DEPTH + k : SMALL_DEPTH + k + 1, :] for k in range(K)]
    CH = 512

    def ffn_forward_fused(index, field, normed, up, down, u_ref, s_ref):
        low = (normed * gains[(0, 1, 2, 3)[index]]).astype(bf16)
        a[index] = low
        for c in range(0, FF, CH):
            u = matmul(low, up[:, c : c + CH])
            u_ref[:, c : c + CH] = u
            s_ref[:, c : c + CH] = (u * jax.nn.sigmoid(u)).astype(bf16)
        return field + 0.5 * matmul_right_t(s_ref[...], down[...])

    down1, up1 = first.at[:, pl.ds(0, FF)], first.at[:, pl.ds(FF, FF)]
    up2, down2 = second.at[:, pl.ds(0, FF)], second.at[:, pl.ds(FF, FF)]
    section1 = ffn_forward_fused(0, x_ref[...], xh[0], up1, down1, r.u1, r.s1)
    r.sec1[...] = section1
    xh1, inv1 = normalize(section1)
    xh[1] = xh1
    a[1] = (xh1 * gains[1]).astype(bf16)
    offsets = matmul(small[0:8, :].astype(bf16), r.hit[...])
    offsets = jnp.where(
        early, pltpu.roll(offsets, 257, 1), pltpu.roll(offsets, (tokens + 257) % 512, 1)
    )
    for h in range(H):
        r.bias[h] = skew(offsets[h : h + 1, :], tokens)[:, : 2 * tokens]
    gather.run_to(*MIDDLE_READY)

    q_ref, kv = r.q, r.kv
    kv[pl.ds(first_row, tokens), :] = matmul(a[1], middle[:, D : 3 * D]).astype(bf16)
    kv_copy = remote(
        kv.at[pl.ds(first_row, tokens)],
        kv.at[pl.ds(first_row, tokens)],
        r.kv_send,
        r.kv_recv,
        across,
    )
    kv_copy.start()
    q_ref[...] = matmul(a[1], middle[:, :D]).astype(bf16)
    gather.run_to(4, 3)
    kv_copy.wait_recv()
    lane = lax.broadcasted_iota(jnp.int32, (1, 128), 1)
    lane_masks = [(lane // DH == e).astype(f32) for e in range(2)]
    low_masks = [m.astype(bf16) for m in lane_masks]
    scale = DH ** (-0.5)
    for p in range(H // 2):
        columns = slice(128 * p, 128 * (p + 1))
        k_pair, v_pair = kv[:, columns], kv[:, D + 128 * p : D + 128 * (p + 1)]
        merged = None
        for e in range(2):
            q_head = q_ref[:, columns] * low_masks[e]
            scores = matmul_right_t(q_head, k_pair) * scale + r.bias[2 * p + e]
            shifted = jnp.exp(scores - jnp.max(scores, axis=1, keepdims=True))
            prob = shifted / jnp.sum(shifted, axis=1, keepdims=True)
            r.prob[2 * p + e] = prob
            out = matmul(prob.astype(bf16), v_pair) * lane_masks[e]
            merged = out if merged is None else merged + out
        r.att[:, columns] = merged
    gather.run_to(*SECOND_READY)
    att_low = r.att[...].astype(bf16)
    r.att_low[...] = att_low
    section2 = r.sec1[...] + matmul(att_low, middle[:, 3 * D : 4 * D])
    r.sec2[...] = section2
    xh2, inv2 = normalize(section2)
    xh[2] = xh2
    a[2] = (xh2 * gains[2]).astype(bf16)
    gate_first = matmul(a[2], middle[:, 4 * D : 5 * D])
    sig = jax.nn.sigmoid(matmul(a[2], middle[:, 5 * D : 6 * D]))
    r.gate[...] = gate_first
    r.sig[...] = sig
    wide = r.wide
    wide[EDGE : EDGE + tokens, :] = gate_first * sig
    edge_row = pl.multiple_of(EDGE + (1 - seq) * (tokens - EDGE), EDGE)
    halo_copy = remote(
        wide.at[pl.ds(edge_row, EDGE)], r.halo, r.halo_send, r.halo_recv, across
    )
    halo_copy.start()
    zero_edge = jnp.zeros((EDGE, D), f32)
    halo_copy.wait()
    wide[0:EDGE, :] = jnp.where(early, zero_edge, r.halo[...])
    wide[EDGE + tokens :, :] = jnp.where(early, r.halo[...], zero_edge)
    conv_ref = r.conv
    for b in range(D // 128):
        cols = slice(128 * b, 128 * (b + 1))
        total = jnp.zeros((tokens, 128), f32)
        for k in range(K):
            total = total + wide[k + 1 : k + 1 + tokens, cols] * taps[k][:, cols]
        conv_ref[:, cols] = total
    conv = conv_ref[...]
    part_sum = jnp.sum(conv, axis=0, keepdims=True)
    part_off = conv - part_sum * (1.0 / tokens)
    part_square = jnp.sum(part_off * part_off, axis=0, keepdims=True)
    row_to_tile(r.tile1, 0, part_sum)
    row_to_tile(r.tile1, 4, part_square)
    stats = Collect(cube, r.tile1, r.slots1, r.c1_send, r.c1_recv)
    stats.start()
    stats.arrive()
    sums = stats.total()
    mean4 = sums[0:4] * (1.0 / token_total)
    spread4 = jnp.zeros((4, 128), f32)
    for i in range(cube.total):
        off = r.slots1[i][0:4] * (1.0 / tokens) - mean4
        spread4 = spread4 + off * off
    var4 = (sums[4:8] + spread4 * tokens) * (1.0 / token_total)
    mean = tile_to_row(mean4)
    inv_std = tile_to_row(lax.rsqrt(var4 + EPS_BATCH))

    xb = (conv_ref[...] - mean) * inv_std
    r.xb[...] = xb
    bn = xb * gains[5] + gains[6]
    r.bn[...] = bn
    sw = (bn * jax.nn.sigmoid(bn)).astype(bf16)
    r.sw[...] = sw
    section3 = r.sec2[...] + matmul(sw, middle[:, 6 * D : 7 * D])
    xh3, inv3 = normalize(section3)
    xh[3] = xh3
    section4 = ffn_forward_fused(3, section3, xh3, up2, down2, r.u2, r.s2)
    xh4, inv4 = normalize(section4)
    r.outputs[...] = xh4 * gains[4]
    r.stores[0].start()

    sg = r.small_grad
    sg[...] = jnp.zeros_like(sg)
    cot = cot_ref[...]
    d4, sg[SMALL_VEC + 4 : SMALL_VEC + 5, :] = norm_grad(cot, xh4, inv4, gains[4])

    def slope(value):
        sigma = jax.nn.sigmoid(value)
        return sigma * (1.0 + value * (1.0 - sigma))

    def slopes(low, down, u_ref, du_ref):
        for c in range(0, FF, CH):
            act = matmul(low, down[:, c : c + CH])
            du_ref[:, c : c + CH] = (act * slope(u_ref[:, c : c + CH])).astype(bf16)

    def weight_grad(left, right_ref, target, start, width):
        for c in range(0, width, CH):
            target[:, start + c : start + c + CH] = matmul_left_t(
                left, right_ref[:, c : c + CH]
            ).astype(bf16)

    r.e_low[...] = (0.5 * d4).astype(bf16)
    slopes(r.e_low[...], down2, r.u2, r.du)
    back = matmul_right_t(r.du[...], up2[...])
    part, sg[SMALL_VEC + 3 : SMALL_VEC + 4, :] = norm_grad(back, xh[3], inv3, gains[3])
    d3 = d4 + part
    r.d[...] = d3
    e3 = d3.astype(bf16)
    r.e3[...] = e3
    dbn = matmul_right_t(e3, middle[:, 6 * D : 7 * D]) * slope(r.bn[...])
    xb = r.xb[...]
    sg[SMALL_VEC + 5 : SMALL_VEC + 6, :] = jnp.sum(dbn * xb, axis=0, keepdims=True)
    sg[SMALL_VEC + 6 : SMALL_VEC + 7, :] = jnp.sum(dbn, axis=0, keepdims=True)
    dxb = dbn * gains[5]
    r.dxb[...] = dxb
    row_to_tile(r.tile2, 0, jnp.sum(dxb, axis=0, keepdims=True))
    row_to_tile(r.tile2, 4, jnp.sum(dxb * xb, axis=0, keepdims=True))
    sums2 = Collect(cube, r.tile2, r.slots2, r.c2_send, r.c2_recv)
    sums2.start()
    token_edge = pl.multiple_of((1 - seq) * (tokens - EDGE), EDGE)
    edges = r.edges
    edges[0:EDGE, :] = r.dxb[pl.ds(token_edge, EDGE), :]
    edges[EDGE:, :] = r.xb[pl.ds(token_edge, EDGE), :]
    edge_copy = remote(edges, r.edges_in, r.edge_send, r.edge_recv, across)
    edge_copy.start()

    weight_grad(r.e_low[...], r.s2, d_second, FF, FF)
    scatter.start(0, 0)
    weight_grad(a[3], r.du, d_second, 0, FF)
    scatter.start(1, 0)
    weight_grad(r.sw[...], r.e3, d_middle, 6 * D, D)
    edge_copy.wait()
    sums2.arrive()
    total2 = sums2.total()
    mean1 = tile_to_row(total2[0:4] * (1.0 / token_total))
    mean2 = tile_to_row(total2[4:8] * (1.0 / token_total))
    dwide = r.dwide
    dwide[EDGE : EDGE + tokens, :] = inv_std * (r.dxb[...] - mean1 - r.xb[...] * mean2)
    edge = inv_std * (r.edges_in[0:EDGE, :] - mean1 - r.edges_in[EDGE:, :] * mean2)
    dwide[0:EDGE, :] = jnp.where(early, zero_edge, edge)
    dwide[EDGE + tokens :, :] = jnp.where(early, edge, zero_edge)
    dglu_ref = r.conv
    for b in range(D // 128):
        cols = slice(128 * b, 128 * (b + 1))
        total = jnp.zeros((tokens, 128), f32)
        for k in range(K):
            total = total + dwide[31 - k : 31 - k + tokens, cols] * taps[k][:, cols]
        dglu_ref[:, cols] = total
    dglu, sig = dglu_ref[...], r.sig[...]
    r.dgates[:, :D] = (dglu * sig).astype(bf16)
    r.dgates[:, D:] = (dglu * r.gate[...] * sig * (1.0 - sig)).astype(bf16)
    scatter.advance(0, 0)
    back = matmul_right_t(r.dgates[...], middle[:, 4 * D : 6 * D])
    part, sg[SMALL_VEC + 2 : SMALL_VEC + 3, :] = norm_grad(back, xh[2], inv2, gains[2])
    d2 = r.d[...] + part
    r.d[...] = d2
    e1 = d2.astype(bf16)
    r.e_low[...] = e1
    dob = matmul_right_t(e1, middle[:, 3 * D : 4 * D]).astype(bf16)
    r.dob[...] = dob
    weight_grad(r.att_low[...], r.e_low, d_middle, 3 * D, D)
    weight_grad(a[2], r.dgates, d_middle, 4 * D, 2 * D)
    scatter.start(2, 0)
    scatter.start(6, 0)

    off_rows = []
    give, keep, got = r.give, r.keep, r.got
    kv_grads = []
    for p in range(H // 2):
        columns = slice(128 * p, 128 * (p + 1))
        k_pair, v_pair = kv[:, columns], kv[:, D + 128 * p : D + 128 * (p + 1)]
        att_pair = r.att[:, columns]
        dq = dk = dv = None
        for e in range(2):
            h = 2 * p + e
            dob_head = r.dob[:, columns] * low_masks[e]
            q_head = q_ref[:, columns] * low_masks[e]
            delta = jnp.sum(dob_head.astype(f32) * att_pair, axis=1, keepdims=True)
            prob = r.prob[h]
            ds = prob * (matmul_right_t(dob_head, v_pair) - delta)
            ds_low = ds.astype(bf16)
            dv_head = matmul_left_t(prob.astype(bf16), dob_head)
            dk_head = matmul_left_t(ds_low, q_head) * scale
            dq_head = matmul(ds_low, k_pair) * (lane_masks[e] * scale)
            dv = dv_head if dv is None else dv + dv_head
            dk = dk_head if dk is None else dk + dk_head
            dq = dq_head if dq is None else dq + dq_head
            padded = jnp.concatenate([ds, jnp.zeros((tokens, 512 - 2 * tokens), f32)], axis=1)
            off_rows.append(unskew_sum(padded))
        r.dqkv[:, columns] = dq.astype(bf16)
        for n, value in enumerate((dk, dv)):
            r.dkv[n] = value
            give[p, n] = r.dkv[n, pl.ds(other_row, tokens), :].astype(bf16)
            keep[p, n] = r.dkv[n, pl.ds(first_row, tokens), :]
        copy = remote(
            give.at[p], got.at[p], r.dkv_send.at[p], r.dkv_recv.at[p], across
        )
        copy.start()
        kv_grads.append(copy)
        if p == 1:
            scatter.advance(1, 0)
    off = jnp.concatenate(off_rows, axis=0)
    off = jnp.where(early, pltpu.roll(off, 255, 1), pltpu.roll(off, 255 - tokens, 1))
    off_high, off_low = split(off)
    sg[0:8, :] = matmul_right_t(off_high, r.hit[...]) + matmul_right_t(off_low, r.hit[...])
    for b in range(D // 128):
        cols = slice(128 * b, 128 * (b + 1))
        dconv = dwide[EDGE : EDGE + tokens, cols]
        for k in range(K):
            sg[SMALL_DEPTH + k : SMALL_DEPTH + k + 1, cols] = jnp.sum(
                dconv * wide[k + 1 : k + 1 + tokens, cols], axis=0, keepdims=True
            )
    for p in range(H // 2):
        kv_grads[p].wait()
        for n in range(2):
            at = D * (n + 1) + 128 * p
            r.dqkv[:, at : at + 128] = (keep[p, n] + got[p, n].astype(f32)).astype(bf16)
    scatter.advance(2, 0)
    scatter.advance(6, 0)
    back = matmul_right_t(r.dqkv[...], middle[:, : 3 * D])
    part, sg[SMALL_VEC + 1 : SMALL_VEC + 2, :] = norm_grad(back, xh[1], inv1, gains[1])
    d1 = r.d[...] + part
    e0 = (0.5 * d1).astype(bf16)
    weight_grad(a[1], r.dqkv, d_middle, 0, 3 * D)
    scatter.start(3, 0)
    weight_grad(e0, r.s1, d_first, 0, FF)
    scatter.start(4, 0)
    slopes(e0, down1, r.u1, r.du)
    back = matmul_right_t(r.du[...], up1[...])
    part, sg[SMALL_VEC : SMALL_VEC + 1, :] = norm_grad(back, xh[0], inv0, gains[0])
    r.input_grad[...] = d1 + part
    r.stores[1].start()
    d_first[:, 2 * FF : 2 * FF + 128] = jnp.transpose(sg[...]).astype(bf16)
    weight_grad(a[0], r.du, d_first, FF, FF)
    scatter.start(5, 0)
    for n, stage in SCATTER_EVENTS:
        scatter.advance(n, stage)
        if stage == scatter.cube.digits - 1:
            for j in SCATTER_MATRICES[n]:
                momenta.send(j)
            for store in SCATTER_STORES[n]:
                r.stores[store].start()
    next_small = MOMENTUM * r.m_small[...] + r.share_first[:, 2 * FF :]
    r.tile3[...] = jnp.zeros_like(r.tile3)
    r.tile3[0:1, :] = jnp.sum(next_small * next_small, axis=0, keepdims=True)
    squares = Collect(cube, r.tile3, r.slots3, r.c3_send, r.c3_recv)
    squares.start()
    momenta.receive()
    orthogonalize(cube, r)
    momenta.send_back()
    squares.arrive()
    r.squares[...] = squares.total()
    r.stores[5].start()
    momenta.receive_back()
    momenta.finish()
    gather.finish()
    scatter.finish()
    for store in r.stores:
        store.wait()
    kv_copy.wait_send()


def fused_step(cube, inputs, cotangent, weights, momenta, bucket, collective_id):
    bf16, f32 = jnp.bfloat16, jnp.float32
    tokens, rows = inputs.shape[0], weights[0].shape[0]
    widths = (2 * FF + 128, 7 * D, 2 * FF)
    lead = (2,) * cube.digits
    named = dict(
        inputs=inputs,
        cotangent=cotangent,
        w_up=weights[0],
        w_down=weights[1],
        w_qkv=weights[2],
        w_out=weights[3],
        w_glu=weights[4],
        w_point=weights[5],
        vec=weights[6],
        depth=weights[7],
        rel=weights[8],
        m_up=momenta[0],
        m_down=momenta[1],
        m_qkv=momenta[2],
        m_out=momenta[3],
        m_glu=momenta[4],
        m_point=momenta[5],
        m_vec=momenta[6],
        m_depth=momenta[7],
        m_rel=momenta[8],
        bucket=bucket,
    )
    outs = dict(
        outputs=jax.ShapeDtypeStruct((tokens, D), f32),
        input_grad=jax.ShapeDtypeStruct((tokens, D), f32),
        share_first=jax.ShapeDtypeStruct((rows, widths[0]), f32),
        share_middle=jax.ShapeDtypeStruct((rows, widths[1]), f32),
        share_second=jax.ShapeDtypeStruct((rows, widths[2]), f32),
        returned=jax.ShapeDtypeStruct((32, rows, BLOCK), bf16),
        squares=jax.ShapeDtypeStruct((8, 128), f32),
    )
    field = pltpu.VMEM((tokens, D), f32)
    low = pltpu.VMEM((tokens, D), bf16)
    wide_low = pltpu.VMEM((tokens, FF), bf16)
    wide_field = pltpu.VMEM((tokens + 2 * EDGE, D), f32)
    grid = pltpu.VMEM((H, tokens, 2 * tokens), f32)
    pairs = pltpu.VMEM((H // 2, 2, tokens, 128), bf16)
    tile = pltpu.VMEM((8, 128), f32)
    slots = pltpu.VMEM((cube.total, 8, 128), f32)
    stages = pltpu.SemaphoreType.DMA((7, 2, cube.digits))
    gather_stages = pltpu.SemaphoreType.DMA((8, 2, cube.digits))
    everyone = pltpu.SemaphoreType.DMA((cube.total,))
    single = pltpu.SemaphoreType.DMA
    bands = [pltpu.VMEM(lead + (rows, w), bf16) for w in widths]
    land = []
    for _, pair, _ in SCATTER_CHUNKS:
        for _, part in pair:
            for stage in range(cube.digits):
                shape = (2,) * (cube.digits - 1 - stage) + (rows, part)
                land.append(pltpu.VMEM(shape, bf16))
    scratch = dict(
        first=bands[0],
        middle=bands[1],
        second=bands[2],
        d_first=bands[0],
        d_middle=bands[1],
        d_second=bands[2],
        land=tuple(land),
        sec1=field,
        sec2=field,
        att=field,
        gate=field,
        sig=field,
        conv=field,
        xb=field,
        bn=field,
        dxb=field,
        d=field,
        q=low,
        att_low=low,
        sw=low,
        e_low=low,
        e3=low,
        dob=low,
        a=pltpu.VMEM((4, tokens, D), bf16),
        xh=pltpu.VMEM((4, tokens, D), f32),
        u1=pltpu.VMEM((tokens, FF), f32),
        u2=pltpu.VMEM((tokens, FF), f32),
        s1=wide_low,
        s2=wide_low,
        du=wide_low,
        kv=pltpu.VMEM((2 * tokens, 2 * D), bf16),
        bias=grid,
        prob=grid,
        wide=wide_field,
        dwide=wide_field,
        halo=pltpu.VMEM((EDGE, D), f32),
        edges=pltpu.VMEM((2 * EDGE, D), f32),
        edges_in=pltpu.VMEM((2 * EDGE, D), f32),
        dgates=pltpu.VMEM((tokens, 2 * D), bf16),
        dqkv=pltpu.VMEM((tokens, 3 * D), bf16),
        dkv=pltpu.VMEM((2, 2 * tokens, 128), f32),
        give=pairs,
        got=pairs,
        keep=pltpu.VMEM((H // 2, 2, tokens, 128), f32),
        small=pltpu.VMEM((rows, 128), f32),
        m_small=pltpu.VMEM((rows, 128), f32),
        turn=pltpu.VMEM((128, 128), f32),
        hit=pltpu.VMEM((D, 512), bf16),
        small_t=pltpu.VMEM((128, D), f32),
        small_grad=pltpu.VMEM((128, D), f32),
        tile1=tile,
        tile2=tile,
        slots1=slots,
        slots2=slots,
        tile3=tile,
        slots3=slots,
        leaving=pltpu.VMEM((32, rows, BLOCK), bf16),
        owned=pltpu.VMEM((cube.total, rows, BLOCK), bf16),
        solved=pltpu.VMEM((cube.total, rows, BLOCK), bf16),
        packed=pltpu.VMEM((2, 5, 128, 128), f32),
        packed_in=pltpu.VMEM((2, 5, 128, 128), f32),
        summed=pltpu.VMEM((5, 128, 128), f32),
        whole=pltpu.VMEM((2, 5, 128, 128), f32),
        gram=pltpu.VMEM((D, D), f32),
        m_send=pltpu.SemaphoreType.DMA((32,)),
        m_recv=everyone,
        b_send=everyone,
        b_recv=pltpu.SemaphoreType.DMA((32,)),
        n_send=pltpu.SemaphoreType.DMA((3, 5)),
        n_recv=pltpu.SemaphoreType.DMA((3, 5)),
        c3_send=everyone,
        c3_recv=everyone,
        g_send=gather_stages,
        g_recv=gather_stages,
        s_send=stages,
        s_recv=stages,
        c1_send=everyone,
        c1_recv=everyone,
        c2_send=everyone,
        c2_recv=everyone,
        kv_send=single,
        kv_recv=single,
        halo_send=single,
        halo_recv=single,
        edge_send=single,
        edge_recv=single,
        dkv_send=pltpu.SemaphoreType.DMA((H // 2,)),
        dkv_recv=pltpu.SemaphoreType.DMA((H // 2,)),
    )

    kept = [n for n in outs if n != "returned"]
    buffers = dict({n: pltpu.VMEM(v.shape, v.dtype) for n, v in named.items()})
    buffers |= {n: pltpu.VMEM(outs[n].shape, outs[n].dtype) for n in kept}
    scratch |= buffers
    scratch |= dict(
        load_sem=pltpu.SemaphoreType.DMA((len(named),)),
        store_sem=pltpu.SemaphoreType.DMA((len(kept),)),
        k_sem=single,
    )

    def body(*refs):
        count = len(named) + len(outs)
        far = dict(zip(list(named) + list(outs), refs[:count]))
        near = dict(zip(scratch, refs[count:]))
        near["returned"] = far["returned"]
        near["loads"] = {
            name: pltpu.make_async_copy(far[name], near[name], near["load_sem"].at[n])
            for n, name in enumerate(named)
        }
        near["stores"] = [
            pltpu.make_async_copy(near[name], far[name], near["store_sem"].at[n])
            for n, name in enumerate(kept)
        ]
        step_kernel(cube, types.SimpleNamespace(**near))

    return pl.pallas_call(
        body,
        out_shape=list(outs.values()),
        in_specs=[pl.BlockSpec(memory_space=pl.ANY)] * len(named),
        out_specs=[pl.BlockSpec(memory_space=pl.ANY)] * len(outs),
        scratch_shapes=list(scratch.values()),
        compiler_params=pltpu.CompilerParams(
            collective_id=collective_id, has_side_effects=True, vmem_limit_bytes=60 << 20
        ),
        name="block_step",
    )(*named.values())


def finish_kernel(r):
    f32 = jnp.float32
    for load in r.loads:
        load.start()
    for load in r.loads:
        load.wait()
    pack_small(r.small, r.turn, r.weight[8], r.weight[6], r.weight[7])
    pack_small(r.m_small, r.turn, r.moment[8], r.moment[6], r.moment[7])
    share_first, share_middle, share_second, returned, squares = r.results
    for j in range(8):
        width = WIDTHS[j]
        if j < 4:
            columns = slice(FF * (j % 2), FF * (j % 2 + 1))
            grad = (share_first, share_second)[j % 2][:, share_columns(j)]
        else:
            columns = slice(0, width)
            start = STARTS[j] - STARTS[4]
            grad = share_middle[:, start : start + width]
        n = j // 2 if j < 4 else j - 2
        updated = MOMENTUM * r.moment[n][:, columns] + grad
        r.grad[n][:, columns] = grad
        r.next[n][:, columns] = updated
        solved = [returned[4 * j + q, :, 0 : width // 4].astype(f32) for q in range(4)]
        r.new[n][:, columns] = r.weight[n][:, columns] - RATE_MATRIX * jnp.concatenate(
            solved, axis=1
        )
    grad = share_first[:, 2 * FF :]
    updated = MOMENTUM * r.m_small[...] + grad
    lane = lax.broadcasted_iota(jnp.int32, (1, 128), 1)
    count = jnp.where(lane < SMALL_VEC, float(NB), float(D))
    scale = lax.rsqrt(squares[0:1, :] / count + EPS_SCALE)
    new = r.small[...] - RATE_VECTOR * updated * scale
    rows, rel_rows = r.small.shape[0], r.weight[8].shape[0]
    for value, outs in ((grad, r.grad), (new, r.new), (updated, r.next)):
        r.turn[...] = jnp.zeros_like(r.turn)
        r.turn[0:rows, :] = value
        turned = jnp.transpose(r.turn[...])
        outs[6][...] = turned[SMALL_VEC : SMALL_VEC + 7, 0:rows]
        outs[7][...] = value[:, SMALL_DEPTH : SMALL_DEPTH + K]
        outs[8][...] = value[0:rel_rows, SMALL_REL : SMALL_REL + H]
    for store in r.stores:
        store.start()
    for store in r.stores:
        store.wait()


def finish_step(fields, shares, returned, squares, weights, momenta):
    sources = (*shares, returned, squares, *weights, *momenta)
    operands = sources + tuple(fields)
    rows, count = weights[0].shape[0], len(sources)
    shapes = [jax.ShapeDtypeStruct(v.shape, v.dtype) for v in weights] * 3
    shapes += [jax.ShapeDtypeStruct(v.shape, v.dtype) for v in fields]

    def body(*refs):
        ins, refs = refs[: len(operands)], refs[len(operands) :]
        outs, refs = refs[: len(shapes)], refs[len(shapes) :]
        near, refs = refs[: count + 2], refs[count + 2 :]
        made, refs = refs[:27], refs[27:]
        small, m_small, turn, sem = refs
        pairs = list(zip(ins, near)) + list(zip(made + near[-2:], outs))
        moves = [pltpu.make_async_copy(a, b, sem.at[n]) for n, (a, b) in enumerate(pairs)]
        finish_kernel(
            types.SimpleNamespace(
                loads=moves[: count + 2],
                stores=moves[count + 2 :],
                results=near[:5],
                weight=near[5:14],
                moment=near[14:23],
                grad=made[:9],
                new=made[9:18],
                next=made[18:27],
                small=small,
                m_small=m_small,
                turn=turn,
            ),
        )

    return pl.pallas_call(
        body,
        out_shape=shapes,
        in_specs=[pl.BlockSpec(memory_space=pl.ANY)] * len(operands),
        out_specs=[pl.BlockSpec(memory_space=pl.ANY)] * len(shapes),
        scratch_shapes=[pltpu.VMEM(v.shape, v.dtype) for v in list(operands) + shapes[:27]]
        + [
            pltpu.VMEM((rows, 128), jnp.float32),
            pltpu.VMEM((rows, 128), jnp.float32),
            pltpu.VMEM((128, 128), jnp.float32),
            pltpu.SemaphoreType.DMA((len(operands) + len(shapes),)),
        ],
        compiler_params=pltpu.CompilerParams(vmem_limit_bytes=60 << 20),
        name="finish_step",
    )(*operands)


def unfused_step(
    cube,
    inputs,
    cotangent,
    w_up,
    w_down,
    w_qkv,
    w_out,
    w_glu,
    w_point,
    small,
    bucket_table,
):
    bf16 = jnp.bfloat16
    rows = w_up.shape[0]
    rel_rows = NB // cube.total
    shard_groups = (
        jnp.concatenate([w_up[:, :FF], w_down[:, :FF], small], axis=1).astype(bf16),
        jnp.concatenate([w_qkv, w_out, w_glu, w_point], axis=1).astype(bf16),
        jnp.concatenate([w_up[:, FF:], w_down[:, FF:]], axis=1).astype(bf16),
    )
    first, middle, second = [
        full.reshape(D, -1) for full in gather_groups(cube, shard_groups, 0)
    ]
    up_first, down_first, small_low = first[:, :FF], first[:, FF : 2 * FF], first[:, 2 * FF :]
    qkv_w, out_w = middle[:, : 3 * D], middle[:, 3 * D : 4 * D]
    glu_w, point_w = middle[:, 4 * D : 6 * D], middle[:, 6 * D :]
    up_second, down_second = second[:, :FF], second[:, FF:]
    gains = small_low[:, SMALL_VEC : SMALL_VEC + 7].astype(jnp.float32)
    kernel = small_low[:, SMALL_DEPTH : SMALL_DEPTH + K].astype(jnp.float32)
    rel_low = small_low[:, :H].reshape(cube.total, rows, H)[:, :rel_rows].reshape(NB, H)
    bucket_hit = (bucket_table[:, None] == jnp.arange(NB, dtype=jnp.int32)[None, :]).astype(
        jnp.float32
    )
    offsets = jnp.dot(bucket_hit, rel_low.astype(jnp.float32), precision=HIGHEST).T
    seq_rows = inputs[0]
    row_count = seq_rows.shape[0]
    first_row = lax.axis_index("seq") * row_count
    token_total = row_count * lax.axis_size(("dp", "seq", "shard"))
    section_one, ffn_saved = ffn_forward(seq_rows, gains[:, 0], up_first, down_first)
    normed_out2, normed2, inverse2 = layer_norm(section_one, gains[:, 1])
    lifted2 = normed_out2.astype(bf16)
    projected = matmul(lifted2, qkv_w).astype(bf16)
    query = projected[:, :D]
    pair = [(0, 1), (1, 0)]
    other = lax.ppermute(projected[:, D:], "seq", pair)
    early = lax.axis_index("seq") == 0
    both = jnp.concatenate(
        [
            jnp.where(early, projected[:, D:], other),
            jnp.where(early, other, projected[:, D:]),
        ],
        axis=0,
    )
    keys, values = both[:, :D], both[:, D:]
    attended, log_total = attention_forward(query, keys, values, offsets, first_row)
    attended_low = attended.astype(bf16)
    section_two = section_one + matmul(attended_low, out_w)
    normed_out3, normed3, inverse3 = layer_norm(section_two, gains[:, 2])
    lifted3 = normed_out3.astype(bf16)
    gates = matmul(lifted3, glu_w)
    first_half = gates[:, :D]
    sig_gate = jax.nn.sigmoid(gates[:, D:])
    glu = first_half * sig_gate
    glu_wide = with_halo(glu, (("seq", 0),), K // 2)
    conv = depthwise(glu_wide, kernel, row_count)
    part_sum = jnp.sum(conv, axis=0)
    part_mean = part_sum / row_count
    part_square = jnp.sum(jnp.square(conv - part_mean), axis=0)
    stats = collect(cube, jnp.concatenate([part_sum, part_square]).reshape(8, 128), 1)
    stats = stats.reshape(cube.total, 2, D)
    mean = jnp.sum(stats[:, 0], axis=0) / token_total
    spread_of_means = jnp.square(stats[:, 0] / row_count - mean) * row_count
    variance = jnp.sum(stats[:, 1] + spread_of_means, axis=0) / token_total
    centred = conv - mean
    inv_std = lax.rsqrt(variance + EPS_BATCH)
    normed_bn = centred * inv_std
    batch_out = normed_bn * gains[:, 5] + gains[:, 6]
    swish_low = jax.nn.silu(batch_out).astype(bf16)
    section_three = section_two + matmul(swish_low, point_w)
    section_four, tail_saved = ffn_forward(
        section_three, gains[:, 3], up_second, down_second
    )
    outputs, normed5, inverse5 = layer_norm(section_four, gains[:, 4])
    grad_four, gain_four = norm_back(cotangent[0], normed5, inverse5, gains[:, 4])
    grad_three, grad_up_two, grad_down_two, gain_three = ffn_backward(
        grad_four, tail_saved, gains[:, 3], up_second, down_second
    )
    grad_three_low = grad_three.astype(bf16)
    grad_point = matmul_left_t(swish_low, grad_three_low)
    grad_batch = matmul_right_t(grad_three_low, point_w) * silu_slope(batch_out)
    grad_normed = grad_batch * gains[:, 5]
    sums = jnp.concatenate(
        [jnp.sum(grad_normed, axis=0), jnp.sum(grad_normed * normed_bn, axis=0)]
    )
    sums = jnp.sum(collect(cube, sums.reshape(8, 128), 2), axis=0).reshape(2, D)
    sum_normed, sum_cross = sums[0], sums[1]
    grad_conv = inv_std * (
        grad_normed - sum_normed / token_total - normed_bn * sum_cross / token_total
    )
    grad_wide = with_halo(grad_conv, (("seq", 0),), K // 2)
    grad_glu = grad_wide[K - 1 : K - 1 + row_count] * kernel[:, 0]
    for tap_idx in range(1, K):
        grad_glu = (
            grad_glu
            + grad_wide[K - 1 - tap_idx : K - 1 - tap_idx + row_count] * kernel[:, tap_idx]
        )
    grad_kernel = jnp.stack(
        [
            jnp.sum(grad_conv * glu_wide[tap_idx : tap_idx + row_count], axis=0)
            for tap_idx in range(K)
        ],
        axis=1,
    )
    grad_gates = jnp.concatenate(
        [grad_glu * sig_gate, grad_glu * first_half * sig_gate * (1.0 - sig_gate)], axis=1
    ).astype(bf16)
    grad_glu_w = matmul_left_t(lifted3, grad_gates)
    grad_two_part, gain_two = norm_back(
        matmul_right_t(grad_gates, glu_w), normed3, inverse3, gains[:, 2]
    )
    grad_two = grad_three + grad_two_part
    grad_two_low = grad_two.astype(bf16)
    grad_out_w = matmul_left_t(attended_low, grad_two_low)
    grad_attended = matmul_right_t(grad_two_low, out_w).astype(bf16)
    delta = jnp.sum(
        (grad_attended.astype(jnp.float32) * attended).reshape(row_count, H, DH), axis=2
    )
    query_grad, key_grad, value_grad, offset_grad = attention_backward(
        query, keys, values, offsets, first_row, log_total, grad_attended, delta
    )
    keys_grad = jnp.concatenate([key_grad, value_grad], axis=1)
    theirs = lax.dynamic_slice_in_dim(keys_grad, row_count - first_row, row_count, 0)
    own = lax.dynamic_slice_in_dim(keys_grad, first_row, row_count, 0)
    own = own + lax.ppermute(theirs, "seq", pair)
    key_own, value_own = own[:, :D], own[:, D:]
    grad_proj = jnp.concatenate([query_grad, key_own, value_own], axis=1).astype(bf16)
    grad_qkv_w = matmul_left_t(lifted2, grad_proj)
    grad_one_part, gain_one = norm_back(
        matmul_right_t(grad_proj, qkv_w), normed2, inverse2, gains[:, 1]
    )
    grad_one = grad_two + grad_one_part
    input_grad, grad_up_one, grad_down_one, gain_zero = ffn_backward(
        grad_one, ffn_saved, gains[:, 0], up_first, down_first
    )
    grad_vec_local = jnp.stack(
        [
            gain_zero,
            gain_one,
            gain_two,
            gain_three,
            gain_four,
            jnp.sum(grad_batch * normed_bn, axis=0),
            jnp.sum(grad_batch, axis=0),
        ],
        axis=1,
    )
    grad_rel_local = jnp.dot(bucket_hit.T, offset_grad.T, precision=HIGHEST)
    rel_padded = jnp.pad(
        grad_rel_local.reshape(cube.total, rel_rows, H), ((0, 0), (0, rows - rel_rows), (0, 0))
    )
    small_grads = jnp.concatenate(
        [rel_padded.reshape(D, H), grad_vec_local, grad_kernel], axis=1
    )
    small_grads = jnp.pad(small_grads, ((0, 0), (0, 128 - SMALL_END)))
    lead = (2,) * cube.digits
    grad_groups = [
        jnp.concatenate(group, axis=1).astype(bf16).reshape(lead + (rows, -1))
        for group in (
            (grad_up_two, grad_down_two),
            (grad_qkv_w, grad_out_w, grad_glu_w, grad_point),
            (grad_up_one, grad_down_one, small_grads),
        )
    ]
    share_second, share_middle, share_first = scatter_groups(cube, grad_groups, 3)
    return outputs, input_grad, share_first, share_middle, share_second


def local(
    cube,
    inputs,
    cotangent,
    w_up,
    w_down,
    w_qkv,
    w_out,
    w_glu,
    w_point,
    vectors,
    depth_kernel,
    rel_bias,
    bucket_table,
    m_up,
    m_down,
    m_qkv,
    m_out,
    m_glu,
    m_point,
    m_vectors,
    m_depth,
    m_rel,
):
    bf16 = jnp.bfloat16
    rows, rel_rows = w_up.shape[0], rel_bias.shape[0]
    pack = lambda rel, vec, depth: jnp.pad(
        jnp.concatenate([jnp.pad(rel, ((0, rows - rel_rows), (0, 0))), vec, depth], axis=1),
        ((0, 0), (0, 128 - SMALL_END)),
    )
    small = pack(rel_bias, vectors, depth_kernel)
    weights = (w_up, w_down, w_qkv, w_out, w_glu, w_point)
    if rows % 16 == 0 and cube.total == 32:
        bucket = bucket_table[None]
        weights += (vectors.T, depth_kernel, rel_bias)
        momenta = (m_up, m_down, m_qkv, m_out, m_glu, m_point, m_vectors.T, m_depth, m_rel)
        outputs, input_grad, *shares, returned, squares = fused_step(
            cube, inputs[0], cotangent[0], weights, momenta, bucket, 0
        )
        *rest, outputs, input_grad = finish_step(
            (outputs, input_grad), shares, returned, squares, weights, momenta
        )
        for n in (6, 15, 24):
            rest[n] = rest[n].T
        return (outputs[None], input_grad[None], *rest)
    outputs, input_grad, share_first, share_middle, share_second = unfused_step(
        cube, inputs, cotangent, *weights, small, bucket_table
    )
    grad_up = jnp.concatenate([share_first[:, :FF], share_second[:, :FF]], axis=1)
    grad_down = jnp.concatenate([share_first[:, FF : 2 * FF], share_second[:, FF:]], axis=1)
    grad_qkv, grad_out = share_middle[:, : 3 * D], share_middle[:, 3 * D : 4 * D]
    grad_glu, grad_pnt = share_middle[:, 4 * D : 6 * D], share_middle[:, 6 * D :]
    share_small = share_first[:, 2 * FF :]
    grad_vectors = share_small[:, SMALL_VEC : SMALL_VEC + 7]
    grad_depth = share_small[:, SMALL_DEPTH : SMALL_DEPTH + K]
    grad_rel = share_small[: rel_bias.shape[0], :H]
    next_m_up = MOMENTUM * m_up + grad_up
    next_m_down = MOMENTUM * m_down + grad_down
    next_m_qkv = MOMENTUM * m_qkv + grad_qkv
    next_m_out = MOMENTUM * m_out + grad_out
    next_m_glu = MOMENTUM * m_glu + grad_glu
    next_m_point = MOMENTUM * m_point + grad_pnt
    stacked = jnp.concatenate(
        [next_m_up, next_m_down, next_m_qkv, next_m_out, next_m_glu, next_m_point], axis=1
    )
    owned = spread(cube, stacked, 4).reshape(D, BLOCK)
    ortho = orthogonalize_blocks(cube, owned, bf16, 5)
    mine = restore(cube, ortho.reshape(cube.total, rows, BLOCK), 6).astype(jnp.float32)
    new_up = w_up - RATE_MATRIX * mine[:, : 2 * FF]
    new_down = w_down - RATE_MATRIX * mine[:, 2 * FF : 4 * FF]
    new_qkv = w_qkv - RATE_MATRIX * mine[:, STARTS[4] : STARTS[5]]
    new_out = w_out - RATE_MATRIX * mine[:, STARTS[5] : STARTS[6]]
    new_glu = w_glu - RATE_MATRIX * mine[:, STARTS[6] : STARTS[7]]
    new_point = w_point - RATE_MATRIX * mine[:, STARTS[7] :]
    next_m_vectors = MOMENTUM * m_vectors + grad_vectors
    next_m_depth = MOMENTUM * m_depth + grad_depth
    next_m_rel = MOMENTUM * m_rel + grad_rel
    squares = jnp.concatenate(
        [
            jnp.sum(next_m_vectors * next_m_vectors, axis=0),
            jnp.sum(next_m_depth * next_m_depth, axis=0),
            jnp.sum(next_m_rel * next_m_rel, axis=0),
        ]
    )
    squares = jnp.pad(squares, (0, 128 - squares.shape[0])).reshape(1, 128)
    squares = jnp.sum(collect(cube, jnp.pad(squares, ((0, 7), (0, 0))), 7), axis=0)[0]
    square_vec, square_depth = squares[:7], squares[7 : 7 + K]
    square_rel = squares[7 + K : 7 + K + H]
    new_vectors = vectors - RATE_VECTOR * next_m_vectors * lax.rsqrt(square_vec / D + EPS_SCALE)
    new_depth = depth_kernel - RATE_VECTOR * next_m_depth * lax.rsqrt(square_depth / D + EPS_SCALE)
    new_rel = rel_bias - RATE_VECTOR * next_m_rel * lax.rsqrt(square_rel / NB + EPS_SCALE)
    return (
        outputs[None],
        input_grad[None],
        grad_up,
        grad_down,
        grad_qkv,
        grad_out,
        grad_glu,
        grad_pnt,
        grad_vectors,
        grad_depth,
        grad_rel,
        new_up,
        new_down,
        new_qkv,
        new_out,
        new_glu,
        new_point,
        new_vectors,
        new_depth,
        new_rel,
        next_m_up,
        next_m_down,
        next_m_qkv,
        next_m_out,
        next_m_glu,
        next_m_point,
        next_m_vectors,
        next_m_depth,
        next_m_rel,
    )


def solution(mesh):
    placed = (
        P(("dp", "shard"), "seq", None),
        P(("dp", "shard"), "seq", None),
        P(("dp", "seq", "shard"), None),
        P(("dp", "seq", "shard"), None),
        P(("dp", "seq", "shard"), None),
        P(("dp", "seq", "shard"), None),
        P(("dp", "seq", "shard"), None),
        P(("dp", "seq", "shard"), None),
        P(("dp", "seq", "shard"), None),
        P(("dp", "seq", "shard"), None),
        P(("dp", "seq", "shard"), None),
        P(),
        P(("dp", "seq", "shard"), None),
        P(("dp", "seq", "shard"), None),
        P(("dp", "seq", "shard"), None),
        P(("dp", "seq", "shard"), None),
        P(("dp", "seq", "shard"), None),
        P(("dp", "seq", "shard"), None),
        P(("dp", "seq", "shard"), None),
        P(("dp", "seq", "shard"), None),
        P(("dp", "seq", "shard"), None),
    )
    return jax.shard_map(
        functools.partial(local, Cube(mesh.shape["dp"])),
        mesh=mesh,
        in_specs=placed,
        out_specs=(
            P(("dp", "shard"), "seq", None),
            P(("dp", "shard"), "seq", None),
            P(("dp", "seq", "shard"), None),
            P(("dp", "seq", "shard"), None),
            P(("dp", "seq", "shard"), None),
            P(("dp", "seq", "shard"), None),
            P(("dp", "seq", "shard"), None),
            P(("dp", "seq", "shard"), None),
            P(("dp", "seq", "shard"), None),
            P(("dp", "seq", "shard"), None),
            P(("dp", "seq", "shard"), None),
            P(("dp", "seq", "shard"), None),
            P(("dp", "seq", "shard"), None),
            P(("dp", "seq", "shard"), None),
            P(("dp", "seq", "shard"), None),
            P(("dp", "seq", "shard"), None),
            P(("dp", "seq", "shard"), None),
            P(("dp", "seq", "shard"), None),
            P(("dp", "seq", "shard"), None),
            P(("dp", "seq", "shard"), None),
            P(("dp", "seq", "shard"), None),
            P(("dp", "seq", "shard"), None),
            P(("dp", "seq", "shard"), None),
            P(("dp", "seq", "shard"), None),
            P(("dp", "seq", "shard"), None),
            P(("dp", "seq", "shard"), None),
            P(("dp", "seq", "shard"), None),
            P(("dp", "seq", "shard"), None),
            P(("dp", "seq", "shard"), None),
        ),
        check_vma=False,
    )
```

```python
import functools
import types

import jax
import jax.numpy as jnp
from jax import lax
from jax.experimental import pallas as pl
from jax.experimental.pallas import tpu as pltpu
from jax.sharding import PartitionSpec as P

D = 512
FF = 2048
H = 8
DH = 64
K = 31
NB = 128


EPS_NORM = 1e-05
EPS_BATCH = 1e-05
EPS_SCALE = 1e-06
MOMENTUM = 0.9
RATE_MATRIX = 1.0
RATE_VECTOR = 0.25
COEF_A = 3.4445
COEF_B = -4.775
COEF_C = 2.0315
HIGHEST = lax.Precision.HIGHEST


AXES = ("dp", "seq", "shard")
MESH = pl.DeviceIdType.MESH
WIDTHS = (FF, FF, FF, FF, 3 * D, D, 2 * D, D)
STARTS = tuple(sum(WIDTHS[:i]) for i in range(9))
BLOCK = 512


class Cube:
    def __init__(self, dp_size):
        self.dp_size = dp_size
        self.levels = dp_size.bit_length() - 1
        self.digits = self.levels + 2
        self.total = dp_size * 4
        high = list(range(self.levels - 1))
        low, seq, core = self.levels - 1, self.levels, self.levels + 1
        self.gather_orders = (high + [low, seq, core], high + [seq, low, core])
        self.gather_late_orders = ([seq, low] + high + [core], [low, seq] + high + [core])
        self.scatter_orders = tuple(order[::-1] for order in self.gather_orders)
        self.scatter_high_orders = tuple(order[::-1] for order in self.gather_late_orders)
        self.scatter_low_orders = ([core, low, seq] + high[::-1],) * 2

    def mine(self):
        d = lax.axis_index("dp")
        bits = [lax.rem(d // (1 << (self.levels - 1 - k)), 2) for k in range(self.levels)]
        return bits + [lax.axis_index("seq"), lax.axis_index("shard")]

    def partner(self, k):
        d, s, c = lax.axis_index("dp"), lax.axis_index("seq"), lax.axis_index("shard")
        if k == self.levels:
            return (d, 1 - s, c)
        if k == self.levels + 1:
            return (d, s, 1 - c)
        step = 1 << (self.levels - 1 - k)
        bit = lax.rem(d // step, 2)
        return (d + (1 - 2 * bit) * step, s, c)

    def index(self):
        return (lax.axis_index("dp") * 2 + lax.axis_index("seq")) * 2 + lax.axis_index("shard")

    def coords(self, index):
        return (index // 4, lax.rem(index // 2, 2), lax.rem(index, 2))

    def greet_partners(self):
        barrier = pltpu.get_barrier_semaphore()
        for k in range(self.digits):
            pl.semaphore_signal(barrier, inc=1, device_id=self.partner(k), device_id_type=MESH)
        pl.semaphore_wait(barrier, self.digits)

    def greet_all(self):
        barrier = pltpu.get_barrier_semaphore()
        me = self.index()

        @pl.loop(1, self.total)
        def _(i):
            peer = self.coords(lax.rem(me + i, self.total))
            pl.semaphore_signal(barrier, inc=1, device_id=peer, device_id_type=MESH)

        pl.semaphore_wait(barrier, self.total - 1)


def halves(width):
    cut = (width // 128 + 1) // 2 * 128
    return ((0, cut), (cut, width - cut))


def remote(src, dst, send_sem, recv_sem, peer):
    return pltpu.make_async_remote_copy(
        src_ref=src,
        dst_ref=dst,
        send_sem=send_sem,
        recv_sem=recv_sem,
        device_id=peer,
        device_id_type=MESH,
    )


def gather_kernel(cube, groups, *refs):
    shards, outs = refs[:groups], refs[groups : 2 * groups]
    own_sem, send_sem, recv_sem = refs[2 * groups :]
    cube.greet_partners()
    mine = cube.mine()
    locals_ = []
    for g in range(groups):
        copy = pltpu.make_async_copy(shards[g], outs[g].at[tuple(mine)], own_sem.at[g])
        copy.start()
        locals_.append(copy)

    def make(g, half, stage):
        order = cube.gather_orders[half]
        columns = pl.ds(*halves(shards[g].shape[-1])[half])
        done = order[:stage]
        index = tuple(slice(None) if k in done else mine[k] for k in range(cube.digits))
        place = outs[g].at[index + (slice(None), columns)]
        source = shards[g].at[:, columns] if stage == 0 else place
        return remote(
            source,
            place,
            send_sem.at[g, half, stage],
            recv_sem.at[g, half, stage],
            cube.partner(order[stage]),
        )

    copies = {}
    for g in range(groups):
        for half in range(2):
            copies[g, half, 0] = make(g, half, 0)
            copies[g, half, 0].start()
    for tick in range(cube.digits + 2 * (groups - 1)):
        for g in range(groups):
            stage = tick - 2 * g
            if not 0 <= stage < cube.digits:
                continue
            for half in range(2):
                copies[g, half, stage].wait_recv()
                if stage == 0 and half == 0:
                    locals_[g].wait()
                if stage + 1 < cube.digits:
                    copies[g, half, stage + 1] = make(g, half, stage + 1)
                    copies[g, half, stage + 1].start()
    for copy in copies.values():
        copy.wait_send()


def gather_groups(cube, shards, collective_id):
    groups = len(shards)
    lead = (2,) * cube.digits
    return pl.pallas_call(
        functools.partial(gather_kernel, cube, groups),
        out_shape=[jax.ShapeDtypeStruct(lead + s.shape, s.dtype) for s in shards],
        in_specs=[pl.BlockSpec(memory_space=pl.ANY)] * groups,
        out_specs=[pl.BlockSpec(memory_space=pl.ANY)] * groups,
        scratch_shapes=[
            pltpu.SemaphoreType.DMA((groups,)),
            pltpu.SemaphoreType.DMA((groups, 2, cube.digits)),
            pltpu.SemaphoreType.DMA((groups, 2, cube.digits)),
        ],
        compiler_params=pltpu.CompilerParams(
            collective_id=collective_id, has_side_effects=True
        ),
        name="gather_weights",
    )(*shards)


def scatter_kernel(cube, groups, *refs):
    parts, outs = refs[:groups], refs[groups : 2 * groups]
    rest = refs[2 * groups :]
    sums = rest[:groups]
    landed = rest[groups : groups + groups * 2 * cube.digits]
    own_sem, send_sem, recv_sem = rest[groups + groups * 2 * cube.digits :]
    cube.greet_partners()
    mine = cube.mine()
    last = cube.digits - 1

    def slot(g, half, stage):
        return landed[(g * 2 + half) * cube.digits + stage]

    def place(g, half, stage, bit_of):
        order = cube.scatter_orders[half]
        columns = pl.ds(*halves(outs[g].shape[-1])[half])
        index = []
        for k in range(cube.digits - 1):
            at = order.index(k)
            if at > stage:
                index.append(slice(None))
            else:
                index.append(bit_of(k) if at == stage else mine[k])
        return tuple(index) + (slice(None), columns)

    def make(g, half, stage):
        order = cube.scatter_orders[half]
        if stage == 0:
            index = (slice(None),) * last + (1 - mine[last],)
            columns = pl.ds(*halves(outs[g].shape[-1])[half])
            source = parts[g].at[index + (slice(None), columns)]
        else:
            source = sums[g].at[place(g, half, stage, lambda k: 1 - mine[k])]
        return remote(
            source,
            slot(g, half, stage),
            send_sem.at[g, half, stage],
            recv_sem.at[g, half, stage],
            cube.partner(order[stage]),
        )

    copies = {}
    locals_ = []
    for g in range(groups):
        copy = pltpu.make_async_copy(
            parts[g].at[(slice(None),) * last + (mine[last],)], sums[g], own_sem.at[g]
        )
        copy.start()
        locals_.append(copy)
        for half in range(2):
            copies[g, half, 0] = make(g, half, 0)
            copies[g, half, 0].start()

    def add(g, half, stage):
        order = cube.scatter_orders[half]
        columns = pl.ds(*halves(outs[g].shape[-1])[half])
        free = [k for k in range(last) if order.index(k) > stage]
        count = 1 << len(free)
        target, extra = sums[g], slot(g, half, stage)

        def one(i):
            digit = {k: lax.rem(i // (1 << (len(free) - 1 - n)), 2) for n, k in enumerate(free)}
            full = tuple(digit.get(k, mine[k]) for k in range(last)) + (slice(None), columns)
            short = tuple(digit[k] for k in free)
            total = target[full].astype(jnp.float32) + extra[short + (slice(None), slice(None))].astype(jnp.float32)
            if stage == last:
                outs[g][:, columns] = total
            else:
                target[full] = total.astype(target.dtype)

        if count == 1:
            one(0)
        else:
            pl.loop(0, count)(one)

    for stage in range(cube.digits):
        for g in range(groups):
            if stage == 0:
                locals_[g].wait()
            for half in range(2):
                copies[g, half, stage].wait_recv()
                add(g, half, stage)
                if stage < last:
                    copies[g, half, stage + 1] = make(g, half, stage + 1)
                    copies[g, half, stage + 1].start()
    for copy in copies.values():
        copy.wait_send()


def scatter_groups(cube, parts, collective_id):
    groups = len(parts)
    scratch = [pltpu.VMEM((2,) * (cube.digits - 1) + p.shape[-2:], p.dtype) for p in parts]
    for p in parts:
        for half in range(2):
            for stage in range(cube.digits):
                lead = (2,) * (cube.digits - 1 - stage)
                scratch.append(pltpu.VMEM(lead + (p.shape[-2], halves(p.shape[-1])[half][1]), p.dtype))
    scratch += [
        pltpu.SemaphoreType.DMA((groups,)),
        pltpu.SemaphoreType.DMA((groups, 2, cube.digits)),
        pltpu.SemaphoreType.DMA((groups, 2, cube.digits)),
    ]
    return pl.pallas_call(
        functools.partial(scatter_kernel, cube, groups),
        out_shape=[jax.ShapeDtypeStruct(p.shape[-2:], jnp.float32) for p in parts],
        in_specs=[pl.BlockSpec(memory_space=pl.ANY)] * groups,
        out_specs=[pl.BlockSpec(memory_space=pltpu.VMEM)] * groups,
        scratch_shapes=scratch,
        compiler_params=pltpu.CompilerParams(
            collective_id=collective_id, has_side_effects=True, vmem_limit_bytes=48 << 20
        ),
        name="scatter_grads",
    )(*parts)


def collect_kernel(cube, x_ref, o_ref, send_sem, recv_sem):
    me = cube.index()
    cube.greet_all()

    def make(i):
        to = lax.rem(me + i, cube.total)
        return remote(x_ref, o_ref.at[i], send_sem.at[i], recv_sem.at[i], cube.coords(to))

    @pl.loop(1, cube.total)
    def _(i):
        make(i).start()

    o_ref[0] = x_ref[...]

    @pl.loop(1, cube.total)
    def _(i):
        make(i).wait()


def collect(cube, x, collective_id):
    return pl.pallas_call(
        functools.partial(collect_kernel, cube),
        out_shape=jax.ShapeDtypeStruct((cube.total,) + x.shape, x.dtype),
        in_specs=[pl.BlockSpec(memory_space=pltpu.VMEM)],
        out_specs=pl.BlockSpec(memory_space=pltpu.VMEM),
        scratch_shapes=[
            pltpu.SemaphoreType.DMA((cube.total,)),
            pltpu.SemaphoreType.DMA((cube.total,)),
        ],
        compiler_params=pltpu.CompilerParams(
            collective_id=collective_id, has_side_effects=True
        ),
        name="collect_stats",
    )(x)


def by_matrix(j, action):
    for width in sorted(set(WIDTHS)):
        members = [i for i in range(8) if WIDTHS[i] == width]
        hit = functools.reduce(jnp.logical_or, [j == i for i in members])
        pl.when(hit)(functools.partial(action, width // 4))


def quarter_start(t):
    j, q = t // 4, lax.rem(t, 4)
    start = 0
    for i in range(8):
        start = start + jnp.where(j == i, STARTS[i] + q * (WIDTHS[i] // 4), 0)
    return pl.multiple_of(start, 128)


def owner_coords(cube, t):
    return ((t // 4) * (cube.dp_size // 8), lax.rem(t // 2, 2), lax.rem(t, 2))


def spread_kernel(cube, x_ref, o_ref, own_sem, send_sem, recv_sem):
    me = cube.index()
    repeat = cube.dp_size // 8
    d, s, c = lax.axis_index("dp"), lax.axis_index("seq"), lax.axis_index("shard")
    owner = lax.rem(d, repeat) == 0
    mine = ((d // repeat) * 2 + s) * 2 + c
    cube.greet_all()

    def send(i, wait):
        t = lax.rem(mine + i, 32)
        peer = owner_coords(cube, t)
        other = jnp.logical_or(jnp.logical_not(owner), i > 0)

        def go(width):
            src = x_ref.at[:, pl.ds(quarter_start(t), width)]
            dst = o_ref.at[me, :, pl.ds(0, width)]
            copy = remote(src, dst, send_sem.at[i], recv_sem.at[me], peer)
            if wait:
                copy.wait_send()
            else:
                copy.start()

        pl.when(other)(lambda: by_matrix(t // 4, go))

    pl.loop(0, 32)(functools.partial(send, wait=False))

    def keep(width):
        copy = pltpu.make_async_copy(
            x_ref.at[:, pl.ds(quarter_start(mine), width)],
            o_ref.at[me, :, pl.ds(0, width)],
            own_sem,
        )
        copy.start()
        copy.wait()

    def receive(width):
        @pl.loop(1, cube.total)
        def _(i):
            source = lax.rem(me + i, cube.total)
            place = o_ref.at[source, :, pl.ds(0, width)]
            remote(
                place, place, send_sem.at[0], recv_sem.at[source], cube.coords(source)
            ).wait_recv()

    @pl.when(owner)
    def _():
        by_matrix(mine // 4, keep)
        by_matrix(mine // 4, receive)

    pl.loop(0, 32)(functools.partial(send, wait=True))


def spread(cube, x, collective_id):
    return pl.pallas_call(
        functools.partial(spread_kernel, cube),
        out_shape=jax.ShapeDtypeStruct((cube.total, x.shape[0], BLOCK), x.dtype),
        in_specs=[pl.BlockSpec(memory_space=pl.ANY)],
        out_specs=pl.BlockSpec(memory_space=pl.ANY),
        scratch_shapes=[
            pltpu.SemaphoreType.DMA,
            pltpu.SemaphoreType.DMA((32,)),
            pltpu.SemaphoreType.DMA((cube.total,)),
        ],
        compiler_params=pltpu.CompilerParams(
            collective_id=collective_id, has_side_effects=True
        ),
        name="spread_momentum",
    )(x)


def restore_kernel(cube, x_ref, o_ref, own_sem, send_sem, recv_sem):
    me = cube.index()
    repeat = cube.dp_size // 8
    d, s, c = lax.axis_index("dp"), lax.axis_index("seq"), lax.axis_index("shard")
    owner = lax.rem(d, repeat) == 0
    mine = ((d // repeat) * 2 + s) * 2 + c
    cube.greet_all()

    def send_all(wait, width):
        @pl.loop(1, cube.total)
        def _(i):
            to = lax.rem(me + i, cube.total)
            src = x_ref.at[to, :, pl.ds(0, width)]
            dst = o_ref.at[:, pl.ds(quarter_start(mine), width)]
            copy = remote(src, dst, send_sem.at[i], recv_sem.at[mine], cube.coords(to))
            if wait:
                copy.wait_send()
            else:
                copy.start()

    def keep(width):
        copy = pltpu.make_async_copy(
            x_ref.at[me, :, pl.ds(0, width)],
            o_ref.at[:, pl.ds(quarter_start(mine), width)],
            own_sem,
        )
        copy.start()
        copy.wait()

    @pl.when(owner)
    def _():
        by_matrix(mine // 4, functools.partial(send_all, False))
        by_matrix(mine // 4, keep)

    def receive(i):
        t = lax.rem(mine + i, 32)
        other = jnp.logical_or(jnp.logical_not(owner), i > 0)

        def go(width):
            place = o_ref.at[:, pl.ds(quarter_start(t), width)]
            remote(
                place, place, send_sem.at[0], recv_sem.at[t], owner_coords(cube, t)
            ).wait_recv()

        pl.when(other)(lambda: by_matrix(t // 4, go))

    pl.loop(0, 32)(receive)

    @pl.when(owner)
    def _():
        by_matrix(mine // 4, functools.partial(send_all, True))


def restore(cube, x, collective_id):
    return pl.pallas_call(
        functools.partial(restore_kernel, cube),
        out_shape=jax.ShapeDtypeStruct((x.shape[1], STARTS[8]), x.dtype),
        in_specs=[pl.BlockSpec(memory_space=pl.ANY)],
        out_specs=pl.BlockSpec(memory_space=pl.ANY),
        scratch_shapes=[
            pltpu.SemaphoreType.DMA,
            pltpu.SemaphoreType.DMA((cube.total,)),
            pltpu.SemaphoreType.DMA((32,)),
        ],
        compiler_params=pltpu.CompilerParams(
            collective_id=collective_id, has_side_effects=True
        ),
        name="restore_rows",
    )(x)


def split(value):
    high = value.astype(jnp.bfloat16)
    low = (value - high.astype(jnp.float32)).astype(jnp.bfloat16)
    return high, low


def product(left, right):
    (lh, ll), (rh, rl) = left, right
    dot = functools.partial(jnp.dot, preferred_element_type=jnp.float32)
    return dot(lh, rh) + (dot(lh, rl) + dot(ll, rh))


def orthogonalize_kernel(cube, x_ref, o_ref, gram_ref, work, landed, send_sem, recv_sem):
    barrier = pltpu.get_barrier_semaphore()
    peers = (cube.partner(cube.levels + 1), cube.partner(cube.levels))
    for peer in peers:
        pl.semaphore_signal(barrier, inc=1, device_id=peer, device_id_type=MESH)
    pl.semaphore_wait(barrier, 2)
    repeat = cube.dp_size // 8
    j = lax.axis_index("dp") // repeat
    width = 0
    for i in range(8):
        width = width + jnp.where(j == i, WIDTHS[i] // 4, 0)
    column = lax.broadcasted_iota(jnp.int32, (D, BLOCK), 1)
    block = jnp.where(column < width, x_ref[...].astype(jnp.float32), 0.0)
    bh, bl = split(block)
    dot_t = lambda a, b: lax.dot_general(
        a, b, (((1,), (1,)), ((), ())), preferred_element_type=jnp.float32
    )
    gram_ref[0] = dot_t(bh, bh) + (dot_t(bh, bl) + dot_t(bl, bh))
    for step in range(2):
        copy = remote(
            gram_ref.at[step], landed.at[step], send_sem.at[step], recv_sem.at[step], peers[step]
        )
        copy.start()
        copy.wait()
        gram_ref[step + 1] = gram_ref[step] + landed[step]
    gram = gram_ref[2]
    row = lax.broadcasted_iota(jnp.int32, (D, D), 0)
    col = lax.broadcasted_iota(jnp.int32, (D, D), 1)
    eye = row == col
    square = jnp.sum(jnp.sum(jnp.where(eye, gram, 0.0), axis=1, keepdims=True), axis=0, keepdims=True)
    scale = 1.0 / (jnp.sqrt(square) + 1e-07)
    gram = gram * (scale * scale)
    block = block * scale
    for step in range(5):
        parts = split(gram)
        mixed = COEF_B * gram + COEF_C * product(parts, parts)
        mixed = jnp.where(eye, mixed + COEF_A, mixed)
        mixed_parts = split(mixed)
        block = product(mixed_parts, split(block))
        if step < 4:
            gram = product(mixed_parts, split(product(mixed_parts, parts)))
    o_ref[...] = block.astype(o_ref.dtype)


def orthogonalize_blocks(cube, x, out_dtype, collective_id):
    return pl.pallas_call(
        functools.partial(orthogonalize_kernel, cube),
        out_shape=jax.ShapeDtypeStruct((D, BLOCK), out_dtype),
        in_specs=[pl.BlockSpec(memory_space=pltpu.VMEM)],
        out_specs=pl.BlockSpec(memory_space=pltpu.VMEM),
        scratch_shapes=[
            pltpu.VMEM((3, D, D), jnp.float32),
            pltpu.VMEM((8, 128), jnp.float32),
            pltpu.VMEM((2, D, D), jnp.float32),
            pltpu.SemaphoreType.DMA((2,)),
            pltpu.SemaphoreType.DMA((2,)),
        ],
        compiler_params=pltpu.CompilerParams(
            collective_id=collective_id, has_side_effects=True, vmem_limit_bytes=48 << 20
        ),
        name="orthogonalize",
    )(x)

def with_halo(value, sides, width):
    for axis, dim in sides:
        devices, length = (lax.axis_size(axis), value.shape[dim])
        up = [(i, (i + 1) % devices) for i in range(devices - 1)]
        down = [(j, i) for i, j in up]
        last = lax.slice_in_dim(value, length - width, length, axis=dim)
        first = lax.slice_in_dim(value, 0, width, axis=dim)
        before = lax.ppermute(last, axis, up)
        after = lax.ppermute(first, axis, down)
        value = jnp.concatenate([before, value, after], axis=dim)
    return value


def matmul(left, right):
    return jnp.dot(left, right, preferred_element_type=jnp.float32)


def matmul_right_t(left, right):
    return lax.dot_general(
        left, right, (((1,), (1,)), ((), ())), preferred_element_type=jnp.float32
    )


def matmul_left_t(left, right):
    return lax.dot_general(
        left, right, (((0,), (0,)), ((), ())), preferred_element_type=jnp.float32
    )


def layer_norm(field, gain):
    centre = jnp.mean(field, axis=-1, keepdims=True)
    shifted = field - centre
    inverse = lax.rsqrt(jnp.mean(shifted * shifted, axis=-1, keepdims=True) + EPS_NORM)
    normed = shifted * inverse
    return (normed * gain, normed, inverse)


def norm_back(grad_out, normed, inverse, gain):
    scaled = grad_out * gain
    grad_in = inverse * (
        scaled
        - jnp.mean(scaled, axis=-1, keepdims=True)
        - normed * jnp.mean(scaled * normed, axis=-1, keepdims=True)
    )
    return (grad_in, jnp.sum(grad_out * normed, axis=0))


def silu_slope(values):
    sigma = jax.nn.sigmoid(values)
    return sigma * (1.0 + values * (1.0 - sigma))


def ffn_forward(field, gain, w_in, w_back):
    normed_out, normed, inverse = layer_norm(field, gain)
    lifted = normed_out.astype(jnp.bfloat16)
    hidden_pre = matmul(lifted, w_in)
    hidden_act = jax.nn.silu(hidden_pre).astype(jnp.bfloat16)
    return (
        field + 0.5 * matmul_right_t(hidden_act, w_back),
        (lifted, hidden_pre, hidden_act, normed, inverse),
    )


def ffn_backward(grad, saved, gain, w_in, w_back):
    lifted, hidden_pre, hidden_act, normed, inverse = saved
    grad_branch = (0.5 * grad).astype(jnp.bfloat16)
    grad_back = matmul_left_t(grad_branch, hidden_act)
    grad_act = matmul(grad_branch, w_back)
    grad_pre = (grad_act * silu_slope(hidden_pre)).astype(jnp.bfloat16)
    grad_in = matmul_left_t(lifted, grad_pre)
    grad_field, grad_gain = norm_back(matmul_right_t(grad_pre, w_in), normed, inverse, gain)
    return (grad + grad_field, grad_in, grad_back, grad_gain)


def depthwise(wide, kernel, count):
    total = wide[0:count] * kernel[:, 0]
    for tap_idx in range(1, K):
        total = total + wide[tap_idx : tap_idx + count] * kernel[:, tap_idx]
    return total


def spread_rows(window, count, keys_len):
    padded = jnp.concatenate([window, jnp.zeros((1,), window.dtype)])
    tiled = jnp.broadcast_to(padded[None, :], (count, keys_len + count)).reshape(-1)
    shaped = tiled[: count * (keys_len + count - 1)].reshape(count, keys_len + count - 1)
    return shaped[:, count - 1 : count - 1 + keys_len]


def collect_rows(grid, count, keys_len):
    placed = jnp.concatenate([jnp.zeros((count, count - 1), grid.dtype), grid], axis=1).reshape(-1)
    placed = jnp.concatenate([placed, jnp.zeros((count,), grid.dtype)])
    return jnp.sum(placed.reshape(count, keys_len + count), axis=0)[: keys_len + count - 1]


def attention_scores(query, keys, offsets, first_row, row_start, block, head_idx):
    length = keys.shape[0]
    columns = slice(head_idx * DH, (head_idx + 1) * DH)
    anchor = length - block - first_row - row_start
    window = lax.dynamic_slice_in_dim(offsets[head_idx], anchor, length + block - 1)
    product = matmul_right_t(query[row_start : row_start + block, columns], keys[:, columns])
    return product * DH ** (-0.5) + spread_rows(window, block, length)


def attention_forward(query, keys, values, offsets, first_row):
    total_rows = query.shape[0]
    block = min(512, total_rows)
    head_outs = []
    head_lse = []
    for head_idx in range(H):
        scores = attention_scores(query, keys, offsets, first_row, 0, block, head_idx)
        row_max = jnp.max(scores, axis=1, keepdims=True)
        shifted_exp = jnp.exp(scores - row_max)
        row_total = jnp.sum(shifted_exp, axis=1, keepdims=True)
        prob_low = (shifted_exp / row_total).astype(jnp.bfloat16)
        head_outs.append(matmul(prob_low, values[:, head_idx * DH : (head_idx + 1) * DH]))
        head_lse.append((row_max + jnp.log(row_total))[:, 0])
    out_blocks = jnp.concatenate(head_outs, axis=1)
    lse_blocks = jnp.stack(head_lse, axis=0)
    return (out_blocks, lse_blocks)


def attention_backward(query, keys, values, offsets, first_row, log_total, grad_attended, delta):
    total_rows = query.shape[0]
    length = keys.shape[0]
    block = min(512, total_rows)
    scale = DH ** (-0.5)
    key_parts = [jnp.zeros((length, DH), jnp.float32) for head_idx in range(H)]
    value_parts = [jnp.zeros((length, DH), jnp.float32) for head_idx in range(H)]
    offset_rows = [jnp.zeros((2 * length - 1,), jnp.float32) for head_idx in range(H)]
    head_grads = []
    for head_idx in range(H):
        columns = slice(head_idx * DH, (head_idx + 1) * DH)
        scores = attention_scores(query, keys, offsets, first_row, 0, block, head_idx)
        prob = jnp.exp(scores - log_total[head_idx, 0:block][:, None])
        prob_low = prob.astype(jnp.bfloat16)
        grad_piece = grad_attended[0:block, columns]
        value_parts[head_idx] = matmul_left_t(prob_low, grad_piece)
        grad_prob = matmul_right_t(grad_piece, values[:, columns])
        grad_score = prob * (grad_prob - delta[0:block, head_idx][:, None])
        score_low = grad_score.astype(jnp.bfloat16)
        head_grads.append(matmul(score_low, keys[:, columns]) * scale)
        key_parts[head_idx] = matmul_left_t(score_low, query[0:block, columns]) * scale
        anchor = length - block - first_row - 0
        offset_rows[head_idx] = lax.dynamic_update_slice_in_dim(
            offset_rows[head_idx], collect_rows(grad_score, block, length), anchor, 0
        )
    query_blocks = jnp.concatenate(head_grads, axis=1)
    return (
        query_blocks,
        jnp.concatenate(key_parts, axis=1),
        jnp.concatenate(value_parts, axis=1),
        jnp.stack(offset_rows, axis=0),
    )


def mean_last(value):
    return jnp.mean(value, axis=-1, keepdims=True)


def normalize(field):
    shifted = field - mean_last(field)
    inverse = lax.rsqrt(mean_last(shifted * shifted) + EPS_NORM)
    return shifted * inverse, inverse


def norm_grad(grad_out, normed, inverse, gain):
    scaled = grad_out * gain
    grad_in = inverse * (scaled - mean_last(scaled) - normed * mean_last(scaled * normed))
    return grad_in, jnp.sum(grad_out * normed, axis=0, keepdims=True)


def row_to_tile(ref, base, row):
    for k in range(4):
        ref[base + k : base + k + 1, :] = row[:, 128 * k : 128 * (k + 1)]


def tile_to_row(tile):
    return jnp.concatenate([tile[k : k + 1, :] for k in range(4)], axis=1)


def skew(row, count):
    sub = lax.broadcasted_iota(jnp.int32, (8, 512), 0)
    block = jnp.broadcast_to(row, (8, 512))
    for bit in (1, 2, 4):
        block = jnp.where((sub // bit) % 2 == 1, pltpu.roll(block, bit, 1), block)
    size = 8
    while size < count:
        block = jnp.concatenate([block, pltpu.roll(block, size, 1)], axis=0)
        size *= 2
    return block


def unskew_sum(grid):
    size = grid.shape[0] // 2
    while size >= 8:
        grid = grid[:size] + pltpu.roll(grid[size:], 512 - size, 1)
        size //= 2
    sub = lax.broadcasted_iota(jnp.int32, (8, 512), 0)
    for bit in (1, 2, 4):
        grid = jnp.where((sub // bit) % 2 == 1, pltpu.roll(grid, 512 - bit, 1), grid)
    return jnp.sum(grid, axis=0, keepdims=True)


def tile_ranges(start, count, parts):
    ranges = []
    for n in range(parts, 0, -1):
        size = -(-count // n)
        ranges.append((128 * start, 128 * size))
        start, count = start + size, count - size
    return ranges


class Gather:
    def __init__(self, cube, mine, bands, send_sem, recv_sem):
        self.cube, self.mine, self.bands = cube, mine, bands
        self.chunks = GATHER_CHUNKS
        self.send_sem, self.recv_sem = send_sem, recv_sem
        self.copies = {}
        self.events = list(GATHER_EVENTS)
        self.last = cube.digits - 1

    def start(self, n, stage):
        g, pair, kind = self.chunks[n]
        for half in range(2):
            order = (self.cube.gather_orders, self.cube.gather_late_orders)[kind][half]
            done = order[:stage]
            index = tuple(
                slice(None) if k in done else self.mine[k] for k in range(self.cube.digits)
            )
            place = self.bands[g].at[index + (slice(None), pl.ds(*pair[half]))]
            copy = remote(
                place,
                place,
                self.send_sem.at[n, half, stage],
                self.recv_sem.at[n, half, stage],
                self.cube.partner(order[stage]),
            )
            copy.start()
            self.copies[n, half, stage] = copy

    def begin(self):
        for n, stage in GATHER_BEGIN:
            self.start(n, stage)

    def advance(self, n, stage):
        for half in range(2):
            self.copies[n, half, stage].wait_recv()
        if stage < self.last and (n, stage + 1) not in GATHER_HELD:
            self.start(n, stage + 1)
        for other in GATHER_AFTER.get((n, stage), ()):
            self.start(*other)

    def run_to(self, n, stage):
        while (n, stage) in self.events:
            self.advance(*self.events.pop(0))

    def finish(self):
        for copy in self.copies.values():
            copy.wait_send()


class Scatter:
    def __init__(self, cube, mine, bands, landed, outs, send_sem, recv_sem):
        self.cube, self.mine, self.landed = cube, mine, landed
        kinds = (cube.scatter_orders, cube.scatter_high_orders, cube.scatter_low_orders)
        self.chunks = [(bands[g], outs[g], pair) for g, pair, _ in SCATTER_CHUNKS]
        self.orders = [kinds[kind] for _, _, kind in SCATTER_CHUNKS]
        self.send_sem, self.recv_sem = send_sem, recv_sem
        self.copies = {}

    def start(self, n, stage):
        band, _, pair = self.chunks[n]
        for half in range(2):
            order = self.orders[n][half]
            index = []
            for k in range(self.cube.digits):
                at = order.index(k)
                if at > stage:
                    index.append(slice(None))
                else:
                    index.append(1 - self.mine[k] if at == stage else self.mine[k])
            copy = remote(
                band.at[tuple(index) + (slice(None), pl.ds(*pair[half]))],
                self.landed[(n * 2 + half) * self.cube.digits + stage],
                self.send_sem.at[n, half, stage],
                self.recv_sem.at[n, half, stage],
                self.cube.partner(order[stage]),
            )
            copy.start()
            self.copies[n, half, stage] = copy

    def add(self, n, half, stage):
        order = self.orders[n][half]
        band, out, pair = self.chunks[n]
        columns = pl.ds(*pair[half])
        free = [k for k in range(self.cube.digits) if order.index(k) > stage]
        extra = self.landed[(n * 2 + half) * self.cube.digits + stage]
        everything = (slice(None), columns)

        def one(i):
            digit = {
                k: lax.rem(i // (1 << (len(free) - 1 - m)), 2) for m, k in enumerate(free)
            }
            full = tuple(digit.get(k, self.mine[k]) for k in range(self.cube.digits)) + everything
            short = tuple(digit[k] for k in free) + (slice(None), slice(None))
            if free:
                band[full] = band[full] + extra[short]
            else:
                out[:, columns] = band[full].astype(jnp.float32) + extra[short].astype(jnp.float32)

        if free:
            pl.loop(0, 1 << len(free))(one)
        else:
            one(0)

    def advance(self, n, stage):
        for half in range(2):
            self.copies[n, half, stage].wait_recv()
            self.add(n, half, stage)
        if stage + 1 < self.cube.digits:
            self.start(n, stage + 1)

    def finish(self):
        for copy in self.copies.values():
            copy.wait_send()


class Collect:
    def __init__(self, cube, tile, slots, send_sem, recv_sem):
        self.cube, self.tile, self.slots = cube, tile, slots
        self.send_sem, self.recv_sem = send_sem, recv_sem

    def make(self, i):
        to = self.cube.coords(lax.rem(self.cube.index() + i, self.cube.total))
        return remote(
            self.tile, self.slots.at[i], self.send_sem.at[i], self.recv_sem.at[i], to
        )

    def start(self):
        pl.loop(1, self.cube.total)(lambda i: self.make(i).start())
        self.slots[0] = self.tile[...]

    def arrive(self):
        pl.loop(1, self.cube.total)(lambda i: self.make(i).wait())

    def total(self):
        result = self.slots[0]
        for i in range(1, self.cube.total):
            result = result + self.slots[i]
        return result


def share_columns(j):
    place = j // 2 if j % 2 else 1 - j // 2
    return slice(FF * place, FF * (place + 1))


def matrix_of(d):
    return sum(jnp.where(d == OWNER_PLACES[i], i, 0) for i in range(8))


def pack_small(target, turn, rel, vec, depth):
    rows = target.shape[0]
    turn[...] = jnp.zeros_like(turn)
    turn[0:7, 0:rows] = vec[...]
    target[...] = jnp.zeros_like(target)
    target[0 : rel.shape[0], SMALL_REL : SMALL_REL + H] = rel[...]
    target[:, SMALL_VEC : SMALL_VEC + 7] = jnp.transpose(turn[...])[0:rows, 0:7]
    target[:, SMALL_DEPTH : SMALL_DEPTH + K] = depth[...]


OWNER_PLACES = (2, 3, 5, 4, 0, 1, 7, 6)


def owner_place(cube, t):
    return (OWNER_PLACES[t // 4] * (cube.dp_size // 8), t // 2 % 2, t % 2)


class Momenta:
    def __init__(self, cube, r):
        self.cube, self.r = cube, r
        self.me = cube.index()
        self.repeat = cube.dp_size // 8
        d = lax.axis_index("dp")
        self.is_owner = lax.rem(d, self.repeat) == 0
        self.matrix = matrix_of(d // self.repeat)
        self.quarter = lax.axis_index("seq") * 2 + lax.axis_index("shard")
        self.owned_index = self.matrix * 4 + self.quarter

    def holds(self, t):
        return jnp.logical_and(self.is_owner, self.owned_index == t)

    def rows(self, j):
        r = self.r
        if j < 4:
            old, share = ((r.m_up, r.m_down)[j // 2], (r.share_first, r.share_second)[j % 2])
            return old[:, FF * (j % 2) : FF * (j % 2 + 1)], share[:, share_columns(j)]
        start = STARTS[j] - STARTS[4]
        old = (r.m_qkv, r.m_out, r.m_glu, r.m_point)[j - 4]
        return old[...], r.share_middle[:, start : start + WIDTHS[j]]

    def copy(self, t):
        width = WIDTHS[t // 4] // 4
        r = self.r
        return remote(
            r.leaving.at[t, :, pl.ds(0, width)],
            r.owned.at[self.me, :, pl.ds(0, width)],
            r.m_send.at[t],
            r.m_recv.at[self.me],
            owner_place(self.cube, t),
        )

    def send(self, j):
        old, share = self.rows(j)
        value = (MOMENTUM * old + share).astype(jnp.bfloat16)
        width = WIDTHS[j] // 4
        for q in range(4):
            t = 4 * j + q
            part = value[:, width * q : width * (q + 1)]
            self.r.leaving[t, :, 0:width] = part
            pl.when(jnp.logical_not(self.holds(t)))(lambda t=t: self.copy(t).start())

            @pl.when(self.holds(t))
            def _(part=part, width=width):
                self.r.owned[self.me, :, 0:width] = part

    def receive(self):
        r, cube = self.r, self.cube

        def go(width):
            @pl.loop(1, cube.total)
            def _(i):
                source = lax.rem(self.me + i, cube.total)
                place = r.owned.at[source, :, pl.ds(0, width)]
                remote(
                    place, place, r.m_send.at[0], r.m_recv.at[source], cube.coords(source)
                ).wait_recv()

        pl.when(self.is_owner)(lambda: by_matrix(self.matrix, go))

    def back(self, i, width):
        r, cube = self.r, self.cube
        to = lax.rem(self.me + i, cube.total)
        return remote(
            r.solved.at[to, :, pl.ds(0, width)],
            r.returned.at[self.owned_index, :, pl.ds(0, width)],
            r.b_send.at[i],
            r.b_recv.at[self.owned_index],
            cube.coords(to),
        )

    def keep(self, width):
        r = self.r
        return pltpu.make_async_copy(
            r.solved.at[self.me, :, pl.ds(0, width)],
            r.returned.at[self.owned_index, :, pl.ds(0, width)],
            r.k_sem,
        )

    def send_back(self):
        r = self.r

        def go(width):
            pl.loop(1, self.cube.total)(lambda i: self.back(i, width).start())
            self.keep(width).start()

        pl.when(self.is_owner)(lambda: by_matrix(self.matrix, go))

    def receive_back(self):
        r = self.r
        for t in range(32):
            place = r.returned.at[t, :, pl.ds(0, WIDTHS[t // 4] // 4)]
            copy = remote(
                place, place, r.b_send.at[0], r.b_recv.at[t], owner_place(self.cube, t)
            )
            pl.when(jnp.logical_not(self.holds(t)))(copy.wait_recv)

    def finish(self):
        for t in range(32):
            pl.when(jnp.logical_not(self.holds(t)))(lambda t=t: self.copy(t).wait_send())

        def go(width):
            pl.loop(1, self.cube.total)(lambda i: self.back(i, width).wait_send())
            self.keep(width).wait()

        pl.when(self.is_owner)(lambda: by_matrix(self.matrix, go))


def symmetric_product(left, right):
    half = D // 2
    (lh, ll), (rh, rl) = left, right
    top = product((lh[:half], ll[:half]), right)
    corner = product((lh[half:], ll[half:]), (rh[:, half:], rl[:, half:]))
    low = jnp.concatenate([jnp.transpose(top[:, half:]), corner], axis=1)
    return jnp.concatenate([top, low], axis=0)


def short_product(left, right):
    half = D // 2
    (lh, ll), rh = left, right[0]
    top = matmul(lh[:half], rh) + matmul(ll[:half], rh)
    corner = matmul(lh[half:], rh[:, half:]) + matmul(ll[half:], rh[:, half:])
    low = jnp.concatenate([jnp.transpose(top[:, half:]), corner], axis=1)
    return jnp.concatenate([top, low], axis=0)


GRAM_SHARES = (
    ((0, 0), (0, 1), (0, 2), (0, 3), (3, 3)),
    ((1, 1), (1, 2), (1, 3), (2, 2), (2, 3)),
)


def orthogonalize(cube, r):
    f32 = jnp.float32
    core, seq = lax.axis_index("shard"), lax.axis_index("seq")
    block = r.owned.reshape(D, BLOCK)
    lines = [slice(128 * i, 128 * (i + 1)) for i in range(4)]
    peers = (cube.partner(cube.levels + 1), cube.partner(cube.levels))
    count = len(GRAM_SHARES[0])

    def piece(step, n):
        source, target, peer = (
            (r.packed.at[1 - core, n], r.packed_in.at[0, n], peers[0]),
            (r.summed.at[n], r.packed_in.at[1, n], peers[1]),
            (r.whole.at[core, n], r.whole.at[core, n], peers[0]),
        )[step]
        return remote(source, target, r.n_send.at[step, n], r.n_recv.at[step, n], peer)

    for n in range(count):
        for share in range(2):
            i, j = GRAM_SHARES[share][n]
            r.packed[share, n] = matmul_right_t(block[lines[i], :], block[lines[j], :])
        piece(0, n).start()
    for n in range(count):
        piece(0, n).wait()
        r.summed[n] = r.packed[core, n] + r.packed_in[0, n]
        piece(1, n).start()
    for n in range(count):
        piece(1, n).wait()
        r.whole[core, n] = r.summed[n] + r.packed_in[1, n]
        piece(2, n).start()
    for n in range(count):
        piece(2, n).wait()
    for share in range(2):
        for n, (i, j) in enumerate(GRAM_SHARES[share]):
            value = r.whole[share, n]
            r.gram[lines[i], lines[j]] = value
            if i != j:
                r.gram[lines[j], lines[i]] = jnp.transpose(value)
    row = lax.broadcasted_iota(jnp.int32, (D, D), 0)
    col = lax.broadcasted_iota(jnp.int32, (D, D), 1)
    eye = row == col
    gram = r.gram[...]
    square = jnp.sum(
        jnp.sum(jnp.where(eye, gram, 0.0), axis=1, keepdims=True), axis=0, keepdims=True
    )
    scale = 1.0 / (jnp.sqrt(square) + 1e-07)
    gram = gram * (scale * scale)
    value = None
    for step in range(4):
        parts = split(gram)
        mixed = COEF_B * gram + COEF_C * symmetric_product(parts, parts)
        mixed = jnp.where(eye, mixed + COEF_A, mixed)
        high, low = split(mixed)
        if step == 0:
            start_high, start_low = split(mixed * scale)
            value = matmul(start_high, block[...]) + matmul(start_low, block[...])
        elif step < 3:
            value = product((high, low), split(value))
        else:
            value = matmul(high, value.astype(jnp.bfloat16))
        times = symmetric_product if step < 3 else short_product
        gram = times((high, low), split(times((high, low), parts)))
    short = gram.astype(jnp.bfloat16)
    mixed = COEF_B * gram + COEF_C * matmul(short, short)
    mixed = jnp.where(eye, mixed + COEF_A, mixed).astype(jnp.bfloat16)
    value = matmul(mixed, value.astype(jnp.bfloat16))
    r.solved.reshape(D, BLOCK)[...] = value.astype(jnp.bfloat16)


SMALL_REL, SMALL_VEC, SMALL_DEPTH = 0, H, H + 7
SMALL_END = H + 7 + K
EDGE = 16
GATHER_CHUNKS = (
    (0, tile_ranges(0, 17, 2), 0),
    (0, tile_ranges(17, 16, 2), 0),
    (1, tile_ranges(0, 20, 2), 0),
    (2, tile_ranges(0, 16, 2), 0),
    (1, tile_ranges(20, 8, 2), 1),
    (2, tile_ranges(16, 16, 2), 1),
)
GATHER_BEGIN = ((0, 0), (4, 0),)
GATHER_EVENTS = (
    ((4, 0), (0, 0), (4, 1), (5, 0), (5, 1), (0, 1), (1, 0), (0, 2), (1, 1), (2, 0))
    + ((2, 1), (3, 0), (1, 2), (0, 3), (0, 4), (4, 2), (3, 1), (2, 2), (1, 3), (1, 4))
    + ((5, 2), (3, 2), (2, 3), (4, 3), (4, 4), (2, 4), (3, 3), (3, 4), (5, 3), (5, 4))
)
SCATTER_EVENTS = (
    ((0, 1), (3, 0), (1, 1), (4, 0), (2, 1), (5, 0), (3, 1), (6, 1), (0, 2), (1, 2), (4, 1))
    + ((2, 2), (5, 1), (6, 2), (3, 2), (1, 3), (2, 3), (0, 3), (4, 2), (3, 3), (1, 4), (2, 4))
    + ((0, 4), (5, 2), (6, 3), (4, 3), (3, 4), (6, 4), (5, 3), (4, 4), (5, 4))
)
SCATTER_STORES = ((4,), (), (), (), (), (2,), (3,))
EARLY_LOADS = tuple("w_up w_down w_qkv w_out".split()) + tuple("w_glu w_point rel vec".split())
EARLY_LOADS += tuple("depth m_rel m_vec m_depth".split())
SCATTER_MATRICES = ((3,), (1,), (5,), (4,), (2,), (0,), (6, 7))
GATHER_HELD = ((4, 2), (5, 2),)
GATHER_AFTER = {
    (4, 0): [(5, 0)],
    (0, 0): [(1, 0)],
    (1, 0): [(2, 0)],
    (2, 0): [(3, 0)],
    (2, 1): [(4, 2)],
    (4, 2): [(5, 2)],
}
FIRST_READY, MIDDLE_READY, SECOND_READY = (1, 4), (2, 4), (5, 4)
SCATTER_CHUNKS = (
    (0, tile_ranges(16, 16, 2), 1),
    (0, tile_ranges(0, 16, 2), 2),
    (1, tile_ranges(12, 4, 2), 0),
    (1, tile_ranges(0, 12, 2), 0),
    (2, tile_ranges(0, 16, 2), 0),
    (2, tile_ranges(16, 17, 2), 0),
    (1, tile_ranges(16, 12, 2), 1),
)


def step_kernel(cube, r):
    bf16, f32 = jnp.bfloat16, jnp.float32
    x_ref, cot_ref, bucket_ref = r.inputs, r.cotangent, r.bucket
    tokens = x_ref.shape[0]
    token_total = tokens * cube.total
    rows = r.w_up.shape[0]
    rel_rows = r.rel.shape[0]
    mine = cube.mine()
    seq = lax.axis_index("seq")
    early = seq == 0
    first_row = pl.multiple_of(seq * tokens, tokens)
    other_row = pl.multiple_of((1 - seq) * tokens, tokens)
    across = cube.partner(cube.levels)
    lengths = [ref.shape[-1] for ref in (r.first, r.middle, r.second)]
    first, middle, second, d_first, d_middle, d_second = (
        ref.reshape(D, ref.shape[-1])
        for ref in (r.first, r.middle, r.second, r.d_first, r.d_middle, r.d_second)
    )
    a, xh = r.a, r.xh

    barrier = pltpu.get_barrier_semaphore()
    me = cube.index()
    momenta = Momenta(cube, r)
    for load in r.loads.values():
        load.start()
    r.owned[...] = jnp.zeros_like(r.owned)

    @pl.loop(1, cube.total)
    def _(i):
        peer = cube.coords(lax.rem(me + i, cube.total))
        pl.semaphore_signal(barrier, inc=1, device_id=peer, device_id_type=MESH)

    for name in EARLY_LOADS:
        r.loads[name].wait()
    pack_small(r.small, r.turn, r.rel, r.vec, r.depth)
    pack_small(r.m_small, r.turn, r.m_rel, r.m_vec, r.m_depth)
    own = tuple(mine)
    r.first[own + (slice(None), slice(FF, 2 * FF))] = r.w_up[:, :FF].astype(bf16)
    r.first[own + (slice(None), slice(0, FF))] = r.w_down[:, :FF].astype(bf16)
    r.first[own + (slice(None), slice(2 * FF, lengths[0]))] = r.small[...].astype(bf16)
    r.middle[own + (slice(None), slice(0, 3 * D))] = r.w_qkv[...].astype(bf16)
    r.middle[own + (slice(None), slice(3 * D, 4 * D))] = r.w_out[...].astype(bf16)
    r.middle[own + (slice(None), slice(4 * D, 6 * D))] = r.w_glu[...].astype(bf16)
    r.middle[own + (slice(None), slice(6 * D, 7 * D))] = r.w_point[...].astype(bf16)
    r.second[own + (slice(None), slice(0, FF))] = r.w_up[:, FF:].astype(bf16)
    r.second[own + (slice(None), slice(FF, 2 * FF))] = r.w_down[:, FF:].astype(bf16)
    pl.semaphore_wait(barrier, cube.total - 1)

    gather = Gather(
        cube, mine, (r.first, r.middle, r.second), r.g_send, r.g_recv
    )
    scatter = Scatter(
        cube,
        mine,
        (r.d_second, r.d_middle, r.d_first),
        r.land,
        (r.share_second, r.share_middle, r.share_first),
        r.s_send,
        r.s_recv,
    )

    gather.begin()
    for name in [name for name in r.loads if name not in EARLY_LOADS]:
        r.loads[name].wait()
    xh0, inv0 = normalize(x_ref[...])
    xh[0] = xh0
    rho = lax.broadcasted_iota(jnp.int32, (D, bucket_ref.shape[1]), 0)
    bucket_of = jnp.where(rho % rows < rel_rows, (rho // rows) * rel_rows + rho % rows, -2)
    r.hit[...] = jnp.zeros_like(r.hit)
    offset_count = bucket_ref.shape[1]
    r.hit[:, 0:offset_count] = (bucket_ref[...] == bucket_of).astype(f32).astype(bf16)
    gather.run_to(*FIRST_READY)

    small = r.small_t
    small[...] = jnp.transpose(first[:, 2 * FF : 2 * FF + 128].astype(f32))
    gains = [small[SMALL_VEC + i : SMALL_VEC + i + 1, :] for i in range(7)]
    taps = [small[SMALL_DEPTH + k : SMALL_DEPTH + k + 1, :] for k in range(K)]
    CH = 512

    def ffn_forward_fused(index, field, normed, up, down, u_ref, s_ref):
        low = (normed * gains[(0, 1, 2, 3)[index]]).astype(bf16)
        a[index] = low
        for c in range(0, FF, CH):
            u = matmul(low, up[:, c : c + CH])
            u_ref[:, c : c + CH] = u
            s_ref[:, c : c + CH] = (u * jax.nn.sigmoid(u)).astype(bf16)
        return field + 0.5 * matmul_right_t(s_ref[...], down[...])

    down1, up1 = first.at[:, pl.ds(0, FF)], first.at[:, pl.ds(FF, FF)]
    up2, down2 = second.at[:, pl.ds(0, FF)], second.at[:, pl.ds(FF, FF)]
    section1 = ffn_forward_fused(0, x_ref[...], xh[0], up1, down1, r.u1, r.s1)
    r.sec1[...] = section1
    xh1, inv1 = normalize(section1)
    xh[1] = xh1
    a[1] = (xh1 * gains[1]).astype(bf16)
    offsets = matmul(small[0:8, :].astype(bf16), r.hit[...])
    offsets = jnp.where(
        early, pltpu.roll(offsets, 257, 1), pltpu.roll(offsets, (tokens + 257) % 512, 1)
    )
    for h in range(H):
        r.bias[h] = skew(offsets[h : h + 1, :], tokens)[:, : 2 * tokens]
    gather.run_to(*MIDDLE_READY)

    q_ref, kv = r.q, r.kv
    kv[pl.ds(first_row, tokens), :] = matmul(a[1], middle[:, D : 3 * D]).astype(bf16)
    kv_copy = remote(
        kv.at[pl.ds(first_row, tokens)],
        kv.at[pl.ds(first_row, tokens)],
        r.kv_send,
        r.kv_recv,
        across,
    )
    kv_copy.start()
    q_ref[...] = matmul(a[1], middle[:, :D]).astype(bf16)
    gather.run_to(*(2, 4))
    kv_copy.wait_recv()
    gather.run_to(*(3, 3))
    lane = lax.broadcasted_iota(jnp.int32, (1, 128), 1)
    lane_masks = [(lane // DH == e).astype(f32) for e in range(2)]
    low_masks = [m.astype(bf16) for m in lane_masks]
    scale = DH ** (-0.5)
    for p in range(H // 2):
        columns = slice(128 * p, 128 * (p + 1))
        k_pair, v_pair = kv[:, columns], kv[:, D + 128 * p : D + 128 * (p + 1)]
        merged = None
        for e in range(2):
            q_head = q_ref[:, columns] * low_masks[e]
            scores = matmul_right_t(q_head, k_pair) * scale + r.bias[2 * p + e]
            shifted = jnp.exp(scores - jnp.max(scores, axis=1, keepdims=True))
            prob = shifted / jnp.sum(shifted, axis=1, keepdims=True)
            r.prob[2 * p + e] = prob
            out = matmul(prob.astype(bf16), v_pair) * lane_masks[e]
            merged = out if merged is None else merged + out
        r.att[:, columns] = merged
        if p == 1:
            gather.run_to(*(3, 4))
    gather.run_to(*SECOND_READY)
    att_low = r.att[...].astype(bf16)
    r.att_low[...] = att_low
    section2 = r.sec1[...] + matmul(att_low, middle[:, 3 * D : 4 * D])
    r.sec2[...] = section2
    xh2, inv2 = normalize(section2)
    xh[2] = xh2
    a[2] = (xh2 * gains[2]).astype(bf16)
    gate_first = matmul(a[2], middle[:, 4 * D : 5 * D])
    sig = jax.nn.sigmoid(matmul(a[2], middle[:, 5 * D : 6 * D]))
    r.gate[...] = gate_first
    r.sig[...] = sig
    wide = r.wide
    wide[EDGE : EDGE + tokens, :] = gate_first * sig
    edge_row = pl.multiple_of(EDGE + (1 - seq) * (tokens - EDGE), EDGE)
    halo_copy = remote(
        wide.at[pl.ds(edge_row, EDGE)], r.halo, r.halo_send, r.halo_recv, across
    )
    halo_copy.start()
    zero_edge = jnp.zeros((EDGE, D), f32)
    halo_copy.wait()
    wide[0:EDGE, :] = jnp.where(early, zero_edge, r.halo[...])
    wide[EDGE + tokens :, :] = jnp.where(early, r.halo[...], zero_edge)
    conv_ref = r.conv
    for b in range(D // 128):
        cols = slice(128 * b, 128 * (b + 1))
        total = jnp.zeros((tokens, 128), f32)
        for k in range(K):
            total = total + wide[k + 1 : k + 1 + tokens, cols] * taps[k][:, cols]
        conv_ref[:, cols] = total
    conv = conv_ref[...]
    part_sum = jnp.sum(conv, axis=0, keepdims=True)
    part_off = conv - part_sum * (1.0 / tokens)
    part_square = jnp.sum(part_off * part_off, axis=0, keepdims=True)
    row_to_tile(r.tile1, 0, part_sum)
    row_to_tile(r.tile1, 4, part_square)
    stats = Collect(cube, r.tile1, r.slots1, r.c1_send, r.c1_recv)
    stats.start()
    stats.arrive()
    sums = stats.total()
    mean4 = sums[0:4] * (1.0 / token_total)
    spread4 = jnp.zeros((4, 128), f32)
    for i in range(cube.total):
        off = r.slots1[i][0:4] * (1.0 / tokens) - mean4
        spread4 = spread4 + off * off
    var4 = (sums[4:8] + spread4 * tokens) * (1.0 / token_total)
    mean = tile_to_row(mean4)
    inv_std = tile_to_row(lax.rsqrt(var4 + EPS_BATCH))

    xb = (conv_ref[...] - mean) * inv_std
    r.xb[...] = xb
    bn = xb * gains[5] + gains[6]
    r.bn[...] = bn
    sw = (bn * jax.nn.sigmoid(bn)).astype(bf16)
    r.sw[...] = sw
    section3 = r.sec2[...] + matmul(sw, middle[:, 6 * D : 7 * D])
    xh3, inv3 = normalize(section3)
    xh[3] = xh3
    section4 = ffn_forward_fused(3, section3, xh3, up2, down2, r.u2, r.s2)
    xh4, inv4 = normalize(section4)
    r.outputs[...] = xh4 * gains[4]
    r.stores[0].start()

    sg = r.small_grad
    sg[...] = jnp.zeros_like(sg)
    cot = cot_ref[...]
    d4, sg[SMALL_VEC + 4 : SMALL_VEC + 5, :] = norm_grad(cot, xh4, inv4, gains[4])

    def slope(value):
        sigma = jax.nn.sigmoid(value)
        return sigma * (1.0 + value * (1.0 - sigma))

    def slopes(low, down, u_ref, du_ref):
        for c in range(0, FF, CH):
            act = matmul(low, down[:, c : c + CH])
            du_ref[:, c : c + CH] = (act * slope(u_ref[:, c : c + CH])).astype(bf16)

    def weight_grad(left, right_ref, target, start, width):
        for c in range(0, width, CH):
            target[:, start + c : start + c + CH] = matmul_left_t(
                left, right_ref[:, c : c + CH]
            ).astype(bf16)

    r.e_low[...] = (0.5 * d4).astype(bf16)
    slopes(r.e_low[...], down2, r.u2, r.du)
    back = matmul_right_t(r.du[...], up2[...])
    part, sg[SMALL_VEC + 3 : SMALL_VEC + 4, :] = norm_grad(back, xh[3], inv3, gains[3])
    d3 = d4 + part
    r.d[...] = d3
    e3 = d3.astype(bf16)
    r.e3[...] = e3
    dbn = matmul_right_t(e3, middle[:, 6 * D : 7 * D]) * slope(r.bn[...])
    xb = r.xb[...]
    sg[SMALL_VEC + 5 : SMALL_VEC + 6, :] = jnp.sum(dbn * xb, axis=0, keepdims=True)
    sg[SMALL_VEC + 6 : SMALL_VEC + 7, :] = jnp.sum(dbn, axis=0, keepdims=True)
    dxb = dbn * gains[5]
    r.dxb[...] = dxb
    row_to_tile(r.tile2, 0, jnp.sum(dxb, axis=0, keepdims=True))
    row_to_tile(r.tile2, 4, jnp.sum(dxb * xb, axis=0, keepdims=True))
    sums2 = Collect(cube, r.tile2, r.slots2, r.c2_send, r.c2_recv)
    sums2.start()
    token_edge = pl.multiple_of((1 - seq) * (tokens - EDGE), EDGE)
    edges = r.edges
    edges[0:EDGE, :] = r.dxb[pl.ds(token_edge, EDGE), :]
    edges[EDGE:, :] = r.xb[pl.ds(token_edge, EDGE), :]
    edge_copy = remote(edges, r.edges_in, r.edge_send, r.edge_recv, across)
    edge_copy.start()

    weight_grad(r.e_low[...], r.s2, d_second, FF, FF)
    scatter.start(0, 0)
    weight_grad(a[3], r.du, d_second, 0, FF)
    scatter.start(1, 0)
    weight_grad(r.sw[...], r.e3, d_middle, 6 * D, D)
    edge_copy.wait()
    sums2.arrive()
    total2 = sums2.total()
    mean1 = tile_to_row(total2[0:4] * (1.0 / token_total))
    mean2 = tile_to_row(total2[4:8] * (1.0 / token_total))
    dwide = r.dwide
    dwide[EDGE : EDGE + tokens, :] = inv_std * (r.dxb[...] - mean1 - r.xb[...] * mean2)
    edge = inv_std * (r.edges_in[0:EDGE, :] - mean1 - r.edges_in[EDGE:, :] * mean2)
    dwide[0:EDGE, :] = jnp.where(early, zero_edge, edge)
    dwide[EDGE + tokens :, :] = jnp.where(early, edge, zero_edge)
    dglu_ref = r.conv
    for b in range(D // 128):
        cols = slice(128 * b, 128 * (b + 1))
        total = jnp.zeros((tokens, 128), f32)
        for k in range(K):
            total = total + dwide[31 - k : 31 - k + tokens, cols] * taps[k][:, cols]
        dglu_ref[:, cols] = total
    dglu, sig = dglu_ref[...], r.sig[...]
    r.dgates[:, :D] = (dglu * sig).astype(bf16)
    r.dgates[:, D:] = (dglu * r.gate[...] * sig * (1.0 - sig)).astype(bf16)
    scatter.advance(0, 0)
    back = matmul_right_t(r.dgates[...], middle[:, 4 * D : 6 * D])
    part, sg[SMALL_VEC + 2 : SMALL_VEC + 3, :] = norm_grad(back, xh[2], inv2, gains[2])
    d2 = r.d[...] + part
    r.d[...] = d2
    e1 = d2.astype(bf16)
    r.e_low[...] = e1
    dob = matmul_right_t(e1, middle[:, 3 * D : 4 * D]).astype(bf16)
    r.dob[...] = dob
    weight_grad(r.att_low[...], r.e_low, d_middle, 3 * D, D)
    weight_grad(a[2], r.dgates, d_middle, 4 * D, 2 * D)
    scatter.start(2, 0)
    scatter.start(6, 0)

    off_rows = []
    give, keep, got = r.give, r.keep, r.got
    kv_grads = []
    for p in range(H // 2):
        columns = slice(128 * p, 128 * (p + 1))
        k_pair, v_pair = kv[:, columns], kv[:, D + 128 * p : D + 128 * (p + 1)]
        att_pair = r.att[:, columns]
        dq = dk = dv = None
        for e in range(2):
            h = 2 * p + e
            dob_head = r.dob[:, columns] * low_masks[e]
            q_head = q_ref[:, columns] * low_masks[e]
            delta = jnp.sum(dob_head.astype(f32) * att_pair, axis=1, keepdims=True)
            prob = r.prob[h]
            ds = prob * (matmul_right_t(dob_head, v_pair) - delta)
            ds_low = ds.astype(bf16)
            dv_head = matmul_left_t(prob.astype(bf16), dob_head)
            dk_head = matmul_left_t(ds_low, q_head) * scale
            dq_head = matmul(ds_low, k_pair) * (lane_masks[e] * scale)
            dv = dv_head if dv is None else dv + dv_head
            dk = dk_head if dk is None else dk + dk_head
            dq = dq_head if dq is None else dq + dq_head
            padded = jnp.concatenate([ds, jnp.zeros((tokens, 512 - 2 * tokens), f32)], axis=1)
            off_rows.append(unskew_sum(padded))
        r.dqkv[:, columns] = dq.astype(bf16)
        for n, value in enumerate((dk, dv)):
            r.dkv[n] = value
            give[p, n] = r.dkv[n, pl.ds(other_row, tokens), :].astype(bf16)
            keep[p, n] = r.dkv[n, pl.ds(first_row, tokens), :]
        copy = remote(
            give.at[p], got.at[p], r.dkv_send.at[p], r.dkv_recv.at[p], across
        )
        copy.start()
        kv_grads.append(copy)
        if p == 1:
            scatter.advance(1, 0)
    off = jnp.concatenate(off_rows, axis=0)
    off = jnp.where(early, pltpu.roll(off, 255, 1), pltpu.roll(off, 255 - tokens, 1))
    off_high, off_low = split(off)
    sg[0:8, :] = matmul_right_t(off_high, r.hit[...]) + matmul_right_t(off_low, r.hit[...])
    for b in range(D // 128):
        cols = slice(128 * b, 128 * (b + 1))
        dconv = dwide[EDGE : EDGE + tokens, cols]
        for k in range(K):
            sg[SMALL_DEPTH + k : SMALL_DEPTH + k + 1, cols] = jnp.sum(
                dconv * wide[k + 1 : k + 1 + tokens, cols], axis=0, keepdims=True
            )
    for p in range(H // 2):
        kv_grads[p].wait()
        for n in range(2):
            at = D * (n + 1) + 128 * p
            r.dqkv[:, at : at + 128] = (keep[p, n] + got[p, n].astype(f32)).astype(bf16)
    scatter.advance(2, 0)
    scatter.advance(6, 0)
    back = matmul_right_t(r.dqkv[...], middle[:, : 3 * D])
    part, sg[SMALL_VEC + 1 : SMALL_VEC + 2, :] = norm_grad(back, xh[1], inv1, gains[1])
    d1 = r.d[...] + part
    e0 = (0.5 * d1).astype(bf16)
    weight_grad(a[1], r.dqkv, d_middle, 0, 3 * D)
    scatter.start(3, 0)
    weight_grad(e0, r.s1, d_first, 0, FF)
    scatter.start(4, 0)
    slopes(e0, down1, r.u1, r.du)
    back = matmul_right_t(r.du[...], up1[...])
    part, sg[SMALL_VEC : SMALL_VEC + 1, :] = norm_grad(back, xh[0], inv0, gains[0])
    r.input_grad[...] = d1 + part
    r.stores[1].start()
    d_first[:, 2 * FF : 2 * FF + 128] = jnp.transpose(sg[...]).astype(bf16)
    weight_grad(a[0], r.du, d_first, FF, FF)
    scatter.start(5, 0)
    for n, stage in SCATTER_EVENTS:
        scatter.advance(n, stage)
        if stage == scatter.cube.digits - 1:
            for j in SCATTER_MATRICES[n]:
                momenta.send(j)
            for store in SCATTER_STORES[n]:
                r.stores[store].start()
    next_small = MOMENTUM * r.m_small[...] + r.share_first[:, 2 * FF :]
    r.tile3[...] = jnp.zeros_like(r.tile3)
    r.tile3[0:1, :] = jnp.sum(next_small * next_small, axis=0, keepdims=True)
    squares = Collect(cube, r.tile3, r.slots3, r.c3_send, r.c3_recv)
    squares.start()
    momenta.receive()
    orthogonalize(cube, r)
    momenta.send_back()
    squares.arrive()
    r.squares[...] = squares.total()
    r.stores[5].start()
    momenta.receive_back()
    momenta.finish()
    gather.finish()
    scatter.finish()
    for store in r.stores:
        store.wait()
    kv_copy.wait_send()


def fused_step(cube, inputs, cotangent, weights, momenta, bucket, collective_id):
    bf16, f32 = jnp.bfloat16, jnp.float32
    tokens, rows = inputs.shape[0], weights[0].shape[0]
    widths = (2 * FF + 128, 7 * D, 2 * FF)
    lead = (2,) * cube.digits
    named = dict(
        inputs=inputs,
        cotangent=cotangent,
        w_up=weights[0],
        w_down=weights[1],
        w_qkv=weights[2],
        w_out=weights[3],
        w_glu=weights[4],
        w_point=weights[5],
        vec=weights[6],
        depth=weights[7],
        rel=weights[8],
        m_up=momenta[0],
        m_down=momenta[1],
        m_qkv=momenta[2],
        m_out=momenta[3],
        m_glu=momenta[4],
        m_point=momenta[5],
        m_vec=momenta[6],
        m_depth=momenta[7],
        m_rel=momenta[8],
        bucket=bucket,
    )
    outs = dict(
        outputs=jax.ShapeDtypeStruct((tokens, D), f32),
        input_grad=jax.ShapeDtypeStruct((tokens, D), f32),
        share_first=jax.ShapeDtypeStruct((rows, widths[0]), f32),
        share_middle=jax.ShapeDtypeStruct((rows, widths[1]), f32),
        share_second=jax.ShapeDtypeStruct((rows, widths[2]), f32),
        returned=jax.ShapeDtypeStruct((32, rows, BLOCK), bf16),
        squares=jax.ShapeDtypeStruct((8, 128), f32),
    )
    field = pltpu.VMEM((tokens, D), f32)
    low = pltpu.VMEM((tokens, D), bf16)
    wide_low = pltpu.VMEM((tokens, FF), bf16)
    wide_field = pltpu.VMEM((tokens + 2 * EDGE, D), f32)
    grid = pltpu.VMEM((H, tokens, 2 * tokens), f32)
    pairs = pltpu.VMEM((H // 2, 2, tokens, 128), bf16)
    tile = pltpu.VMEM((8, 128), f32)
    slots = pltpu.VMEM((cube.total, 8, 128), f32)
    stages = pltpu.SemaphoreType.DMA((7, 2, cube.digits))
    gather_stages = pltpu.SemaphoreType.DMA((6, 2, cube.digits))
    everyone = pltpu.SemaphoreType.DMA((cube.total,))
    single = pltpu.SemaphoreType.DMA
    bands = [pltpu.VMEM(lead + (rows, w), bf16) for w in widths]
    land = []
    for _, pair, _ in SCATTER_CHUNKS:
        for _, part in pair:
            for stage in range(cube.digits):
                shape = (2,) * (cube.digits - 1 - stage) + (rows, part)
                land.append(pltpu.VMEM(shape, bf16))
    scratch = dict(
        first=bands[0],
        middle=bands[1],
        second=bands[2],
        d_first=bands[0],
        d_middle=bands[1],
        d_second=bands[2],
        land=tuple(land),
        sec1=field,
        sec2=field,
        att=field,
        gate=field,
        sig=field,
        conv=field,
        xb=field,
        bn=field,
        dxb=field,
        d=field,
        q=low,
        att_low=low,
        sw=low,
        e_low=low,
        e3=low,
        dob=low,
        a=pltpu.VMEM((4, tokens, D), bf16),
        xh=pltpu.VMEM((4, tokens, D), f32),
        u1=pltpu.VMEM((tokens, FF), f32),
        u2=pltpu.VMEM((tokens, FF), f32),
        s1=wide_low,
        s2=wide_low,
        du=wide_low,
        kv=pltpu.VMEM((2 * tokens, 2 * D), bf16),
        bias=grid,
        prob=grid,
        wide=wide_field,
        dwide=wide_field,
        halo=pltpu.VMEM((EDGE, D), f32),
        edges=pltpu.VMEM((2 * EDGE, D), f32),
        edges_in=pltpu.VMEM((2 * EDGE, D), f32),
        dgates=pltpu.VMEM((tokens, 2 * D), bf16),
        dqkv=pltpu.VMEM((tokens, 3 * D), bf16),
        dkv=pltpu.VMEM((2, 2 * tokens, 128), f32),
        give=pairs,
        got=pairs,
        keep=pltpu.VMEM((H // 2, 2, tokens, 128), f32),
        small=pltpu.VMEM((rows, 128), f32),
        m_small=pltpu.VMEM((rows, 128), f32),
        turn=pltpu.VMEM((128, 128), f32),
        hit=pltpu.VMEM((D, 512), bf16),
        small_t=pltpu.VMEM((128, D), f32),
        small_grad=pltpu.VMEM((128, D), f32),
        tile1=tile,
        tile2=tile,
        slots1=slots,
        slots2=slots,
        tile3=tile,
        slots3=slots,
        leaving=pltpu.VMEM((32, rows, BLOCK), bf16),
        owned=pltpu.VMEM((cube.total, rows, BLOCK), bf16),
        solved=pltpu.VMEM((cube.total, rows, BLOCK), bf16),
        packed=pltpu.VMEM((2, 5, 128, 128), f32),
        packed_in=pltpu.VMEM((2, 5, 128, 128), f32),
        summed=pltpu.VMEM((5, 128, 128), f32),
        whole=pltpu.VMEM((2, 5, 128, 128), f32),
        gram=pltpu.VMEM((D, D), f32),
        m_send=pltpu.SemaphoreType.DMA((32,)),
        m_recv=everyone,
        b_send=everyone,
        b_recv=pltpu.SemaphoreType.DMA((32,)),
        n_send=pltpu.SemaphoreType.DMA((3, 5)),
        n_recv=pltpu.SemaphoreType.DMA((3, 5)),
        c3_send=everyone,
        c3_recv=everyone,
        g_send=gather_stages,
        g_recv=gather_stages,
        s_send=stages,
        s_recv=stages,
        c1_send=everyone,
        c1_recv=everyone,
        c2_send=everyone,
        c2_recv=everyone,
        kv_send=single,
        kv_recv=single,
        halo_send=single,
        halo_recv=single,
        edge_send=single,
        edge_recv=single,
        dkv_send=pltpu.SemaphoreType.DMA((H // 2,)),
        dkv_recv=pltpu.SemaphoreType.DMA((H // 2,)),
    )

    kept = [n for n in outs if n != "returned"]
    buffers = dict({n: pltpu.VMEM(v.shape, v.dtype) for n, v in named.items()})
    buffers |= {n: pltpu.VMEM(outs[n].shape, outs[n].dtype) for n in kept}
    scratch |= buffers
    scratch |= dict(
        load_sem=pltpu.SemaphoreType.DMA((len(named),)),
        store_sem=pltpu.SemaphoreType.DMA((len(kept),)),
        k_sem=single,
    )

    def body(*refs):
        count = len(named) + len(outs)
        far = dict(zip(list(named) + list(outs), refs[:count]))
        near = dict(zip(scratch, refs[count:]))
        near["returned"] = far["returned"]
        near["loads"] = {
            name: pltpu.make_async_copy(far[name], near[name], near["load_sem"].at[n])
            for n, name in enumerate(named)
        }
        near["stores"] = [
            pltpu.make_async_copy(near[name], far[name], near["store_sem"].at[n])
            for n, name in enumerate(kept)
        ]
        step_kernel(cube, types.SimpleNamespace(**near))

    return pl.pallas_call(
        body,
        out_shape=list(outs.values()),
        in_specs=[pl.BlockSpec(memory_space=pl.ANY)] * len(named),
        out_specs=[pl.BlockSpec(memory_space=pl.ANY)] * len(outs),
        scratch_shapes=list(scratch.values()),
        compiler_params=pltpu.CompilerParams(
            collective_id=collective_id, has_side_effects=True, vmem_limit_bytes=60 << 20
        ),
        name="block_step",
    )(*named.values())


def finish_kernel(r):
    f32 = jnp.float32
    for load in r.loads:
        load.start()
    for load in r.loads[:5]:
        load.wait()
    share_first, share_middle, share_second, returned, squares = r.results
    for j in range(8):
        width = WIDTHS[j]
        if j < 4:
            columns = slice(FF * (j % 2), FF * (j % 2 + 1))
            grad = (share_first, share_second)[j % 2][:, share_columns(j)]
        else:
            columns = slice(0, width)
            start = STARTS[j] - STARTS[4]
            grad = share_middle[:, start : start + width]
        n = j // 2 if j < 4 else j - 2
        if j not in (1, 3):
            r.loads[5 + n].wait()
            r.loads[14 + n].wait()
        updated = MOMENTUM * r.moment[n][:, columns] + grad
        r.grad[n][:, columns] = grad
        r.next[n][:, columns] = updated
        solved = [returned[4 * j + q, :, 0 : width // 4].astype(f32) for q in range(4)]
        r.new[n][:, columns] = r.weight[n][:, columns] - RATE_MATRIX * jnp.concatenate(
            solved, axis=1
        )
        if j not in (0, 2):
            for store in (r.stores[n], r.stores[9 + n], r.stores[18 + n]):
                store.start()
    for n in (6, 7, 8):
        r.loads[5 + n].wait()
        r.loads[14 + n].wait()
    pack_small(r.small, r.turn, r.weight[8], r.weight[6], r.weight[7])
    pack_small(r.m_small, r.turn, r.moment[8], r.moment[6], r.moment[7])
    grad = share_first[:, 2 * FF :]
    updated = MOMENTUM * r.m_small[...] + grad
    lane = lax.broadcasted_iota(jnp.int32, (1, 128), 1)
    count = jnp.where(lane < SMALL_VEC, float(NB), float(D))
    scale = lax.rsqrt(squares[0:1, :] / count + EPS_SCALE)
    new = r.small[...] - RATE_VECTOR * updated * scale
    rows, rel_rows = r.small.shape[0], r.weight[8].shape[0]
    for value, outs in ((grad, r.grad), (new, r.new), (updated, r.next)):
        r.turn[...] = jnp.zeros_like(r.turn)
        r.turn[0:rows, :] = value
        turned = jnp.transpose(r.turn[...])
        outs[6][...] = turned[SMALL_VEC : SMALL_VEC + 7, 0:rows]
        outs[7][...] = value[:, SMALL_DEPTH : SMALL_DEPTH + K]
        outs[8][...] = value[0:rel_rows, SMALL_REL : SMALL_REL + H]
    for n in (6, 7, 8):
        for store in (r.stores[n], r.stores[9 + n], r.stores[18 + n]):
            store.start()
    for n in range(2):
        r.loads[23 + n].wait()
        r.stores[27 + n].start()
    for store in r.stores:
        store.wait()


def finish_step(fields, shares, returned, squares, weights, momenta):
    sources = (*shares, returned, squares, *weights, *momenta)
    operands = sources + tuple(fields)
    rows, count = weights[0].shape[0], len(sources)
    shapes = [jax.ShapeDtypeStruct(v.shape, v.dtype) for v in weights] * 3
    shapes += [jax.ShapeDtypeStruct(v.shape, v.dtype) for v in fields]

    def body(*refs):
        ins, refs = refs[: len(operands)], refs[len(operands) :]
        outs, refs = refs[: len(shapes)], refs[len(shapes) :]
        near, refs = refs[: count + 2], refs[count + 2 :]
        made, refs = refs[:27], refs[27:]
        small, m_small, turn, sem = refs
        pairs = list(zip(ins, near)) + list(zip(made + near[-2:], outs))
        moves = [pltpu.make_async_copy(a, b, sem.at[n]) for n, (a, b) in enumerate(pairs)]
        finish_kernel(
            types.SimpleNamespace(
                loads=moves[: count + 2],
                stores=moves[count + 2 :],
                results=near[:5],
                weight=near[5:14],
                moment=near[14:23],
                grad=made[:9],
                new=made[9:18],
                next=made[18:27],
                small=small,
                m_small=m_small,
                turn=turn,
            ),
        )

    return pl.pallas_call(
        body,
        out_shape=shapes,
        in_specs=[pl.BlockSpec(memory_space=pl.ANY)] * len(operands),
        out_specs=[pl.BlockSpec(memory_space=pl.ANY)] * len(shapes),
        scratch_shapes=[pltpu.VMEM(v.shape, v.dtype) for v in list(operands) + shapes[:27]]
        + [
            pltpu.VMEM((rows, 128), jnp.float32),
            pltpu.VMEM((rows, 128), jnp.float32),
            pltpu.VMEM((128, 128), jnp.float32),
            pltpu.SemaphoreType.DMA((len(operands) + len(shapes),)),
        ],
        compiler_params=pltpu.CompilerParams(vmem_limit_bytes=60 << 20),
        name="finish_step",
    )(*operands)


def unfused_step(
    cube,
    inputs,
    cotangent,
    w_up,
    w_down,
    w_qkv,
    w_out,
    w_glu,
    w_point,
    small,
    bucket_table,
):
    bf16 = jnp.bfloat16
    rows = w_up.shape[0]
    rel_rows = NB // cube.total
    shard_groups = (
        jnp.concatenate([w_up[:, :FF], w_down[:, :FF], small], axis=1).astype(bf16),
        jnp.concatenate([w_qkv, w_out, w_glu, w_point], axis=1).astype(bf16),
        jnp.concatenate([w_up[:, FF:], w_down[:, FF:]], axis=1).astype(bf16),
    )
    first, middle, second = [
        full.reshape(D, -1) for full in gather_groups(cube, shard_groups, 0)
    ]
    up_first, down_first, small_low = first[:, :FF], first[:, FF : 2 * FF], first[:, 2 * FF :]
    qkv_w, out_w = middle[:, : 3 * D], middle[:, 3 * D : 4 * D]
    glu_w, point_w = middle[:, 4 * D : 6 * D], middle[:, 6 * D :]
    up_second, down_second = second[:, :FF], second[:, FF:]
    gains = small_low[:, SMALL_VEC : SMALL_VEC + 7].astype(jnp.float32)
    kernel = small_low[:, SMALL_DEPTH : SMALL_DEPTH + K].astype(jnp.float32)
    rel_low = small_low[:, :H].reshape(cube.total, rows, H)[:, :rel_rows].reshape(NB, H)
    bucket_hit = (bucket_table[:, None] == jnp.arange(NB, dtype=jnp.int32)[None, :]).astype(
        jnp.float32
    )
    offsets = jnp.dot(bucket_hit, rel_low.astype(jnp.float32), precision=HIGHEST).T
    seq_rows = inputs[0]
    row_count = seq_rows.shape[0]
    first_row = lax.axis_index("seq") * row_count
    token_total = row_count * lax.axis_size(("dp", "seq", "shard"))
    section_one, ffn_saved = ffn_forward(seq_rows, gains[:, 0], up_first, down_first)
    normed_out2, normed2, inverse2 = layer_norm(section_one, gains[:, 1])
    lifted2 = normed_out2.astype(bf16)
    projected = matmul(lifted2, qkv_w).astype(bf16)
    query = projected[:, :D]
    pair = [(0, 1), (1, 0)]
    other = lax.ppermute(projected[:, D:], "seq", pair)
    early = lax.axis_index("seq") == 0
    both = jnp.concatenate(
        [
            jnp.where(early, projected[:, D:], other),
            jnp.where(early, other, projected[:, D:]),
        ],
        axis=0,
    )
    keys, values = both[:, :D], both[:, D:]
    attended, log_total = attention_forward(query, keys, values, offsets, first_row)
    attended_low = attended.astype(bf16)
    section_two = section_one + matmul(attended_low, out_w)
    normed_out3, normed3, inverse3 = layer_norm(section_two, gains[:, 2])
    lifted3 = normed_out3.astype(bf16)
    gates = matmul(lifted3, glu_w)
    first_half = gates[:, :D]
    sig_gate = jax.nn.sigmoid(gates[:, D:])
    glu = first_half * sig_gate
    glu_wide = with_halo(glu, (("seq", 0),), K // 2)
    conv = depthwise(glu_wide, kernel, row_count)
    part_sum = jnp.sum(conv, axis=0)
    part_mean = part_sum / row_count
    part_square = jnp.sum(jnp.square(conv - part_mean), axis=0)
    stats = collect(cube, jnp.concatenate([part_sum, part_square]).reshape(8, 128), 1)
    stats = stats.reshape(cube.total, 2, D)
    mean = jnp.sum(stats[:, 0], axis=0) / token_total
    spread_of_means = jnp.square(stats[:, 0] / row_count - mean) * row_count
    variance = jnp.sum(stats[:, 1] + spread_of_means, axis=0) / token_total
    centred = conv - mean
    inv_std = lax.rsqrt(variance + EPS_BATCH)
    normed_bn = centred * inv_std
    batch_out = normed_bn * gains[:, 5] + gains[:, 6]
    swish_low = jax.nn.silu(batch_out).astype(bf16)
    section_three = section_two + matmul(swish_low, point_w)
    section_four, tail_saved = ffn_forward(
        section_three, gains[:, 3], up_second, down_second
    )
    outputs, normed5, inverse5 = layer_norm(section_four, gains[:, 4])
    grad_four, gain_four = norm_back(cotangent[0], normed5, inverse5, gains[:, 4])
    grad_three, grad_up_two, grad_down_two, gain_three = ffn_backward(
        grad_four, tail_saved, gains[:, 3], up_second, down_second
    )
    grad_three_low = grad_three.astype(bf16)
    grad_point = matmul_left_t(swish_low, grad_three_low)
    grad_batch = matmul_right_t(grad_three_low, point_w) * silu_slope(batch_out)
    grad_normed = grad_batch * gains[:, 5]
    sums = jnp.concatenate(
        [jnp.sum(grad_normed, axis=0), jnp.sum(grad_normed * normed_bn, axis=0)]
    )
    sums = jnp.sum(collect(cube, sums.reshape(8, 128), 2), axis=0).reshape(2, D)
    sum_normed, sum_cross = sums[0], sums[1]
    grad_conv = inv_std * (
        grad_normed - sum_normed / token_total - normed_bn * sum_cross / token_total
    )
    grad_wide = with_halo(grad_conv, (("seq", 0),), K // 2)
    grad_glu = grad_wide[K - 1 : K - 1 + row_count] * kernel[:, 0]
    for tap_idx in range(1, K):
        grad_glu = (
            grad_glu
            + grad_wide[K - 1 - tap_idx : K - 1 - tap_idx + row_count] * kernel[:, tap_idx]
        )
    grad_kernel = jnp.stack(
        [
            jnp.sum(grad_conv * glu_wide[tap_idx : tap_idx + row_count], axis=0)
            for tap_idx in range(K)
        ],
        axis=1,
    )
    grad_gates = jnp.concatenate(
        [grad_glu * sig_gate, grad_glu * first_half * sig_gate * (1.0 - sig_gate)], axis=1
    ).astype(bf16)
    grad_glu_w = matmul_left_t(lifted3, grad_gates)
    grad_two_part, gain_two = norm_back(
        matmul_right_t(grad_gates, glu_w), normed3, inverse3, gains[:, 2]
    )
    grad_two = grad_three + grad_two_part
    grad_two_low = grad_two.astype(bf16)
    grad_out_w = matmul_left_t(attended_low, grad_two_low)
    grad_attended = matmul_right_t(grad_two_low, out_w).astype(bf16)
    delta = jnp.sum(
        (grad_attended.astype(jnp.float32) * attended).reshape(row_count, H, DH), axis=2
    )
    query_grad, key_grad, value_grad, offset_grad = attention_backward(
        query, keys, values, offsets, first_row, log_total, grad_attended, delta
    )
    keys_grad = jnp.concatenate([key_grad, value_grad], axis=1)
    theirs = lax.dynamic_slice_in_dim(keys_grad, row_count - first_row, row_count, 0)
    own = lax.dynamic_slice_in_dim(keys_grad, first_row, row_count, 0)
    own = own + lax.ppermute(theirs, "seq", pair)
    key_own, value_own = own[:, :D], own[:, D:]
    grad_proj = jnp.concatenate([query_grad, key_own, value_own], axis=1).astype(bf16)
    grad_qkv_w = matmul_left_t(lifted2, grad_proj)
    grad_one_part, gain_one = norm_back(
        matmul_right_t(grad_proj, qkv_w), normed2, inverse2, gains[:, 1]
    )
    grad_one = grad_two + grad_one_part
    input_grad, grad_up_one, grad_down_one, gain_zero = ffn_backward(
        grad_one, ffn_saved, gains[:, 0], up_first, down_first
    )
    grad_vec_local = jnp.stack(
        [
            gain_zero,
            gain_one,
            gain_two,
            gain_three,
            gain_four,
            jnp.sum(grad_batch * normed_bn, axis=0),
            jnp.sum(grad_batch, axis=0),
        ],
        axis=1,
    )
    grad_rel_local = jnp.dot(bucket_hit.T, offset_grad.T, precision=HIGHEST)
    rel_padded = jnp.pad(
        grad_rel_local.reshape(cube.total, rel_rows, H), ((0, 0), (0, rows - rel_rows), (0, 0))
    )
    small_grads = jnp.concatenate(
        [rel_padded.reshape(D, H), grad_vec_local, grad_kernel], axis=1
    )
    small_grads = jnp.pad(small_grads, ((0, 0), (0, 128 - SMALL_END)))
    lead = (2,) * cube.digits
    grad_groups = [
        jnp.concatenate(group, axis=1).astype(bf16).reshape(lead + (rows, -1))
        for group in (
            (grad_up_two, grad_down_two),
            (grad_qkv_w, grad_out_w, grad_glu_w, grad_point),
            (grad_up_one, grad_down_one, small_grads),
        )
    ]
    share_second, share_middle, share_first = scatter_groups(cube, grad_groups, 3)
    return outputs, input_grad, share_first, share_middle, share_second


def local(
    cube,
    inputs,
    cotangent,
    w_up,
    w_down,
    w_qkv,
    w_out,
    w_glu,
    w_point,
    vectors,
    depth_kernel,
    rel_bias,
    bucket_table,
    m_up,
    m_down,
    m_qkv,
    m_out,
    m_glu,
    m_point,
    m_vectors,
    m_depth,
    m_rel,
):
    bf16 = jnp.bfloat16
    rows, rel_rows = w_up.shape[0], rel_bias.shape[0]
    pack = lambda rel, vec, depth: jnp.pad(
        jnp.concatenate([jnp.pad(rel, ((0, rows - rel_rows), (0, 0))), vec, depth], axis=1),
        ((0, 0), (0, 128 - SMALL_END)),
    )
    small = pack(rel_bias, vectors, depth_kernel)
    weights = (w_up, w_down, w_qkv, w_out, w_glu, w_point)
    if rows % 16 == 0 and cube.total == 32:
        bucket = bucket_table[None]
        weights += (vectors.T, depth_kernel, rel_bias)
        momenta = (m_up, m_down, m_qkv, m_out, m_glu, m_point, m_vectors.T, m_depth, m_rel)
        outputs, input_grad, *shares, returned, squares = fused_step(
            cube, inputs[0], cotangent[0], weights, momenta, bucket, 0
        )
        *rest, outputs, input_grad = finish_step(
            (outputs, input_grad), shares, returned, squares, weights, momenta
        )
        for n in (6, 15, 24):
            rest[n] = rest[n].T
        return (outputs[None], input_grad[None], *rest)
    outputs, input_grad, share_first, share_middle, share_second = unfused_step(
        cube, inputs, cotangent, *weights, small, bucket_table
    )
    grad_up = jnp.concatenate([share_first[:, :FF], share_second[:, :FF]], axis=1)
    grad_down = jnp.concatenate([share_first[:, FF : 2 * FF], share_second[:, FF:]], axis=1)
    grad_qkv, grad_out = share_middle[:, : 3 * D], share_middle[:, 3 * D : 4 * D]
    grad_glu, grad_pnt = share_middle[:, 4 * D : 6 * D], share_middle[:, 6 * D :]
    share_small = share_first[:, 2 * FF :]
    grad_vectors = share_small[:, SMALL_VEC : SMALL_VEC + 7]
    grad_depth = share_small[:, SMALL_DEPTH : SMALL_DEPTH + K]
    grad_rel = share_small[: rel_bias.shape[0], :H]
    next_m_up = MOMENTUM * m_up + grad_up
    next_m_down = MOMENTUM * m_down + grad_down
    next_m_qkv = MOMENTUM * m_qkv + grad_qkv
    next_m_out = MOMENTUM * m_out + grad_out
    next_m_glu = MOMENTUM * m_glu + grad_glu
    next_m_point = MOMENTUM * m_point + grad_pnt
    stacked = jnp.concatenate(
        [next_m_up, next_m_down, next_m_qkv, next_m_out, next_m_glu, next_m_point], axis=1
    )
    owned = spread(cube, stacked, 4).reshape(D, BLOCK)
    ortho = orthogonalize_blocks(cube, owned, bf16, 5)
    mine = restore(cube, ortho.reshape(cube.total, rows, BLOCK), 6).astype(jnp.float32)
    new_up = w_up - RATE_MATRIX * mine[:, : 2 * FF]
    new_down = w_down - RATE_MATRIX * mine[:, 2 * FF : 4 * FF]
    new_qkv = w_qkv - RATE_MATRIX * mine[:, STARTS[4] : STARTS[5]]
    new_out = w_out - RATE_MATRIX * mine[:, STARTS[5] : STARTS[6]]
    new_glu = w_glu - RATE_MATRIX * mine[:, STARTS[6] : STARTS[7]]
    new_point = w_point - RATE_MATRIX * mine[:, STARTS[7] :]
    next_m_vectors = MOMENTUM * m_vectors + grad_vectors
    next_m_depth = MOMENTUM * m_depth + grad_depth
    next_m_rel = MOMENTUM * m_rel + grad_rel
    squares = jnp.concatenate(
        [
            jnp.sum(next_m_vectors * next_m_vectors, axis=0),
            jnp.sum(next_m_depth * next_m_depth, axis=0),
            jnp.sum(next_m_rel * next_m_rel, axis=0),
        ]
    )
    squares = jnp.pad(squares, (0, 128 - squares.shape[0])).reshape(1, 128)
    squares = jnp.sum(collect(cube, jnp.pad(squares, ((0, 7), (0, 0))), 7), axis=0)[0]
    square_vec, square_depth = squares[:7], squares[7 : 7 + K]
    square_rel = squares[7 + K : 7 + K + H]
    new_vectors = vectors - RATE_VECTOR * next_m_vectors * lax.rsqrt(square_vec / D + EPS_SCALE)
    new_depth = depth_kernel - RATE_VECTOR * next_m_depth * lax.rsqrt(square_depth / D + EPS_SCALE)
    new_rel = rel_bias - RATE_VECTOR * next_m_rel * lax.rsqrt(square_rel / NB + EPS_SCALE)
    return (
        outputs[None],
        input_grad[None],
        grad_up,
        grad_down,
        grad_qkv,
        grad_out,
        grad_glu,
        grad_pnt,
        grad_vectors,
        grad_depth,
        grad_rel,
        new_up,
        new_down,
        new_qkv,
        new_out,
        new_glu,
        new_point,
        new_vectors,
        new_depth,
        new_rel,
        next_m_up,
        next_m_down,
        next_m_qkv,
        next_m_out,
        next_m_glu,
        next_m_point,
        next_m_vectors,
        next_m_depth,
        next_m_rel,
    )


def solution(mesh):
    placed = (
        P(("dp", "shard"), "seq", None),
        P(("dp", "shard"), "seq", None),
        P(("dp", "seq", "shard"), None),
        P(("dp", "seq", "shard"), None),
        P(("dp", "seq", "shard"), None),
        P(("dp", "seq", "shard"), None),
        P(("dp", "seq", "shard"), None),
        P(("dp", "seq", "shard"), None),
        P(("dp", "seq", "shard"), None),
        P(("dp", "seq", "shard"), None),
        P(("dp", "seq", "shard"), None),
        P(),
        P(("dp", "seq", "shard"), None),
        P(("dp", "seq", "shard"), None),
        P(("dp", "seq", "shard"), None),
        P(("dp", "seq", "shard"), None),
        P(("dp", "seq", "shard"), None),
        P(("dp", "seq", "shard"), None),
        P(("dp", "seq", "shard"), None),
        P(("dp", "seq", "shard"), None),
        P(("dp", "seq", "shard"), None),
    )
    return jax.shard_map(
        functools.partial(local, Cube(mesh.shape["dp"])),
        mesh=mesh,
        in_specs=placed,
        out_specs=(
            P(("dp", "shard"), "seq", None),
            P(("dp", "shard"), "seq", None),
            P(("dp", "seq", "shard"), None),
            P(("dp", "seq", "shard"), None),
            P(("dp", "seq", "shard"), None),
            P(("dp", "seq", "shard"), None),
            P(("dp", "seq", "shard"), None),
            P(("dp", "seq", "shard"), None),
            P(("dp", "seq", "shard"), None),
            P(("dp", "seq", "shard"), None),
            P(("dp", "seq", "shard"), None),
            P(("dp", "seq", "shard"), None),
            P(("dp", "seq", "shard"), None),
            P(("dp", "seq", "shard"), None),
            P(("dp", "seq", "shard"), None),
            P(("dp", "seq", "shard"), None),
            P(("dp", "seq", "shard"), None),
            P(("dp", "seq", "shard"), None),
            P(("dp", "seq", "shard"), None),
            P(("dp", "seq", "shard"), None),
            P(("dp", "seq", "shard"), None),
            P(("dp", "seq", "shard"), None),
            P(("dp", "seq", "shard"), None),
            P(("dp", "seq", "shard"), None),
            P(("dp", "seq", "shard"), None),
            P(("dp", "seq", "shard"), None),
            P(("dp", "seq", "shard"), None),
            P(("dp", "seq", "shard"), None),
            P(("dp", "seq", "shard"), None),
        ),
        check_vma=False,
    )
```

```python
import functools
import types

import jax
import jax.numpy as jnp
from jax import lax
from jax.experimental import pallas as pl
from jax.experimental.pallas import tpu as pltpu
from jax.sharding import PartitionSpec as P

D = 512
FF = 2048
H = 8
DH = 64
K = 31
NB = 128


EPS_NORM = 1e-05
EPS_BATCH = 1e-05
EPS_SCALE = 1e-06
MOMENTUM = 0.9
RATE_MATRIX = 1.0
RATE_VECTOR = 0.25
COEF_A = 3.4445
COEF_B = -4.775
COEF_C = 2.0315
HIGHEST = lax.Precision.HIGHEST


AXES = ("dp", "seq", "shard")
MESH = pl.DeviceIdType.MESH
WIDTHS = (FF, FF, FF, FF, 3 * D, D, 2 * D, D)
STARTS = tuple(sum(WIDTHS[:i]) for i in range(9))
BLOCK = 512


class Cube:
    def __init__(self, dp_size):
        self.dp_size = dp_size
        self.levels = dp_size.bit_length() - 1
        self.digits = self.levels + 2
        self.total = dp_size * 4
        high = list(range(self.levels - 1))
        low, seq, core = self.levels - 1, self.levels, self.levels + 1
        self.gather_orders = (high + [low, seq, core], high + [seq, low, core])
        self.gather_late_orders = ([seq, low] + high + [core], [low, seq] + high + [core])
        self.scatter_orders = tuple(order[::-1] for order in self.gather_orders)
        self.scatter_high_orders = tuple(order[::-1] for order in self.gather_late_orders)
        self.scatter_low_orders = ([core, low, seq] + high[::-1],) * 2
        self.scatter_kinds = (
            self.scatter_orders,
            self.scatter_high_orders,
            self.scatter_low_orders,
        )

    def mine(self):
        d = lax.axis_index("dp")
        bits = [lax.rem(d // (1 << (self.levels - 1 - k)), 2) for k in range(self.levels)]
        return bits + [lax.axis_index("seq"), lax.axis_index("shard")]

    def partner(self, k):
        d, s, c = lax.axis_index("dp"), lax.axis_index("seq"), lax.axis_index("shard")
        if k == self.levels:
            return (d, 1 - s, c)
        if k == self.levels + 1:
            return (d, s, 1 - c)
        step = 1 << (self.levels - 1 - k)
        bit = lax.rem(d // step, 2)
        return (d + (1 - 2 * bit) * step, s, c)

    def index(self):
        return (lax.axis_index("dp") * 2 + lax.axis_index("seq")) * 2 + lax.axis_index("shard")

    def coords(self, index):
        return (index // 4, lax.rem(index // 2, 2), lax.rem(index, 2))

    def greet_partners(self):
        barrier = pltpu.get_barrier_semaphore()
        for k in range(self.digits):
            pl.semaphore_signal(barrier, inc=1, device_id=self.partner(k), device_id_type=MESH)
        pl.semaphore_wait(barrier, self.digits)

    def greet_all(self):
        barrier = pltpu.get_barrier_semaphore()
        me = self.index()

        @pl.loop(1, self.total)
        def _(i):
            peer = self.coords(lax.rem(me + i, self.total))
            pl.semaphore_signal(barrier, inc=1, device_id=peer, device_id_type=MESH)

        pl.semaphore_wait(barrier, self.total - 1)


def halves(width):
    cut = (width // 128 + 1) // 2 * 128
    return ((0, cut), (cut, width - cut))


def remote(src, dst, send_sem, recv_sem, peer):
    return pltpu.make_async_remote_copy(
        src_ref=src,
        dst_ref=dst,
        send_sem=send_sem,
        recv_sem=recv_sem,
        device_id=peer,
        device_id_type=MESH,
    )


def gather_kernel(cube, groups, *refs):
    shards, outs = refs[:groups], refs[groups : 2 * groups]
    own_sem, send_sem, recv_sem = refs[2 * groups :]
    cube.greet_partners()
    mine = cube.mine()
    locals_ = []
    for g in range(groups):
        copy = pltpu.make_async_copy(shards[g], outs[g].at[tuple(mine)], own_sem.at[g])
        copy.start()
        locals_.append(copy)

    def make(g, half, stage):
        order = cube.gather_orders[half]
        columns = pl.ds(*halves(shards[g].shape[-1])[half])
        done = order[:stage]
        index = tuple(slice(None) if k in done else mine[k] for k in range(cube.digits))
        place = outs[g].at[index + (slice(None), columns)]
        source = shards[g].at[:, columns] if stage == 0 else place
        return remote(
            source,
            place,
            send_sem.at[g, half, stage],
            recv_sem.at[g, half, stage],
            cube.partner(order[stage]),
        )

    copies = {}
    for g in range(groups):
        for half in range(2):
            copies[g, half, 0] = make(g, half, 0)
            copies[g, half, 0].start()
    for tick in range(cube.digits + 2 * (groups - 1)):
        for g in range(groups):
            stage = tick - 2 * g
            if not 0 <= stage < cube.digits:
                continue
            for half in range(2):
                copies[g, half, stage].wait_recv()
                if stage == 0 and half == 0:
                    locals_[g].wait()
                if stage + 1 < cube.digits:
                    copies[g, half, stage + 1] = make(g, half, stage + 1)
                    copies[g, half, stage + 1].start()
    for copy in copies.values():
        copy.wait_send()


def gather_groups(cube, shards, collective_id):
    groups = len(shards)
    lead = (2,) * cube.digits
    return pl.pallas_call(
        functools.partial(gather_kernel, cube, groups),
        out_shape=[jax.ShapeDtypeStruct(lead + s.shape, s.dtype) for s in shards],
        in_specs=[pl.BlockSpec(memory_space=pl.ANY)] * groups,
        out_specs=[pl.BlockSpec(memory_space=pl.ANY)] * groups,
        scratch_shapes=[
            pltpu.SemaphoreType.DMA((groups,)),
            pltpu.SemaphoreType.DMA((groups, 2, cube.digits)),
            pltpu.SemaphoreType.DMA((groups, 2, cube.digits)),
        ],
        compiler_params=pltpu.CompilerParams(
            collective_id=collective_id, has_side_effects=True
        ),
        name="gather_weights",
    )(*shards)


def scatter_kernel(cube, groups, *refs):
    parts, outs = refs[:groups], refs[groups : 2 * groups]
    rest = refs[2 * groups :]
    sums = rest[:groups]
    landed = rest[groups : groups + groups * 2 * cube.digits]
    own_sem, send_sem, recv_sem = rest[groups + groups * 2 * cube.digits :]
    cube.greet_partners()
    mine = cube.mine()
    last = cube.digits - 1

    def slot(g, half, stage):
        return landed[(g * 2 + half) * cube.digits + stage]

    def place(g, half, stage, bit_of):
        order = cube.scatter_orders[half]
        columns = pl.ds(*halves(outs[g].shape[-1])[half])
        index = []
        for k in range(cube.digits - 1):
            at = order.index(k)
            if at > stage:
                index.append(slice(None))
            else:
                index.append(bit_of(k) if at == stage else mine[k])
        return tuple(index) + (slice(None), columns)

    def make(g, half, stage):
        order = cube.scatter_orders[half]
        if stage == 0:
            index = (slice(None),) * last + (1 - mine[last],)
            columns = pl.ds(*halves(outs[g].shape[-1])[half])
            source = parts[g].at[index + (slice(None), columns)]
        else:
            source = sums[g].at[place(g, half, stage, lambda k: 1 - mine[k])]
        return remote(
            source,
            slot(g, half, stage),
            send_sem.at[g, half, stage],
            recv_sem.at[g, half, stage],
            cube.partner(order[stage]),
        )

    copies = {}
    locals_ = []
    for g in range(groups):
        copy = pltpu.make_async_copy(
            parts[g].at[(slice(None),) * last + (mine[last],)], sums[g], own_sem.at[g]
        )
        copy.start()
        locals_.append(copy)
        for half in range(2):
            copies[g, half, 0] = make(g, half, 0)
            copies[g, half, 0].start()

    def add(g, half, stage):
        order = cube.scatter_orders[half]
        columns = pl.ds(*halves(outs[g].shape[-1])[half])
        free = [k for k in range(last) if order.index(k) > stage]
        count = 1 << len(free)
        target, extra = sums[g], slot(g, half, stage)

        def one(i):
            digit = {k: lax.rem(i // (1 << (len(free) - 1 - n)), 2) for n, k in enumerate(free)}
            full = tuple(digit.get(k, mine[k]) for k in range(last)) + (slice(None), columns)
            short = tuple(digit[k] for k in free)
            total = target[full].astype(jnp.float32) + extra[short + (slice(None), slice(None))].astype(jnp.float32)
            if stage == last:
                outs[g][:, columns] = total
            else:
                target[full] = total.astype(target.dtype)

        if count == 1:
            one(0)
        else:
            pl.loop(0, count)(one)

    for stage in range(cube.digits):
        for g in range(groups):
            if stage == 0:
                locals_[g].wait()
            for half in range(2):
                copies[g, half, stage].wait_recv()
                add(g, half, stage)
                if stage < last:
                    copies[g, half, stage + 1] = make(g, half, stage + 1)
                    copies[g, half, stage + 1].start()
    for copy in copies.values():
        copy.wait_send()


def scatter_groups(cube, parts, collective_id):
    groups = len(parts)
    scratch = [pltpu.VMEM((2,) * (cube.digits - 1) + p.shape[-2:], p.dtype) for p in parts]
    for p in parts:
        for half in range(2):
            for stage in range(cube.digits):
                lead = (2,) * (cube.digits - 1 - stage)
                scratch.append(pltpu.VMEM(lead + (p.shape[-2], halves(p.shape[-1])[half][1]), p.dtype))
    scratch += [
        pltpu.SemaphoreType.DMA((groups,)),
        pltpu.SemaphoreType.DMA((groups, 2, cube.digits)),
        pltpu.SemaphoreType.DMA((groups, 2, cube.digits)),
    ]
    return pl.pallas_call(
        functools.partial(scatter_kernel, cube, groups),
        out_shape=[jax.ShapeDtypeStruct(p.shape[-2:], jnp.float32) for p in parts],
        in_specs=[pl.BlockSpec(memory_space=pl.ANY)] * groups,
        out_specs=[pl.BlockSpec(memory_space=pltpu.VMEM)] * groups,
        scratch_shapes=scratch,
        compiler_params=pltpu.CompilerParams(
            collective_id=collective_id, has_side_effects=True, vmem_limit_bytes=48 << 20
        ),
        name="scatter_grads",
    )(*parts)


def collect_kernel(cube, x_ref, o_ref, send_sem, recv_sem):
    me = cube.index()
    cube.greet_all()

    def make(i):
        to = lax.rem(me + i, cube.total)
        return remote(x_ref, o_ref.at[i], send_sem.at[i], recv_sem.at[i], cube.coords(to))

    @pl.loop(1, cube.total)
    def _(i):
        make(i).start()

    o_ref[0] = x_ref[...]

    @pl.loop(1, cube.total)
    def _(i):
        make(i).wait()


def collect(cube, x, collective_id):
    return pl.pallas_call(
        functools.partial(collect_kernel, cube),
        out_shape=jax.ShapeDtypeStruct((cube.total,) + x.shape, x.dtype),
        in_specs=[pl.BlockSpec(memory_space=pltpu.VMEM)],
        out_specs=pl.BlockSpec(memory_space=pltpu.VMEM),
        scratch_shapes=[
            pltpu.SemaphoreType.DMA((cube.total,)),
            pltpu.SemaphoreType.DMA((cube.total,)),
        ],
        compiler_params=pltpu.CompilerParams(
            collective_id=collective_id, has_side_effects=True
        ),
        name="collect_stats",
    )(x)


def by_matrix(j, action):
    for width in sorted(set(WIDTHS)):
        members = [i for i in range(8) if WIDTHS[i] == width]
        hit = functools.reduce(jnp.logical_or, [j == i for i in members])
        pl.when(hit)(functools.partial(action, width // 4))


def quarter_start(t):
    j, q = t // 4, lax.rem(t, 4)
    start = 0
    for i in range(8):
        start = start + jnp.where(j == i, STARTS[i] + q * (WIDTHS[i] // 4), 0)
    return pl.multiple_of(start, 128)


def owner_coords(cube, t):
    return ((t // 4) * (cube.dp_size // 8), lax.rem(t // 2, 2), lax.rem(t, 2))


def spread_kernel(cube, x_ref, o_ref, own_sem, send_sem, recv_sem):
    me = cube.index()
    repeat = cube.dp_size // 8
    d, s, c = lax.axis_index("dp"), lax.axis_index("seq"), lax.axis_index("shard")
    owner = lax.rem(d, repeat) == 0
    mine = ((d // repeat) * 2 + s) * 2 + c
    cube.greet_all()

    def send(i, wait):
        t = lax.rem(mine + i, 32)
        peer = owner_coords(cube, t)
        other = jnp.logical_or(jnp.logical_not(owner), i > 0)

        def go(width):
            src = x_ref.at[:, pl.ds(quarter_start(t), width)]
            dst = o_ref.at[me, :, pl.ds(0, width)]
            copy = remote(src, dst, send_sem.at[i], recv_sem.at[me], peer)
            if wait:
                copy.wait_send()
            else:
                copy.start()

        pl.when(other)(lambda: by_matrix(t // 4, go))

    pl.loop(0, 32)(functools.partial(send, wait=False))

    def keep(width):
        copy = pltpu.make_async_copy(
            x_ref.at[:, pl.ds(quarter_start(mine), width)],
            o_ref.at[me, :, pl.ds(0, width)],
            own_sem,
        )
        copy.start()
        copy.wait()

    def receive(width):
        @pl.loop(1, cube.total)
        def _(i):
            source = lax.rem(me + i, cube.total)
            place = o_ref.at[source, :, pl.ds(0, width)]
            remote(
                place, place, send_sem.at[0], recv_sem.at[source], cube.coords(source)
            ).wait_recv()

    @pl.when(owner)
    def _():
        by_matrix(mine // 4, keep)
        by_matrix(mine // 4, receive)

    pl.loop(0, 32)(functools.partial(send, wait=True))


def spread(cube, x, collective_id):
    return pl.pallas_call(
        functools.partial(spread_kernel, cube),
        out_shape=jax.ShapeDtypeStruct((cube.total, x.shape[0], BLOCK), x.dtype),
        in_specs=[pl.BlockSpec(memory_space=pl.ANY)],
        out_specs=pl.BlockSpec(memory_space=pl.ANY),
        scratch_shapes=[
            pltpu.SemaphoreType.DMA,
            pltpu.SemaphoreType.DMA((32,)),
            pltpu.SemaphoreType.DMA((cube.total,)),
        ],
        compiler_params=pltpu.CompilerParams(
            collective_id=collective_id, has_side_effects=True
        ),
        name="spread_momentum",
    )(x)


def restore_kernel(cube, x_ref, o_ref, own_sem, send_sem, recv_sem):
    me = cube.index()
    repeat = cube.dp_size // 8
    d, s, c = lax.axis_index("dp"), lax.axis_index("seq"), lax.axis_index("shard")
    owner = lax.rem(d, repeat) == 0
    mine = ((d // repeat) * 2 + s) * 2 + c
    cube.greet_all()

    def send_all(wait, width):
        @pl.loop(1, cube.total)
        def _(i):
            to = lax.rem(me + i, cube.total)
            src = x_ref.at[to, :, pl.ds(0, width)]
            dst = o_ref.at[:, pl.ds(quarter_start(mine), width)]
            copy = remote(src, dst, send_sem.at[i], recv_sem.at[mine], cube.coords(to))
            if wait:
                copy.wait_send()
            else:
                copy.start()

    def keep(width):
        copy = pltpu.make_async_copy(
            x_ref.at[me, :, pl.ds(0, width)],
            o_ref.at[:, pl.ds(quarter_start(mine), width)],
            own_sem,
        )
        copy.start()
        copy.wait()

    @pl.when(owner)
    def _():
        by_matrix(mine // 4, functools.partial(send_all, False))
        by_matrix(mine // 4, keep)

    def receive(i):
        t = lax.rem(mine + i, 32)
        other = jnp.logical_or(jnp.logical_not(owner), i > 0)

        def go(width):
            place = o_ref.at[:, pl.ds(quarter_start(t), width)]
            remote(
                place, place, send_sem.at[0], recv_sem.at[t], owner_coords(cube, t)
            ).wait_recv()

        pl.when(other)(lambda: by_matrix(t // 4, go))

    pl.loop(0, 32)(receive)

    @pl.when(owner)
    def _():
        by_matrix(mine // 4, functools.partial(send_all, True))


def restore(cube, x, collective_id):
    return pl.pallas_call(
        functools.partial(restore_kernel, cube),
        out_shape=jax.ShapeDtypeStruct((x.shape[1], STARTS[8]), x.dtype),
        in_specs=[pl.BlockSpec(memory_space=pl.ANY)],
        out_specs=pl.BlockSpec(memory_space=pl.ANY),
        scratch_shapes=[
            pltpu.SemaphoreType.DMA,
            pltpu.SemaphoreType.DMA((cube.total,)),
            pltpu.SemaphoreType.DMA((32,)),
        ],
        compiler_params=pltpu.CompilerParams(
            collective_id=collective_id, has_side_effects=True
        ),
        name="restore_rows",
    )(x)


def split(value):
    high = value.astype(jnp.bfloat16)
    low = (value - high.astype(jnp.float32)).astype(jnp.bfloat16)
    return high, low


def product(left, right):
    (lh, ll), (rh, rl) = left, right
    dot = functools.partial(jnp.dot, preferred_element_type=jnp.float32)
    return dot(lh, rh) + (dot(lh, rl) + dot(ll, rh))


def orthogonalize_kernel(cube, x_ref, o_ref, gram_ref, work, landed, send_sem, recv_sem):
    barrier = pltpu.get_barrier_semaphore()
    peers = (cube.partner(cube.levels + 1), cube.partner(cube.levels))
    for peer in peers:
        pl.semaphore_signal(barrier, inc=1, device_id=peer, device_id_type=MESH)
    pl.semaphore_wait(barrier, 2)
    repeat = cube.dp_size // 8
    j = lax.axis_index("dp") // repeat
    width = 0
    for i in range(8):
        width = width + jnp.where(j == i, WIDTHS[i] // 4, 0)
    column = lax.broadcasted_iota(jnp.int32, (D, BLOCK), 1)
    block = jnp.where(column < width, x_ref[...].astype(jnp.float32), 0.0)
    bh, bl = split(block)
    dot_t = lambda a, b: lax.dot_general(
        a, b, (((1,), (1,)), ((), ())), preferred_element_type=jnp.float32
    )
    gram_ref[0] = dot_t(bh, bh) + (dot_t(bh, bl) + dot_t(bl, bh))
    for step in range(2):
        copy = remote(
            gram_ref.at[step], landed.at[step], send_sem.at[step], recv_sem.at[step], peers[step]
        )
        copy.start()
        copy.wait()
        gram_ref[step + 1] = gram_ref[step] + landed[step]
    gram = gram_ref[2]
    row = lax.broadcasted_iota(jnp.int32, (D, D), 0)
    col = lax.broadcasted_iota(jnp.int32, (D, D), 1)
    eye = row == col
    square = jnp.sum(jnp.sum(jnp.where(eye, gram, 0.0), axis=1, keepdims=True), axis=0, keepdims=True)
    scale = 1.0 / (jnp.sqrt(square) + 1e-07)
    gram = gram * (scale * scale)
    block = block * scale
    for step in range(5):
        parts = split(gram)
        mixed = COEF_B * gram + COEF_C * product(parts, parts)
        mixed = jnp.where(eye, mixed + COEF_A, mixed)
        mixed_parts = split(mixed)
        block = product(mixed_parts, split(block))
        if step < 4:
            gram = product(mixed_parts, split(product(mixed_parts, parts)))
    o_ref[...] = block.astype(o_ref.dtype)


def orthogonalize_blocks(cube, x, out_dtype, collective_id):
    return pl.pallas_call(
        functools.partial(orthogonalize_kernel, cube),
        out_shape=jax.ShapeDtypeStruct((D, BLOCK), out_dtype),
        in_specs=[pl.BlockSpec(memory_space=pltpu.VMEM)],
        out_specs=pl.BlockSpec(memory_space=pltpu.VMEM),
        scratch_shapes=[
            pltpu.VMEM((3, D, D), jnp.float32),
            pltpu.VMEM((8, 128), jnp.float32),
            pltpu.VMEM((2, D, D), jnp.float32),
            pltpu.SemaphoreType.DMA((2,)),
            pltpu.SemaphoreType.DMA((2,)),
        ],
        compiler_params=pltpu.CompilerParams(
            collective_id=collective_id, has_side_effects=True, vmem_limit_bytes=48 << 20
        ),
        name="orthogonalize",
    )(x)

def with_halo(value, sides, width):
    for axis, dim in sides:
        devices, length = (lax.axis_size(axis), value.shape[dim])
        up = [(i, (i + 1) % devices) for i in range(devices - 1)]
        down = [(j, i) for i, j in up]
        last = lax.slice_in_dim(value, length - width, length, axis=dim)
        first = lax.slice_in_dim(value, 0, width, axis=dim)
        before = lax.ppermute(last, axis, up)
        after = lax.ppermute(first, axis, down)
        value = jnp.concatenate([before, value, after], axis=dim)
    return value


def matmul(left, right):
    return jnp.dot(left, right, preferred_element_type=jnp.float32)


def matmul_right_t(left, right):
    return lax.dot_general(
        left, right, (((1,), (1,)), ((), ())), preferred_element_type=jnp.float32
    )


def matmul_left_t(left, right):
    return lax.dot_general(
        left, right, (((0,), (0,)), ((), ())), preferred_element_type=jnp.float32
    )


def layer_norm(field, gain):
    centre = jnp.mean(field, axis=-1, keepdims=True)
    shifted = field - centre
    inverse = lax.rsqrt(jnp.mean(shifted * shifted, axis=-1, keepdims=True) + EPS_NORM)
    normed = shifted * inverse
    return (normed * gain, normed, inverse)


def norm_back(grad_out, normed, inverse, gain):
    scaled = grad_out * gain
    grad_in = inverse * (
        scaled
        - jnp.mean(scaled, axis=-1, keepdims=True)
        - normed * jnp.mean(scaled * normed, axis=-1, keepdims=True)
    )
    return (grad_in, jnp.sum(grad_out * normed, axis=0))


def silu_slope(values):
    sigma = jax.nn.sigmoid(values)
    return sigma * (1.0 + values * (1.0 - sigma))


def ffn_forward(field, gain, w_in, w_back):
    normed_out, normed, inverse = layer_norm(field, gain)
    lifted = normed_out.astype(jnp.bfloat16)
    hidden_pre = matmul(lifted, w_in)
    hidden_act = jax.nn.silu(hidden_pre).astype(jnp.bfloat16)
    return (
        field + 0.5 * matmul_right_t(hidden_act, w_back),
        (lifted, hidden_pre, hidden_act, normed, inverse),
    )


def ffn_backward(grad, saved, gain, w_in, w_back):
    lifted, hidden_pre, hidden_act, normed, inverse = saved
    grad_branch = (0.5 * grad).astype(jnp.bfloat16)
    grad_back = matmul_left_t(grad_branch, hidden_act)
    grad_act = matmul(grad_branch, w_back)
    grad_pre = (grad_act * silu_slope(hidden_pre)).astype(jnp.bfloat16)
    grad_in = matmul_left_t(lifted, grad_pre)
    grad_field, grad_gain = norm_back(matmul_right_t(grad_pre, w_in), normed, inverse, gain)
    return (grad + grad_field, grad_in, grad_back, grad_gain)


def depthwise(wide, kernel, count):
    total = wide[0:count] * kernel[:, 0]
    for tap_idx in range(1, K):
        total = total + wide[tap_idx : tap_idx + count] * kernel[:, tap_idx]
    return total


def spread_rows(window, count, keys_len):
    padded = jnp.concatenate([window, jnp.zeros((1,), window.dtype)])
    tiled = jnp.broadcast_to(padded[None, :], (count, keys_len + count)).reshape(-1)
    shaped = tiled[: count * (keys_len + count - 1)].reshape(count, keys_len + count - 1)
    return shaped[:, count - 1 : count - 1 + keys_len]


def collect_rows(grid, count, keys_len):
    placed = jnp.concatenate([jnp.zeros((count, count - 1), grid.dtype), grid], axis=1).reshape(-1)
    placed = jnp.concatenate([placed, jnp.zeros((count,), grid.dtype)])
    return jnp.sum(placed.reshape(count, keys_len + count), axis=0)[: keys_len + count - 1]


def attention_scores(query, keys, offsets, first_row, row_start, block, head_idx):
    length = keys.shape[0]
    columns = slice(head_idx * DH, (head_idx + 1) * DH)
    anchor = length - block - first_row - row_start
    window = lax.dynamic_slice_in_dim(offsets[head_idx], anchor, length + block - 1)
    product = matmul_right_t(query[row_start : row_start + block, columns], keys[:, columns])
    return product * DH ** (-0.5) + spread_rows(window, block, length)


def attention_forward(query, keys, values, offsets, first_row):
    total_rows = query.shape[0]
    block = min(512, total_rows)
    head_outs = []
    head_lse = []
    for head_idx in range(H):
        scores = attention_scores(query, keys, offsets, first_row, 0, block, head_idx)
        row_max = jnp.max(scores, axis=1, keepdims=True)
        shifted_exp = jnp.exp(scores - row_max)
        row_total = jnp.sum(shifted_exp, axis=1, keepdims=True)
        prob_low = (shifted_exp / row_total).astype(jnp.bfloat16)
        head_outs.append(matmul(prob_low, values[:, head_idx * DH : (head_idx + 1) * DH]))
        head_lse.append((row_max + jnp.log(row_total))[:, 0])
    out_blocks = jnp.concatenate(head_outs, axis=1)
    lse_blocks = jnp.stack(head_lse, axis=0)
    return (out_blocks, lse_blocks)


def attention_backward(query, keys, values, offsets, first_row, log_total, grad_attended, delta):
    total_rows = query.shape[0]
    length = keys.shape[0]
    block = min(512, total_rows)
    scale = DH ** (-0.5)
    key_parts = [jnp.zeros((length, DH), jnp.float32) for head_idx in range(H)]
    value_parts = [jnp.zeros((length, DH), jnp.float32) for head_idx in range(H)]
    offset_rows = [jnp.zeros((2 * length - 1,), jnp.float32) for head_idx in range(H)]
    head_grads = []
    for head_idx in range(H):
        columns = slice(head_idx * DH, (head_idx + 1) * DH)
        scores = attention_scores(query, keys, offsets, first_row, 0, block, head_idx)
        prob = jnp.exp(scores - log_total[head_idx, 0:block][:, None])
        prob_low = prob.astype(jnp.bfloat16)
        grad_piece = grad_attended[0:block, columns]
        value_parts[head_idx] = matmul_left_t(prob_low, grad_piece)
        grad_prob = matmul_right_t(grad_piece, values[:, columns])
        grad_score = prob * (grad_prob - delta[0:block, head_idx][:, None])
        score_low = grad_score.astype(jnp.bfloat16)
        head_grads.append(matmul(score_low, keys[:, columns]) * scale)
        key_parts[head_idx] = matmul_left_t(score_low, query[0:block, columns]) * scale
        anchor = length - block - first_row - 0
        offset_rows[head_idx] = lax.dynamic_update_slice_in_dim(
            offset_rows[head_idx], collect_rows(grad_score, block, length), anchor, 0
        )
    query_blocks = jnp.concatenate(head_grads, axis=1)
    return (
        query_blocks,
        jnp.concatenate(key_parts, axis=1),
        jnp.concatenate(value_parts, axis=1),
        jnp.stack(offset_rows, axis=0),
    )


def mean_last(value):
    return jnp.mean(value, axis=-1, keepdims=True)


def normalize(field):
    shifted = field - mean_last(field)
    inverse = lax.rsqrt(mean_last(shifted * shifted) + EPS_NORM)
    return shifted * inverse, inverse


def norm_grad(grad_out, normed, inverse, gain):
    scaled = grad_out * gain
    grad_in = inverse * (scaled - mean_last(scaled) - normed * mean_last(scaled * normed))
    return grad_in, jnp.sum(grad_out * normed, axis=0, keepdims=True)


def row_to_tile(ref, base, row):
    for k in range(4):
        ref[base + k : base + k + 1, :] = row[:, 128 * k : 128 * (k + 1)]


def tile_to_row(tile):
    return jnp.concatenate([tile[k : k + 1, :] for k in range(4)], axis=1)


def skew(row, count):
    sub = lax.broadcasted_iota(jnp.int32, (8, 512), 0)
    block = jnp.broadcast_to(row, (8, 512))
    for bit in (1, 2, 4):
        block = jnp.where((sub // bit) % 2 == 1, pltpu.roll(block, bit, 1), block)
    size = 8
    while size < count:
        block = jnp.concatenate([block, pltpu.roll(block, size, 1)], axis=0)
        size *= 2
    return block


def unskew_sum(grid):
    size = grid.shape[0] // 2
    while size >= 8:
        grid = grid[:size] + pltpu.roll(grid[size:], 512 - size, 1)
        size //= 2
    sub = lax.broadcasted_iota(jnp.int32, (8, 512), 0)
    for bit in (1, 2, 4):
        grid = jnp.where((sub // bit) % 2 == 1, pltpu.roll(grid, 512 - bit, 1), grid)
    return jnp.sum(grid, axis=0, keepdims=True)


def tile_ranges(start, count, parts):
    ranges = []
    for n in range(parts, 0, -1):
        size = -(-count // n)
        ranges.append((128 * start, 128 * size))
        start, count = start + size, count - size
    return ranges


def joined(orders, pair, stage):
    one, two = orders
    if one[stage] == two[stage] and set(one[:stage]) == set(two[:stage]):
        return [(pair[0][0], pair[0][1] + pair[1][1])]
    return list(pair)


class Gather:
    def __init__(self, cube, mine, bands, send_sem, recv_sem):
        self.cube, self.mine, self.bands = cube, mine, bands
        self.chunks = GATHER_CHUNKS
        self.send_sem, self.recv_sem = send_sem, recv_sem
        self.copies = {}
        self.events = list(GATHER_EVENTS)
        self.last = cube.digits - 1

    def start(self, n, stage):
        g, pair, kind = self.chunks[n]
        orders = (self.cube.gather_orders, self.cube.gather_late_orders)[kind]
        for half, columns in enumerate(joined(orders, pair, stage)):
            order = orders[half]
            done = order[:stage]
            index = tuple(
                slice(None) if k in done else self.mine[k] for k in range(self.cube.digits)
            )
            place = self.bands[g].at[index + (slice(None), pl.ds(*columns))]
            copy = remote(
                place,
                place,
                self.send_sem.at[n, half, stage],
                self.recv_sem.at[n, half, stage],
                self.cube.partner(order[stage]),
            )
            copy.start()
            self.copies[n, half, stage] = copy

    def begin(self):
        for n, stage in GATHER_BEGIN:
            self.start(n, stage)

    def advance(self, n, stage):
        for half in range(2):
            if (n, half, stage) in self.copies:
                self.copies[n, half, stage].wait_recv()
        if stage < self.last and (n, stage + 1) not in GATHER_HELD:
            self.start(n, stage + 1)
        for other in GATHER_AFTER.get((n, stage), ()):
            self.start(*other)

    def run_to(self, n, stage):
        while (n, stage) in self.events:
            self.advance(*self.events.pop(0))

    def finish(self):
        for copy in self.copies.values():
            copy.wait_send()


class Scatter:
    def __init__(self, cube, mine, bands, landed, outs, send_sem, recv_sem):
        self.cube, self.mine, self.landed = cube, mine, landed
        self.chunks = [(bands[g], outs[g], pair) for g, pair, _ in SCATTER_CHUNKS]
        self.orders = [cube.scatter_kinds[kind] for _, _, kind in SCATTER_CHUNKS]
        self.send_sem, self.recv_sem = send_sem, recv_sem
        self.copies = {}

    def start(self, n, stage):
        band, _, pair = self.chunks[n]
        for half, columns in enumerate(joined(self.orders[n], pair, stage)):
            order = self.orders[n][half]
            index = []
            for k in range(self.cube.digits):
                at = order.index(k)
                if at > stage:
                    index.append(slice(None))
                else:
                    index.append(1 - self.mine[k] if at == stage else self.mine[k])
            copy = remote(
                band.at[tuple(index) + (slice(None), pl.ds(*columns))],
                self.landed[(n * 2 + half) * self.cube.digits + stage],
                self.send_sem.at[n, half, stage],
                self.recv_sem.at[n, half, stage],
                self.cube.partner(order[stage]),
            )
            copy.start()
            self.copies[n, half, stage] = copy

    def add(self, n, half, stage):
        order = self.orders[n][half]
        band, out, pair = self.chunks[n]
        columns = pl.ds(*joined(self.orders[n], pair, stage)[half])
        free = [k for k in range(self.cube.digits) if order.index(k) > stage]
        extra = self.landed[(n * 2 + half) * self.cube.digits + stage]
        everything = (slice(None), columns)

        def one(i):
            digit = {
                k: lax.rem(i // (1 << (len(free) - 1 - m)), 2) for m, k in enumerate(free)
            }
            full = tuple(digit.get(k, self.mine[k]) for k in range(self.cube.digits)) + everything
            short = tuple(digit[k] for k in free) + (slice(None), slice(None))
            if free:
                band[full] = band[full] + extra[short]
            else:
                out[:, columns] = band[full].astype(jnp.float32) + extra[short].astype(jnp.float32)

        if free:
            pl.loop(0, 1 << len(free))(one)
        else:
            one(0)

    def advance(self, n, stage):
        for half in range(2):
            if (n, half, stage) in self.copies:
                self.copies[n, half, stage].wait_recv()
                self.add(n, half, stage)
        if stage + 1 < self.cube.digits:
            self.start(n, stage + 1)

    def finish(self):
        for copy in self.copies.values():
            copy.wait_send()


class Collect:
    def __init__(self, cube, tile, slots, send_sem, recv_sem):
        self.cube, self.tile, self.slots = cube, tile, slots
        self.send_sem, self.recv_sem = send_sem, recv_sem

    def make(self, i):
        to = self.cube.coords(lax.rem(self.cube.index() + i, self.cube.total))
        return remote(
            self.tile, self.slots.at[i], self.send_sem.at[i], self.recv_sem.at[i], to
        )

    def start(self):
        pl.loop(1, self.cube.total)(lambda i: self.make(i).start())
        self.slots[0] = self.tile[...]

    def arrive(self):
        pl.loop(1, self.cube.total)(lambda i: self.make(i).wait())

    def total(self):
        result = self.slots[0]
        for i in range(1, self.cube.total):
            result = result + self.slots[i]
        return result


def share_columns(j):
    place = j // 2 if j % 2 else 1 - j // 2
    return slice(FF * place, FF * (place + 1))


def matrix_of(d):
    return sum(jnp.where(d == OWNER_PLACES[i], i, 0) for i in range(8))


def pack_small(target, turn, rel, vec, depth):
    rows = target.shape[0]
    turn[...] = jnp.zeros_like(turn)
    turn[0:7, 0:rows] = vec[...]
    target[...] = jnp.zeros_like(target)
    target[0 : rel.shape[0], SMALL_REL : SMALL_REL + H] = rel[...]
    target[:, SMALL_VEC : SMALL_VEC + 7] = jnp.transpose(turn[...])[0:rows, 0:7]
    target[:, SMALL_DEPTH : SMALL_DEPTH + K] = depth[...]


OWNER_PLACES = (2, 3, 5, 4, 0, 1, 7, 6)


def owner_place(cube, t):
    return (OWNER_PLACES[t // 4] * (cube.dp_size // 8), t // 2 % 2, t % 2)


class Momenta:
    def __init__(self, cube, r):
        self.cube, self.r = cube, r
        self.me = cube.index()
        self.repeat = cube.dp_size // 8
        d = lax.axis_index("dp")
        self.is_owner = lax.rem(d, self.repeat) == 0
        self.matrix = matrix_of(d // self.repeat)
        self.quarter = lax.axis_index("seq") * 2 + lax.axis_index("shard")
        self.owned_index = self.matrix * 4 + self.quarter

    def holds(self, t):
        return jnp.logical_and(self.is_owner, self.owned_index == t)

    def rows(self, j):
        r = self.r
        if j < 4:
            old, share = ((r.m_up, r.m_down)[j // 2], (r.share_first, r.share_second)[j % 2])
            return old[:, FF * (j % 2) : FF * (j % 2 + 1)], share[:, share_columns(j)]
        start = STARTS[j] - STARTS[4]
        old = (r.m_qkv, r.m_out, r.m_glu, r.m_point)[j - 4]
        return old[...], r.share_middle[:, start : start + WIDTHS[j]]

    def copy(self, t):
        width = WIDTHS[t // 4] // 4
        r = self.r
        return remote(
            r.leaving.at[t, :, pl.ds(0, width)],
            r.owned.at[self.me, :, pl.ds(0, width)],
            r.m_send.at[t],
            r.m_recv.at[self.me],
            owner_place(self.cube, t),
        )

    def send(self, j):
        old, share = self.rows(j)
        value = (MOMENTUM * old + share).astype(jnp.bfloat16)
        width = WIDTHS[j] // 4
        for q in range(4):
            t = 4 * j + q
            part = value[:, width * q : width * (q + 1)]
            self.r.leaving[t, :, 0:width] = part
            pl.when(jnp.logical_not(self.holds(t)))(lambda t=t: self.copy(t).start())

            @pl.when(self.holds(t))
            def _(part=part, width=width):
                self.r.owned[self.me, :, 0:width] = part

    def receive(self):
        r, cube = self.r, self.cube

        def go(width):
            @pl.loop(1, cube.total)
            def _(i):
                source = lax.rem(self.me + i, cube.total)
                place = r.owned.at[source, :, pl.ds(0, width)]
                remote(
                    place, place, r.m_send.at[0], r.m_recv.at[source], cube.coords(source)
                ).wait_recv()

        pl.when(self.is_owner)(lambda: by_matrix(self.matrix, go))

    def back(self, i, width):
        r, cube = self.r, self.cube
        to = lax.rem(self.me + i, cube.total)
        return remote(
            r.solved.at[to, :, pl.ds(0, width)],
            r.returned.at[self.owned_index, :, pl.ds(0, width)],
            r.b_send.at[i],
            r.b_recv.at[self.owned_index],
            cube.coords(to),
        )

    def keep(self, width):
        r = self.r
        return pltpu.make_async_copy(
            r.solved.at[self.me, :, pl.ds(0, width)],
            r.returned.at[self.owned_index, :, pl.ds(0, width)],
            r.k_sem,
        )

    def send_back(self):
        r = self.r

        def go(width):
            pl.loop(1, self.cube.total)(lambda i: self.back(i, width).start())
            self.keep(width).start()

        pl.when(self.is_owner)(lambda: by_matrix(self.matrix, go))

    def receive_back(self):
        r = self.r
        for t in range(32):
            place = r.returned.at[t, :, pl.ds(0, WIDTHS[t // 4] // 4)]
            copy = remote(
                place, place, r.b_send.at[0], r.b_recv.at[t], owner_place(self.cube, t)
            )
            pl.when(jnp.logical_not(self.holds(t)))(copy.wait_recv)

    def finish(self):
        for t in range(32):
            pl.when(jnp.logical_not(self.holds(t)))(lambda t=t: self.copy(t).wait_send())

        def go(width):
            pl.loop(1, self.cube.total)(lambda i: self.back(i, width).wait_send())
            self.keep(width).wait()

        pl.when(self.is_owner)(lambda: by_matrix(self.matrix, go))


def symmetric_product(left, right):
    half = D // 2
    (lh, ll), (rh, rl) = left, right
    top = product((lh[:half], ll[:half]), right)
    corner = product((lh[half:], ll[half:]), (rh[:, half:], rl[:, half:]))
    low = jnp.concatenate([jnp.transpose(top[:, half:]), corner], axis=1)
    return jnp.concatenate([top, low], axis=0)


def short_product(left, right):
    half = D // 2
    (lh, ll), rh = left, right[0]
    top = matmul(lh[:half], rh) + matmul(ll[:half], rh)
    corner = matmul(lh[half:], rh[:, half:]) + matmul(ll[half:], rh[:, half:])
    low = jnp.concatenate([jnp.transpose(top[:, half:]), corner], axis=1)
    return jnp.concatenate([top, low], axis=0)


GRAM_SHARES = (
    ((0, 0), (0, 1), (0, 2), (0, 3), (3, 3)),
    ((1, 1), (1, 2), (1, 3), (2, 2), (2, 3)),
)


def orthogonalize(cube, r):
    f32 = jnp.float32
    core, seq = lax.axis_index("shard"), lax.axis_index("seq")
    block = r.owned.reshape(D, BLOCK)
    lines = [slice(128 * i, 128 * (i + 1)) for i in range(4)]
    peers = (cube.partner(cube.levels + 1), cube.partner(cube.levels))
    count = len(GRAM_SHARES[0])

    def piece(step, n):
        source, target, peer = (
            (r.packed.at[1 - core, n], r.packed_in.at[0, n], peers[0]),
            (r.summed.at[n], r.packed_in.at[1, n], peers[1]),
            (r.whole.at[core, n], r.whole.at[core, n], peers[0]),
        )[step]
        return remote(source, target, r.n_send.at[step, n], r.n_recv.at[step, n], peer)

    for n in range(count):
        for share in range(2):
            i, j = GRAM_SHARES[share][n]
            r.packed[share, n] = matmul_right_t(block[lines[i], :], block[lines[j], :])
        piece(0, n).start()
    for n in range(count):
        piece(0, n).wait()
        r.summed[n] = r.packed[core, n] + r.packed_in[0, n]
        piece(1, n).start()
    for n in range(count):
        piece(1, n).wait()
        r.whole[core, n] = r.summed[n] + r.packed_in[1, n]
        piece(2, n).start()
    for n in range(count):
        piece(2, n).wait()
    for share in range(2):
        for n, (i, j) in enumerate(GRAM_SHARES[share]):
            value = r.whole[share, n]
            r.gram[lines[i], lines[j]] = value
            if i != j:
                r.gram[lines[j], lines[i]] = jnp.transpose(value)
    row = lax.broadcasted_iota(jnp.int32, (D, D), 0)
    col = lax.broadcasted_iota(jnp.int32, (D, D), 1)
    eye = row == col
    gram = r.gram[...]
    square = jnp.sum(
        jnp.sum(jnp.where(eye, gram, 0.0), axis=1, keepdims=True), axis=0, keepdims=True
    )
    scale = 1.0 / (jnp.sqrt(square) + 1e-07)
    gram = gram * (scale * scale)
    value = None
    for step in range(4):
        parts = split(gram)
        mixed = COEF_B * gram + COEF_C * symmetric_product(parts, parts)
        mixed = jnp.where(eye, mixed + COEF_A, mixed)
        high, low = split(mixed)
        if step == 0:
            start_high, start_low = split(mixed * scale)
            value = matmul(start_high, block[...]) + matmul(start_low, block[...])
        elif step < 3:
            value = product((high, low), split(value))
        else:
            value = matmul(high, value.astype(jnp.bfloat16))
        times = symmetric_product if step < 3 else short_product
        gram = times((high, low), split(times((high, low), parts)))
    short = gram.astype(jnp.bfloat16)
    mixed = COEF_B * gram + COEF_C * matmul(short, short)
    mixed = jnp.where(eye, mixed + COEF_A, mixed).astype(jnp.bfloat16)
    value = matmul(mixed, value.astype(jnp.bfloat16))
    r.solved.reshape(D, BLOCK)[...] = value.astype(jnp.bfloat16)


SMALL_REL, SMALL_VEC, SMALL_DEPTH = 0, H, H + 7
SMALL_END = H + 7 + K
EDGE = 16
GATHER_CHUNKS = (
    (0, tile_ranges(0, 17, 2), 0),
    (0, tile_ranges(17, 16, 2), 0),
    (1, tile_ranges(0, 20, 2), 0),
    (2, tile_ranges(0, 16, 2), 0),
    (1, tile_ranges(20, 8, 2), 1),
    (2, tile_ranges(16, 16, 2), 1),
)
GATHER_BEGIN = ((0, 0), (4, 0),)
GATHER_EVENTS = (
    ((4, 0), (0, 0), (4, 1), (5, 0), (5, 1), (0, 1), (1, 0), (0, 2), (1, 1), (2, 0))
    + ((2, 1), (3, 0), (1, 2), (0, 3), (0, 4), (4, 2), (3, 1), (2, 2), (1, 3), (1, 4))
    + ((5, 2), (3, 2), (2, 3), (4, 3), (4, 4), (2, 4), (3, 3), (3, 4), (5, 3), (5, 4))
)
SCATTER_EVENTS = (
    ((0, 1), (3, 0), (1, 1), (4, 0), (2, 1), (5, 0), (3, 1), (6, 1), (0, 2), (1, 2), (4, 1))
    + ((2, 2), (5, 1), (6, 2), (3, 2), (1, 3), (2, 3), (0, 3), (4, 2), (3, 3), (1, 4), (2, 4))
    + ((0, 4), (5, 2), (6, 3), (4, 3), (3, 4), (6, 4), (5, 3), (4, 4), (5, 4))
)
SCATTER_STORES = ((4,), (), (), (), (), (2,), (3,))
EARLY_LOADS = tuple("w_up w_down w_qkv w_out".split()) + tuple("w_glu w_point rel vec".split())
EARLY_LOADS += tuple("depth m_rel m_vec m_depth".split())
SCATTER_MATRICES = ((3,), (1,), (5,), (4,), (2,), (0,), (6, 7))
GATHER_HELD = ((4, 2), (5, 2),)
GATHER_AFTER = {
    (4, 0): [(5, 0)],
    (0, 0): [(1, 0)],
    (1, 0): [(2, 0)],
    (2, 0): [(3, 0)],
    (2, 1): [(4, 2)],
    (4, 2): [(5, 2)],
}
FIRST_READY, MIDDLE_READY, SECOND_READY = (1, 4), (2, 4), (5, 4)
SCATTER_CHUNKS = (
    (0, tile_ranges(16, 16, 2), 1),
    (0, tile_ranges(0, 16, 2), 2),
    (1, tile_ranges(12, 4, 2), 0),
    (1, tile_ranges(0, 12, 2), 0),
    (2, tile_ranges(0, 16, 2), 0),
    (2, tile_ranges(16, 17, 2), 0),
    (1, tile_ranges(16, 12, 2), 1),
)


def step_kernel(cube, r):
    bf16, f32 = jnp.bfloat16, jnp.float32
    x_ref, cot_ref, bucket_ref = r.inputs, r.cotangent, r.bucket
    tokens = x_ref.shape[0]
    token_total = tokens * cube.total
    rows = r.w_up.shape[0]
    rel_rows = r.rel.shape[0]
    mine = cube.mine()
    seq = lax.axis_index("seq")
    early = seq == 0
    first_row = pl.multiple_of(seq * tokens, tokens)
    other_row = pl.multiple_of((1 - seq) * tokens, tokens)
    across = cube.partner(cube.levels)
    lengths = [ref.shape[-1] for ref in (r.first, r.middle, r.second)]
    first, middle, second, d_first, d_middle, d_second = (
        ref.reshape(D, ref.shape[-1])
        for ref in (r.first, r.middle, r.second, r.d_first, r.d_middle, r.d_second)
    )
    a, xh = r.a, r.xh

    barrier = pltpu.get_barrier_semaphore()
    me = cube.index()
    momenta = Momenta(cube, r)
    for load in r.loads.values():
        load.start()
    r.owned[...] = jnp.zeros_like(r.owned)

    @pl.loop(1, cube.total)
    def _(i):
        peer = cube.coords(lax.rem(me + i, cube.total))
        pl.semaphore_signal(barrier, inc=1, device_id=peer, device_id_type=MESH)

    for name in EARLY_LOADS:
        r.loads[name].wait()
    pack_small(r.small, r.turn, r.rel, r.vec, r.depth)
    pack_small(r.m_small, r.turn, r.m_rel, r.m_vec, r.m_depth)
    own = tuple(mine)
    r.first[own + (slice(None), slice(FF, 2 * FF))] = r.w_up[:, :FF].astype(bf16)
    r.first[own + (slice(None), slice(0, FF))] = r.w_down[:, :FF].astype(bf16)
    r.first[own + (slice(None), slice(2 * FF, lengths[0]))] = r.small[...].astype(bf16)
    r.middle[own + (slice(None), slice(0, 3 * D))] = r.w_qkv[...].astype(bf16)
    r.middle[own + (slice(None), slice(3 * D, 4 * D))] = r.w_out[...].astype(bf16)
    r.middle[own + (slice(None), slice(4 * D, 6 * D))] = r.w_glu[...].astype(bf16)
    r.middle[own + (slice(None), slice(6 * D, 7 * D))] = r.w_point[...].astype(bf16)
    r.second[own + (slice(None), slice(0, FF))] = r.w_up[:, FF:].astype(bf16)
    r.second[own + (slice(None), slice(FF, 2 * FF))] = r.w_down[:, FF:].astype(bf16)
    pl.semaphore_wait(barrier, cube.total - 1)

    gather = Gather(
        cube, mine, (r.first, r.middle, r.second), r.g_send, r.g_recv
    )
    scatter = Scatter(
        cube,
        mine,
        (r.d_second, r.d_middle, r.d_first),
        r.land,
        (r.share_second, r.share_middle, r.share_first),
        r.s_send,
        r.s_recv,
    )

    gather.begin()
    for name in [name for name in r.loads if name not in EARLY_LOADS]:
        r.loads[name].wait()
    xh0, inv0 = normalize(x_ref[...])
    xh[0] = xh0
    rho = lax.broadcasted_iota(jnp.int32, (D, bucket_ref.shape[1]), 0)
    bucket_of = jnp.where(rho % rows < rel_rows, (rho // rows) * rel_rows + rho % rows, -2)
    r.hit[...] = jnp.zeros_like(r.hit)
    offset_count = bucket_ref.shape[1]
    r.hit[:, 0:offset_count] = (bucket_ref[...] == bucket_of).astype(f32).astype(bf16)
    gather.run_to(*FIRST_READY)

    small = r.small_t
    small[...] = jnp.transpose(first[:, 2 * FF : 2 * FF + 128].astype(f32))
    gains = [small[SMALL_VEC + i : SMALL_VEC + i + 1, :] for i in range(7)]
    taps = [small[SMALL_DEPTH + k : SMALL_DEPTH + k + 1, :] for k in range(K)]
    CH = 512

    def ffn_forward_fused(index, field, normed, up, down, u_ref, s_ref):
        low = (normed * gains[(0, 1, 2, 3)[index]]).astype(bf16)
        a[index] = low
        for c in range(0, FF, CH):
            u = matmul(low, up[:, c : c + CH])
            u_ref[:, c : c + CH] = u
            s_ref[:, c : c + CH] = (u * jax.nn.sigmoid(u)).astype(bf16)
        return field + 0.5 * matmul_right_t(s_ref[...], down[...])

    down1, up1 = first.at[:, pl.ds(0, FF)], first.at[:, pl.ds(FF, FF)]
    up2, down2 = second.at[:, pl.ds(0, FF)], second.at[:, pl.ds(FF, FF)]
    section1 = ffn_forward_fused(0, x_ref[...], xh[0], up1, down1, r.u1, r.s1)
    r.sec1[...] = section1
    xh1, inv1 = normalize(section1)
    xh[1] = xh1
    a[1] = (xh1 * gains[1]).astype(bf16)
    offsets = matmul(small[0:8, :].astype(bf16), r.hit[...])
    offsets = jnp.where(
        early, pltpu.roll(offsets, 257, 1), pltpu.roll(offsets, (tokens + 257) % 512, 1)
    )
    for h in range(H):
        r.bias[h] = skew(offsets[h : h + 1, :], tokens)[:, : 2 * tokens]
    gather.run_to(*MIDDLE_READY)

    q_ref, kv = r.q, r.kv
    kv[pl.ds(first_row, tokens), :] = matmul(a[1], middle[:, D : 3 * D]).astype(bf16)
    kv_copy = remote(
        kv.at[pl.ds(first_row, tokens)],
        kv.at[pl.ds(first_row, tokens)],
        r.kv_send,
        r.kv_recv,
        across,
    )
    kv_copy.start()
    q_ref[...] = matmul(a[1], middle[:, :D]).astype(bf16)
    gather.run_to(*(2, 4))
    kv_copy.wait_recv()
    gather.run_to(*(3, 3))
    lane = lax.broadcasted_iota(jnp.int32, (1, 128), 1)
    lane_masks = [(lane // DH == e).astype(f32) for e in range(2)]
    low_masks = [m.astype(bf16) for m in lane_masks]
    scale = DH ** (-0.5)
    for p in range(H // 2):
        columns = slice(128 * p, 128 * (p + 1))
        k_pair, v_pair = kv[:, columns], kv[:, D + 128 * p : D + 128 * (p + 1)]
        merged = None
        for e in range(2):
            q_head = q_ref[:, columns] * low_masks[e]
            scores = matmul_right_t(q_head, k_pair) * scale + r.bias[2 * p + e]
            shifted = jnp.exp(scores - jnp.max(scores, axis=1, keepdims=True))
            prob = shifted / jnp.sum(shifted, axis=1, keepdims=True)
            r.prob[2 * p + e] = prob
            out = matmul(prob.astype(bf16), v_pair) * lane_masks[e]
            merged = out if merged is None else merged + out
        r.att[:, columns] = merged
        if p == 1:
            gather.run_to(*(3, 4))
    gather.run_to(*SECOND_READY)
    att_low = r.att[...].astype(bf16)
    r.att_low[...] = att_low
    section2 = r.sec1[...] + matmul(att_low, middle[:, 3 * D : 4 * D])
    r.sec2[...] = section2
    xh2, inv2 = normalize(section2)
    xh[2] = xh2
    a[2] = (xh2 * gains[2]).astype(bf16)
    gate_first = matmul(a[2], middle[:, 4 * D : 5 * D])
    sig = jax.nn.sigmoid(matmul(a[2], middle[:, 5 * D : 6 * D]))
    r.gate[...] = gate_first
    r.sig[...] = sig
    wide = r.wide
    wide[EDGE : EDGE + tokens, :] = gate_first * sig
    edge_row = pl.multiple_of(EDGE + (1 - seq) * (tokens - EDGE), EDGE)
    halo_copy = remote(
        wide.at[pl.ds(edge_row, EDGE)], r.halo, r.halo_send, r.halo_recv, across
    )
    halo_copy.start()
    zero_edge = jnp.zeros((EDGE, D), f32)
    wide[0:EDGE, :] = zero_edge
    wide[EDGE + tokens :, :] = zero_edge
    conv_ref = r.conv
    for b in range(D // 128):
        cols = slice(128 * b, 128 * (b + 1))
        total = jnp.zeros((tokens, 128), f32)
        for k in range(K):
            total = total + wide[k + 1 : k + 1 + tokens, cols] * taps[k][:, cols]
        conv_ref[:, cols] = total
    halo_copy.wait()
    rim = r.rim
    rim[...] = jnp.zeros_like(rim)
    rim[0:EDGE, :] = jnp.where(early, zero_edge, r.halo[...])
    rim[3 * EDGE :, :] = jnp.where(early, r.halo[...], zero_edge)
    wide[0:EDGE, :] = rim[0:EDGE, :]
    wide[EDGE + tokens :, :] = rim[3 * EDGE :, :]
    for b in range(D // 128):
        cols = slice(128 * b, 128 * (b + 1))
        before = jnp.zeros((EDGE, 128), f32)
        after = jnp.zeros((EDGE, 128), f32)
        for k in range(K // 2):
            before = before + rim[k + 1 : k + 1 + EDGE, cols] * taps[k][:, cols]
        for k in range(K // 2 + 1, K):
            after = after + rim[k + 17 : k + 17 + EDGE, cols] * taps[k][:, cols]
        conv_ref[0:EDGE, cols] = conv_ref[0:EDGE, cols] + before
        conv_ref[tokens - EDGE :, cols] = conv_ref[tokens - EDGE :, cols] + after
    conv = conv_ref[...]
    part_sum = jnp.sum(conv, axis=0, keepdims=True)
    part_off = conv - part_sum * (1.0 / tokens)
    part_square = jnp.sum(part_off * part_off, axis=0, keepdims=True)
    row_to_tile(r.tile1, 0, part_sum)
    row_to_tile(r.tile1, 4, part_square)
    stats = Collect(cube, r.tile1, r.slots1, r.c1_send, r.c1_recv)
    stats.start()
    stats.arrive()
    sums = stats.total()
    mean4 = sums[0:4] * (1.0 / token_total)
    spread4 = jnp.zeros((4, 128), f32)
    for i in range(cube.total):
        off = r.slots1[i][0:4] * (1.0 / tokens) - mean4
        spread4 = spread4 + off * off
    var4 = (sums[4:8] + spread4 * tokens) * (1.0 / token_total)
    mean = tile_to_row(mean4)
    inv_std = tile_to_row(lax.rsqrt(var4 + EPS_BATCH))

    xb = (conv_ref[...] - mean) * inv_std
    r.xb[...] = xb
    bn = xb * gains[5] + gains[6]
    r.bn[...] = bn
    sw = (bn * jax.nn.sigmoid(bn)).astype(bf16)
    r.sw[...] = sw
    section3 = r.sec2[...] + matmul(sw, middle[:, 6 * D : 7 * D])
    xh3, inv3 = normalize(section3)
    xh[3] = xh3
    section4 = ffn_forward_fused(3, section3, xh3, up2, down2, r.u2, r.s2)
    xh4, inv4 = normalize(section4)
    r.outputs[...] = xh4 * gains[4]
    r.stores[0].start()

    sg = r.small_grad
    sg[...] = jnp.zeros_like(sg)
    cot = cot_ref[...]
    d4, sg[SMALL_VEC + 4 : SMALL_VEC + 5, :] = norm_grad(cot, xh4, inv4, gains[4])

    def slope(value):
        sigma = jax.nn.sigmoid(value)
        return sigma * (1.0 + value * (1.0 - sigma))

    def slopes(low, down, u_ref, du_ref):
        for c in range(0, FF, CH):
            act = matmul(low, down[:, c : c + CH])
            du_ref[:, c : c + CH] = (act * slope(u_ref[:, c : c + CH])).astype(bf16)

    def weight_grad(left, right_ref, target, start, width):
        for c in range(0, width, CH):
            target[:, start + c : start + c + CH] = matmul_left_t(
                left, right_ref[:, c : c + CH]
            ).astype(bf16)

    r.e_low[...] = (0.5 * d4).astype(bf16)
    slopes(r.e_low[...], down2, r.u2, r.du)
    back = matmul_right_t(r.du[...], up2[...])
    part, sg[SMALL_VEC + 3 : SMALL_VEC + 4, :] = norm_grad(back, xh[3], inv3, gains[3])
    d3 = d4 + part
    r.d[...] = d3
    e3 = d3.astype(bf16)
    r.e3[...] = e3
    dbn = matmul_right_t(e3, middle[:, 6 * D : 7 * D]) * slope(r.bn[...])
    xb = r.xb[...]
    sg[SMALL_VEC + 5 : SMALL_VEC + 6, :] = jnp.sum(dbn * xb, axis=0, keepdims=True)
    sg[SMALL_VEC + 6 : SMALL_VEC + 7, :] = jnp.sum(dbn, axis=0, keepdims=True)
    dxb = dbn * gains[5]
    r.dxb[...] = dxb
    row_to_tile(r.tile2, 0, jnp.sum(dxb, axis=0, keepdims=True))
    row_to_tile(r.tile2, 4, jnp.sum(dxb * xb, axis=0, keepdims=True))
    sums2 = Collect(cube, r.tile2, r.slots2, r.c2_send, r.c2_recv)
    sums2.start()
    token_edge = pl.multiple_of((1 - seq) * (tokens - EDGE), EDGE)
    edges = r.edges
    edges[0:EDGE, :] = r.dxb[pl.ds(token_edge, EDGE), :]
    edges[EDGE:, :] = r.xb[pl.ds(token_edge, EDGE), :]
    edge_copy = remote(edges, r.edges_in, r.edge_send, r.edge_recv, across)
    edge_copy.start()

    weight_grad(r.e_low[...], r.s2, d_second, FF, FF)
    scatter.start(0, 0)
    weight_grad(a[3], r.du, d_second, 0, FF)
    scatter.start(1, 0)
    weight_grad(r.sw[...], r.e3, d_middle, 6 * D, D)
    edge_copy.wait()
    sums2.arrive()
    total2 = sums2.total()
    mean1 = tile_to_row(total2[0:4] * (1.0 / token_total))
    mean2 = tile_to_row(total2[4:8] * (1.0 / token_total))
    dwide = r.dwide
    dwide[EDGE : EDGE + tokens, :] = inv_std * (r.dxb[...] - mean1 - r.xb[...] * mean2)
    edge = inv_std * (r.edges_in[0:EDGE, :] - mean1 - r.edges_in[EDGE:, :] * mean2)
    dwide[0:EDGE, :] = jnp.where(early, zero_edge, edge)
    dwide[EDGE + tokens :, :] = jnp.where(early, edge, zero_edge)
    dglu_ref = r.conv
    for b in range(D // 128):
        cols = slice(128 * b, 128 * (b + 1))
        total = jnp.zeros((tokens, 128), f32)
        for k in range(K):
            total = total + dwide[31 - k : 31 - k + tokens, cols] * taps[k][:, cols]
        dglu_ref[:, cols] = total
    dglu, sig = dglu_ref[...], r.sig[...]
    r.dgates[:, :D] = (dglu * sig).astype(bf16)
    r.dgates[:, D:] = (dglu * r.gate[...] * sig * (1.0 - sig)).astype(bf16)
    scatter.advance(0, 0)
    back = matmul_right_t(r.dgates[...], middle[:, 4 * D : 6 * D])
    part, sg[SMALL_VEC + 2 : SMALL_VEC + 3, :] = norm_grad(back, xh[2], inv2, gains[2])
    d2 = r.d[...] + part
    r.d[...] = d2
    e1 = d2.astype(bf16)
    r.e_low[...] = e1
    dob = matmul_right_t(e1, middle[:, 3 * D : 4 * D]).astype(bf16)
    r.dob[...] = dob
    weight_grad(r.att_low[...], r.e_low, d_middle, 3 * D, D)
    weight_grad(a[2], r.dgates, d_middle, 4 * D, 2 * D)
    scatter.start(2, 0)
    scatter.start(6, 0)

    off_rows = []
    give, keep, got = r.give, r.keep, r.got
    kv_grads = []
    for p in range(H // 2):
        columns = slice(128 * p, 128 * (p + 1))
        k_pair, v_pair = kv[:, columns], kv[:, D + 128 * p : D + 128 * (p + 1)]
        att_pair = r.att[:, columns]
        dq = dk = dv = None
        for e in range(2):
            h = 2 * p + e
            dob_head = r.dob[:, columns] * low_masks[e]
            q_head = q_ref[:, columns] * low_masks[e]
            delta = jnp.sum(dob_head.astype(f32) * att_pair, axis=1, keepdims=True)
            prob = r.prob[h]
            ds = prob * (matmul_right_t(dob_head, v_pair) - delta)
            ds_low = ds.astype(bf16)
            dv_head = matmul_left_t(prob.astype(bf16), dob_head)
            dk_head = matmul_left_t(ds_low, q_head) * scale
            dq_head = matmul(ds_low, k_pair) * (lane_masks[e] * scale)
            dv = dv_head if dv is None else dv + dv_head
            dk = dk_head if dk is None else dk + dk_head
            dq = dq_head if dq is None else dq + dq_head
            padded = jnp.concatenate([ds, jnp.zeros((tokens, 512 - 2 * tokens), f32)], axis=1)
            off_rows.append(unskew_sum(padded))
        r.dqkv[:, columns] = dq.astype(bf16)
        for n, value in enumerate((dk, dv)):
            r.dkv[n] = value
            give[p, n] = r.dkv[n, pl.ds(other_row, tokens), :].astype(bf16)
            keep[p, n] = r.dkv[n, pl.ds(first_row, tokens), :]
        copy = remote(
            give.at[p], got.at[p], r.dkv_send.at[p], r.dkv_recv.at[p], across
        )
        copy.start()
        kv_grads.append(copy)
        if p == 1:
            scatter.advance(1, 0)
    off = jnp.concatenate(off_rows, axis=0)
    off = jnp.where(early, pltpu.roll(off, 255, 1), pltpu.roll(off, 255 - tokens, 1))
    off_high, off_low = split(off)
    sg[0:8, :] = matmul_right_t(off_high, r.hit[...]) + matmul_right_t(off_low, r.hit[...])
    for b in range(D // 128):
        cols = slice(128 * b, 128 * (b + 1))
        dconv = dwide[EDGE : EDGE + tokens, cols]
        for k in range(K):
            sg[SMALL_DEPTH + k : SMALL_DEPTH + k + 1, cols] = jnp.sum(
                dconv * wide[k + 1 : k + 1 + tokens, cols], axis=0, keepdims=True
            )
    for p in range(H // 2):
        kv_grads[p].wait()
        for n in range(2):
            at = D * (n + 1) + 128 * p
            r.dqkv[:, at : at + 128] = (keep[p, n] + got[p, n].astype(f32)).astype(bf16)
    scatter.advance(2, 0)
    scatter.advance(6, 0)
    back = matmul_right_t(r.dqkv[...], middle[:, : 3 * D])
    part, sg[SMALL_VEC + 1 : SMALL_VEC + 2, :] = norm_grad(back, xh[1], inv1, gains[1])
    d1 = r.d[...] + part
    e0 = (0.5 * d1).astype(bf16)
    weight_grad(a[1], r.dqkv, d_middle, 0, 3 * D)
    scatter.start(3, 0)
    weight_grad(e0, r.s1, d_first, 0, FF)
    scatter.start(4, 0)
    slopes(e0, down1, r.u1, r.du)
    back = matmul_right_t(r.du[...], up1[...])
    part, sg[SMALL_VEC : SMALL_VEC + 1, :] = norm_grad(back, xh[0], inv0, gains[0])
    r.input_grad[...] = d1 + part
    r.stores[1].start()
    d_first[:, 2 * FF : 2 * FF + 128] = jnp.transpose(sg[...]).astype(bf16)
    weight_grad(a[0], r.du, d_first, FF, FF)
    scatter.start(5, 0)
    for n, stage in SCATTER_EVENTS:
        scatter.advance(n, stage)
        if stage == scatter.cube.digits - 1:
            for j in SCATTER_MATRICES[n]:
                momenta.send(j)
            for store in SCATTER_STORES[n]:
                r.stores[store].start()
    next_small = MOMENTUM * r.m_small[...] + r.share_first[:, 2 * FF :]
    r.tile3[...] = jnp.zeros_like(r.tile3)
    r.tile3[0:1, :] = jnp.sum(next_small * next_small, axis=0, keepdims=True)
    squares = Collect(cube, r.tile3, r.slots3, r.c3_send, r.c3_recv)
    squares.start()
    momenta.receive()
    orthogonalize(cube, r)
    momenta.send_back()
    squares.arrive()
    r.squares[...] = squares.total()
    r.stores[5].start()
    momenta.receive_back()
    momenta.finish()
    gather.finish()
    scatter.finish()
    for store in r.stores:
        store.wait()
    kv_copy.wait_send()


def fused_step(cube, inputs, cotangent, weights, momenta, bucket, collective_id):
    bf16, f32 = jnp.bfloat16, jnp.float32
    tokens, rows = inputs.shape[0], weights[0].shape[0]
    widths = (2 * FF + 128, 7 * D, 2 * FF)
    lead = (2,) * cube.digits
    named = dict(
        inputs=inputs,
        cotangent=cotangent,
        w_up=weights[0],
        w_down=weights[1],
        w_qkv=weights[2],
        w_out=weights[3],
        w_glu=weights[4],
        w_point=weights[5],
        vec=weights[6],
        depth=weights[7],
        rel=weights[8],
        m_up=momenta[0],
        m_down=momenta[1],
        m_qkv=momenta[2],
        m_out=momenta[3],
        m_glu=momenta[4],
        m_point=momenta[5],
        m_vec=momenta[6],
        m_depth=momenta[7],
        m_rel=momenta[8],
        bucket=bucket,
    )
    outs = dict(
        outputs=jax.ShapeDtypeStruct((tokens, D), f32),
        input_grad=jax.ShapeDtypeStruct((tokens, D), f32),
        share_first=jax.ShapeDtypeStruct((rows, widths[0]), f32),
        share_middle=jax.ShapeDtypeStruct((rows, widths[1]), f32),
        share_second=jax.ShapeDtypeStruct((rows, widths[2]), f32),
        returned=jax.ShapeDtypeStruct((32, rows, BLOCK), bf16),
        squares=jax.ShapeDtypeStruct((8, 128), f32),
    )
    field = pltpu.VMEM((tokens, D), f32)
    low = pltpu.VMEM((tokens, D), bf16)
    wide_low = pltpu.VMEM((tokens, FF), bf16)
    wide_field = pltpu.VMEM((tokens + 2 * EDGE, D), f32)
    grid = pltpu.VMEM((H, tokens, 2 * tokens), f32)
    pairs = pltpu.VMEM((H // 2, 2, tokens, 128), bf16)
    tile = pltpu.VMEM((8, 128), f32)
    slots = pltpu.VMEM((cube.total, 8, 128), f32)
    stages = pltpu.SemaphoreType.DMA((7, 2, cube.digits))
    gather_stages = pltpu.SemaphoreType.DMA((6, 2, cube.digits))
    everyone = pltpu.SemaphoreType.DMA((cube.total,))
    single = pltpu.SemaphoreType.DMA
    bands = [pltpu.VMEM(lead + (rows, w), bf16) for w in widths]
    land = []
    for _, pair, kind in SCATTER_CHUNKS:
        for half in range(2):
            for stage in range(cube.digits):
                columns = joined(cube.scatter_kinds[kind], pair, stage)
                part = columns[half][1] if half < len(columns) else 0
                lead_shape = (2,) * (cube.digits - 1 - stage) + (rows, part)
                shape = lead_shape if part else (rows, 128)
                land.append(pltpu.VMEM(shape, bf16))
    scratch = dict(
        first=bands[0],
        middle=bands[1],
        second=bands[2],
        d_first=bands[0],
        d_middle=bands[1],
        d_second=bands[2],
        land=tuple(land),
        sec1=field,
        sec2=field,
        att=field,
        gate=field,
        sig=field,
        conv=field,
        xb=field,
        bn=field,
        dxb=field,
        d=field,
        q=low,
        att_low=low,
        sw=low,
        e_low=low,
        e3=low,
        dob=low,
        a=pltpu.VMEM((4, tokens, D), bf16),
        xh=pltpu.VMEM((4, tokens, D), f32),
        u1=pltpu.VMEM((tokens, FF), f32),
        u2=pltpu.VMEM((tokens, FF), f32),
        s1=wide_low,
        s2=wide_low,
        du=wide_low,
        kv=pltpu.VMEM((2 * tokens, 2 * D), bf16),
        bias=grid,
        prob=grid,
        wide=wide_field,
        dwide=wide_field,
        halo=pltpu.VMEM((EDGE, D), f32),
        rim=pltpu.VMEM((4 * EDGE, D), f32),
        edges=pltpu.VMEM((2 * EDGE, D), f32),
        edges_in=pltpu.VMEM((2 * EDGE, D), f32),
        dgates=pltpu.VMEM((tokens, 2 * D), bf16),
        dqkv=pltpu.VMEM((tokens, 3 * D), bf16),
        dkv=pltpu.VMEM((2, 2 * tokens, 128), f32),
        give=pairs,
        got=pairs,
        keep=pltpu.VMEM((H // 2, 2, tokens, 128), f32),
        small=pltpu.VMEM((rows, 128), f32),
        m_small=pltpu.VMEM((rows, 128), f32),
        turn=pltpu.VMEM((128, 128), f32),
        hit=pltpu.VMEM((D, 512), bf16),
        small_t=pltpu.VMEM((128, D), f32),
        small_grad=pltpu.VMEM((128, D), f32),
        tile1=tile,
        tile2=tile,
        slots1=slots,
        slots2=slots,
        tile3=tile,
        slots3=slots,
        leaving=pltpu.VMEM((32, rows, BLOCK), bf16),
        owned=pltpu.VMEM((cube.total, rows, BLOCK), bf16),
        solved=pltpu.VMEM((cube.total, rows, BLOCK), bf16),
        packed=pltpu.VMEM((2, 5, 128, 128), f32),
        packed_in=pltpu.VMEM((2, 5, 128, 128), f32),
        summed=pltpu.VMEM((5, 128, 128), f32),
        whole=pltpu.VMEM((2, 5, 128, 128), f32),
        gram=pltpu.VMEM((D, D), f32),
        m_send=pltpu.SemaphoreType.DMA((32,)),
        m_recv=everyone,
        b_send=everyone,
        b_recv=pltpu.SemaphoreType.DMA((32,)),
        n_send=pltpu.SemaphoreType.DMA((3, 5)),
        n_recv=pltpu.SemaphoreType.DMA((3, 5)),
        c3_send=everyone,
        c3_recv=everyone,
        g_send=gather_stages,
        g_recv=gather_stages,
        s_send=stages,
        s_recv=stages,
        c1_send=everyone,
        c1_recv=everyone,
        c2_send=everyone,
        c2_recv=everyone,
        kv_send=single,
        kv_recv=single,
        halo_send=single,
        halo_recv=single,
        edge_send=single,
        edge_recv=single,
        dkv_send=pltpu.SemaphoreType.DMA((H // 2,)),
        dkv_recv=pltpu.SemaphoreType.DMA((H // 2,)),
    )

    kept = [n for n in outs if n != "returned"]
    buffers = dict({n: pltpu.VMEM(v.shape, v.dtype) for n, v in named.items()})
    buffers |= {n: pltpu.VMEM(outs[n].shape, outs[n].dtype) for n in kept}
    scratch |= buffers
    scratch |= dict(
        load_sem=pltpu.SemaphoreType.DMA((len(named),)),
        store_sem=pltpu.SemaphoreType.DMA((len(kept),)),
        k_sem=single,
    )

    def body(*refs):
        count = len(named) + len(outs)
        far = dict(zip(list(named) + list(outs), refs[:count]))
        near = dict(zip(scratch, refs[count:]))
        near["returned"] = far["returned"]
        near["loads"] = {
            name: pltpu.make_async_copy(far[name], near[name], near["load_sem"].at[n])
            for n, name in enumerate(named)
        }
        near["stores"] = [
            pltpu.make_async_copy(near[name], far[name], near["store_sem"].at[n])
            for n, name in enumerate(kept)
        ]
        step_kernel(cube, types.SimpleNamespace(**near))

    return pl.pallas_call(
        body,
        out_shape=list(outs.values()),
        in_specs=[pl.BlockSpec(memory_space=pl.ANY)] * len(named),
        out_specs=[pl.BlockSpec(memory_space=pl.ANY)] * len(outs),
        scratch_shapes=list(scratch.values()),
        compiler_params=pltpu.CompilerParams(
            collective_id=collective_id, has_side_effects=True, vmem_limit_bytes=60 << 20
        ),
        name="block_step",
    )(*named.values())


def finish_kernel(r):
    f32 = jnp.float32
    for load in r.loads:
        load.start()
    for load in r.loads[:5]:
        load.wait()
    share_first, share_middle, share_second, returned, squares = r.results
    for j in range(8):
        width = WIDTHS[j]
        if j < 4:
            columns = slice(FF * (j % 2), FF * (j % 2 + 1))
            grad = (share_first, share_second)[j % 2][:, share_columns(j)]
        else:
            columns = slice(0, width)
            start = STARTS[j] - STARTS[4]
            grad = share_middle[:, start : start + width]
        n = j // 2 if j < 4 else j - 2
        if j not in (1, 3):
            r.loads[5 + n].wait()
            r.loads[14 + n].wait()
        updated = MOMENTUM * r.moment[n][:, columns] + grad
        r.grad[n][:, columns] = grad
        r.next[n][:, columns] = updated
        solved = [returned[4 * j + q, :, 0 : width // 4].astype(f32) for q in range(4)]
        r.new[n][:, columns] = r.weight[n][:, columns] - RATE_MATRIX * jnp.concatenate(
            solved, axis=1
        )
        if j not in (0, 2):
            for store in (r.stores[n], r.stores[9 + n], r.stores[18 + n]):
                store.start()
    for n in (6, 7, 8):
        r.loads[5 + n].wait()
        r.loads[14 + n].wait()
    pack_small(r.small, r.turn, r.weight[8], r.weight[6], r.weight[7])
    pack_small(r.m_small, r.turn, r.moment[8], r.moment[6], r.moment[7])
    grad = share_first[:, 2 * FF :]
    updated = MOMENTUM * r.m_small[...] + grad
    lane = lax.broadcasted_iota(jnp.int32, (1, 128), 1)
    count = jnp.where(lane < SMALL_VEC, float(NB), float(D))
    scale = lax.rsqrt(squares[0:1, :] / count + EPS_SCALE)
    new = r.small[...] - RATE_VECTOR * updated * scale
    rows, rel_rows = r.small.shape[0], r.weight[8].shape[0]
    for value, outs in ((grad, r.grad), (new, r.new), (updated, r.next)):
        r.turn[...] = jnp.zeros_like(r.turn)
        r.turn[0:rows, :] = value
        turned = jnp.transpose(r.turn[...])
        outs[6][...] = turned[SMALL_VEC : SMALL_VEC + 7, 0:rows]
        outs[7][...] = value[:, SMALL_DEPTH : SMALL_DEPTH + K]
        outs[8][...] = value[0:rel_rows, SMALL_REL : SMALL_REL + H]
    for n in (6, 7, 8):
        for store in (r.stores[n], r.stores[9 + n], r.stores[18 + n]):
            store.start()
    for n in range(2):
        r.loads[23 + n].wait()
        r.stores[27 + n].start()
    for store in r.stores:
        store.wait()


def finish_step(fields, shares, returned, squares, weights, momenta):
    sources = (*shares, returned, squares, *weights, *momenta)
    operands = sources + tuple(fields)
    rows, count = weights[0].shape[0], len(sources)
    shapes = [jax.ShapeDtypeStruct(v.shape, v.dtype) for v in weights] * 3
    shapes += [jax.ShapeDtypeStruct(v.shape, v.dtype) for v in fields]

    def body(*refs):
        ins, refs = refs[: len(operands)], refs[len(operands) :]
        outs, refs = refs[: len(shapes)], refs[len(shapes) :]
        near, refs = refs[: count + 2], refs[count + 2 :]
        made, refs = refs[:27], refs[27:]
        small, m_small, turn, sem = refs
        pairs = list(zip(ins, near)) + list(zip(made + near[-2:], outs))
        moves = [pltpu.make_async_copy(a, b, sem.at[n]) for n, (a, b) in enumerate(pairs)]
        finish_kernel(
            types.SimpleNamespace(
                loads=moves[: count + 2],
                stores=moves[count + 2 :],
                results=near[:5],
                weight=near[5:14],
                moment=near[14:23],
                grad=made[:9],
                new=made[9:18],
                next=made[18:27],
                small=small,
                m_small=m_small,
                turn=turn,
            ),
        )

    return pl.pallas_call(
        body,
        out_shape=shapes,
        in_specs=[pl.BlockSpec(memory_space=pl.ANY)] * len(operands),
        out_specs=[pl.BlockSpec(memory_space=pl.ANY)] * len(shapes),
        scratch_shapes=[pltpu.VMEM(v.shape, v.dtype) for v in list(operands) + shapes[:27]]
        + [
            pltpu.VMEM((rows, 128), jnp.float32),
            pltpu.VMEM((rows, 128), jnp.float32),
            pltpu.VMEM((128, 128), jnp.float32),
            pltpu.SemaphoreType.DMA((len(operands) + len(shapes),)),
        ],
        compiler_params=pltpu.CompilerParams(vmem_limit_bytes=60 << 20),
        name="finish_step",
    )(*operands)


def unfused_step(
    cube,
    inputs,
    cotangent,
    w_up,
    w_down,
    w_qkv,
    w_out,
    w_glu,
    w_point,
    small,
    bucket_table,
):
    bf16 = jnp.bfloat16
    rows = w_up.shape[0]
    rel_rows = NB // cube.total
    shard_groups = (
        jnp.concatenate([w_up[:, :FF], w_down[:, :FF], small], axis=1).astype(bf16),
        jnp.concatenate([w_qkv, w_out, w_glu, w_point], axis=1).astype(bf16),
        jnp.concatenate([w_up[:, FF:], w_down[:, FF:]], axis=1).astype(bf16),
    )
    first, middle, second = [
        full.reshape(D, -1) for full in gather_groups(cube, shard_groups, 0)
    ]
    up_first, down_first, small_low = first[:, :FF], first[:, FF : 2 * FF], first[:, 2 * FF :]
    qkv_w, out_w = middle[:, : 3 * D], middle[:, 3 * D : 4 * D]
    glu_w, point_w = middle[:, 4 * D : 6 * D], middle[:, 6 * D :]
    up_second, down_second = second[:, :FF], second[:, FF:]
    gains = small_low[:, SMALL_VEC : SMALL_VEC + 7].astype(jnp.float32)
    kernel = small_low[:, SMALL_DEPTH : SMALL_DEPTH + K].astype(jnp.float32)
    rel_low = small_low[:, :H].reshape(cube.total, rows, H)[:, :rel_rows].reshape(NB, H)
    bucket_hit = (bucket_table[:, None] == jnp.arange(NB, dtype=jnp.int32)[None, :]).astype(
        jnp.float32
    )
    offsets = jnp.dot(bucket_hit, rel_low.astype(jnp.float32), precision=HIGHEST).T
    seq_rows = inputs[0]
    row_count = seq_rows.shape[0]
    first_row = lax.axis_index("seq") * row_count
    token_total = row_count * lax.axis_size(("dp", "seq", "shard"))
    section_one, ffn_saved = ffn_forward(seq_rows, gains[:, 0], up_first, down_first)
    normed_out2, normed2, inverse2 = layer_norm(section_one, gains[:, 1])
    lifted2 = normed_out2.astype(bf16)
    projected = matmul(lifted2, qkv_w).astype(bf16)
    query = projected[:, :D]
    pair = [(0, 1), (1, 0)]
    other = lax.ppermute(projected[:, D:], "seq", pair)
    early = lax.axis_index("seq") == 0
    both = jnp.concatenate(
        [
            jnp.where(early, projected[:, D:], other),
            jnp.where(early, other, projected[:, D:]),
        ],
        axis=0,
    )
    keys, values = both[:, :D], both[:, D:]
    attended, log_total = attention_forward(query, keys, values, offsets, first_row)
    attended_low = attended.astype(bf16)
    section_two = section_one + matmul(attended_low, out_w)
    normed_out3, normed3, inverse3 = layer_norm(section_two, gains[:, 2])
    lifted3 = normed_out3.astype(bf16)
    gates = matmul(lifted3, glu_w)
    first_half = gates[:, :D]
    sig_gate = jax.nn.sigmoid(gates[:, D:])
    glu = first_half * sig_gate
    glu_wide = with_halo(glu, (("seq", 0),), K // 2)
    conv = depthwise(glu_wide, kernel, row_count)
    part_sum = jnp.sum(conv, axis=0)
    part_mean = part_sum / row_count
    part_square = jnp.sum(jnp.square(conv - part_mean), axis=0)
    stats = collect(cube, jnp.concatenate([part_sum, part_square]).reshape(8, 128), 1)
    stats = stats.reshape(cube.total, 2, D)
    mean = jnp.sum(stats[:, 0], axis=0) / token_total
    spread_of_means = jnp.square(stats[:, 0] / row_count - mean) * row_count
    variance = jnp.sum(stats[:, 1] + spread_of_means, axis=0) / token_total
    centred = conv - mean
    inv_std = lax.rsqrt(variance + EPS_BATCH)
    normed_bn = centred * inv_std
    batch_out = normed_bn * gains[:, 5] + gains[:, 6]
    swish_low = jax.nn.silu(batch_out).astype(bf16)
    section_three = section_two + matmul(swish_low, point_w)
    section_four, tail_saved = ffn_forward(
        section_three, gains[:, 3], up_second, down_second
    )
    outputs, normed5, inverse5 = layer_norm(section_four, gains[:, 4])
    grad_four, gain_four = norm_back(cotangent[0], normed5, inverse5, gains[:, 4])
    grad_three, grad_up_two, grad_down_two, gain_three = ffn_backward(
        grad_four, tail_saved, gains[:, 3], up_second, down_second
    )
    grad_three_low = grad_three.astype(bf16)
    grad_point = matmul_left_t(swish_low, grad_three_low)
    grad_batch = matmul_right_t(grad_three_low, point_w) * silu_slope(batch_out)
    grad_normed = grad_batch * gains[:, 5]
    sums = jnp.concatenate(
        [jnp.sum(grad_normed, axis=0), jnp.sum(grad_normed * normed_bn, axis=0)]
    )
    sums = jnp.sum(collect(cube, sums.reshape(8, 128), 2), axis=0).reshape(2, D)
    sum_normed, sum_cross = sums[0], sums[1]
    grad_conv = inv_std * (
        grad_normed - sum_normed / token_total - normed_bn * sum_cross / token_total
    )
    grad_wide = with_halo(grad_conv, (("seq", 0),), K // 2)
    grad_glu = grad_wide[K - 1 : K - 1 + row_count] * kernel[:, 0]
    for tap_idx in range(1, K):
        grad_glu = (
            grad_glu
            + grad_wide[K - 1 - tap_idx : K - 1 - tap_idx + row_count] * kernel[:, tap_idx]
        )
    grad_kernel = jnp.stack(
        [
            jnp.sum(grad_conv * glu_wide[tap_idx : tap_idx + row_count], axis=0)
            for tap_idx in range(K)
        ],
        axis=1,
    )
    grad_gates = jnp.concatenate(
        [grad_glu * sig_gate, grad_glu * first_half * sig_gate * (1.0 - sig_gate)], axis=1
    ).astype(bf16)
    grad_glu_w = matmul_left_t(lifted3, grad_gates)
    grad_two_part, gain_two = norm_back(
        matmul_right_t(grad_gates, glu_w), normed3, inverse3, gains[:, 2]
    )
    grad_two = grad_three + grad_two_part
    grad_two_low = grad_two.astype(bf16)
    grad_out_w = matmul_left_t(attended_low, grad_two_low)
    grad_attended = matmul_right_t(grad_two_low, out_w).astype(bf16)
    delta = jnp.sum(
        (grad_attended.astype(jnp.float32) * attended).reshape(row_count, H, DH), axis=2
    )
    query_grad, key_grad, value_grad, offset_grad = attention_backward(
        query, keys, values, offsets, first_row, log_total, grad_attended, delta
    )
    keys_grad = jnp.concatenate([key_grad, value_grad], axis=1)
    theirs = lax.dynamic_slice_in_dim(keys_grad, row_count - first_row, row_count, 0)
    own = lax.dynamic_slice_in_dim(keys_grad, first_row, row_count, 0)
    own = own + lax.ppermute(theirs, "seq", pair)
    key_own, value_own = own[:, :D], own[:, D:]
    grad_proj = jnp.concatenate([query_grad, key_own, value_own], axis=1).astype(bf16)
    grad_qkv_w = matmul_left_t(lifted2, grad_proj)
    grad_one_part, gain_one = norm_back(
        matmul_right_t(grad_proj, qkv_w), normed2, inverse2, gains[:, 1]
    )
    grad_one = grad_two + grad_one_part
    input_grad, grad_up_one, grad_down_one, gain_zero = ffn_backward(
        grad_one, ffn_saved, gains[:, 0], up_first, down_first
    )
    grad_vec_local = jnp.stack(
        [
            gain_zero,
            gain_one,
            gain_two,
            gain_three,
            gain_four,
            jnp.sum(grad_batch * normed_bn, axis=0),
            jnp.sum(grad_batch, axis=0),
        ],
        axis=1,
    )
    grad_rel_local = jnp.dot(bucket_hit.T, offset_grad.T, precision=HIGHEST)
    rel_padded = jnp.pad(
        grad_rel_local.reshape(cube.total, rel_rows, H), ((0, 0), (0, rows - rel_rows), (0, 0))
    )
    small_grads = jnp.concatenate(
        [rel_padded.reshape(D, H), grad_vec_local, grad_kernel], axis=1
    )
    small_grads = jnp.pad(small_grads, ((0, 0), (0, 128 - SMALL_END)))
    lead = (2,) * cube.digits
    grad_groups = [
        jnp.concatenate(group, axis=1).astype(bf16).reshape(lead + (rows, -1))
        for group in (
            (grad_up_two, grad_down_two),
            (grad_qkv_w, grad_out_w, grad_glu_w, grad_point),
            (grad_up_one, grad_down_one, small_grads),
        )
    ]
    share_second, share_middle, share_first = scatter_groups(cube, grad_groups, 3)
    return outputs, input_grad, share_first, share_middle, share_second


def local(
    cube,
    inputs,
    cotangent,
    w_up,
    w_down,
    w_qkv,
    w_out,
    w_glu,
    w_point,
    vectors,
    depth_kernel,
    rel_bias,
    bucket_table,
    m_up,
    m_down,
    m_qkv,
    m_out,
    m_glu,
    m_point,
    m_vectors,
    m_depth,
    m_rel,
):
    bf16 = jnp.bfloat16
    rows, rel_rows = w_up.shape[0], rel_bias.shape[0]
    pack = lambda rel, vec, depth: jnp.pad(
        jnp.concatenate([jnp.pad(rel, ((0, rows - rel_rows), (0, 0))), vec, depth], axis=1),
        ((0, 0), (0, 128 - SMALL_END)),
    )
    small = pack(rel_bias, vectors, depth_kernel)
    weights = (w_up, w_down, w_qkv, w_out, w_glu, w_point)
    if rows % 16 == 0 and cube.total == 32:
        bucket = bucket_table[None]
        weights += (vectors.T, depth_kernel, rel_bias)
        momenta = (m_up, m_down, m_qkv, m_out, m_glu, m_point, m_vectors.T, m_depth, m_rel)
        outputs, input_grad, *shares, returned, squares = fused_step(
            cube, inputs[0], cotangent[0], weights, momenta, bucket, 0
        )
        *rest, outputs, input_grad = finish_step(
            (outputs, input_grad), shares, returned, squares, weights, momenta
        )
        for n in (6, 15, 24):
            rest[n] = rest[n].T
        return (outputs[None], input_grad[None], *rest)
    outputs, input_grad, share_first, share_middle, share_second = unfused_step(
        cube, inputs, cotangent, *weights, small, bucket_table
    )
    grad_up = jnp.concatenate([share_first[:, :FF], share_second[:, :FF]], axis=1)
    grad_down = jnp.concatenate([share_first[:, FF : 2 * FF], share_second[:, FF:]], axis=1)
    grad_qkv, grad_out = share_middle[:, : 3 * D], share_middle[:, 3 * D : 4 * D]
    grad_glu, grad_pnt = share_middle[:, 4 * D : 6 * D], share_middle[:, 6 * D :]
    share_small = share_first[:, 2 * FF :]
    grad_vectors = share_small[:, SMALL_VEC : SMALL_VEC + 7]
    grad_depth = share_small[:, SMALL_DEPTH : SMALL_DEPTH + K]
    grad_rel = share_small[: rel_bias.shape[0], :H]
    next_m_up = MOMENTUM * m_up + grad_up
    next_m_down = MOMENTUM * m_down + grad_down
    next_m_qkv = MOMENTUM * m_qkv + grad_qkv
    next_m_out = MOMENTUM * m_out + grad_out
    next_m_glu = MOMENTUM * m_glu + grad_glu
    next_m_point = MOMENTUM * m_point + grad_pnt
    stacked = jnp.concatenate(
        [next_m_up, next_m_down, next_m_qkv, next_m_out, next_m_glu, next_m_point], axis=1
    )
    owned = spread(cube, stacked, 4).reshape(D, BLOCK)
    ortho = orthogonalize_blocks(cube, owned, bf16, 5)
    mine = restore(cube, ortho.reshape(cube.total, rows, BLOCK), 6).astype(jnp.float32)
    new_up = w_up - RATE_MATRIX * mine[:, : 2 * FF]
    new_down = w_down - RATE_MATRIX * mine[:, 2 * FF : 4 * FF]
    new_qkv = w_qkv - RATE_MATRIX * mine[:, STARTS[4] : STARTS[5]]
    new_out = w_out - RATE_MATRIX * mine[:, STARTS[5] : STARTS[6]]
    new_glu = w_glu - RATE_MATRIX * mine[:, STARTS[6] : STARTS[7]]
    new_point = w_point - RATE_MATRIX * mine[:, STARTS[7] :]
    next_m_vectors = MOMENTUM * m_vectors + grad_vectors
    next_m_depth = MOMENTUM * m_depth + grad_depth
    next_m_rel = MOMENTUM * m_rel + grad_rel
    squares = jnp.concatenate(
        [
            jnp.sum(next_m_vectors * next_m_vectors, axis=0),
            jnp.sum(next_m_depth * next_m_depth, axis=0),
            jnp.sum(next_m_rel * next_m_rel, axis=0),
        ]
    )
    squares = jnp.pad(squares, (0, 128 - squares.shape[0])).reshape(1, 128)
    squares = jnp.sum(collect(cube, jnp.pad(squares, ((0, 7), (0, 0))), 7), axis=0)[0]
    square_vec, square_depth = squares[:7], squares[7 : 7 + K]
    square_rel = squares[7 + K : 7 + K + H]
    new_vectors = vectors - RATE_VECTOR * next_m_vectors * lax.rsqrt(square_vec / D + EPS_SCALE)
    new_depth = depth_kernel - RATE_VECTOR * next_m_depth * lax.rsqrt(square_depth / D + EPS_SCALE)
    new_rel = rel_bias - RATE_VECTOR * next_m_rel * lax.rsqrt(square_rel / NB + EPS_SCALE)
    return (
        outputs[None],
        input_grad[None],
        grad_up,
        grad_down,
        grad_qkv,
        grad_out,
        grad_glu,
        grad_pnt,
        grad_vectors,
        grad_depth,
        grad_rel,
        new_up,
        new_down,
        new_qkv,
        new_out,
        new_glu,
        new_point,
        new_vectors,
        new_depth,
        new_rel,
        next_m_up,
        next_m_down,
        next_m_qkv,
        next_m_out,
        next_m_glu,
        next_m_point,
        next_m_vectors,
        next_m_depth,
        next_m_rel,
    )


def solution(mesh):
    placed = (
        P(("dp", "shard"), "seq", None),
        P(("dp", "shard"), "seq", None),
        P(("dp", "seq", "shard"), None),
        P(("dp", "seq", "shard"), None),
        P(("dp", "seq", "shard"), None),
        P(("dp", "seq", "shard"), None),
        P(("dp", "seq", "shard"), None),
        P(("dp", "seq", "shard"), None),
        P(("dp", "seq", "shard"), None),
        P(("dp", "seq", "shard"), None),
        P(("dp", "seq", "shard"), None),
        P(),
        P(("dp", "seq", "shard"), None),
        P(("dp", "seq", "shard"), None),
        P(("dp", "seq", "shard"), None),
        P(("dp", "seq", "shard"), None),
        P(("dp", "seq", "shard"), None),
        P(("dp", "seq", "shard"), None),
        P(("dp", "seq", "shard"), None),
        P(("dp", "seq", "shard"), None),
        P(("dp", "seq", "shard"), None),
    )
    return jax.shard_map(
        functools.partial(local, Cube(mesh.shape["dp"])),
        mesh=mesh,
        in_specs=placed,
        out_specs=(
            P(("dp", "shard"), "seq", None),
            P(("dp", "shard"), "seq", None),
            P(("dp", "seq", "shard"), None),
            P(("dp", "seq", "shard"), None),
            P(("dp", "seq", "shard"), None),
            P(("dp", "seq", "shard"), None),
            P(("dp", "seq", "shard"), None),
            P(("dp", "seq", "shard"), None),
            P(("dp", "seq", "shard"), None),
            P(("dp", "seq", "shard"), None),
            P(("dp", "seq", "shard"), None),
            P(("dp", "seq", "shard"), None),
            P(("dp", "seq", "shard"), None),
            P(("dp", "seq", "shard"), None),
            P(("dp", "seq", "shard"), None),
            P(("dp", "seq", "shard"), None),
            P(("dp", "seq", "shard"), None),
            P(("dp", "seq", "shard"), None),
            P(("dp", "seq", "shard"), None),
            P(("dp", "seq", "shard"), None),
            P(("dp", "seq", "shard"), None),
            P(("dp", "seq", "shard"), None),
            P(("dp", "seq", "shard"), None),
            P(("dp", "seq", "shard"), None),
            P(("dp", "seq", "shard"), None),
            P(("dp", "seq", "shard"), None),
            P(("dp", "seq", "shard"), None),
            P(("dp", "seq", "shard"), None),
            P(("dp", "seq", "shard"), None),
        ),
        check_vma=False,
    )
```

```python
import functools
import types

import jax
import jax.numpy as jnp
from jax import lax
from jax.experimental import pallas as pl
from jax.experimental.pallas import tpu as pltpu
from jax.sharding import PartitionSpec as P

D = 512
FF = 2048
H = 8
DH = 64
K = 31
NB = 128


EPS_NORM = 1e-05
EPS_BATCH = 1e-05
EPS_SCALE = 1e-06
MOMENTUM = 0.9
RATE_MATRIX = 1.0
RATE_VECTOR = 0.25
COEF_A = 3.4445
COEF_B = -4.775
COEF_C = 2.0315
HIGHEST = lax.Precision.HIGHEST


AXES = ("dp", "seq", "shard")
MESH = pl.DeviceIdType.MESH
WIDTHS = (FF, FF, FF, FF, 3 * D, D, 2 * D, D)
STARTS = tuple(sum(WIDTHS[:i]) for i in range(9))
BLOCK = 512


class Cube:
    def __init__(self, dp_size):
        self.dp_size = dp_size
        self.levels = dp_size.bit_length() - 1
        self.digits = self.levels + 2
        self.total = dp_size * 4
        high = list(range(self.levels - 1))
        low, seq, core = self.levels - 1, self.levels, self.levels + 1
        self.gather_orders = (high + [low, seq, core], high + [seq, low, core])
        self.gather_late_orders = ([seq, low] + high + [core], [low, seq] + high + [core])
        self.scatter_orders = tuple(order[::-1] for order in self.gather_orders)
        self.scatter_high_orders = tuple(order[::-1] for order in self.gather_late_orders)
        self.scatter_low_orders = ([core, low, seq] + high[::-1],) * 2
        self.scatter_kinds = (
            self.scatter_orders,
            self.scatter_high_orders,
            self.scatter_low_orders,
        )

    def mine(self):
        d = lax.axis_index("dp")
        bits = [lax.rem(d // (1 << (self.levels - 1 - k)), 2) for k in range(self.levels)]
        return bits + [lax.axis_index("seq"), lax.axis_index("shard")]

    def partner(self, k):
        d, s, c = lax.axis_index("dp"), lax.axis_index("seq"), lax.axis_index("shard")
        if k == self.levels:
            return (d, 1 - s, c)
        if k == self.levels + 1:
            return (d, s, 1 - c)
        step = 1 << (self.levels - 1 - k)
        bit = lax.rem(d // step, 2)
        return (d + (1 - 2 * bit) * step, s, c)

    def index(self):
        return (lax.axis_index("dp") * 2 + lax.axis_index("seq")) * 2 + lax.axis_index("shard")

    def coords(self, index):
        return (index // 4, lax.rem(index // 2, 2), lax.rem(index, 2))

    def greet_partners(self):
        barrier = pltpu.get_barrier_semaphore()
        for k in range(self.digits):
            pl.semaphore_signal(barrier, inc=1, device_id=self.partner(k), device_id_type=MESH)
        pl.semaphore_wait(barrier, self.digits)

    def greet_all(self):
        barrier = pltpu.get_barrier_semaphore()
        me = self.index()

        @pl.loop(1, self.total)
        def _(i):
            peer = self.coords(lax.rem(me + i, self.total))
            pl.semaphore_signal(barrier, inc=1, device_id=peer, device_id_type=MESH)

        pl.semaphore_wait(barrier, self.total - 1)


def halves(width):
    cut = (width // 128 + 1) // 2 * 128
    return ((0, cut), (cut, width - cut))


def remote(src, dst, send_sem, recv_sem, peer):
    return pltpu.make_async_remote_copy(
        src_ref=src,
        dst_ref=dst,
        send_sem=send_sem,
        recv_sem=recv_sem,
        device_id=peer,
        device_id_type=MESH,
    )


def gather_kernel(cube, groups, *refs):
    shards, outs = refs[:groups], refs[groups : 2 * groups]
    own_sem, send_sem, recv_sem = refs[2 * groups :]
    cube.greet_partners()
    mine = cube.mine()
    locals_ = []
    for g in range(groups):
        copy = pltpu.make_async_copy(shards[g], outs[g].at[tuple(mine)], own_sem.at[g])
        copy.start()
        locals_.append(copy)

    def make(g, half, stage):
        order = cube.gather_orders[half]
        columns = pl.ds(*halves(shards[g].shape[-1])[half])
        done = order[:stage]
        index = tuple(slice(None) if k in done else mine[k] for k in range(cube.digits))
        place = outs[g].at[index + (slice(None), columns)]
        source = shards[g].at[:, columns] if stage == 0 else place
        return remote(
            source,
            place,
            send_sem.at[g, half, stage],
            recv_sem.at[g, half, stage],
            cube.partner(order[stage]),
        )

    copies = {}
    for g in range(groups):
        for half in range(2):
            copies[g, half, 0] = make(g, half, 0)
            copies[g, half, 0].start()
    for tick in range(cube.digits + 2 * (groups - 1)):
        for g in range(groups):
            stage = tick - 2 * g
            if not 0 <= stage < cube.digits:
                continue
            for half in range(2):
                copies[g, half, stage].wait_recv()
                if stage == 0 and half == 0:
                    locals_[g].wait()
                if stage + 1 < cube.digits:
                    copies[g, half, stage + 1] = make(g, half, stage + 1)
                    copies[g, half, stage + 1].start()
    for copy in copies.values():
        copy.wait_send()


def gather_groups(cube, shards, collective_id):
    groups = len(shards)
    lead = (2,) * cube.digits
    return pl.pallas_call(
        functools.partial(gather_kernel, cube, groups),
        out_shape=[jax.ShapeDtypeStruct(lead + s.shape, s.dtype) for s in shards],
        in_specs=[pl.BlockSpec(memory_space=pl.ANY)] * groups,
        out_specs=[pl.BlockSpec(memory_space=pl.ANY)] * groups,
        scratch_shapes=[
            pltpu.SemaphoreType.DMA((groups,)),
            pltpu.SemaphoreType.DMA((groups, 2, cube.digits)),
            pltpu.SemaphoreType.DMA((groups, 2, cube.digits)),
        ],
        compiler_params=pltpu.CompilerParams(
            collective_id=collective_id, has_side_effects=True
        ),
        name="gather_weights",
    )(*shards)


def scatter_kernel(cube, groups, *refs):
    parts, outs = refs[:groups], refs[groups : 2 * groups]
    rest = refs[2 * groups :]
    sums = rest[:groups]
    landed = rest[groups : groups + groups * 2 * cube.digits]
    own_sem, send_sem, recv_sem = rest[groups + groups * 2 * cube.digits :]
    cube.greet_partners()
    mine = cube.mine()
    last = cube.digits - 1

    def slot(g, half, stage):
        return landed[(g * 2 + half) * cube.digits + stage]

    def place(g, half, stage, bit_of):
        order = cube.scatter_orders[half]
        columns = pl.ds(*halves(outs[g].shape[-1])[half])
        index = []
        for k in range(cube.digits - 1):
            at = order.index(k)
            if at > stage:
                index.append(slice(None))
            else:
                index.append(bit_of(k) if at == stage else mine[k])
        return tuple(index) + (slice(None), columns)

    def make(g, half, stage):
        order = cube.scatter_orders[half]
        if stage == 0:
            index = (slice(None),) * last + (1 - mine[last],)
            columns = pl.ds(*halves(outs[g].shape[-1])[half])
            source = parts[g].at[index + (slice(None), columns)]
        else:
            source = sums[g].at[place(g, half, stage, lambda k: 1 - mine[k])]
        return remote(
            source,
            slot(g, half, stage),
            send_sem.at[g, half, stage],
            recv_sem.at[g, half, stage],
            cube.partner(order[stage]),
        )

    copies = {}
    locals_ = []
    for g in range(groups):
        copy = pltpu.make_async_copy(
            parts[g].at[(slice(None),) * last + (mine[last],)], sums[g], own_sem.at[g]
        )
        copy.start()
        locals_.append(copy)
        for half in range(2):
            copies[g, half, 0] = make(g, half, 0)
            copies[g, half, 0].start()

    def add(g, half, stage):
        order = cube.scatter_orders[half]
        columns = pl.ds(*halves(outs[g].shape[-1])[half])
        free = [k for k in range(last) if order.index(k) > stage]
        count = 1 << len(free)
        target, extra = sums[g], slot(g, half, stage)

        def one(i):
            digit = {k: lax.rem(i // (1 << (len(free) - 1 - n)), 2) for n, k in enumerate(free)}
            full = tuple(digit.get(k, mine[k]) for k in range(last)) + (slice(None), columns)
            short = tuple(digit[k] for k in free)
            total = target[full].astype(jnp.float32) + extra[short + (slice(None), slice(None))].astype(jnp.float32)
            if stage == last:
                outs[g][:, columns] = total
            else:
                target[full] = total.astype(target.dtype)

        if count == 1:
            one(0)
        else:
            pl.loop(0, count)(one)

    for stage in range(cube.digits):
        for g in range(groups):
            if stage == 0:
                locals_[g].wait()
            for half in range(2):
                copies[g, half, stage].wait_recv()
                add(g, half, stage)
                if stage < last:
                    copies[g, half, stage + 1] = make(g, half, stage + 1)
                    copies[g, half, stage + 1].start()
    for copy in copies.values():
        copy.wait_send()


def scatter_groups(cube, parts, collective_id):
    groups = len(parts)
    scratch = [pltpu.VMEM((2,) * (cube.digits - 1) + p.shape[-2:], p.dtype) for p in parts]
    for p in parts:
        for half in range(2):
            for stage in range(cube.digits):
                lead = (2,) * (cube.digits - 1 - stage)
                scratch.append(pltpu.VMEM(lead + (p.shape[-2], halves(p.shape[-1])[half][1]), p.dtype))
    scratch += [
        pltpu.SemaphoreType.DMA((groups,)),
        pltpu.SemaphoreType.DMA((groups, 2, cube.digits)),
        pltpu.SemaphoreType.DMA((groups, 2, cube.digits)),
    ]
    return pl.pallas_call(
        functools.partial(scatter_kernel, cube, groups),
        out_shape=[jax.ShapeDtypeStruct(p.shape[-2:], jnp.float32) for p in parts],
        in_specs=[pl.BlockSpec(memory_space=pl.ANY)] * groups,
        out_specs=[pl.BlockSpec(memory_space=pltpu.VMEM)] * groups,
        scratch_shapes=scratch,
        compiler_params=pltpu.CompilerParams(
            collective_id=collective_id, has_side_effects=True, vmem_limit_bytes=48 << 20
        ),
        name="scatter_grads",
    )(*parts)


def collect_kernel(cube, x_ref, o_ref, send_sem, recv_sem):
    me = cube.index()
    cube.greet_all()

    def make(i):
        to = lax.rem(me + i, cube.total)
        return remote(x_ref, o_ref.at[i], send_sem.at[i], recv_sem.at[i], cube.coords(to))

    @pl.loop(1, cube.total)
    def _(i):
        make(i).start()

    o_ref[0] = x_ref[...]

    @pl.loop(1, cube.total)
    def _(i):
        make(i).wait()


def collect(cube, x, collective_id):
    return pl.pallas_call(
        functools.partial(collect_kernel, cube),
        out_shape=jax.ShapeDtypeStruct((cube.total,) + x.shape, x.dtype),
        in_specs=[pl.BlockSpec(memory_space=pltpu.VMEM)],
        out_specs=pl.BlockSpec(memory_space=pltpu.VMEM),
        scratch_shapes=[
            pltpu.SemaphoreType.DMA((cube.total,)),
            pltpu.SemaphoreType.DMA((cube.total,)),
        ],
        compiler_params=pltpu.CompilerParams(
            collective_id=collective_id, has_side_effects=True
        ),
        name="collect_stats",
    )(x)


def by_matrix(j, action):
    for width in sorted(set(WIDTHS)):
        members = [i for i in range(8) if WIDTHS[i] == width]
        hit = functools.reduce(jnp.logical_or, [j == i for i in members])
        pl.when(hit)(functools.partial(action, width // 4))


def quarter_start(t):
    j, q = t // 4, lax.rem(t, 4)
    start = 0
    for i in range(8):
        start = start + jnp.where(j == i, STARTS[i] + q * (WIDTHS[i] // 4), 0)
    return pl.multiple_of(start, 128)


def owner_coords(cube, t):
    return ((t // 4) * (cube.dp_size // 8), lax.rem(t // 2, 2), lax.rem(t, 2))


def spread_kernel(cube, x_ref, o_ref, own_sem, send_sem, recv_sem):
    me = cube.index()
    repeat = cube.dp_size // 8
    d, s, c = lax.axis_index("dp"), lax.axis_index("seq"), lax.axis_index("shard")
    owner = lax.rem(d, repeat) == 0
    mine = ((d // repeat) * 2 + s) * 2 + c
    cube.greet_all()

    def send(i, wait):
        t = lax.rem(mine + i, 32)
        peer = owner_coords(cube, t)
        other = jnp.logical_or(jnp.logical_not(owner), i > 0)

        def go(width):
            src = x_ref.at[:, pl.ds(quarter_start(t), width)]
            dst = o_ref.at[me, :, pl.ds(0, width)]
            copy = remote(src, dst, send_sem.at[i], recv_sem.at[me], peer)
            if wait:
                copy.wait_send()
            else:
                copy.start()

        pl.when(other)(lambda: by_matrix(t // 4, go))

    pl.loop(0, 32)(functools.partial(send, wait=False))

    def keep(width):
        copy = pltpu.make_async_copy(
            x_ref.at[:, pl.ds(quarter_start(mine), width)],
            o_ref.at[me, :, pl.ds(0, width)],
            own_sem,
        )
        copy.start()
        copy.wait()

    def receive(width):
        @pl.loop(1, cube.total)
        def _(i):
            source = lax.rem(me + i, cube.total)
            place = o_ref.at[source, :, pl.ds(0, width)]
            remote(
                place, place, send_sem.at[0], recv_sem.at[source], cube.coords(source)
            ).wait_recv()

    @pl.when(owner)
    def _():
        by_matrix(mine // 4, keep)
        by_matrix(mine // 4, receive)

    pl.loop(0, 32)(functools.partial(send, wait=True))


def spread(cube, x, collective_id):
    return pl.pallas_call(
        functools.partial(spread_kernel, cube),
        out_shape=jax.ShapeDtypeStruct((cube.total, x.shape[0], BLOCK), x.dtype),
        in_specs=[pl.BlockSpec(memory_space=pl.ANY)],
        out_specs=pl.BlockSpec(memory_space=pl.ANY),
        scratch_shapes=[
            pltpu.SemaphoreType.DMA,
            pltpu.SemaphoreType.DMA((32,)),
            pltpu.SemaphoreType.DMA((cube.total,)),
        ],
        compiler_params=pltpu.CompilerParams(
            collective_id=collective_id, has_side_effects=True
        ),
        name="spread_momentum",
    )(x)


def restore_kernel(cube, x_ref, o_ref, own_sem, send_sem, recv_sem):
    me = cube.index()
    repeat = cube.dp_size // 8
    d, s, c = lax.axis_index("dp"), lax.axis_index("seq"), lax.axis_index("shard")
    owner = lax.rem(d, repeat) == 0
    mine = ((d // repeat) * 2 + s) * 2 + c
    cube.greet_all()

    def send_all(wait, width):
        @pl.loop(1, cube.total)
        def _(i):
            to = lax.rem(me + i, cube.total)
            src = x_ref.at[to, :, pl.ds(0, width)]
            dst = o_ref.at[:, pl.ds(quarter_start(mine), width)]
            copy = remote(src, dst, send_sem.at[i], recv_sem.at[mine], cube.coords(to))
            if wait:
                copy.wait_send()
            else:
                copy.start()

    def keep(width):
        copy = pltpu.make_async_copy(
            x_ref.at[me, :, pl.ds(0, width)],
            o_ref.at[:, pl.ds(quarter_start(mine), width)],
            own_sem,
        )
        copy.start()
        copy.wait()

    @pl.when(owner)
    def _():
        by_matrix(mine // 4, functools.partial(send_all, False))
        by_matrix(mine // 4, keep)

    def receive(i):
        t = lax.rem(mine + i, 32)
        other = jnp.logical_or(jnp.logical_not(owner), i > 0)

        def go(width):
            place = o_ref.at[:, pl.ds(quarter_start(t), width)]
            remote(
                place, place, send_sem.at[0], recv_sem.at[t], owner_coords(cube, t)
            ).wait_recv()

        pl.when(other)(lambda: by_matrix(t // 4, go))

    pl.loop(0, 32)(receive)

    @pl.when(owner)
    def _():
        by_matrix(mine // 4, functools.partial(send_all, True))


def restore(cube, x, collective_id):
    return pl.pallas_call(
        functools.partial(restore_kernel, cube),
        out_shape=jax.ShapeDtypeStruct((x.shape[1], STARTS[8]), x.dtype),
        in_specs=[pl.BlockSpec(memory_space=pl.ANY)],
        out_specs=pl.BlockSpec(memory_space=pl.ANY),
        scratch_shapes=[
            pltpu.SemaphoreType.DMA,
            pltpu.SemaphoreType.DMA((cube.total,)),
            pltpu.SemaphoreType.DMA((32,)),
        ],
        compiler_params=pltpu.CompilerParams(
            collective_id=collective_id, has_side_effects=True
        ),
        name="restore_rows",
    )(x)


def split(value):
    high = value.astype(jnp.bfloat16)
    low = (value - high.astype(jnp.float32)).astype(jnp.bfloat16)
    return high, low


def product(left, right):
    (lh, ll), (rh, rl) = left, right
    dot = functools.partial(jnp.dot, preferred_element_type=jnp.float32)
    return dot(lh, rh) + (dot(lh, rl) + dot(ll, rh))


def orthogonalize_kernel(cube, x_ref, o_ref, gram_ref, work, landed, send_sem, recv_sem):
    barrier = pltpu.get_barrier_semaphore()
    peers = (cube.partner(cube.levels + 1), cube.partner(cube.levels))
    for peer in peers:
        pl.semaphore_signal(barrier, inc=1, device_id=peer, device_id_type=MESH)
    pl.semaphore_wait(barrier, 2)
    repeat = cube.dp_size // 8
    j = lax.axis_index("dp") // repeat
    width = 0
    for i in range(8):
        width = width + jnp.where(j == i, WIDTHS[i] // 4, 0)
    column = lax.broadcasted_iota(jnp.int32, (D, BLOCK), 1)
    block = jnp.where(column < width, x_ref[...].astype(jnp.float32), 0.0)
    bh, bl = split(block)
    dot_t = lambda a, b: lax.dot_general(
        a, b, (((1,), (1,)), ((), ())), preferred_element_type=jnp.float32
    )
    gram_ref[0] = dot_t(bh, bh) + (dot_t(bh, bl) + dot_t(bl, bh))
    for step in range(2):
        copy = remote(
            gram_ref.at[step], landed.at[step], send_sem.at[step], recv_sem.at[step], peers[step]
        )
        copy.start()
        copy.wait()
        gram_ref[step + 1] = gram_ref[step] + landed[step]
    gram = gram_ref[2]
    row = lax.broadcasted_iota(jnp.int32, (D, D), 0)
    col = lax.broadcasted_iota(jnp.int32, (D, D), 1)
    eye = row == col
    square = jnp.sum(jnp.sum(jnp.where(eye, gram, 0.0), axis=1, keepdims=True), axis=0, keepdims=True)
    scale = 1.0 / (jnp.sqrt(square) + 1e-07)
    gram = gram * (scale * scale)
    block = block * scale
    for step in range(5):
        parts = split(gram)
        mixed = COEF_B * gram + COEF_C * product(parts, parts)
        mixed = jnp.where(eye, mixed + COEF_A, mixed)
        mixed_parts = split(mixed)
        block = product(mixed_parts, split(block))
        if step < 4:
            gram = product(mixed_parts, split(product(mixed_parts, parts)))
    o_ref[...] = block.astype(o_ref.dtype)


def orthogonalize_blocks(cube, x, out_dtype, collective_id):
    return pl.pallas_call(
        functools.partial(orthogonalize_kernel, cube),
        out_shape=jax.ShapeDtypeStruct((D, BLOCK), out_dtype),
        in_specs=[pl.BlockSpec(memory_space=pltpu.VMEM)],
        out_specs=pl.BlockSpec(memory_space=pltpu.VMEM),
        scratch_shapes=[
            pltpu.VMEM((3, D, D), jnp.float32),
            pltpu.VMEM((8, 128), jnp.float32),
            pltpu.VMEM((2, D, D), jnp.float32),
            pltpu.SemaphoreType.DMA((2,)),
            pltpu.SemaphoreType.DMA((2,)),
        ],
        compiler_params=pltpu.CompilerParams(
            collective_id=collective_id, has_side_effects=True, vmem_limit_bytes=48 << 20
        ),
        name="orthogonalize",
    )(x)

def with_halo(value, sides, width):
    for axis, dim in sides:
        devices, length = (lax.axis_size(axis), value.shape[dim])
        up = [(i, (i + 1) % devices) for i in range(devices - 1)]
        down = [(j, i) for i, j in up]
        last = lax.slice_in_dim(value, length - width, length, axis=dim)
        first = lax.slice_in_dim(value, 0, width, axis=dim)
        before = lax.ppermute(last, axis, up)
        after = lax.ppermute(first, axis, down)
        value = jnp.concatenate([before, value, after], axis=dim)
    return value


def matmul(left, right):
    return jnp.dot(left, right, preferred_element_type=jnp.float32)


def matmul_right_t(left, right):
    return lax.dot_general(
        left, right, (((1,), (1,)), ((), ())), preferred_element_type=jnp.float32
    )


def matmul_left_t(left, right):
    return lax.dot_general(
        left, right, (((0,), (0,)), ((), ())), preferred_element_type=jnp.float32
    )


def layer_norm(field, gain):
    centre = jnp.mean(field, axis=-1, keepdims=True)
    shifted = field - centre
    inverse = lax.rsqrt(jnp.mean(shifted * shifted, axis=-1, keepdims=True) + EPS_NORM)
    normed = shifted * inverse
    return (normed * gain, normed, inverse)


def norm_back(grad_out, normed, inverse, gain):
    scaled = grad_out * gain
    grad_in = inverse * (
        scaled
        - jnp.mean(scaled, axis=-1, keepdims=True)
        - normed * jnp.mean(scaled * normed, axis=-1, keepdims=True)
    )
    return (grad_in, jnp.sum(grad_out * normed, axis=0))


def silu_slope(values):
    sigma = jax.nn.sigmoid(values)
    return sigma * (1.0 + values * (1.0 - sigma))


def ffn_forward(field, gain, w_in, w_back):
    normed_out, normed, inverse = layer_norm(field, gain)
    lifted = normed_out.astype(jnp.bfloat16)
    hidden_pre = matmul(lifted, w_in)
    hidden_act = jax.nn.silu(hidden_pre).astype(jnp.bfloat16)
    return (
        field + 0.5 * matmul_right_t(hidden_act, w_back),
        (lifted, hidden_pre, hidden_act, normed, inverse),
    )


def ffn_backward(grad, saved, gain, w_in, w_back):
    lifted, hidden_pre, hidden_act, normed, inverse = saved
    grad_branch = (0.5 * grad).astype(jnp.bfloat16)
    grad_back = matmul_left_t(grad_branch, hidden_act)
    grad_act = matmul(grad_branch, w_back)
    grad_pre = (grad_act * silu_slope(hidden_pre)).astype(jnp.bfloat16)
    grad_in = matmul_left_t(lifted, grad_pre)
    grad_field, grad_gain = norm_back(matmul_right_t(grad_pre, w_in), normed, inverse, gain)
    return (grad + grad_field, grad_in, grad_back, grad_gain)


def depthwise(wide, kernel, count):
    total = wide[0:count] * kernel[:, 0]
    for tap_idx in range(1, K):
        total = total + wide[tap_idx : tap_idx + count] * kernel[:, tap_idx]
    return total


def spread_rows(window, count, keys_len):
    padded = jnp.concatenate([window, jnp.zeros((1,), window.dtype)])
    tiled = jnp.broadcast_to(padded[None, :], (count, keys_len + count)).reshape(-1)
    shaped = tiled[: count * (keys_len + count - 1)].reshape(count, keys_len + count - 1)
    return shaped[:, count - 1 : count - 1 + keys_len]


def collect_rows(grid, count, keys_len):
    placed = jnp.concatenate([jnp.zeros((count, count - 1), grid.dtype), grid], axis=1).reshape(-1)
    placed = jnp.concatenate([placed, jnp.zeros((count,), grid.dtype)])
    return jnp.sum(placed.reshape(count, keys_len + count), axis=0)[: keys_len + count - 1]


def attention_scores(query, keys, offsets, first_row, row_start, block, head_idx):
    length = keys.shape[0]
    columns = slice(head_idx * DH, (head_idx + 1) * DH)
    anchor = length - block - first_row - row_start
    window = lax.dynamic_slice_in_dim(offsets[head_idx], anchor, length + block - 1)
    product = matmul_right_t(query[row_start : row_start + block, columns], keys[:, columns])
    return product * DH ** (-0.5) + spread_rows(window, block, length)


def attention_forward(query, keys, values, offsets, first_row):
    total_rows = query.shape[0]
    block = min(512, total_rows)
    head_outs = []
    head_lse = []
    for head_idx in range(H):
        scores = attention_scores(query, keys, offsets, first_row, 0, block, head_idx)
        row_max = jnp.max(scores, axis=1, keepdims=True)
        shifted_exp = jnp.exp(scores - row_max)
        row_total = jnp.sum(shifted_exp, axis=1, keepdims=True)
        prob_low = (shifted_exp / row_total).astype(jnp.bfloat16)
        head_outs.append(matmul(prob_low, values[:, head_idx * DH : (head_idx + 1) * DH]))
        head_lse.append((row_max + jnp.log(row_total))[:, 0])
    out_blocks = jnp.concatenate(head_outs, axis=1)
    lse_blocks = jnp.stack(head_lse, axis=0)
    return (out_blocks, lse_blocks)


def attention_backward(query, keys, values, offsets, first_row, log_total, grad_attended, delta):
    total_rows = query.shape[0]
    length = keys.shape[0]
    block = min(512, total_rows)
    scale = DH ** (-0.5)
    key_parts = [jnp.zeros((length, DH), jnp.float32) for head_idx in range(H)]
    value_parts = [jnp.zeros((length, DH), jnp.float32) for head_idx in range(H)]
    offset_rows = [jnp.zeros((2 * length - 1,), jnp.float32) for head_idx in range(H)]
    head_grads = []
    for head_idx in range(H):
        columns = slice(head_idx * DH, (head_idx + 1) * DH)
        scores = attention_scores(query, keys, offsets, first_row, 0, block, head_idx)
        prob = jnp.exp(scores - log_total[head_idx, 0:block][:, None])
        prob_low = prob.astype(jnp.bfloat16)
        grad_piece = grad_attended[0:block, columns]
        value_parts[head_idx] = matmul_left_t(prob_low, grad_piece)
        grad_prob = matmul_right_t(grad_piece, values[:, columns])
        grad_score = prob * (grad_prob - delta[0:block, head_idx][:, None])
        score_low = grad_score.astype(jnp.bfloat16)
        head_grads.append(matmul(score_low, keys[:, columns]) * scale)
        key_parts[head_idx] = matmul_left_t(score_low, query[0:block, columns]) * scale
        anchor = length - block - first_row - 0
        offset_rows[head_idx] = lax.dynamic_update_slice_in_dim(
            offset_rows[head_idx], collect_rows(grad_score, block, length), anchor, 0
        )
    query_blocks = jnp.concatenate(head_grads, axis=1)
    return (
        query_blocks,
        jnp.concatenate(key_parts, axis=1),
        jnp.concatenate(value_parts, axis=1),
        jnp.stack(offset_rows, axis=0),
    )


def mean_last(value):
    return jnp.mean(value, axis=-1, keepdims=True)


def normalize(field):
    shifted = field - mean_last(field)
    inverse = lax.rsqrt(mean_last(shifted * shifted) + EPS_NORM)
    return shifted * inverse, inverse


def norm_grad(grad_out, normed, inverse, gain):
    scaled = grad_out * gain
    grad_in = inverse * (scaled - mean_last(scaled) - normed * mean_last(scaled * normed))
    return grad_in, jnp.sum(grad_out * normed, axis=0, keepdims=True)


def row_to_tile(ref, base, row):
    for k in range(4):
        ref[base + k : base + k + 1, :] = row[:, 128 * k : 128 * (k + 1)]


def tile_to_row(tile):
    return jnp.concatenate([tile[k : k + 1, :] for k in range(4)], axis=1)


def skew(row, count):
    sub = lax.broadcasted_iota(jnp.int32, (8, 512), 0)
    block = jnp.broadcast_to(row, (8, 512))
    for bit in (1, 2, 4):
        block = jnp.where((sub // bit) % 2 == 1, pltpu.roll(block, bit, 1), block)
    size = 8
    while size < count:
        block = jnp.concatenate([block, pltpu.roll(block, size, 1)], axis=0)
        size *= 2
    return block


def unskew_sum(grid):
    size = grid.shape[0] // 2
    while size >= 8:
        grid = grid[:size] + pltpu.roll(grid[size:], 512 - size, 1)
        size //= 2
    sub = lax.broadcasted_iota(jnp.int32, (8, 512), 0)
    for bit in (1, 2, 4):
        grid = jnp.where((sub // bit) % 2 == 1, pltpu.roll(grid, 512 - bit, 1), grid)
    return jnp.sum(grid, axis=0, keepdims=True)


def tile_ranges(start, count, parts):
    ranges = []
    for n in range(parts, 0, -1):
        size = -(-count // n)
        ranges.append((128 * start, 128 * size))
        start, count = start + size, count - size
    return ranges


def joined(orders, pair, stage):
    one, two = orders
    if one[stage] == two[stage] and set(one[:stage]) == set(two[:stage]):
        return [(pair[0][0], pair[0][1] + pair[1][1])]
    return list(pair)


class Gather:
    def __init__(self, cube, mine, bands, send_sem, recv_sem):
        self.cube, self.mine, self.bands = cube, mine, bands
        self.chunks = GATHER_CHUNKS
        self.send_sem, self.recv_sem = send_sem, recv_sem
        self.copies = {}
        self.events = list(GATHER_EVENTS)
        self.last = cube.digits - 1

    def start(self, n, stage):
        g, pair, kind = self.chunks[n]
        orders = (self.cube.gather_orders, self.cube.gather_late_orders)[kind]
        for half, columns in enumerate(joined(orders, pair, stage)):
            order = orders[half]
            done = order[:stage]
            index = tuple(
                slice(None) if k in done else self.mine[k] for k in range(self.cube.digits)
            )
            place = self.bands[g].at[index + (slice(None), pl.ds(*columns))]
            copy = remote(
                place,
                place,
                self.send_sem.at[n, half, stage],
                self.recv_sem.at[n, half, stage],
                self.cube.partner(order[stage]),
            )
            copy.start()
            self.copies[n, half, stage] = copy

    def begin(self):
        for n, stage in GATHER_BEGIN:
            self.start(n, stage)

    def advance(self, n, stage):
        for half in range(2):
            if (n, half, stage) in self.copies:
                self.copies[n, half, stage].wait_recv()
        if stage < self.last and (n, stage + 1) not in GATHER_HELD:
            self.start(n, stage + 1)
        for other in GATHER_AFTER.get((n, stage), ()):
            self.start(*other)

    def run_to(self, n, stage):
        while (n, stage) in self.events:
            self.advance(*self.events.pop(0))

    def finish(self):
        for copy in self.copies.values():
            copy.wait_send()


class Scatter:
    def __init__(self, cube, mine, bands, landed, outs, send_sem, recv_sem):
        self.cube, self.mine, self.landed = cube, mine, landed
        self.chunks = [(bands[g], outs[g], pair) for g, pair, _ in SCATTER_CHUNKS]
        self.orders = [cube.scatter_kinds[kind] for _, _, kind in SCATTER_CHUNKS]
        self.send_sem, self.recv_sem = send_sem, recv_sem
        self.copies = {}

    def start(self, n, stage):
        band, _, pair = self.chunks[n]
        for half, columns in enumerate(joined(self.orders[n], pair, stage)):
            order = self.orders[n][half]
            index = []
            for k in range(self.cube.digits):
                at = order.index(k)
                if at > stage:
                    index.append(slice(None))
                else:
                    index.append(1 - self.mine[k] if at == stage else self.mine[k])
            copy = remote(
                band.at[tuple(index) + (slice(None), pl.ds(*columns))],
                self.landed[(n * 2 + half) * self.cube.digits + stage],
                self.send_sem.at[n, half, stage],
                self.recv_sem.at[n, half, stage],
                self.cube.partner(order[stage]),
            )
            copy.start()
            self.copies[n, half, stage] = copy

    def add(self, n, half, stage):
        order = self.orders[n][half]
        band, out, pair = self.chunks[n]
        columns = pl.ds(*joined(self.orders[n], pair, stage)[half])
        free = [k for k in range(self.cube.digits) if order.index(k) > stage]
        extra = self.landed[(n * 2 + half) * self.cube.digits + stage]
        everything = (slice(None), columns)

        def one(i):
            digit = {
                k: lax.rem(i // (1 << (len(free) - 1 - m)), 2) for m, k in enumerate(free)
            }
            full = tuple(digit.get(k, self.mine[k]) for k in range(self.cube.digits)) + everything
            short = tuple(digit[k] for k in free) + (slice(None), slice(None))
            if free:
                band[full] = band[full] + extra[short]
            else:
                out[:, columns] = band[full].astype(jnp.float32) + extra[short].astype(jnp.float32)

        if free:
            pl.loop(0, 1 << len(free))(one)
        else:
            one(0)

    def advance(self, n, stage):
        for half in range(2):
            if (n, half, stage) in self.copies:
                self.copies[n, half, stage].wait_recv()
                self.add(n, half, stage)
        if stage + 1 < self.cube.digits:
            self.start(n, stage + 1)

    def finish(self):
        for copy in self.copies.values():
            copy.wait_send()


class Collect:
    def __init__(self, cube, tile, slots, send_sem, recv_sem):
        self.cube, self.tile, self.slots = cube, tile, slots
        self.send_sem, self.recv_sem = send_sem, recv_sem

    def make(self, i):
        to = self.cube.coords(lax.rem(self.cube.index() + i, self.cube.total))
        return remote(
            self.tile, self.slots.at[i], self.send_sem.at[i], self.recv_sem.at[i], to
        )

    def start(self):
        pl.loop(1, self.cube.total)(lambda i: self.make(i).start())
        self.slots[0] = self.tile[...]

    def arrive(self):
        pl.loop(1, self.cube.total)(lambda i: self.make(i).wait())

    def total(self):
        result = self.slots[0]
        for i in range(1, self.cube.total):
            result = result + self.slots[i]
        return result


def share_columns(j):
    place = j // 2 if j % 2 else 1 - j // 2
    return slice(FF * place, FF * (place + 1))


def matrix_of(d):
    return sum(jnp.where(d == OWNER_PLACES[i], i, 0) for i in range(8))


def pack_small(target, turn, rel, vec, depth):
    rows = target.shape[0]
    turn[...] = jnp.zeros_like(turn)
    turn[0:7, 0:rows] = vec[...]
    target[...] = jnp.zeros_like(target)
    target[0 : rel.shape[0], SMALL_REL : SMALL_REL + H] = rel[...]
    target[:, SMALL_VEC : SMALL_VEC + 7] = jnp.transpose(turn[...])[0:rows, 0:7]
    target[:, SMALL_DEPTH : SMALL_DEPTH + K] = depth[...]


OWNER_PLACES = (2, 3, 5, 4, 0, 1, 7, 6)


def owner_place(cube, t):
    return (OWNER_PLACES[t // 4] * (cube.dp_size // 8), t // 2 % 2, t % 2)


class Momenta:
    def __init__(self, cube, r):
        self.cube, self.r = cube, r
        self.me = cube.index()
        self.repeat = cube.dp_size // 8
        d = lax.axis_index("dp")
        self.is_owner = lax.rem(d, self.repeat) == 0
        self.matrix = matrix_of(d // self.repeat)
        self.quarter = lax.axis_index("seq") * 2 + lax.axis_index("shard")
        self.owned_index = self.matrix * 4 + self.quarter

    def holds(self, t):
        return jnp.logical_and(self.is_owner, self.owned_index == t)

    def rows(self, j):
        r = self.r
        if j < 4:
            old, share = ((r.m_up, r.m_down)[j // 2], (r.share_first, r.share_second)[j % 2])
            return old[:, FF * (j % 2) : FF * (j % 2 + 1)], share[:, share_columns(j)]
        start = STARTS[j] - STARTS[4]
        old = (r.m_qkv, r.m_out, r.m_glu, r.m_point)[j - 4]
        return old[...], r.share_middle[:, start : start + WIDTHS[j]]

    def copy(self, t):
        width = WIDTHS[t // 4] // 4
        r = self.r
        return remote(
            r.leaving.at[t, :, pl.ds(0, width)],
            r.owned.at[self.me, :, pl.ds(0, width)],
            r.m_send.at[t],
            r.m_recv.at[self.me],
            owner_place(self.cube, t),
        )

    def send(self, j):
        old, share = self.rows(j)
        value = (MOMENTUM * old + share).astype(jnp.bfloat16)
        width = WIDTHS[j] // 4
        for q in range(4):
            t = 4 * j + q
            part = value[:, width * q : width * (q + 1)]
            self.r.leaving[t, :, 0:width] = part
            pl.when(jnp.logical_not(self.holds(t)))(lambda t=t: self.copy(t).start())

            @pl.when(self.holds(t))
            def _(part=part, width=width):
                self.r.owned[self.me, :, 0:width] = part

    def receive(self):
        r, cube = self.r, self.cube

        def go(width):
            @pl.loop(1, cube.total)
            def _(i):
                source = lax.rem(self.me + i, cube.total)
                place = r.owned.at[source, :, pl.ds(0, width)]
                remote(
                    place, place, r.m_send.at[0], r.m_recv.at[source], cube.coords(source)
                ).wait_recv()

        pl.when(self.is_owner)(lambda: by_matrix(self.matrix, go))

    def back(self, i, width):
        r, cube = self.r, self.cube
        to = lax.rem(self.me + i, cube.total)
        return remote(
            r.solved.at[to, :, pl.ds(0, width)],
            r.returned.at[self.owned_index, :, pl.ds(0, width)],
            r.b_send.at[i],
            r.b_recv.at[self.owned_index],
            cube.coords(to),
        )

    def keep(self, width):
        r = self.r
        return pltpu.make_async_copy(
            r.solved.at[self.me, :, pl.ds(0, width)],
            r.returned.at[self.owned_index, :, pl.ds(0, width)],
            r.k_sem,
        )

    def send_back(self):
        r = self.r

        def go(width):
            pl.loop(1, self.cube.total)(lambda i: self.back(i, width).start())
            self.keep(width).start()

        pl.when(self.is_owner)(lambda: by_matrix(self.matrix, go))

    def receive_back(self):
        r = self.r
        for t in range(32):
            place = r.returned.at[t, :, pl.ds(0, WIDTHS[t // 4] // 4)]
            copy = remote(
                place, place, r.b_send.at[0], r.b_recv.at[t], owner_place(self.cube, t)
            )
            pl.when(jnp.logical_not(self.holds(t)))(copy.wait_recv)

    def finish(self):
        for t in range(32):
            pl.when(jnp.logical_not(self.holds(t)))(lambda t=t: self.copy(t).wait_send())

        def go(width):
            pl.loop(1, self.cube.total)(lambda i: self.back(i, width).wait_send())
            self.keep(width).wait()

        pl.when(self.is_owner)(lambda: by_matrix(self.matrix, go))


def symmetric_product(left, right):
    half = D // 2
    (lh, ll), (rh, rl) = left, right
    top = product((lh[:half], ll[:half]), right)
    corner = product((lh[half:], ll[half:]), (rh[:, half:], rl[:, half:]))
    low = jnp.concatenate([jnp.transpose(top[:, half:]), corner], axis=1)
    return jnp.concatenate([top, low], axis=0)


def short_product(left, right):
    half = D // 2
    (lh, ll), rh = left, right[0]
    top = matmul(lh[:half], rh) + matmul(ll[:half], rh)
    corner = matmul(lh[half:], rh[:, half:]) + matmul(ll[half:], rh[:, half:])
    low = jnp.concatenate([jnp.transpose(top[:, half:]), corner], axis=1)
    return jnp.concatenate([top, low], axis=0)


GRAM_SHARES = (
    ((0, 0), (0, 1), (0, 2), (0, 3), (3, 3)),
    ((1, 1), (1, 2), (1, 3), (2, 2), (2, 3)),
)


def orthogonalize(cube, r, squares):
    f32 = jnp.float32
    core, seq = lax.axis_index("shard"), lax.axis_index("seq")
    block = r.owned.reshape(D, BLOCK)
    lines = [slice(128 * i, 128 * (i + 1)) for i in range(4)]
    peers = (cube.partner(cube.levels + 1), cube.partner(cube.levels))
    count = len(GRAM_SHARES[0])

    def piece(step, n):
        source, target, peer = (
            (r.packed.at[1 - core, n], r.packed_in.at[0, n], peers[0]),
            (r.summed.at[n], r.packed_in.at[1, n], peers[1]),
            (r.whole.at[core, n], r.whole.at[core, n], peers[0]),
        )[step]
        return remote(source, target, r.n_send.at[step, n], r.n_recv.at[step, n], peer)

    for n in range(count):
        for share in range(2):
            i, j = GRAM_SHARES[share][n]
            r.packed[share, n] = matmul_right_t(block[lines[i], :], block[lines[j], :])
        piece(0, n).start()
    squares.start()
    for n in range(count):
        piece(0, n).wait()
        r.summed[n] = r.packed[core, n] + r.packed_in[0, n]
        piece(1, n).start()
    for n in range(count):
        piece(1, n).wait()
        r.whole[core, n] = r.summed[n] + r.packed_in[1, n]
        piece(2, n).start()
    for n in range(count):
        piece(2, n).wait()
    for share in range(2):
        for n, (i, j) in enumerate(GRAM_SHARES[share]):
            value = r.whole[share, n]
            r.gram[lines[i], lines[j]] = value
            if i != j:
                r.gram[lines[j], lines[i]] = jnp.transpose(value)
    row = lax.broadcasted_iota(jnp.int32, (D, D), 0)
    col = lax.broadcasted_iota(jnp.int32, (D, D), 1)
    eye = row == col
    gram = r.gram[...]
    square = jnp.sum(
        jnp.sum(jnp.where(eye, gram, 0.0), axis=1, keepdims=True), axis=0, keepdims=True
    )
    scale = 1.0 / (jnp.sqrt(square) + 1e-07)
    gram = gram * (scale * scale)
    value = None
    for step in range(4):
        parts = split(gram)
        mixed = COEF_B * gram + COEF_C * symmetric_product(parts, parts)
        mixed = jnp.where(eye, mixed + COEF_A, mixed)
        high, low = split(mixed)
        if step == 0:
            start_high, start_low = split(mixed * scale)
            value = matmul(start_high, block[...]) + matmul(start_low, block[...])
        elif step < 3:
            value = product((high, low), split(value))
        else:
            value = matmul(high, value.astype(jnp.bfloat16))
        times = symmetric_product if step < 3 else short_product
        gram = times((high, low), split(times((high, low), parts)))
    short = gram.astype(jnp.bfloat16)
    mixed = COEF_B * gram + COEF_C * matmul(short, short)
    mixed = jnp.where(eye, mixed + COEF_A, mixed).astype(jnp.bfloat16)
    value = matmul(mixed, value.astype(jnp.bfloat16))
    r.solved.reshape(D, BLOCK)[...] = value.astype(jnp.bfloat16)


SMALL_REL, SMALL_VEC, SMALL_DEPTH = 0, H, H + 7
SMALL_END = H + 7 + K
EDGE = 16
GATHER_CHUNKS = (
    (0, tile_ranges(0, 17, 2), 0),
    (0, tile_ranges(17, 16, 2), 0),
    (1, tile_ranges(0, 20, 2), 0),
    (2, tile_ranges(0, 16, 2), 0),
    (1, tile_ranges(20, 8, 2), 1),
    (2, tile_ranges(16, 16, 2), 1),
)
GATHER_BEGIN = ((0, 0), (4, 0),)
GATHER_EVENTS = (
    ((4, 0), (0, 0), (4, 1), (5, 0), (5, 1), (0, 1), (1, 0), (0, 2), (1, 1), (2, 0))
    + ((2, 1), (3, 0), (1, 2), (0, 3), (0, 4), (4, 2), (3, 1), (2, 2), (1, 3), (1, 4))
    + ((5, 2), (3, 2), (2, 3), (4, 3), (4, 4), (2, 4), (3, 3), (3, 4), (5, 3), (5, 4))
)
SCATTER_EVENTS = (
    ((0, 1), (3, 0), (1, 1), (4, 0), (2, 1), (5, 0), (3, 1), (6, 1), (0, 2), (1, 2), (4, 1))
    + ((2, 2), (5, 1), (6, 2), (3, 2), (1, 3), (2, 3), (0, 3), (4, 2), (3, 3), (1, 4), (2, 4))
    + ((0, 4), (5, 2), (6, 3), (4, 3), (3, 4), (6, 4), (5, 3), (4, 4), (5, 4))
)
SCATTER_STORES = ((4,), (), (), (), (), (2,), (3,))
EARLY_LOADS = tuple("w_up w_down w_qkv w_out".split()) + tuple("w_glu w_point rel vec".split())
EARLY_LOADS += tuple("depth m_rel m_vec m_depth".split())
SCATTER_MATRICES = ((3,), (1,), (5,), (4,), (2,), (0,), (6, 7))
GATHER_HELD = ((4, 2), (5, 2),)
GATHER_AFTER = {
    (4, 0): [(5, 0)],
    (0, 0): [(1, 0)],
    (1, 0): [(2, 0)],
    (2, 0): [(3, 0)],
    (2, 1): [(4, 2)],
    (4, 2): [(5, 2)],
}
FIRST_READY, MIDDLE_READY, SECOND_READY = (1, 4), (2, 4), (5, 4)
SCATTER_CHUNKS = (
    (0, tile_ranges(16, 16, 2), 1),
    (0, tile_ranges(0, 16, 2), 2),
    (1, tile_ranges(12, 4, 2), 0),
    (1, tile_ranges(0, 12, 2), 0),
    (2, tile_ranges(0, 16, 2), 0),
    (2, tile_ranges(16, 17, 2), 0),
    (1, tile_ranges(16, 12, 2), 1),
)


def step_kernel(cube, r):
    bf16, f32 = jnp.bfloat16, jnp.float32
    x_ref, cot_ref, bucket_ref = r.inputs, r.cotangent, r.bucket
    tokens = x_ref.shape[0]
    token_total = tokens * cube.total
    rows = r.w_up.shape[0]
    rel_rows = r.rel.shape[0]
    mine = cube.mine()
    seq = lax.axis_index("seq")
    early = seq == 0
    first_row = pl.multiple_of(seq * tokens, tokens)
    other_row = pl.multiple_of((1 - seq) * tokens, tokens)
    across = cube.partner(cube.levels)
    lengths = [ref.shape[-1] for ref in (r.first, r.middle, r.second)]
    first, middle, second, d_first, d_middle, d_second = (
        ref.reshape(D, ref.shape[-1])
        for ref in (r.first, r.middle, r.second, r.d_first, r.d_middle, r.d_second)
    )
    a, xh = r.a, r.xh

    barrier = pltpu.get_barrier_semaphore()
    me = cube.index()
    momenta = Momenta(cube, r)
    for load in r.loads.values():
        load.start()
    r.owned[...] = jnp.zeros_like(r.owned)

    @pl.loop(1, cube.total)
    def _(i):
        peer = cube.coords(lax.rem(me + i, cube.total))
        pl.semaphore_signal(barrier, inc=1, device_id=peer, device_id_type=MESH)

    for name in EARLY_LOADS:
        r.loads[name].wait()
    pack_small(r.small, r.turn, r.rel, r.vec, r.depth)
    pack_small(r.m_small, r.turn, r.m_rel, r.m_vec, r.m_depth)
    own = tuple(mine)
    r.first[own + (slice(None), slice(FF, 2 * FF))] = r.w_up[:, :FF].astype(bf16)
    r.first[own + (slice(None), slice(0, FF))] = r.w_down[:, :FF].astype(bf16)
    r.first[own + (slice(None), slice(2 * FF, lengths[0]))] = r.small[...].astype(bf16)
    r.middle[own + (slice(None), slice(0, 3 * D))] = r.w_qkv[...].astype(bf16)
    r.middle[own + (slice(None), slice(3 * D, 4 * D))] = r.w_out[...].astype(bf16)
    r.middle[own + (slice(None), slice(4 * D, 6 * D))] = r.w_glu[...].astype(bf16)
    r.middle[own + (slice(None), slice(6 * D, 7 * D))] = r.w_point[...].astype(bf16)
    r.second[own + (slice(None), slice(0, FF))] = r.w_up[:, FF:].astype(bf16)
    r.second[own + (slice(None), slice(FF, 2 * FF))] = r.w_down[:, FF:].astype(bf16)
    pl.semaphore_wait(barrier, cube.total - 1)

    gather = Gather(
        cube, mine, (r.first, r.middle, r.second), r.g_send, r.g_recv
    )
    scatter = Scatter(
        cube,
        mine,
        (r.d_second, r.d_middle, r.d_first),
        r.land,
        (r.share_second, r.share_middle, r.share_first),
        r.s_send,
        r.s_recv,
    )

    gather.begin()
    for name in [name for name in r.loads if name not in EARLY_LOADS]:
        r.loads[name].wait()
    xh0, inv0 = normalize(x_ref[...])
    xh[0] = xh0
    rho = lax.broadcasted_iota(jnp.int32, (D, bucket_ref.shape[1]), 0)
    bucket_of = jnp.where(rho % rows < rel_rows, (rho // rows) * rel_rows + rho % rows, -2)
    r.hit[...] = jnp.zeros_like(r.hit)
    offset_count = bucket_ref.shape[1]
    r.hit[:, 0:offset_count] = (bucket_ref[...] == bucket_of).astype(f32).astype(bf16)
    gather.run_to(*FIRST_READY)

    small = r.small_t
    small[...] = jnp.transpose(first[:, 2 * FF : 2 * FF + 128].astype(f32))
    gains = [small[SMALL_VEC + i : SMALL_VEC + i + 1, :] for i in range(7)]
    taps = [small[SMALL_DEPTH + k : SMALL_DEPTH + k + 1, :] for k in range(K)]
    CH = 512

    def ffn_forward_fused(index, field, normed, up, down, u_ref, s_ref):
        low = (normed * gains[(0, 1, 2, 3)[index]]).astype(bf16)
        a[index] = low
        for c in range(0, FF, CH):
            u = matmul(low, up[:, c : c + CH])
            u_ref[:, c : c + CH] = u
            s_ref[:, c : c + CH] = (u * jax.nn.sigmoid(u)).astype(bf16)
        return field + 0.5 * matmul_right_t(s_ref[...], down[...])

    down1, up1 = first.at[:, pl.ds(0, FF)], first.at[:, pl.ds(FF, FF)]
    up2, down2 = second.at[:, pl.ds(0, FF)], second.at[:, pl.ds(FF, FF)]
    section1 = ffn_forward_fused(0, x_ref[...], xh[0], up1, down1, r.u1, r.s1)
    r.sec1[...] = section1
    xh1, inv1 = normalize(section1)
    xh[1] = xh1
    a[1] = (xh1 * gains[1]).astype(bf16)
    offsets = matmul(small[0:8, :].astype(bf16), r.hit[...])
    offsets = jnp.where(
        early, pltpu.roll(offsets, 257, 1), pltpu.roll(offsets, (tokens + 257) % 512, 1)
    )
    for h in range(H):
        r.bias[h] = skew(offsets[h : h + 1, :], tokens)[:, : 2 * tokens]
    gather.run_to(*MIDDLE_READY)

    q_ref, kv = r.q, r.kv
    kv_copies = []
    for n in range(2):
        place = kv.at[pl.ds(first_row, tokens), pl.ds(D * n, D)]
        place[...] = matmul(a[1], middle[:, D * (n + 1) : D * (n + 2)]).astype(bf16)
        copy = remote(place, place, r.kv_send.at[n], r.kv_recv.at[n], across)
        copy.start()
        kv_copies.append(copy)
    q_ref[...] = matmul(a[1], middle[:, :D]).astype(bf16)
    gather.run_to(*(2, 4))
    kv_copies[0].wait_recv()
    gather.run_to(*(3, 3))
    lane = lax.broadcasted_iota(jnp.int32, (1, 128), 1)
    lane_masks = [(lane // DH == e).astype(f32) for e in range(2)]
    low_masks = [m.astype(bf16) for m in lane_masks]
    scale = DH ** (-0.5)
    for p in range(H // 2):
        columns = slice(128 * p, 128 * (p + 1))
        k_pair = kv[:, columns]
        merged = None
        for e in range(2):
            q_head = q_ref[:, columns] * low_masks[e]
            scores = matmul_right_t(q_head, k_pair) * scale + r.bias[2 * p + e]
            shifted = jnp.exp(scores - jnp.max(scores, axis=1, keepdims=True))
            prob = shifted / jnp.sum(shifted, axis=1, keepdims=True)
            r.prob[2 * p + e] = prob
            if p + e == 0:
                kv_copies[1].wait_recv()
            v_pair = kv[:, D + 128 * p : D + 128 * (p + 1)]
            out = matmul(prob.astype(bf16), v_pair) * lane_masks[e]
            merged = out if merged is None else merged + out
        r.att[:, columns] = merged
        if p == 1:
            gather.run_to(*(3, 4))
    gather.run_to(*SECOND_READY)
    att_low = r.att[...].astype(bf16)
    r.att_low[...] = att_low
    section2 = r.sec1[...] + matmul(att_low, middle[:, 3 * D : 4 * D])
    r.sec2[...] = section2
    xh2, inv2 = normalize(section2)
    xh[2] = xh2
    a[2] = (xh2 * gains[2]).astype(bf16)
    gate_first = matmul(a[2], middle[:, 4 * D : 5 * D])
    sig = jax.nn.sigmoid(matmul(a[2], middle[:, 5 * D : 6 * D]))
    r.gate[...] = gate_first
    r.sig[...] = sig
    wide = r.wide
    wide[EDGE : EDGE + tokens, :] = gate_first * sig
    edge_row = pl.multiple_of(EDGE + (1 - seq) * (tokens - EDGE), EDGE)
    halo_copy = remote(
        wide.at[pl.ds(edge_row, EDGE)], r.halo, r.halo_send, r.halo_recv, across
    )
    halo_copy.start()
    zero_edge = jnp.zeros((EDGE, D), f32)
    wide[0:EDGE, :] = zero_edge
    wide[EDGE + tokens :, :] = zero_edge
    conv_ref = r.conv
    for b in range(D // 128):
        cols = slice(128 * b, 128 * (b + 1))
        total = jnp.zeros((tokens, 128), f32)
        for k in range(K):
            total = total + wide[k + 1 : k + 1 + tokens, cols] * taps[k][:, cols]
        conv_ref[:, cols] = total
    halo_copy.wait()
    rim = r.rim
    rim[...] = jnp.zeros_like(rim)
    rim[0:EDGE, :] = jnp.where(early, zero_edge, r.halo[...])
    rim[3 * EDGE :, :] = jnp.where(early, r.halo[...], zero_edge)
    wide[0:EDGE, :] = rim[0:EDGE, :]
    wide[EDGE + tokens :, :] = rim[3 * EDGE :, :]
    for b in range(D // 128):
        cols = slice(128 * b, 128 * (b + 1))
        before = jnp.zeros((EDGE, 128), f32)
        after = jnp.zeros((EDGE, 128), f32)
        for k in range(K // 2):
            before = before + rim[k + 1 : k + 1 + EDGE, cols] * taps[k][:, cols]
        for k in range(K // 2 + 1, K):
            after = after + rim[k + 17 : k + 17 + EDGE, cols] * taps[k][:, cols]
        conv_ref[0:EDGE, cols] = conv_ref[0:EDGE, cols] + before
        conv_ref[tokens - EDGE :, cols] = conv_ref[tokens - EDGE :, cols] + after
    conv = conv_ref[...]
    part_sum = jnp.sum(conv, axis=0, keepdims=True)
    part_off = conv - part_sum * (1.0 / tokens)
    part_square = jnp.sum(part_off * part_off, axis=0, keepdims=True)
    row_to_tile(r.tile1, 0, part_sum)
    row_to_tile(r.tile1, 4, part_square)
    stats = Collect(cube, r.tile1, r.slots1, r.c1_send, r.c1_recv)
    stats.start()
    stats.arrive()
    sums = stats.total()
    mean4 = sums[0:4] * (1.0 / token_total)
    spread4 = jnp.zeros((4, 128), f32)
    for i in range(cube.total):
        off = r.slots1[i][0:4] * (1.0 / tokens) - mean4
        spread4 = spread4 + off * off
    var4 = (sums[4:8] + spread4 * tokens) * (1.0 / token_total)
    mean = tile_to_row(mean4)
    inv_std = tile_to_row(lax.rsqrt(var4 + EPS_BATCH))

    xb = (conv_ref[...] - mean) * inv_std
    r.xb[...] = xb
    bn = xb * gains[5] + gains[6]
    r.bn[...] = bn
    sw = (bn * jax.nn.sigmoid(bn)).astype(bf16)
    r.sw[...] = sw
    section3 = r.sec2[...] + matmul(sw, middle[:, 6 * D : 7 * D])
    xh3, inv3 = normalize(section3)
    xh[3] = xh3
    section4 = ffn_forward_fused(3, section3, xh3, up2, down2, r.u2, r.s2)
    xh4, inv4 = normalize(section4)
    r.outputs[...] = xh4 * gains[4]
    r.stores[0].start()

    sg = r.small_grad
    sg[...] = jnp.zeros_like(sg)
    cot = cot_ref[...]
    d4, sg[SMALL_VEC + 4 : SMALL_VEC + 5, :] = norm_grad(cot, xh4, inv4, gains[4])

    def slope(value):
        sigma = jax.nn.sigmoid(value)
        return sigma * (1.0 + value * (1.0 - sigma))

    def slopes(low, down, u_ref, du_ref):
        for c in range(0, FF, CH):
            act = matmul(low, down[:, c : c + CH])
            du_ref[:, c : c + CH] = (act * slope(u_ref[:, c : c + CH])).astype(bf16)

    def weight_grad(left, right_ref, target, start, width):
        for c in range(0, width, CH):
            target[:, start + c : start + c + CH] = matmul_left_t(
                left, right_ref[:, c : c + CH]
            ).astype(bf16)

    r.e_low[...] = (0.5 * d4).astype(bf16)
    slopes(r.e_low[...], down2, r.u2, r.du)
    back = matmul_right_t(r.du[...], up2[...])
    part, sg[SMALL_VEC + 3 : SMALL_VEC + 4, :] = norm_grad(back, xh[3], inv3, gains[3])
    d3 = d4 + part
    r.d[...] = d3
    e3 = d3.astype(bf16)
    r.e3[...] = e3
    dbn = matmul_right_t(e3, middle[:, 6 * D : 7 * D]) * slope(r.bn[...])
    xb = r.xb[...]
    sg[SMALL_VEC + 5 : SMALL_VEC + 6, :] = jnp.sum(dbn * xb, axis=0, keepdims=True)
    sg[SMALL_VEC + 6 : SMALL_VEC + 7, :] = jnp.sum(dbn, axis=0, keepdims=True)
    dxb = dbn * gains[5]
    r.dxb[...] = dxb
    row_to_tile(r.tile2, 0, jnp.sum(dxb, axis=0, keepdims=True))
    row_to_tile(r.tile2, 4, jnp.sum(dxb * xb, axis=0, keepdims=True))
    sums2 = Collect(cube, r.tile2, r.slots2, r.c2_send, r.c2_recv)
    sums2.start()
    token_edge = pl.multiple_of((1 - seq) * (tokens - EDGE), EDGE)
    edges = r.edges
    edges[0:EDGE, :] = r.dxb[pl.ds(token_edge, EDGE), :]
    edges[EDGE:, :] = r.xb[pl.ds(token_edge, EDGE), :]
    edge_copy = remote(edges, r.edges_in, r.edge_send, r.edge_recv, across)
    edge_copy.start()

    weight_grad(r.e_low[...], r.s2, d_second, FF, FF)
    scatter.start(0, 0)
    weight_grad(a[3], r.du, d_second, 0, FF)
    scatter.start(1, 0)
    weight_grad(r.sw[...], r.e3, d_middle, 6 * D, D)
    edge_copy.wait()
    sums2.arrive()
    total2 = sums2.total()
    mean1 = tile_to_row(total2[0:4] * (1.0 / token_total))
    mean2 = tile_to_row(total2[4:8] * (1.0 / token_total))
    dwide = r.dwide
    dwide[EDGE : EDGE + tokens, :] = inv_std * (r.dxb[...] - mean1 - r.xb[...] * mean2)
    edge = inv_std * (r.edges_in[0:EDGE, :] - mean1 - r.edges_in[EDGE:, :] * mean2)
    dwide[0:EDGE, :] = jnp.where(early, zero_edge, edge)
    dwide[EDGE + tokens :, :] = jnp.where(early, edge, zero_edge)
    dglu_ref = r.conv
    for b in range(D // 128):
        cols = slice(128 * b, 128 * (b + 1))
        total = jnp.zeros((tokens, 128), f32)
        for k in range(K):
            total = total + dwide[31 - k : 31 - k + tokens, cols] * taps[k][:, cols]
        dglu_ref[:, cols] = total
    dglu, sig = dglu_ref[...], r.sig[...]
    r.dgates[:, :D] = (dglu * sig).astype(bf16)
    r.dgates[:, D:] = (dglu * r.gate[...] * sig * (1.0 - sig)).astype(bf16)
    scatter.advance(0, 0)
    back = matmul_right_t(r.dgates[...], middle[:, 4 * D : 6 * D])
    part, sg[SMALL_VEC + 2 : SMALL_VEC + 3, :] = norm_grad(back, xh[2], inv2, gains[2])
    d2 = r.d[...] + part
    r.d[...] = d2
    e1 = d2.astype(bf16)
    r.e_low[...] = e1
    dob = matmul_right_t(e1, middle[:, 3 * D : 4 * D]).astype(bf16)
    r.dob[...] = dob
    weight_grad(r.att_low[...], r.e_low, d_middle, 3 * D, D)
    weight_grad(a[2], r.dgates, d_middle, 4 * D, 2 * D)
    scatter.start(2, 0)
    scatter.start(6, 0)

    off_rows = []
    give, keep, got = r.give, r.keep, r.got
    kv_grads = []
    for p in range(H // 2):
        columns = slice(128 * p, 128 * (p + 1))
        k_pair, v_pair = kv[:, columns], kv[:, D + 128 * p : D + 128 * (p + 1)]
        att_pair = r.att[:, columns]
        dq = dk = dv = None
        for e in range(2):
            h = 2 * p + e
            dob_head = r.dob[:, columns] * low_masks[e]
            q_head = q_ref[:, columns] * low_masks[e]
            delta = jnp.sum(dob_head.astype(f32) * att_pair, axis=1, keepdims=True)
            prob = r.prob[h]
            ds = prob * (matmul_right_t(dob_head, v_pair) - delta)
            ds_low = ds.astype(bf16)
            dv_head = matmul_left_t(prob.astype(bf16), dob_head)
            dk_head = matmul_left_t(ds_low, q_head) * scale
            dq_head = matmul(ds_low, k_pair) * (lane_masks[e] * scale)
            dv = dv_head if dv is None else dv + dv_head
            dk = dk_head if dk is None else dk + dk_head
            dq = dq_head if dq is None else dq + dq_head
            padded = jnp.concatenate([ds, jnp.zeros((tokens, 512 - 2 * tokens), f32)], axis=1)
            off_rows.append(unskew_sum(padded))
        r.dqkv[:, columns] = dq.astype(bf16)
        for n, value in enumerate((dk, dv)):
            r.dkv[n] = value
            give[p, n] = r.dkv[n, pl.ds(other_row, tokens), :].astype(bf16)
            keep[p, n] = r.dkv[n, pl.ds(first_row, tokens), :]
        copy = remote(
            give.at[p], got.at[p], r.dkv_send.at[p], r.dkv_recv.at[p], across
        )
        copy.start()
        kv_grads.append(copy)
        if p == 1:
            scatter.advance(1, 0)
    off = jnp.concatenate(off_rows, axis=0)
    off = jnp.where(early, pltpu.roll(off, 255, 1), pltpu.roll(off, 255 - tokens, 1))
    off_high, off_low = split(off)
    sg[0:8, :] = matmul_right_t(off_high, r.hit[...]) + matmul_right_t(off_low, r.hit[...])
    for b in range(D // 128):
        cols = slice(128 * b, 128 * (b + 1))
        dconv = dwide[EDGE : EDGE + tokens, cols]
        for k in range(K):
            sg[SMALL_DEPTH + k : SMALL_DEPTH + k + 1, cols] = jnp.sum(
                dconv * wide[k + 1 : k + 1 + tokens, cols], axis=0, keepdims=True
            )
    for p in range(H // 2):
        kv_grads[p].wait()
        for n in range(2):
            at = D * (n + 1) + 128 * p
            r.dqkv[:, at : at + 128] = (keep[p, n] + got[p, n].astype(f32)).astype(bf16)
    scatter.advance(2, 0)
    scatter.advance(6, 0)
    back = matmul_right_t(r.dqkv[...], middle[:, : 3 * D])
    part, sg[SMALL_VEC + 1 : SMALL_VEC + 2, :] = norm_grad(back, xh[1], inv1, gains[1])
    d1 = r.d[...] + part
    e0 = (0.5 * d1).astype(bf16)
    weight_grad(a[1], r.dqkv, d_middle, 0, 3 * D)
    scatter.start(3, 0)
    weight_grad(e0, r.s1, d_first, 0, FF)
    scatter.start(4, 0)
    slopes(e0, down1, r.u1, r.du)
    back = matmul_right_t(r.du[...], up1[...])
    part, sg[SMALL_VEC : SMALL_VEC + 1, :] = norm_grad(back, xh[0], inv0, gains[0])
    r.input_grad[...] = d1 + part
    r.stores[1].start()
    d_first[:, 2 * FF : 2 * FF + 128] = jnp.transpose(sg[...]).astype(bf16)
    weight_grad(a[0], r.du, d_first, FF, FF)
    scatter.start(5, 0)
    for n, stage in SCATTER_EVENTS:
        scatter.advance(n, stage)
        if stage == scatter.cube.digits - 1:
            for j in SCATTER_MATRICES[n]:
                momenta.send(j)
            for store in SCATTER_STORES[n]:
                r.stores[store].start()
    next_small = MOMENTUM * r.m_small[...] + r.share_first[:, 2 * FF :]
    r.tile3[...] = jnp.zeros_like(r.tile3)
    r.tile3[0:1, :] = jnp.sum(next_small * next_small, axis=0, keepdims=True)
    squares = Collect(cube, r.tile3, r.slots3, r.c3_send, r.c3_recv)
    momenta.receive()
    orthogonalize(cube, r, squares)
    momenta.send_back()
    squares.arrive()
    r.squares[...] = squares.total()
    r.stores[5].start()
    momenta.receive_back()
    momenta.finish()
    gather.finish()
    scatter.finish()
    for store in r.stores:
        store.wait()
    for copy in kv_copies:
        copy.wait_send()


def fused_step(cube, inputs, cotangent, weights, momenta, bucket, collective_id):
    bf16, f32 = jnp.bfloat16, jnp.float32
    tokens, rows = inputs.shape[0], weights[0].shape[0]
    widths = (2 * FF + 128, 7 * D, 2 * FF)
    lead = (2,) * cube.digits
    named = dict(
        inputs=inputs,
        cotangent=cotangent,
        w_up=weights[0],
        w_down=weights[1],
        w_qkv=weights[2],
        w_out=weights[3],
        w_glu=weights[4],
        w_point=weights[5],
        vec=weights[6],
        depth=weights[7],
        rel=weights[8],
        m_up=momenta[0],
        m_down=momenta[1],
        m_qkv=momenta[2],
        m_out=momenta[3],
        m_glu=momenta[4],
        m_point=momenta[5],
        m_vec=momenta[6],
        m_depth=momenta[7],
        m_rel=momenta[8],
        bucket=bucket,
    )
    outs = dict(
        outputs=jax.ShapeDtypeStruct((tokens, D), f32),
        input_grad=jax.ShapeDtypeStruct((tokens, D), f32),
        share_first=jax.ShapeDtypeStruct((rows, widths[0]), f32),
        share_middle=jax.ShapeDtypeStruct((rows, widths[1]), f32),
        share_second=jax.ShapeDtypeStruct((rows, widths[2]), f32),
        returned=jax.ShapeDtypeStruct((32, rows, BLOCK), bf16),
        squares=jax.ShapeDtypeStruct((8, 128), f32),
    )
    field = pltpu.VMEM((tokens, D), f32)
    low = pltpu.VMEM((tokens, D), bf16)
    wide_low = pltpu.VMEM((tokens, FF), bf16)
    wide_field = pltpu.VMEM((tokens + 2 * EDGE, D), f32)
    grid = pltpu.VMEM((H, tokens, 2 * tokens), f32)
    pairs = pltpu.VMEM((H // 2, 2, tokens, 128), bf16)
    tile = pltpu.VMEM((8, 128), f32)
    slots = pltpu.VMEM((cube.total, 8, 128), f32)
    stages = pltpu.SemaphoreType.DMA((7, 2, cube.digits))
    gather_stages = pltpu.SemaphoreType.DMA((6, 2, cube.digits))
    everyone = pltpu.SemaphoreType.DMA((cube.total,))
    single = pltpu.SemaphoreType.DMA
    bands = [pltpu.VMEM(lead + (rows, w), bf16) for w in widths]
    land = []
    for _, pair, kind in SCATTER_CHUNKS:
        for half in range(2):
            for stage in range(cube.digits):
                columns = joined(cube.scatter_kinds[kind], pair, stage)
                part = columns[half][1] if half < len(columns) else 0
                lead_shape = (2,) * (cube.digits - 1 - stage) + (rows, part)
                shape = lead_shape if part else (rows, 128)
                land.append(pltpu.VMEM(shape, bf16))
    scratch = dict(
        first=bands[0],
        middle=bands[1],
        second=bands[2],
        d_first=bands[0],
        d_middle=bands[1],
        d_second=bands[2],
        land=tuple(land),
        sec1=field,
        sec2=field,
        att=field,
        gate=field,
        sig=field,
        conv=field,
        xb=field,
        bn=field,
        dxb=field,
        d=field,
        q=low,
        att_low=low,
        sw=low,
        e_low=low,
        e3=low,
        dob=low,
        a=pltpu.VMEM((4, tokens, D), bf16),
        xh=pltpu.VMEM((4, tokens, D), f32),
        u1=pltpu.VMEM((tokens, FF), f32),
        u2=pltpu.VMEM((tokens, FF), f32),
        s1=wide_low,
        s2=wide_low,
        du=wide_low,
        kv=pltpu.VMEM((2 * tokens, 2 * D), bf16),
        bias=grid,
        prob=grid,
        wide=wide_field,
        dwide=wide_field,
        halo=pltpu.VMEM((EDGE, D), f32),
        rim=pltpu.VMEM((4 * EDGE, D), f32),
        edges=pltpu.VMEM((2 * EDGE, D), f32),
        edges_in=pltpu.VMEM((2 * EDGE, D), f32),
        dgates=pltpu.VMEM((tokens, 2 * D), bf16),
        dqkv=pltpu.VMEM((tokens, 3 * D), bf16),
        dkv=pltpu.VMEM((2, 2 * tokens, 128), f32),
        give=pairs,
        got=pairs,
        keep=pltpu.VMEM((H // 2, 2, tokens, 128), f32),
        small=pltpu.VMEM((rows, 128), f32),
        m_small=pltpu.VMEM((rows, 128), f32),
        turn=pltpu.VMEM((128, 128), f32),
        hit=pltpu.VMEM((D, 512), bf16),
        small_t=pltpu.VMEM((128, D), f32),
        small_grad=pltpu.VMEM((128, D), f32),
        tile1=tile,
        tile2=tile,
        slots1=slots,
        slots2=slots,
        tile3=tile,
        slots3=slots,
        leaving=pltpu.VMEM((32, rows, BLOCK), bf16),
        owned=pltpu.VMEM((cube.total, rows, BLOCK), bf16),
        solved=pltpu.VMEM((cube.total, rows, BLOCK), bf16),
        packed=pltpu.VMEM((2, 5, 128, 128), f32),
        packed_in=pltpu.VMEM((2, 5, 128, 128), f32),
        summed=pltpu.VMEM((5, 128, 128), f32),
        whole=pltpu.VMEM((2, 5, 128, 128), f32),
        gram=pltpu.VMEM((D, D), f32),
        m_send=pltpu.SemaphoreType.DMA((32,)),
        m_recv=everyone,
        b_send=everyone,
        b_recv=pltpu.SemaphoreType.DMA((32,)),
        n_send=pltpu.SemaphoreType.DMA((3, 5)),
        n_recv=pltpu.SemaphoreType.DMA((3, 5)),
        c3_send=everyone,
        c3_recv=everyone,
        g_send=gather_stages,
        g_recv=gather_stages,
        s_send=stages,
        s_recv=stages,
        c1_send=everyone,
        c1_recv=everyone,
        c2_send=everyone,
        c2_recv=everyone,
        kv_send=pltpu.SemaphoreType.DMA((2,)),
        kv_recv=pltpu.SemaphoreType.DMA((2,)),
        halo_send=single,
        halo_recv=single,
        edge_send=single,
        edge_recv=single,
        dkv_send=pltpu.SemaphoreType.DMA((H // 2,)),
        dkv_recv=pltpu.SemaphoreType.DMA((H // 2,)),
    )

    kept = [n for n in outs if n != "returned"]
    buffers = dict({n: pltpu.VMEM(v.shape, v.dtype) for n, v in named.items()})
    buffers |= {n: pltpu.VMEM(outs[n].shape, outs[n].dtype) for n in kept}
    scratch |= buffers
    scratch |= dict(
        load_sem=pltpu.SemaphoreType.DMA((len(named),)),
        store_sem=pltpu.SemaphoreType.DMA((len(kept),)),
        k_sem=single,
    )

    def body(*refs):
        count = len(named) + len(outs)
        far = dict(zip(list(named) + list(outs), refs[:count]))
        near = dict(zip(scratch, refs[count:]))
        near["returned"] = far["returned"]
        near["loads"] = {
            name: pltpu.make_async_copy(far[name], near[name], near["load_sem"].at[n])
            for n, name in enumerate(named)
        }
        near["stores"] = [
            pltpu.make_async_copy(near[name], far[name], near["store_sem"].at[n])
            for n, name in enumerate(kept)
        ]
        step_kernel(cube, types.SimpleNamespace(**near))

    return pl.pallas_call(
        body,
        out_shape=list(outs.values()),
        in_specs=[pl.BlockSpec(memory_space=pl.ANY)] * len(named),
        out_specs=[pl.BlockSpec(memory_space=pl.ANY)] * len(outs),
        scratch_shapes=list(scratch.values()),
        compiler_params=pltpu.CompilerParams(
            collective_id=collective_id, has_side_effects=True, vmem_limit_bytes=60 << 20
        ),
        name="block_step",
    )(*named.values())


def finish_kernel(r):
    f32 = jnp.float32
    for load in r.loads:
        load.start()
    for load in r.loads[:5]:
        load.wait()
    share_first, share_middle, share_second, returned, squares = r.results
    for j in range(8):
        width = WIDTHS[j]
        if j < 4:
            columns = slice(FF * (j % 2), FF * (j % 2 + 1))
            grad = (share_first, share_second)[j % 2][:, share_columns(j)]
        else:
            columns = slice(0, width)
            start = STARTS[j] - STARTS[4]
            grad = share_middle[:, start : start + width]
        n = j // 2 if j < 4 else j - 2
        if j not in (1, 3):
            r.loads[5 + n].wait()
            r.loads[14 + n].wait()
        updated = MOMENTUM * r.moment[n][:, columns] + grad
        r.grad[n][:, columns] = grad
        r.next[n][:, columns] = updated
        solved = [returned[4 * j + q, :, 0 : width // 4].astype(f32) for q in range(4)]
        r.new[n][:, columns] = r.weight[n][:, columns] - RATE_MATRIX * jnp.concatenate(
            solved, axis=1
        )
        if j not in (0, 2):
            for store in (r.stores[n], r.stores[9 + n], r.stores[18 + n]):
                store.start()
    for n in (6, 7, 8):
        r.loads[5 + n].wait()
        r.loads[14 + n].wait()
    pack_small(r.small, r.turn, r.weight[8], r.weight[6], r.weight[7])
    pack_small(r.m_small, r.turn, r.moment[8], r.moment[6], r.moment[7])
    grad = share_first[:, 2 * FF :]
    updated = MOMENTUM * r.m_small[...] + grad
    lane = lax.broadcasted_iota(jnp.int32, (1, 128), 1)
    count = jnp.where(lane < SMALL_VEC, float(NB), float(D))
    scale = lax.rsqrt(squares[0:1, :] / count + EPS_SCALE)
    new = r.small[...] - RATE_VECTOR * updated * scale
    rows, rel_rows = r.small.shape[0], r.weight[8].shape[0]
    for value, outs in ((grad, r.grad), (new, r.new), (updated, r.next)):
        r.turn[...] = jnp.zeros_like(r.turn)
        r.turn[0:rows, :] = value
        turned = jnp.transpose(r.turn[...])
        outs[6][...] = turned[SMALL_VEC : SMALL_VEC + 7, 0:rows]
        outs[7][...] = value[:, SMALL_DEPTH : SMALL_DEPTH + K]
        outs[8][...] = value[0:rel_rows, SMALL_REL : SMALL_REL + H]
    for n in (6, 7, 8):
        for store in (r.stores[n], r.stores[9 + n], r.stores[18 + n]):
            store.start()
    for n in range(2):
        r.loads[23 + n].wait()
        r.stores[27 + n].start()
    for store in r.stores:
        store.wait()


def finish_step(fields, shares, returned, squares, weights, momenta):
    sources = (*shares, returned, squares, *weights, *momenta)
    operands = sources + tuple(fields)
    rows, count = weights[0].shape[0], len(sources)
    shapes = [jax.ShapeDtypeStruct(v.shape, v.dtype) for v in weights] * 3
    shapes += [jax.ShapeDtypeStruct(v.shape, v.dtype) for v in fields]

    def body(*refs):
        ins, refs = refs[: len(operands)], refs[len(operands) :]
        outs, refs = refs[: len(shapes)], refs[len(shapes) :]
        near, refs = refs[: count + 2], refs[count + 2 :]
        made, refs = refs[:27], refs[27:]
        small, m_small, turn, sem = refs
        pairs = list(zip(ins, near)) + list(zip(made + near[-2:], outs))
        moves = [pltpu.make_async_copy(a, b, sem.at[n]) for n, (a, b) in enumerate(pairs)]
        finish_kernel(
            types.SimpleNamespace(
                loads=moves[: count + 2],
                stores=moves[count + 2 :],
                results=near[:5],
                weight=near[5:14],
                moment=near[14:23],
                grad=made[:9],
                new=made[9:18],
                next=made[18:27],
                small=small,
                m_small=m_small,
                turn=turn,
            ),
        )

    return pl.pallas_call(
        body,
        out_shape=shapes,
        in_specs=[pl.BlockSpec(memory_space=pl.ANY)] * len(operands),
        out_specs=[pl.BlockSpec(memory_space=pl.ANY)] * len(shapes),
        scratch_shapes=[pltpu.VMEM(v.shape, v.dtype) for v in list(operands) + shapes[:27]]
        + [
            pltpu.VMEM((rows, 128), jnp.float32),
            pltpu.VMEM((rows, 128), jnp.float32),
            pltpu.VMEM((128, 128), jnp.float32),
            pltpu.SemaphoreType.DMA((len(operands) + len(shapes),)),
        ],
        compiler_params=pltpu.CompilerParams(vmem_limit_bytes=60 << 20),
        name="finish_step",
    )(*operands)


def unfused_step(
    cube,
    inputs,
    cotangent,
    w_up,
    w_down,
    w_qkv,
    w_out,
    w_glu,
    w_point,
    small,
    bucket_table,
):
    bf16 = jnp.bfloat16
    rows = w_up.shape[0]
    rel_rows = NB // cube.total
    shard_groups = (
        jnp.concatenate([w_up[:, :FF], w_down[:, :FF], small], axis=1).astype(bf16),
        jnp.concatenate([w_qkv, w_out, w_glu, w_point], axis=1).astype(bf16),
        jnp.concatenate([w_up[:, FF:], w_down[:, FF:]], axis=1).astype(bf16),
    )
    first, middle, second = [
        full.reshape(D, -1) for full in gather_groups(cube, shard_groups, 0)
    ]
    up_first, down_first, small_low = first[:, :FF], first[:, FF : 2 * FF], first[:, 2 * FF :]
    qkv_w, out_w = middle[:, : 3 * D], middle[:, 3 * D : 4 * D]
    glu_w, point_w = middle[:, 4 * D : 6 * D], middle[:, 6 * D :]
    up_second, down_second = second[:, :FF], second[:, FF:]
    gains = small_low[:, SMALL_VEC : SMALL_VEC + 7].astype(jnp.float32)
    kernel = small_low[:, SMALL_DEPTH : SMALL_DEPTH + K].astype(jnp.float32)
    rel_low = small_low[:, :H].reshape(cube.total, rows, H)[:, :rel_rows].reshape(NB, H)
    bucket_hit = (bucket_table[:, None] == jnp.arange(NB, dtype=jnp.int32)[None, :]).astype(
        jnp.float32
    )
    offsets = jnp.dot(bucket_hit, rel_low.astype(jnp.float32), precision=HIGHEST).T
    seq_rows = inputs[0]
    row_count = seq_rows.shape[0]
    first_row = lax.axis_index("seq") * row_count
    token_total = row_count * lax.axis_size(("dp", "seq", "shard"))
    section_one, ffn_saved = ffn_forward(seq_rows, gains[:, 0], up_first, down_first)
    normed_out2, normed2, inverse2 = layer_norm(section_one, gains[:, 1])
    lifted2 = normed_out2.astype(bf16)
    projected = matmul(lifted2, qkv_w).astype(bf16)
    query = projected[:, :D]
    pair = [(0, 1), (1, 0)]
    other = lax.ppermute(projected[:, D:], "seq", pair)
    early = lax.axis_index("seq") == 0
    both = jnp.concatenate(
        [
            jnp.where(early, projected[:, D:], other),
            jnp.where(early, other, projected[:, D:]),
        ],
        axis=0,
    )
    keys, values = both[:, :D], both[:, D:]
    attended, log_total = attention_forward(query, keys, values, offsets, first_row)
    attended_low = attended.astype(bf16)
    section_two = section_one + matmul(attended_low, out_w)
    normed_out3, normed3, inverse3 = layer_norm(section_two, gains[:, 2])
    lifted3 = normed_out3.astype(bf16)
    gates = matmul(lifted3, glu_w)
    first_half = gates[:, :D]
    sig_gate = jax.nn.sigmoid(gates[:, D:])
    glu = first_half * sig_gate
    glu_wide = with_halo(glu, (("seq", 0),), K // 2)
    conv = depthwise(glu_wide, kernel, row_count)
    part_sum = jnp.sum(conv, axis=0)
    part_mean = part_sum / row_count
    part_square = jnp.sum(jnp.square(conv - part_mean), axis=0)
    stats = collect(cube, jnp.concatenate([part_sum, part_square]).reshape(8, 128), 1)
    stats = stats.reshape(cube.total, 2, D)
    mean = jnp.sum(stats[:, 0], axis=0) / token_total
    spread_of_means = jnp.square(stats[:, 0] / row_count - mean) * row_count
    variance = jnp.sum(stats[:, 1] + spread_of_means, axis=0) / token_total
    centred = conv - mean
    inv_std = lax.rsqrt(variance + EPS_BATCH)
    normed_bn = centred * inv_std
    batch_out = normed_bn * gains[:, 5] + gains[:, 6]
    swish_low = jax.nn.silu(batch_out).astype(bf16)
    section_three = section_two + matmul(swish_low, point_w)
    section_four, tail_saved = ffn_forward(
        section_three, gains[:, 3], up_second, down_second
    )
    outputs, normed5, inverse5 = layer_norm(section_four, gains[:, 4])
    grad_four, gain_four = norm_back(cotangent[0], normed5, inverse5, gains[:, 4])
    grad_three, grad_up_two, grad_down_two, gain_three = ffn_backward(
        grad_four, tail_saved, gains[:, 3], up_second, down_second
    )
    grad_three_low = grad_three.astype(bf16)
    grad_point = matmul_left_t(swish_low, grad_three_low)
    grad_batch = matmul_right_t(grad_three_low, point_w) * silu_slope(batch_out)
    grad_normed = grad_batch * gains[:, 5]
    sums = jnp.concatenate(
        [jnp.sum(grad_normed, axis=0), jnp.sum(grad_normed * normed_bn, axis=0)]
    )
    sums = jnp.sum(collect(cube, sums.reshape(8, 128), 2), axis=0).reshape(2, D)
    sum_normed, sum_cross = sums[0], sums[1]
    grad_conv = inv_std * (
        grad_normed - sum_normed / token_total - normed_bn * sum_cross / token_total
    )
    grad_wide = with_halo(grad_conv, (("seq", 0),), K // 2)
    grad_glu = grad_wide[K - 1 : K - 1 + row_count] * kernel[:, 0]
    for tap_idx in range(1, K):
        grad_glu = (
            grad_glu
            + grad_wide[K - 1 - tap_idx : K - 1 - tap_idx + row_count] * kernel[:, tap_idx]
        )
    grad_kernel = jnp.stack(
        [
            jnp.sum(grad_conv * glu_wide[tap_idx : tap_idx + row_count], axis=0)
            for tap_idx in range(K)
        ],
        axis=1,
    )
    grad_gates = jnp.concatenate(
        [grad_glu * sig_gate, grad_glu * first_half * sig_gate * (1.0 - sig_gate)], axis=1
    ).astype(bf16)
    grad_glu_w = matmul_left_t(lifted3, grad_gates)
    grad_two_part, gain_two = norm_back(
        matmul_right_t(grad_gates, glu_w), normed3, inverse3, gains[:, 2]
    )
    grad_two = grad_three + grad_two_part
    grad_two_low = grad_two.astype(bf16)
    grad_out_w = matmul_left_t(attended_low, grad_two_low)
    grad_attended = matmul_right_t(grad_two_low, out_w).astype(bf16)
    delta = jnp.sum(
        (grad_attended.astype(jnp.float32) * attended).reshape(row_count, H, DH), axis=2
    )
    query_grad, key_grad, value_grad, offset_grad = attention_backward(
        query, keys, values, offsets, first_row, log_total, grad_attended, delta
    )
    keys_grad = jnp.concatenate([key_grad, value_grad], axis=1)
    theirs = lax.dynamic_slice_in_dim(keys_grad, row_count - first_row, row_count, 0)
    own = lax.dynamic_slice_in_dim(keys_grad, first_row, row_count, 0)
    own = own + lax.ppermute(theirs, "seq", pair)
    key_own, value_own = own[:, :D], own[:, D:]
    grad_proj = jnp.concatenate([query_grad, key_own, value_own], axis=1).astype(bf16)
    grad_qkv_w = matmul_left_t(lifted2, grad_proj)
    grad_one_part, gain_one = norm_back(
        matmul_right_t(grad_proj, qkv_w), normed2, inverse2, gains[:, 1]
    )
    grad_one = grad_two + grad_one_part
    input_grad, grad_up_one, grad_down_one, gain_zero = ffn_backward(
        grad_one, ffn_saved, gains[:, 0], up_first, down_first
    )
    grad_vec_local = jnp.stack(
        [
            gain_zero,
            gain_one,
            gain_two,
            gain_three,
            gain_four,
            jnp.sum(grad_batch * normed_bn, axis=0),
            jnp.sum(grad_batch, axis=0),
        ],
        axis=1,
    )
    grad_rel_local = jnp.dot(bucket_hit.T, offset_grad.T, precision=HIGHEST)
    rel_padded = jnp.pad(
        grad_rel_local.reshape(cube.total, rel_rows, H), ((0, 0), (0, rows - rel_rows), (0, 0))
    )
    small_grads = jnp.concatenate(
        [rel_padded.reshape(D, H), grad_vec_local, grad_kernel], axis=1
    )
    small_grads = jnp.pad(small_grads, ((0, 0), (0, 128 - SMALL_END)))
    lead = (2,) * cube.digits
    grad_groups = [
        jnp.concatenate(group, axis=1).astype(bf16).reshape(lead + (rows, -1))
        for group in (
            (grad_up_two, grad_down_two),
            (grad_qkv_w, grad_out_w, grad_glu_w, grad_point),
            (grad_up_one, grad_down_one, small_grads),
        )
    ]
    share_second, share_middle, share_first = scatter_groups(cube, grad_groups, 3)
    return outputs, input_grad, share_first, share_middle, share_second


def local(
    cube,
    inputs,
    cotangent,
    w_up,
    w_down,
    w_qkv,
    w_out,
    w_glu,
    w_point,
    vectors,
    depth_kernel,
    rel_bias,
    bucket_table,
    m_up,
    m_down,
    m_qkv,
    m_out,
    m_glu,
    m_point,
    m_vectors,
    m_depth,
    m_rel,
):
    bf16 = jnp.bfloat16
    rows, rel_rows = w_up.shape[0], rel_bias.shape[0]
    pack = lambda rel, vec, depth: jnp.pad(
        jnp.concatenate([jnp.pad(rel, ((0, rows - rel_rows), (0, 0))), vec, depth], axis=1),
        ((0, 0), (0, 128 - SMALL_END)),
    )
    small = pack(rel_bias, vectors, depth_kernel)
    weights = (w_up, w_down, w_qkv, w_out, w_glu, w_point)
    if rows % 16 == 0 and cube.total == 32:
        bucket = bucket_table[None]
        weights += (vectors.T, depth_kernel, rel_bias)
        momenta = (m_up, m_down, m_qkv, m_out, m_glu, m_point, m_vectors.T, m_depth, m_rel)
        outputs, input_grad, *shares, returned, squares = fused_step(
            cube, inputs[0], cotangent[0], weights, momenta, bucket, 0
        )
        *rest, outputs, input_grad = finish_step(
            (outputs, input_grad), shares, returned, squares, weights, momenta
        )
        for n in (6, 15, 24):
            rest[n] = rest[n].T
        return (outputs[None], input_grad[None], *rest)
    outputs, input_grad, share_first, share_middle, share_second = unfused_step(
        cube, inputs, cotangent, *weights, small, bucket_table
    )
    grad_up = jnp.concatenate([share_first[:, :FF], share_second[:, :FF]], axis=1)
    grad_down = jnp.concatenate([share_first[:, FF : 2 * FF], share_second[:, FF:]], axis=1)
    grad_qkv, grad_out = share_middle[:, : 3 * D], share_middle[:, 3 * D : 4 * D]
    grad_glu, grad_pnt = share_middle[:, 4 * D : 6 * D], share_middle[:, 6 * D :]
    share_small = share_first[:, 2 * FF :]
    grad_vectors = share_small[:, SMALL_VEC : SMALL_VEC + 7]
    grad_depth = share_small[:, SMALL_DEPTH : SMALL_DEPTH + K]
    grad_rel = share_small[: rel_bias.shape[0], :H]
    next_m_up = MOMENTUM * m_up + grad_up
    next_m_down = MOMENTUM * m_down + grad_down
    next_m_qkv = MOMENTUM * m_qkv + grad_qkv
    next_m_out = MOMENTUM * m_out + grad_out
    next_m_glu = MOMENTUM * m_glu + grad_glu
    next_m_point = MOMENTUM * m_point + grad_pnt
    stacked = jnp.concatenate(
        [next_m_up, next_m_down, next_m_qkv, next_m_out, next_m_glu, next_m_point], axis=1
    )
    owned = spread(cube, stacked, 4).reshape(D, BLOCK)
    ortho = orthogonalize_blocks(cube, owned, bf16, 5)
    mine = restore(cube, ortho.reshape(cube.total, rows, BLOCK), 6).astype(jnp.float32)
    new_up = w_up - RATE_MATRIX * mine[:, : 2 * FF]
    new_down = w_down - RATE_MATRIX * mine[:, 2 * FF : 4 * FF]
    new_qkv = w_qkv - RATE_MATRIX * mine[:, STARTS[4] : STARTS[5]]
    new_out = w_out - RATE_MATRIX * mine[:, STARTS[5] : STARTS[6]]
    new_glu = w_glu - RATE_MATRIX * mine[:, STARTS[6] : STARTS[7]]
    new_point = w_point - RATE_MATRIX * mine[:, STARTS[7] :]
    next_m_vectors = MOMENTUM * m_vectors + grad_vectors
    next_m_depth = MOMENTUM * m_depth + grad_depth
    next_m_rel = MOMENTUM * m_rel + grad_rel
    squares = jnp.concatenate(
        [
            jnp.sum(next_m_vectors * next_m_vectors, axis=0),
            jnp.sum(next_m_depth * next_m_depth, axis=0),
            jnp.sum(next_m_rel * next_m_rel, axis=0),
        ]
    )
    squares = jnp.pad(squares, (0, 128 - squares.shape[0])).reshape(1, 128)
    squares = jnp.sum(collect(cube, jnp.pad(squares, ((0, 7), (0, 0))), 7), axis=0)[0]
    square_vec, square_depth = squares[:7], squares[7 : 7 + K]
    square_rel = squares[7 + K : 7 + K + H]
    new_vectors = vectors - RATE_VECTOR * next_m_vectors * lax.rsqrt(square_vec / D + EPS_SCALE)
    new_depth = depth_kernel - RATE_VECTOR * next_m_depth * lax.rsqrt(square_depth / D + EPS_SCALE)
    new_rel = rel_bias - RATE_VECTOR * next_m_rel * lax.rsqrt(square_rel / NB + EPS_SCALE)
    return (
        outputs[None],
        input_grad[None],
        grad_up,
        grad_down,
        grad_qkv,
        grad_out,
        grad_glu,
        grad_pnt,
        grad_vectors,
        grad_depth,
        grad_rel,
        new_up,
        new_down,
        new_qkv,
        new_out,
        new_glu,
        new_point,
        new_vectors,
        new_depth,
        new_rel,
        next_m_up,
        next_m_down,
        next_m_qkv,
        next_m_out,
        next_m_glu,
        next_m_point,
        next_m_vectors,
        next_m_depth,
        next_m_rel,
    )


def solution(mesh):
    placed = (
        P(("dp", "shard"), "seq", None),
        P(("dp", "shard"), "seq", None),
        P(("dp", "seq", "shard"), None),
        P(("dp", "seq", "shard"), None),
        P(("dp", "seq", "shard"), None),
        P(("dp", "seq", "shard"), None),
        P(("dp", "seq", "shard"), None),
        P(("dp", "seq", "shard"), None),
        P(("dp", "seq", "shard"), None),
        P(("dp", "seq", "shard"), None),
        P(("dp", "seq", "shard"), None),
        P(),
        P(("dp", "seq", "shard"), None),
        P(("dp", "seq", "shard"), None),
        P(("dp", "seq", "shard"), None),
        P(("dp", "seq", "shard"), None),
        P(("dp", "seq", "shard"), None),
        P(("dp", "seq", "shard"), None),
        P(("dp", "seq", "shard"), None),
        P(("dp", "seq", "shard"), None),
        P(("dp", "seq", "shard"), None),
    )
    return jax.shard_map(
        functools.partial(local, Cube(mesh.shape["dp"])),
        mesh=mesh,
        in_specs=placed,
        out_specs=(
            P(("dp", "shard"), "seq", None),
            P(("dp", "shard"), "seq", None),
            P(("dp", "seq", "shard"), None),
            P(("dp", "seq", "shard"), None),
            P(("dp", "seq", "shard"), None),
            P(("dp", "seq", "shard"), None),
            P(("dp", "seq", "shard"), None),
            P(("dp", "seq", "shard"), None),
            P(("dp", "seq", "shard"), None),
            P(("dp", "seq", "shard"), None),
            P(("dp", "seq", "shard"), None),
            P(("dp", "seq", "shard"), None),
            P(("dp", "seq", "shard"), None),
            P(("dp", "seq", "shard"), None),
            P(("dp", "seq", "shard"), None),
            P(("dp", "seq", "shard"), None),
            P(("dp", "seq", "shard"), None),
            P(("dp", "seq", "shard"), None),
            P(("dp", "seq", "shard"), None),
            P(("dp", "seq", "shard"), None),
            P(("dp", "seq", "shard"), None),
            P(("dp", "seq", "shard"), None),
            P(("dp", "seq", "shard"), None),
            P(("dp", "seq", "shard"), None),
            P(("dp", "seq", "shard"), None),
            P(("dp", "seq", "shard"), None),
            P(("dp", "seq", "shard"), None),
            P(("dp", "seq", "shard"), None),
            P(("dp", "seq", "shard"), None),
        ),
        check_vma=False,
    )
```
